128 devices in a mesh: tile: 32 (over x, z, core), member: 4 (over y).
Axes of the slice: x: 4, y: 4, z: 4, core: 2. Of those that a mesh axis runs over, the one named last changes fastest.
Arguments:
- log_perm: float32 [128, 4, 256, 256], P('member', None, 'tile'), may hold values from -3.4 to 3.4
- start_pressure: float32 [4, 256, 256], P(None, 'tile'), may hold values from -5 to 5
- start_sat: float32 [4, 256, 256], P(None, 'tile'), may hold values from 0.1 to 0.9
- source: float32 [4, 256, 256], P(None, 'tile'), may hold values from -5 to 5
- storage: float32 [4, 256, 256], P(None, 'tile'), may hold values from 0.05 to 0.5
- well_press: float32 [1024], replicated, may hold values from -4 to 4
- perf_cell: int32 [8192], P('tile'), may hold values from 0 to 8191
- perf_well: int32 [8192], P('tile'), may hold values from 0 to 1023
- perf_count: int32 [32], P('tile'), may hold values from 64 to 256, as said below
- observed: float32 [1024], replicated, may hold values from -8 to 8
- obs_var: float32 [1024], replicated, may hold values from 0.5 to 5
- obs_noise: float32 [128, 1024], P('member'), may hold values from -5 to 5
Outputs:
- new_log_perm: float32 [128, 4, 256, 256], P('member', None, 'tile')
- pressure: float32 [128, 4, 256, 256], P('member', None, 'tile')
- saturation: float32 [128, 4, 256, 256], P('member', None, 'tile')
- well_rates: float32 [128, 1024], P('member', 'tile')
The draws below stay inside these ranges and needn't reach their ends.
Inputs may be any that keep to these rules, and one draw needn't show every extreme that they name: `perf_count`: one strip has all 256 slots live.
All inputs are finite; a program needn't handle non-finite values.
Results may differ from the reference program's by a relative error of at most 0.017.
Values may be sent and summed in bfloat16 or wider, within the bound.
A program may use at most 64 MiB of HBM per device.

```python
import math
import jax
import jax.numpy as jnp
from jax import lax

LAYERS = 4
CX = 8
NY = 256
PERF_DEV = 256
SWEEPS = 2
MEMBERS = 128
NX = 256
WELLS = 1024
PERFS = 8192
N_TILE = 32


def draw_log_perm(key, part):
    mean_key = jax.random.fold_in(key, 11)
    member_key = jax.random.fold_in(key, 12)
    trend_field = jax.random.uniform(mean_key, (LAYERS, NX, NY), jnp.float32, -1.0, 1.0)
    deviation = jnp.clip(0.6 * jax.random.normal(member_key, (MEMBERS, LAYERS, NX, NY), jnp.float32), -2.4, 2.4)
    return trend_field[None] + deviation


def draw_perf_count(key, part):
    counts = jax.random.randint(jax.random.fold_in(key, 21), (N_TILE,), PERF_DEV // 4, PERF_DEV + 1)
    full_tile = jax.random.randint(jax.random.fold_in(key, 22), (), 0, N_TILE)
    return jnp.where(jnp.arange(N_TILE) == full_tile, PERF_DEV, counts).astype(jnp.int32)


def plant(result, own_key, least, top_value):
    dims = result.shape
    index_at = [jax.random.randint(jax.random.fold_in(own_key, axis), (), 0, dims[axis]) for axis in range(len(dims))]
    result = result.at[tuple(index_at)].set(least)
    longest = dims.index(max(dims))
    index_at[longest] = (index_at[longest] + 1) % dims[longest]
    return result.at[tuple(index_at)].set(top_value)


def steps_of(rng, shape, cuts, least, top_value):
    factor_of, own = 1.0, jax.random.fold_in(rng, 6)
    for axis_at, shards_of in cuts:
        draws = jnp.exp(jax.random.uniform(jax.random.fold_in(own, axis_at), (shards_of,), jnp.float32, least / len(cuts), top_value / len(cuts)))
        factor_of = factor_of * jnp.repeat(draws, shape[axis_at] // shards_of).reshape([-1 if axis == axis_at else 1 for axis in range(len(shape))])
    return factor_of


def centred(stream_key, shape, scale, bound, shards=(), kind=jnp.bfloat16):
    values = scale * jax.random.normal(stream_key, shape, jnp.float32)
    if shards:
        values = values * steps_of(stream_key, shape, shards, -0.22, 0.18)
    return jnp.clip(values, -bound, bound).astype(kind)


def setup_inputs(seed: int = 0) -> dict:
    arg_keys = jax.random.split(jax.random.key(seed), 13)
    log_perm = draw_log_perm(jax.random.fold_in(arg_keys[12], 71), 0)
    start_pressure = centred(arg_keys[1], (LAYERS, NX, NY), 1.0, 5.0, ((1, 32),), jnp.float32)
    start_sat = jnp.clip(0.1 + 0.79999997 * jax.random.uniform(arg_keys[2], (LAYERS, NX, NY), jnp.float32) ** steps_of(arg_keys[2], (LAYERS, NX, NY), ((1, 32),), -0.2, 0.2), 0.1, 0.9)
    source = centred(arg_keys[3], (LAYERS, NX, NY), 1.0, 5.0, ((1, 32),), jnp.float32)
    storage = jnp.clip(jnp.exp(math.log(0.5) - 2.3025851 * jax.random.uniform(arg_keys[4], (LAYERS, NX, NY), jnp.float32) ** steps_of(arg_keys[4], (LAYERS, NX, NY), ((1, 32),), -0.2, 0.2)), 0.05, 0.5)
    well_press = centred(arg_keys[5], (WELLS,), 1.0, 4.0, (), jnp.float32)
    perf_cell = plant(jax.random.randint(arg_keys[6], (PERFS,), 0, LAYERS * CX * NY), jax.random.fold_in(arg_keys[6], 1), 0, (LAYERS * CX * NY) - 1).astype(jnp.int32)
    perf_well = plant(jax.random.randint(arg_keys[7], (PERFS,), 0, WELLS), jax.random.fold_in(arg_keys[7], 1), 0, WELLS - 1).astype(jnp.int32)
    perf_count = draw_perf_count(jax.random.fold_in(arg_keys[12], 71), 0)
    observed = centred(arg_keys[9], (WELLS,), 2.0, 8.0, (), jnp.float32)
    obs_var = jnp.clip(jnp.exp(jax.random.uniform(arg_keys[10], (WELLS,), jnp.float32, math.log(0.5), math.log(5.0))), 0.5, 5.0)
    obs_noise = centred(arg_keys[11], (MEMBERS, WELLS), 1.0, 5.0, ((0, 4),), jnp.float32)
    return dict(log_perm=log_perm, start_pressure=start_pressure, start_sat=start_sat, source=source, storage=storage, well_press=well_press, perf_cell=perf_cell, perf_well=perf_well, perf_count=perf_count, observed=observed, obs_var=obs_var, obs_noise=obs_noise)


VERTICAL = 0.5
VISCOSITY_RATIO = 2.0
STEP_COEF = 0.1
INFLATION = 4.0

def harmonic(lower_val, upper_val):
    return 2.0 * lower_val * upper_val / (lower_val + upper_val)

def pad_face(values_in, along_dim, before):
    widths = [(0, 0)] * values_in.ndim
    widths[along_dim] = (1, 0) if before else (0, 1)
    return jnp.pad(values_in, widths)

def slide_by(values_in, along_dim, before):
    extent = values_in.shape[along_dim]
    if before:
        remain = lax.slice_in_dim(values_in, 0, extent - 1, axis=along_dim)
    else:
        remain = lax.slice_in_dim(values_in, 1, extent, axis=along_dim)
    return pad_face(remain, along_dim, before)

def face_terms(permeab, inside):
    face_x = harmonic(permeab[:, :, :-1, :], permeab[:, :, 1:, :]) * (inside[:-1] * inside[1:])[:, None]
    face_y = harmonic(permeab[:, :, :, :-1], permeab[:, :, :, 1:])
    face_z = VERTICAL * harmonic(permeab[:, :-1], permeab[:, 1:])
    return (face_x, face_y, face_z)

def neighbours(face_sets, values_in):
    flow_sum = 0.0
    weight_sum = 0.0
    for faces_dim, along_dim in zip(face_sets, (2, 3, 1)):
        lower = pad_face(faces_dim, along_dim, True)
        upper = pad_face(faces_dim, along_dim, False)
        flow_sum = flow_sum + lower * slide_by(values_in, along_dim, True) + upper * slide_by(values_in, along_dim, False)
        weight_sum = weight_sum + lower + upper
    return (flow_sum, weight_sum)

def jacobi(pressure, baseline, storage_term, face_sets):
    flow_sum, weight_sum = neighbours(face_sets, pressure)
    return (baseline + flow_sum) / (storage_term + weight_sum)

def water_frac(values_in):
    squared = values_in * values_in
    return squared / (squared + VISCOSITY_RATIO * (1.0 - values_in) * (1.0 - values_in))

def transport(pressure, saturation, face_sets):
    fraction = water_frac(saturation)
    change = 0.0
    for faces_dim, along_dim in zip(face_sets, (2, 3, 1)):
        extent = pressure.shape[along_dim]
        lower_press = lax.slice_in_dim(pressure, 0, extent - 1, axis=along_dim)
        upper_press = lax.slice_in_dim(pressure, 1, extent, axis=along_dim)
        lower_frac = lax.slice_in_dim(fraction, 0, extent - 1, axis=along_dim)
        upper_frac = lax.slice_in_dim(fraction, 1, extent, axis=along_dim)
        velocity = faces_dim * (lower_press - upper_press)
        carried = velocity * jnp.where(velocity > 0, lower_frac, upper_frac)
        change = change + pad_face(carried, along_dim, True) - pad_face(carried, along_dim, False)
    return saturation + STEP_COEF * change

def solve_spd(gram_matrix, cross_matrix):
    factor = jnp.linalg.cholesky(gram_matrix + jnp.eye(gram_matrix.shape[0], dtype=jnp.float32))
    halfway = lax.linalg.triangular_solve(factor, cross_matrix, left_side=True, lower=True)
    return lax.linalg.triangular_solve(factor, halfway, left_side=True, lower=True, transpose_a=True)

def reference(log_perm, start_pressure, start_sat, source, storage, well_press, perf_cell, perf_well, perf_count, observed, obs_var, obs_noise):
    permeab = jnp.exp(log_perm)
    face_sets = face_terms(permeab, jnp.ones((NX,), jnp.float32))
    baseline = (source + storage * start_pressure)[None]
    storage_term = storage[None]
    pressure = jnp.broadcast_to(start_pressure[None], log_perm.shape)
    for sweep_idx in range(SWEEPS):
        pressure = jacobi(pressure, baseline, storage_term, face_sets)
    saturation = transport(pressure, start_sat[None], face_sets)

    def by_strip(values_in):
        shaped = values_in.reshape(MEMBERS, LAYERS, N_TILE, CX, NY).transpose(0, 2, 1, 3, 4)
        return shaped.reshape(MEMBERS, N_TILE, LAYERS * CX * NY)
    mobility = by_strip(permeab * water_frac(saturation))
    cell_press = by_strip(pressure)
    slots = jnp.arange(PERFS, dtype=jnp.int32)
    owner_tile = slots // PERF_DEV
    live_mask = (slots % PERF_DEV < perf_count[owner_tile]).astype(jnp.float32)
    perf_mob = mobility[:, owner_tile, perf_cell]
    perf_press = cell_press[:, owner_tile, perf_cell]
    perf_terms = perf_mob * (perf_press - well_press[perf_well][None]) * live_mask[None]
    well_rates = jax.ops.segment_sum(perf_terms.T, perf_well, num_segments=WELLS).T
    member_root = (MEMBERS - 1) ** 0.5
    spread = jnp.sqrt(INFLATION * obs_var)
    mean_rate = lax.optimization_barrier(jnp.sum(well_rates, 0)) / MEMBERS
    scaled = (well_rates - mean_rate) / (spread * member_root)
    innovation = (observed - well_rates) / spread + obs_noise
    gram_matrix = jnp.dot(scaled.astype(jnp.float32), scaled.T.astype(jnp.float32), precision=lax.Precision.HIGHEST, preferred_element_type=jnp.float32)
    cross_matrix = jnp.dot(scaled.astype(jnp.float32), innovation.T.astype(jnp.float32), precision=lax.Precision.HIGHEST, preferred_element_type=jnp.float32)
    weights_low = solve_spd(gram_matrix, cross_matrix).astype(jnp.bfloat16)
    anomaly = (log_perm / member_root).astype(jnp.bfloat16)
    update_sum = jnp.dot(weights_low.astype(jnp.float32).T, anomaly.astype(jnp.float32).reshape(MEMBERS, -1), precision=lax.Precision.HIGHEST)
    new_log_perm = log_perm + update_sum.reshape(log_perm.shape)
    return (new_log_perm, pressure, saturation, well_rates)
```

```python
import functools

import jax
import jax.numpy as jnp
from jax import lax
from jax.experimental import pallas as pl
from jax.experimental.pallas import tpu as pltpu
from jax.sharding import PartitionSpec as P

SWEEPS = 2


VERTICAL = 0.5
VISCOSITY_RATIO = 2.0
STEP_COEF = 0.1
INFLATION = 4.0


def extended_2(block, sides, width):
    for axis, dim in sides:
        count = lax.axis_size(axis)
        forward = [(i, i + 1) for i in range(count - 1)]
        backward = [(target, source) for source, target in forward]
        low = lax.ppermute(
            lax.slice_in_dim(block, block.shape[dim] - width, None, axis=dim), axis, forward
        )
        high = lax.ppermute(lax.slice_in_dim(block, 0, width, axis=dim), axis, backward)
        block = jnp.concatenate([low, block, high], axis=dim)
    return block


def harmonic(lower_val, upper_val):
    return 2.0 * lower_val * upper_val / (lower_val + upper_val)


def pad_face(values_in, along_dim, before):
    widths = [(0, 0)] * values_in.ndim
    widths[along_dim] = (1, 0) if before else (0, 1)
    return jnp.pad(values_in, widths)


def slide_by(values_in, along_dim, before):
    extent = values_in.shape[along_dim]
    if before:
        remain = lax.slice_in_dim(values_in, 0, extent - 1, axis=along_dim)
    else:
        remain = lax.slice_in_dim(values_in, 1, extent, axis=along_dim)
    return pad_face(remain, along_dim, before)


def face_terms(permeab, inside):
    face_x = (
        harmonic(permeab[:, :, :-1, :], permeab[:, :, 1:, :]) * (inside[:-1] * inside[1:])[:, None]
    )
    face_y = harmonic(permeab[:, :, :, :-1], permeab[:, :, :, 1:])
    face_z = VERTICAL * harmonic(permeab[:, :-1], permeab[:, 1:])
    return (face_x, face_y, face_z)


def neighbours(face_sets, values_in):
    flow_sum = 0.0
    weight_sum = 0.0
    for faces_dim, along_dim in zip(face_sets, (2, 3, 1)):
        lower = pad_face(faces_dim, along_dim, True)
        upper = pad_face(faces_dim, along_dim, False)
        flow_sum = (
            flow_sum
            + lower * slide_by(values_in, along_dim, True)
            + upper * slide_by(values_in, along_dim, False)
        )
        weight_sum = weight_sum + lower + upper
    return (flow_sum, weight_sum)


def jacobi(pressure, baseline, storage_term, face_sets):
    flow_sum, weight_sum = neighbours(face_sets, pressure)
    return (baseline + flow_sum) / (storage_term + weight_sum)


def water_frac(values_in):
    squared = values_in * values_in
    return squared / (squared + VISCOSITY_RATIO * (1.0 - values_in) * (1.0 - values_in))


def transport(pressure, saturation, face_sets):
    fraction = water_frac(saturation)
    change = 0.0
    for faces_dim, along_dim in zip(face_sets, (2, 3, 1)):
        extent = pressure.shape[along_dim]
        lower_press = lax.slice_in_dim(pressure, 0, extent - 1, axis=along_dim)
        upper_press = lax.slice_in_dim(pressure, 1, extent, axis=along_dim)
        lower_frac = lax.slice_in_dim(fraction, 0, extent - 1, axis=along_dim)
        upper_frac = lax.slice_in_dim(fraction, 1, extent, axis=along_dim)
        velocity = faces_dim * (lower_press - upper_press)
        carried = velocity * jnp.where(velocity > 0, lower_frac, upper_frac)
        change = change + pad_face(carried, along_dim, True) - pad_face(carried, along_dim, False)
    return saturation + STEP_COEF * change


def solve_spd(gram_matrix, cross_matrix):
    factor = jnp.linalg.cholesky(gram_matrix + jnp.eye(gram_matrix.shape[0], dtype=jnp.float32))
    halfway = lax.linalg.triangular_solve(factor, cross_matrix, left_side=True, lower=True)
    return lax.linalg.triangular_solve(
        factor, halfway, left_side=True, lower=True, transpose_a=True
    )


def trim_rim(values_in, rim_cut):
    return values_in[:, :, rim_cut : values_in.shape[2] - rim_cut, :]


def exchange_kernel(member_count, part_ref, obs_ref, spr_ref, noise_ref, full_ref,
                    recv_a, mine, send_a, recv_a_sem, send_b, recv_b_sem):
    tile_count = part_ref.shape[0]
    total = tile_count * member_count
    me_t = lax.axis_index("tile")
    me_m = lax.axis_index("member")
    me = me_t * member_count + me_m
    mesh_ids = pl.DeviceIdType.MESH

    barrier = pltpu.get_barrier_semaphore()

    def greet(k, carry):
        peer = lax.rem(me + k, total)
        pl.semaphore_signal(
            barrier, 1, device_id=(peer // member_count, lax.rem(peer, member_count)),
            device_id_type=mesh_ids,
        )
        return carry

    lax.fori_loop(1, total, greet, 0)
    pl.semaphore_wait(barrier, total - 1)

    def copy_a(dst_t, src_t):
        return pltpu.make_async_remote_copy(
            src_ref=part_ref.at[dst_t], dst_ref=recv_a.at[src_t],
            send_sem=send_a.at[dst_t], recv_sem=recv_a_sem.at[src_t],
            device_id=(dst_t, me_m), device_id_type=mesh_ids,
        )

    def start_a(k, carry):
        copy_a(lax.rem(me_t + k, tile_count), me_t).start()
        return carry

    lax.fori_loop(1, tile_count, start_a, 0)

    def wait_a(k, acc):
        src_t = lax.rem(me_t + k, tile_count)
        copy_a(me_t, src_t).wait_recv()
        return acc + recv_a[src_t]

    acc = lax.fori_loop(1, tile_count, wait_a, part_ref[me_t])

    def wait_a_send(k, carry):
        copy_a(lax.rem(me_t + k, tile_count), me_t).wait_send()
        return carry

    lax.fori_loop(1, tile_count, wait_a_send, 0)

    innov = (obs_ref[...] - acc) / spr_ref[...] + noise_ref[...]
    mine[0] = acc
    mine[1] = innov
    full_ref[me_m, me_t, 0] = acc
    full_ref[me_m, me_t, 1] = innov

    def copy_b(dst, src):
        return pltpu.make_async_remote_copy(
            src_ref=mine, dst_ref=full_ref.at[lax.rem(src, member_count), src // member_count],
            send_sem=send_b.at[dst], recv_sem=recv_b_sem.at[src],
            device_id=(dst // member_count, lax.rem(dst, member_count)), device_id_type=mesh_ids,
        )

    def start_b(k, carry):
        copy_b(lax.rem(me + k, total), me).start()
        return carry

    lax.fori_loop(1, total, start_b, 0)

    def wait_b(k, carry):
        copy_b(me, lax.rem(me + k, total)).wait_recv()
        return carry

    lax.fori_loop(1, total, wait_b, 0)

    def wait_b_send(k, carry):
        copy_b(lax.rem(me + k, total), me).wait_send()
        return carry

    lax.fori_loop(1, total, wait_b_send, 0)


def rates_exchange(pieces, obs_blk, spr_blk, noise_blk, member_count):
    tile_count, rows, lanes = pieces.shape
    total = tile_count * member_count
    vmem = pl.BlockSpec(memory_space=pltpu.VMEM)
    return pl.pallas_call(
        functools.partial(exchange_kernel, member_count),
        out_shape=jax.ShapeDtypeStruct((member_count, tile_count, 2, rows, lanes), jnp.float32),
        in_specs=[vmem] * 4,
        out_specs=vmem,
        scratch_shapes=[
            pltpu.VMEM((tile_count, rows, lanes), jnp.float32),
            pltpu.VMEM((2, rows, lanes), jnp.float32),
            pltpu.SemaphoreType.DMA((tile_count,)),
            pltpu.SemaphoreType.DMA((tile_count,)),
            pltpu.SemaphoreType.DMA((total,)),
            pltpu.SemaphoreType.DMA((total,)),
        ],
        compiler_params=pltpu.CompilerParams(collective_id=0, has_side_effects=True),
    )(pieces, obs_blk, spr_blk, noise_blk)


def per_device(
    log_perm,
    start_pressure,
    start_sat,
    source,
    storage,
    well_press,
    perf_cell,
    perf_well,
    perf_count,
    observed,
    obs_var,
    obs_noise,
):
    local_count, layers, strip_width, strip_depth = log_perm.shape
    tile_count = lax.axis_size("tile")
    members = local_count * lax.axis_size("member")
    well_count = well_press.shape[0]
    well_share = well_count // tile_count
    tile_rank = lax.axis_index("tile")
    member_rank = lax.axis_index("member")
    permeab = jnp.exp(extended_2(log_perm, (("tile", 2),), 1))
    shared = extended_2(jnp.stack([start_pressure, start_sat]), (("tile", 2),), 1)
    column = tile_rank * strip_width - 1 + jnp.arange(strip_width + 2 * 1, dtype=jnp.int32)
    face_sets = face_terms(
        permeab, ((column >= 0) & (column < strip_width * tile_count)).astype(jnp.float32)
    )
    baseline = jnp.pad(source + storage * start_pressure, ((0, 0), (1, 1), (0, 0)))[None]
    storage_term = jnp.pad(storage, ((0, 0), (1, 1), (0, 0)), constant_values=1.0)[None]
    extended = jnp.broadcast_to(shared[0:1], (local_count,) + shared.shape[1:])
    for sweep_idx in range(SWEEPS):
        pressure = trim_rim(jacobi(extended, baseline, storage_term, face_sets), 1)
        extended = extended_2(pressure, (("tile", 2),), 1)
    saturation = trim_rim(transport(extended, shared[1:2], face_sets), 1)
    permeab = trim_rim(permeab, 1)
    cell_count = layers * strip_width * strip_depth
    mobility = (permeab * water_frac(saturation)).reshape(local_count, cell_count)
    cell_press = pressure.reshape(local_count, cell_count)
    perf_mob = jnp.take(mobility, perf_cell, axis=1)
    perf_press = jnp.take(cell_press, perf_cell, axis=1)
    selector = (perf_well[:, None] == jnp.arange(well_count, dtype=jnp.int32)[None, :]).astype(
        jnp.float32
    )
    perf_bhp = jnp.dot(selector, well_press, precision=lax.Precision.HIGHEST)
    live_mask = (jnp.arange(perf_cell.shape[0], dtype=jnp.int32) < perf_count[0]).astype(
        jnp.float32
    )
    perf_terms = perf_mob * (perf_press - perf_bhp[None]) * live_mask[None]
    partial_rates = jnp.dot(
        perf_terms, selector, precision=lax.Precision.HIGHEST, preferred_element_type=jnp.float32
    )
    member_root = (members - 1) ** 0.5
    spread = jnp.sqrt(INFLATION * obs_var)
    member_count = lax.axis_size("member")
    well_first = tile_rank * well_share
    spread_part = lax.dynamic_slice_in_dim(spread, well_first, well_share, 0)
    observed_part = lax.dynamic_slice_in_dim(observed, well_first, well_share, 0)
    noise_part = lax.dynamic_slice_in_dim(obs_noise, well_first, well_share, 1)
    block_rows = local_count * well_share // 128
    pieces = partial_rates.reshape(local_count, tile_count, well_share).transpose(1, 0, 2)
    pieces = pieces.reshape(tile_count, block_rows, 128)
    obs_blk = jnp.broadcast_to(observed_part[None, :], (local_count, well_share)).reshape(block_rows, 128)
    spr_blk = jnp.broadcast_to(spread_part[None, :], (local_count, well_share)).reshape(block_rows, 128)
    noise_blk = noise_part.reshape(block_rows, 128)
    full = rates_exchange(pieces, obs_blk, spr_blk, noise_blk, member_count)
    full = full.reshape(member_count, tile_count, 2, local_count, well_share)
    rates_all = full[:, :, 0].transpose(0, 2, 1, 3).reshape(members, well_count)
    innov_all = full[:, :, 1].transpose(0, 2, 1, 3).reshape(members, well_count)
    own_block = lax.dynamic_index_in_dim(
        lax.dynamic_index_in_dim(full, member_rank, 0, keepdims=False), tile_rank, 0, keepdims=False
    )
    well_rates = own_block[0]
    mean_rate = jnp.sum(rates_all, 0) / members
    scaled_all = (rates_all - mean_rate) / (spread * member_root)
    gram_matrix = jnp.dot(
        scaled_all, scaled_all.T, precision=lax.Precision.HIGHEST, preferred_element_type=jnp.float32
    )
    cross_matrix = jnp.dot(
        scaled_all, innov_all.T, precision=lax.Precision.HIGHEST, preferred_element_type=jnp.float32
    )
    weights_low = solve_spd(gram_matrix, cross_matrix).astype(jnp.bfloat16)
    anomaly = (log_perm / member_root).astype(jnp.bfloat16).reshape(local_count, cell_count)
    anomaly_all = lax.all_gather(anomaly, "member", axis=0, tiled=True)
    first_member = member_rank * local_count
    own_cols = lax.dynamic_slice_in_dim(weights_low, first_member, local_count, 1)
    contract = (((0,), (0,)), ((), ()))
    update_sum = lax.dot_general(own_cols, anomaly_all, contract, preferred_element_type=jnp.float32)
    new_log_perm = log_perm + update_sum.reshape(log_perm.shape)
    return (new_log_perm, pressure, saturation, well_rates)


def solution(mesh):
    return jax.shard_map(
        per_device,
        mesh=mesh,
        in_specs=(
            P("member", None, "tile", None),
            P(None, "tile", None),
            P(None, "tile", None),
            P(None, "tile", None),
            P(None, "tile", None),
            P(),
            P("tile"),
            P("tile"),
            P("tile"),
            P(),
            P(),
            P("member", None),
        ),
        out_specs=(
            P("member", None, "tile", None),
            P("member", None, "tile", None),
            P("member", None, "tile", None),
            P("member", "tile"),
        ),
        check_vma=False,
    )
```

```python
import functools

import jax
import jax.numpy as jnp
from jax import lax
from jax.experimental import pallas as pl
from jax.experimental.pallas import tpu as pltpu
from jax.sharding import PartitionSpec as P

SWEEPS = 2


VERTICAL = 0.5
VISCOSITY_RATIO = 2.0
STEP_COEF = 0.1
INFLATION = 4.0


def extended_2(block, sides, width):
    for axis, dim in sides:
        count = lax.axis_size(axis)
        forward = [(i, i + 1) for i in range(count - 1)]
        backward = [(target, source) for source, target in forward]
        low = lax.ppermute(
            lax.slice_in_dim(block, block.shape[dim] - width, None, axis=dim), axis, forward
        )
        high = lax.ppermute(lax.slice_in_dim(block, 0, width, axis=dim), axis, backward)
        block = jnp.concatenate([low, block, high], axis=dim)
    return block


def harmonic(lower_val, upper_val):
    return 2.0 * lower_val * upper_val / (lower_val + upper_val)


def pad_face(values_in, along_dim, before):
    widths = [(0, 0)] * values_in.ndim
    widths[along_dim] = (1, 0) if before else (0, 1)
    return jnp.pad(values_in, widths)


def slide_by(values_in, along_dim, before):
    extent = values_in.shape[along_dim]
    if before:
        remain = lax.slice_in_dim(values_in, 0, extent - 1, axis=along_dim)
    else:
        remain = lax.slice_in_dim(values_in, 1, extent, axis=along_dim)
    return pad_face(remain, along_dim, before)


def face_terms(permeab, inside):
    face_x = (
        harmonic(permeab[:, :, :-1, :], permeab[:, :, 1:, :]) * (inside[:-1] * inside[1:])[:, None]
    )
    face_y = harmonic(permeab[:, :, :, :-1], permeab[:, :, :, 1:])
    face_z = VERTICAL * harmonic(permeab[:, :-1], permeab[:, 1:])
    return (face_x, face_y, face_z)


def neighbours(face_sets, values_in):
    flow_sum = 0.0
    weight_sum = 0.0
    for faces_dim, along_dim in zip(face_sets, (2, 3, 1)):
        lower = pad_face(faces_dim, along_dim, True)
        upper = pad_face(faces_dim, along_dim, False)
        flow_sum = (
            flow_sum
            + lower * slide_by(values_in, along_dim, True)
            + upper * slide_by(values_in, along_dim, False)
        )
        weight_sum = weight_sum + lower + upper
    return (flow_sum, weight_sum)


def jacobi(pressure, baseline, storage_term, face_sets):
    flow_sum, weight_sum = neighbours(face_sets, pressure)
    return (baseline + flow_sum) / (storage_term + weight_sum)


def water_frac(values_in):
    squared = values_in * values_in
    return squared / (squared + VISCOSITY_RATIO * (1.0 - values_in) * (1.0 - values_in))


def transport(pressure, saturation, face_sets):
    fraction = water_frac(saturation)
    change = 0.0
    for faces_dim, along_dim in zip(face_sets, (2, 3, 1)):
        extent = pressure.shape[along_dim]
        lower_press = lax.slice_in_dim(pressure, 0, extent - 1, axis=along_dim)
        upper_press = lax.slice_in_dim(pressure, 1, extent, axis=along_dim)
        lower_frac = lax.slice_in_dim(fraction, 0, extent - 1, axis=along_dim)
        upper_frac = lax.slice_in_dim(fraction, 1, extent, axis=along_dim)
        velocity = faces_dim * (lower_press - upper_press)
        carried = velocity * jnp.where(velocity > 0, lower_frac, upper_frac)
        change = change + pad_face(carried, along_dim, True) - pad_face(carried, along_dim, False)
    return saturation + STEP_COEF * change


def solve_spd(gram_matrix, cross_matrix):
    factor = jnp.linalg.cholesky(gram_matrix + jnp.eye(gram_matrix.shape[0], dtype=jnp.float32))
    halfway = lax.linalg.triangular_solve(factor, cross_matrix, left_side=True, lower=True)
    return lax.linalg.triangular_solve(
        factor, halfway, left_side=True, lower=True, transpose_a=True
    )


def trim_rim(values_in, rim_cut):
    return values_in[:, :, rim_cut : values_in.shape[2] - rim_cut, :]


def exchange_kernel(member_count, part_ref, obs_ref, spr_ref, noise_ref, full_ref,
                    recv_a, mine, send_a, recv_a_sem, send_b, recv_b_sem):
    tile_count = part_ref.shape[0]
    total = tile_count * member_count
    me_t = lax.axis_index("tile")
    me_m = lax.axis_index("member")
    me = me_t * member_count + me_m
    mesh_ids = pl.DeviceIdType.MESH

    barrier = pltpu.get_barrier_semaphore()

    def greet(k, carry):
        peer = lax.rem(me + k, total)
        pl.semaphore_signal(
            barrier, 1, device_id=(peer // member_count, lax.rem(peer, member_count)),
            device_id_type=mesh_ids,
        )
        return carry

    lax.fori_loop(1, total, greet, 0)
    pl.semaphore_wait(barrier, total - 1)

    def copy_a(dst_t, src_t):
        return pltpu.make_async_remote_copy(
            src_ref=part_ref.at[dst_t], dst_ref=recv_a.at[src_t],
            send_sem=send_a.at[dst_t], recv_sem=recv_a_sem.at[src_t],
            device_id=(dst_t, me_m), device_id_type=mesh_ids,
        )

    def start_a(k, carry):
        copy_a(lax.rem(me_t + k, tile_count), me_t).start()
        return carry

    lax.fori_loop(1, tile_count, start_a, 0)

    def wait_a(k, acc):
        src_t = lax.rem(me_t + k, tile_count)
        copy_a(me_t, src_t).wait_recv()
        return acc + recv_a[src_t]

    acc = lax.fori_loop(1, tile_count, wait_a, part_ref[me_t])

    def wait_a_send(k, carry):
        copy_a(lax.rem(me_t + k, tile_count), me_t).wait_send()
        return carry

    lax.fori_loop(1, tile_count, wait_a_send, 0)

    innov = (obs_ref[...] - acc) / spr_ref[...] + noise_ref[...]
    mine[0] = acc
    mine[1] = innov
    full_ref[me_m, me_t, 0] = acc
    full_ref[me_m, me_t, 1] = innov

    def copy_b(dst, src):
        return pltpu.make_async_remote_copy(
            src_ref=mine, dst_ref=full_ref.at[lax.rem(src, member_count), src // member_count],
            send_sem=send_b.at[dst], recv_sem=recv_b_sem.at[src],
            device_id=(dst // member_count, lax.rem(dst, member_count)), device_id_type=mesh_ids,
        )

    def start_b(k, carry):
        copy_b(lax.rem(me + k, total), me).start()
        return carry

    lax.fori_loop(1, total, start_b, 0)

    def wait_b(k, carry):
        copy_b(me, lax.rem(me + k, total)).wait_recv()
        return carry

    lax.fori_loop(1, total, wait_b, 0)

    def wait_b_send(k, carry):
        copy_b(lax.rem(me + k, total), me).wait_send()
        return carry

    lax.fori_loop(1, total, wait_b_send, 0)


def rates_exchange(pieces, obs_blk, spr_blk, noise_blk, member_count):
    tile_count, rows, lanes = pieces.shape
    total = tile_count * member_count
    vmem = pl.BlockSpec(memory_space=pltpu.VMEM)
    return pl.pallas_call(
        functools.partial(exchange_kernel, member_count),
        out_shape=jax.ShapeDtypeStruct((member_count, tile_count, 2, rows, lanes), jnp.float32),
        in_specs=[vmem] * 4,
        out_specs=vmem,
        scratch_shapes=[
            pltpu.VMEM((tile_count, rows, lanes), jnp.float32),
            pltpu.VMEM((2, rows, lanes), jnp.float32),
            pltpu.SemaphoreType.DMA((tile_count,)),
            pltpu.SemaphoreType.DMA((tile_count,)),
            pltpu.SemaphoreType.DMA((total,)),
            pltpu.SemaphoreType.DMA((total,)),
        ],
        compiler_params=pltpu.CompilerParams(collective_id=0, has_side_effects=True),
    )(pieces, obs_blk, spr_blk, noise_blk)


def per_device(
    log_perm,
    start_pressure,
    start_sat,
    source,
    storage,
    well_press,
    perf_cell,
    perf_well,
    perf_count,
    observed,
    obs_var,
    obs_noise,
):
    local_count, layers, strip_width, strip_depth = log_perm.shape
    tile_count = lax.axis_size("tile")
    members = local_count * lax.axis_size("member")
    well_count = well_press.shape[0]
    well_share = well_count // tile_count
    tile_rank = lax.axis_index("tile")
    member_rank = lax.axis_index("member")
    permeab = jnp.exp(extended_2(log_perm, (("tile", 2),), 1))
    shared = extended_2(jnp.stack([start_pressure, start_sat]), (("tile", 2),), 1)
    column = tile_rank * strip_width - 1 + jnp.arange(strip_width + 2 * 1, dtype=jnp.int32)
    face_sets = face_terms(
        permeab, ((column >= 0) & (column < strip_width * tile_count)).astype(jnp.float32)
    )
    baseline = jnp.pad(source + storage * start_pressure, ((0, 0), (1, 1), (0, 0)))[None]
    storage_term = jnp.pad(storage, ((0, 0), (1, 1), (0, 0)), constant_values=1.0)[None]
    extended = jnp.broadcast_to(shared[0:1], (local_count,) + shared.shape[1:])
    for sweep_idx in range(SWEEPS):
        pressure = trim_rim(jacobi(extended, baseline, storage_term, face_sets), 1)
        extended = extended_2(pressure, (("tile", 2),), 1)
    saturation = trim_rim(transport(extended, shared[1:2], face_sets), 1)
    permeab = trim_rim(permeab, 1)
    cell_count = layers * strip_width * strip_depth
    mobility = (permeab * water_frac(saturation)).reshape(local_count, cell_count)
    cell_press = pressure.reshape(local_count, cell_count)
    perf_mob = jnp.take(mobility, perf_cell, axis=1)
    perf_press = jnp.take(cell_press, perf_cell, axis=1)
    selector = (perf_well[:, None] == jnp.arange(well_count, dtype=jnp.int32)[None, :]).astype(
        jnp.float32
    )
    perf_bhp = jnp.dot(selector, well_press, precision=lax.Precision.HIGHEST)
    live_mask = (jnp.arange(perf_cell.shape[0], dtype=jnp.int32) < perf_count[0]).astype(
        jnp.float32
    )
    perf_terms = perf_mob * (perf_press - perf_bhp[None]) * live_mask[None]
    partial_rates = jnp.dot(
        perf_terms, selector, precision=lax.Precision.HIGHEST, preferred_element_type=jnp.float32
    )
    member_root = (members - 1) ** 0.5
    spread = jnp.sqrt(INFLATION * obs_var)
    member_count = lax.axis_size("member")
    well_first = tile_rank * well_share
    spread_part = lax.dynamic_slice_in_dim(spread, well_first, well_share, 0)
    observed_part = lax.dynamic_slice_in_dim(observed, well_first, well_share, 0)
    noise_part = lax.dynamic_slice_in_dim(obs_noise, well_first, well_share, 1)
    block_rows = local_count * well_share // 128
    pieces = partial_rates.reshape(local_count, tile_count, well_share).transpose(1, 0, 2)
    pieces = pieces.reshape(tile_count, block_rows, 128)
    obs_blk = jnp.broadcast_to(observed_part[None, :], (local_count, well_share)).reshape(block_rows, 128)
    spr_blk = jnp.broadcast_to(spread_part[None, :], (local_count, well_share)).reshape(block_rows, 128)
    noise_blk = noise_part.reshape(block_rows, 128)
    full = rates_exchange(pieces, obs_blk, spr_blk, noise_blk, member_count)
    full = full.reshape(member_count, tile_count, 2, local_count, well_share)
    rates_all = full[:, :, 0].transpose(0, 2, 1, 3).reshape(members, well_count)
    innov_all = full[:, :, 1].transpose(0, 2, 1, 3).reshape(members, well_count)
    own_block = lax.dynamic_index_in_dim(
        lax.dynamic_index_in_dim(full, member_rank, 0, keepdims=False), tile_rank, 0, keepdims=False
    )
    well_rates = own_block[0]
    mean_rate = jnp.sum(rates_all, 0) / members
    scaled_all = (rates_all - mean_rate) / (spread * member_root)
    gram_matrix = jnp.dot(
        scaled_all, scaled_all.T, precision=lax.Precision.HIGHEST, preferred_element_type=jnp.float32
    )
    cross_matrix = jnp.dot(
        scaled_all, innov_all.T, precision=lax.Precision.HIGHEST, preferred_element_type=jnp.float32
    )
    weights_low = solve_spd(gram_matrix, cross_matrix).astype(jnp.bfloat16)
    anomaly = (log_perm / member_root).astype(jnp.bfloat16).reshape(local_count, cell_count)
    anomaly_parts = [anomaly]
    for shift in range(1, member_count):
        pairs = [(i, (i + shift) % member_count) for i in range(member_count)]
        anomaly_parts.append(lax.ppermute(anomaly, "member", pairs))
    anomaly_all = jnp.concatenate(anomaly_parts, axis=0)
    first_member = member_rank * local_count
    own_cols = lax.dynamic_slice_in_dim(weights_low, first_member, local_count, 1)
    own_cols = jnp.concatenate(
        [
            lax.dynamic_slice_in_dim(
                own_cols, lax.rem(member_rank - shift + member_count, member_count) * local_count,
                local_count, 0,
            )
            for shift in range(member_count)
        ],
        axis=0,
    )
    contract = (((0,), (0,)), ((), ()))
    update_sum = lax.dot_general(own_cols, anomaly_all, contract, preferred_element_type=jnp.float32)
    new_log_perm = log_perm + update_sum.reshape(log_perm.shape)
    return (new_log_perm, pressure, saturation, well_rates)


def solution(mesh):
    return jax.shard_map(
        per_device,
        mesh=mesh,
        in_specs=(
            P("member", None, "tile", None),
            P(None, "tile", None),
            P(None, "tile", None),
            P(None, "tile", None),
            P(None, "tile", None),
            P(),
            P("tile"),
            P("tile"),
            P("tile"),
            P(),
            P(),
            P("member", None),
        ),
        out_specs=(
            P("member", None, "tile", None),
            P("member", None, "tile", None),
            P("member", None, "tile", None),
            P("member", "tile"),
        ),
        check_vma=False,
    )
```

```python
import functools

import jax
import jax.numpy as jnp
from jax import lax
from jax.experimental import pallas as pl
from jax.experimental.pallas import tpu as pltpu
from jax.sharding import PartitionSpec as P

SWEEPS = 2


VERTICAL = 0.5
VISCOSITY_RATIO = 2.0
STEP_COEF = 0.1
INFLATION = 4.0


def extended_2(block, sides, width):
    for axis, dim in sides:
        count = lax.axis_size(axis)
        forward = [(i, i + 1) for i in range(count - 1)]
        backward = [(target, source) for source, target in forward]
        low = lax.ppermute(
            lax.slice_in_dim(block, block.shape[dim] - width, None, axis=dim), axis, forward
        )
        high = lax.ppermute(lax.slice_in_dim(block, 0, width, axis=dim), axis, backward)
        block = jnp.concatenate([low, block, high], axis=dim)
    return block


def harmonic(lower_val, upper_val):
    return 2.0 * lower_val * upper_val / (lower_val + upper_val)


def pad_face(values_in, along_dim, before):
    widths = [(0, 0)] * values_in.ndim
    widths[along_dim] = (1, 0) if before else (0, 1)
    return jnp.pad(values_in, widths)


def slide_by(values_in, along_dim, before):
    extent = values_in.shape[along_dim]
    if before:
        remain = lax.slice_in_dim(values_in, 0, extent - 1, axis=along_dim)
    else:
        remain = lax.slice_in_dim(values_in, 1, extent, axis=along_dim)
    return pad_face(remain, along_dim, before)


def face_terms(permeab, inside):
    face_x = (
        harmonic(permeab[:, :, :-1, :], permeab[:, :, 1:, :]) * (inside[:-1] * inside[1:])[:, None]
    )
    face_y = harmonic(permeab[:, :, :, :-1], permeab[:, :, :, 1:])
    face_z = VERTICAL * harmonic(permeab[:, :-1], permeab[:, 1:])
    return (face_x, face_y, face_z)


def neighbours(face_sets, values_in):
    flow_sum = 0.0
    weight_sum = 0.0
    for faces_dim, along_dim in zip(face_sets, (2, 3, 1)):
        lower = pad_face(faces_dim, along_dim, True)
        upper = pad_face(faces_dim, along_dim, False)
        flow_sum = (
            flow_sum
            + lower * slide_by(values_in, along_dim, True)
            + upper * slide_by(values_in, along_dim, False)
        )
        weight_sum = weight_sum + lower + upper
    return (flow_sum, weight_sum)


def jacobi(pressure, baseline, storage_term, face_sets):
    flow_sum, weight_sum = neighbours(face_sets, pressure)
    return (baseline + flow_sum) / (storage_term + weight_sum)


def water_frac(values_in):
    squared = values_in * values_in
    return squared / (squared + VISCOSITY_RATIO * (1.0 - values_in) * (1.0 - values_in))


def transport(pressure, saturation, face_sets):
    fraction = water_frac(saturation)
    change = 0.0
    for faces_dim, along_dim in zip(face_sets, (2, 3, 1)):
        extent = pressure.shape[along_dim]
        lower_press = lax.slice_in_dim(pressure, 0, extent - 1, axis=along_dim)
        upper_press = lax.slice_in_dim(pressure, 1, extent, axis=along_dim)
        lower_frac = lax.slice_in_dim(fraction, 0, extent - 1, axis=along_dim)
        upper_frac = lax.slice_in_dim(fraction, 1, extent, axis=along_dim)
        velocity = faces_dim * (lower_press - upper_press)
        carried = velocity * jnp.where(velocity > 0, lower_frac, upper_frac)
        change = change + pad_face(carried, along_dim, True) - pad_face(carried, along_dim, False)
    return saturation + STEP_COEF * change


def solve_spd(gram_matrix, cross_matrix):
    factor = jnp.linalg.cholesky(gram_matrix + jnp.eye(gram_matrix.shape[0], dtype=jnp.float32))
    halfway = lax.linalg.triangular_solve(factor, cross_matrix, left_side=True, lower=True)
    return lax.linalg.triangular_solve(
        factor, halfway, left_side=True, lower=True, transpose_a=True
    )


def trim_rim(values_in, rim_cut):
    return values_in[:, :, rim_cut : values_in.shape[2] - rim_cut, :]


def exchange_kernel(member_count, part_ref, full_ref,
                    recv_a, send_a, recv_a_sem, send_m, recv_m_sem, send_t, recv_t_sem):
    tile_count = part_ref.shape[0]
    me_t = lax.axis_index("tile")
    me_m = lax.axis_index("member")
    mesh_ids = pl.DeviceIdType.MESH

    barrier = pltpu.get_barrier_semaphore()

    def greet_tile(k, carry):
        pl.semaphore_signal(
            barrier, 1, device_id=(lax.rem(me_t + k, tile_count), me_m), device_id_type=mesh_ids
        )
        return carry

    def greet_member(k, carry):
        pl.semaphore_signal(
            barrier, 1, device_id=(me_t, lax.rem(me_m + k, member_count)), device_id_type=mesh_ids
        )
        return carry

    lax.fori_loop(1, tile_count, greet_tile, 0)
    lax.fori_loop(1, member_count, greet_member, 0)
    pl.semaphore_wait(barrier, tile_count + member_count - 2)

    def copy_a(dst_t, src_t):
        return pltpu.make_async_remote_copy(
            src_ref=part_ref.at[dst_t], dst_ref=recv_a.at[src_t],
            send_sem=send_a.at[dst_t], recv_sem=recv_a_sem.at[src_t],
            device_id=(dst_t, me_m), device_id_type=mesh_ids,
        )

    def start_a(k, carry):
        copy_a(lax.rem(me_t + k, tile_count), me_t).start()
        return carry

    lax.fori_loop(1, tile_count, start_a, 0)

    def wait_a(k, acc):
        src_t = lax.rem(me_t + k, tile_count)
        copy_a(me_t, src_t).wait_recv()
        return acc + recv_a[src_t]

    acc = lax.fori_loop(1, tile_count, wait_a, part_ref[me_t])

    def wait_a_send(k, carry):
        copy_a(lax.rem(me_t + k, tile_count), me_t).wait_send()
        return carry

    lax.fori_loop(1, tile_count, wait_a_send, 0)

    full_ref[me_t, me_m] = acc

    def copy_m(dst_m, src_m):
        return pltpu.make_async_remote_copy(
            src_ref=full_ref.at[me_t, src_m], dst_ref=full_ref.at[me_t, src_m],
            send_sem=send_m.at[dst_m], recv_sem=recv_m_sem.at[src_m],
            device_id=(me_t, dst_m), device_id_type=mesh_ids,
        )

    def start_m(k, carry):
        copy_m(lax.rem(me_m + k, member_count), me_m).start()
        return carry

    lax.fori_loop(1, member_count, start_m, 0)

    def wait_m(k, carry):
        copy_m(me_m, lax.rem(me_m + k, member_count)).wait_recv()
        return carry

    lax.fori_loop(1, member_count, wait_m, 0)

    def wait_m_send(k, carry):
        copy_m(lax.rem(me_m + k, member_count), me_m).wait_send()
        return carry

    lax.fori_loop(1, member_count, wait_m_send, 0)

    def copy_t(dst_t, src_t):
        return pltpu.make_async_remote_copy(
            src_ref=full_ref.at[src_t], dst_ref=full_ref.at[src_t],
            send_sem=send_t.at[dst_t], recv_sem=recv_t_sem.at[src_t],
            device_id=(dst_t, me_m), device_id_type=mesh_ids,
        )

    def start_t(k, carry):
        copy_t(lax.rem(me_t + k, tile_count), me_t).start()
        return carry

    lax.fori_loop(1, tile_count, start_t, 0)

    def wait_t(k, carry):
        copy_t(me_t, lax.rem(me_t + k, tile_count)).wait_recv()
        return carry

    lax.fori_loop(1, tile_count, wait_t, 0)

    def wait_t_send(k, carry):
        copy_t(lax.rem(me_t + k, tile_count), me_t).wait_send()
        return carry

    lax.fori_loop(1, tile_count, wait_t_send, 0)


def rates_exchange(pieces, member_count):
    tile_count, rows, lanes = pieces.shape
    vmem = pl.BlockSpec(memory_space=pltpu.VMEM)
    return pl.pallas_call(
        functools.partial(exchange_kernel, member_count),
        out_shape=jax.ShapeDtypeStruct((tile_count, member_count, rows, lanes), jnp.float32),
        in_specs=[vmem],
        out_specs=vmem,
        scratch_shapes=[
            pltpu.VMEM((tile_count, rows, lanes), jnp.float32),
            pltpu.SemaphoreType.DMA((tile_count,)),
            pltpu.SemaphoreType.DMA((tile_count,)),
            pltpu.SemaphoreType.DMA((member_count,)),
            pltpu.SemaphoreType.DMA((member_count,)),
            pltpu.SemaphoreType.DMA((tile_count,)),
            pltpu.SemaphoreType.DMA((tile_count,)),
        ],
        compiler_params=pltpu.CompilerParams(collective_id=0, has_side_effects=True),
    )(pieces)


def per_device(
    log_perm,
    start_pressure,
    start_sat,
    source,
    storage,
    well_press,
    perf_cell,
    perf_well,
    perf_count,
    observed,
    obs_var,
    obs_noise,
):
    local_count, layers, strip_width, strip_depth = log_perm.shape
    tile_count = lax.axis_size("tile")
    members = local_count * lax.axis_size("member")
    well_count = well_press.shape[0]
    well_share = well_count // tile_count
    tile_rank = lax.axis_index("tile")
    member_rank = lax.axis_index("member")
    permeab = jnp.exp(extended_2(log_perm, (("tile", 2),), 1))
    shared = extended_2(jnp.stack([start_pressure, start_sat]), (("tile", 2),), 1)
    column = tile_rank * strip_width - 1 + jnp.arange(strip_width + 2 * 1, dtype=jnp.int32)
    face_sets = face_terms(
        permeab, ((column >= 0) & (column < strip_width * tile_count)).astype(jnp.float32)
    )
    baseline = jnp.pad(source + storage * start_pressure, ((0, 0), (1, 1), (0, 0)))[None]
    storage_term = jnp.pad(storage, ((0, 0), (1, 1), (0, 0)), constant_values=1.0)[None]
    extended = jnp.broadcast_to(shared[0:1], (local_count,) + shared.shape[1:])
    for sweep_idx in range(SWEEPS):
        pressure = trim_rim(jacobi(extended, baseline, storage_term, face_sets), 1)
        extended = extended_2(pressure, (("tile", 2),), 1)
    saturation = trim_rim(transport(extended, shared[1:2], face_sets), 1)
    permeab = trim_rim(permeab, 1)
    cell_count = layers * strip_width * strip_depth
    mobility = (permeab * water_frac(saturation)).reshape(local_count, cell_count)
    cell_press = pressure.reshape(local_count, cell_count)
    perf_mob = jnp.take(mobility, perf_cell, axis=1)
    perf_press = jnp.take(cell_press, perf_cell, axis=1)
    selector = (perf_well[:, None] == jnp.arange(well_count, dtype=jnp.int32)[None, :]).astype(
        jnp.float32
    )
    perf_bhp = jnp.dot(selector, well_press, precision=lax.Precision.HIGHEST)
    live_mask = (jnp.arange(perf_cell.shape[0], dtype=jnp.int32) < perf_count[0]).astype(
        jnp.float32
    )
    perf_terms = perf_mob * (perf_press - perf_bhp[None]) * live_mask[None]
    partial_rates = jnp.dot(
        perf_terms, selector, precision=lax.Precision.HIGHEST, preferred_element_type=jnp.float32
    )
    member_root = (members - 1) ** 0.5
    spread = jnp.sqrt(INFLATION * obs_var)
    member_count = lax.axis_size("member")
    block_rows = local_count * well_share // 128
    pieces = partial_rates.reshape(local_count, tile_count, well_share).transpose(1, 0, 2)
    pieces = pieces.reshape(tile_count, block_rows, 128)
    full = rates_exchange(pieces, member_count)
    full = full.reshape(tile_count, member_count, local_count, well_share)
    rates_all = full.transpose(1, 2, 0, 3).reshape(members, well_count)
    well_rates = lax.dynamic_index_in_dim(
        lax.dynamic_index_in_dim(full, tile_rank, 0, keepdims=False), member_rank, 0, keepdims=False
    )
    rates_own = lax.dynamic_index_in_dim(full, member_rank, 1, keepdims=False)
    rates_own = rates_own.transpose(1, 0, 2).reshape(local_count, well_count)
    innov_own = (observed - rates_own) / spread + obs_noise
    mean_rate = jnp.sum(rates_all, 0) / members
    scaled_all = (rates_all - mean_rate) / (spread * member_root)
    gram_matrix = jnp.dot(
        scaled_all, scaled_all.T, precision=lax.Precision.HIGHEST, preferred_element_type=jnp.float32
    )
    cross_matrix = jnp.dot(
        scaled_all, innov_own.T, precision=lax.Precision.HIGHEST, preferred_element_type=jnp.float32
    )
    weights_low = solve_spd(gram_matrix, cross_matrix).astype(jnp.bfloat16)
    anomaly = (log_perm / member_root).astype(jnp.bfloat16).reshape(local_count, cell_count)
    anomaly_parts = [anomaly]
    for shift in range(1, member_count):
        pairs = [(i, (i + shift) % member_count) for i in range(member_count)]
        anomaly_parts.append(lax.ppermute(anomaly, "member", pairs))
    anomaly_all = jnp.concatenate(anomaly_parts, axis=0)
    own_cols = jnp.concatenate(
        [
            lax.dynamic_slice_in_dim(
                weights_low, lax.rem(member_rank - shift + member_count, member_count) * local_count,
                local_count, 0,
            )
            for shift in range(member_count)
        ],
        axis=0,
    )
    contract = (((0,), (0,)), ((), ()))
    update_sum = lax.dot_general(own_cols, anomaly_all, contract, preferred_element_type=jnp.float32)
    new_log_perm = log_perm + update_sum.reshape(log_perm.shape)
    return (new_log_perm, pressure, saturation, well_rates)


def solution(mesh):
    return jax.shard_map(
        per_device,
        mesh=mesh,
        in_specs=(
            P("member", None, "tile", None),
            P(None, "tile", None),
            P(None, "tile", None),
            P(None, "tile", None),
            P(None, "tile", None),
            P(),
            P("tile"),
            P("tile"),
            P("tile"),
            P(),
            P(),
            P("member", None),
        ),
        out_specs=(
            P("member", None, "tile", None),
            P("member", None, "tile", None),
            P("member", None, "tile", None),
            P("member", "tile"),
        ),
        check_vma=False,
    )
```

```python
import functools

import jax
import jax.numpy as jnp
from jax import lax
from jax.experimental import pallas as pl
from jax.experimental.pallas import tpu as pltpu
from jax.sharding import PartitionSpec as P

SWEEPS = 2


VERTICAL = 0.5
VISCOSITY_RATIO = 2.0
STEP_COEF = 0.1
INFLATION = 4.0


def extended_2(block, sides, width):
    for axis, dim in sides:
        count = lax.axis_size(axis)
        forward = [(i, i + 1) for i in range(count - 1)]
        backward = [(target, source) for source, target in forward]
        low = lax.ppermute(
            lax.slice_in_dim(block, block.shape[dim] - width, None, axis=dim), axis, forward
        )
        high = lax.ppermute(lax.slice_in_dim(block, 0, width, axis=dim), axis, backward)
        block = jnp.concatenate([low, block, high], axis=dim)
    return block


def harmonic(lower_val, upper_val):
    return 2.0 * lower_val * upper_val / (lower_val + upper_val)


def pad_face(values_in, along_dim, before):
    widths = [(0, 0)] * values_in.ndim
    widths[along_dim] = (1, 0) if before else (0, 1)
    return jnp.pad(values_in, widths)


def slide_by(values_in, along_dim, before):
    extent = values_in.shape[along_dim]
    if before:
        remain = lax.slice_in_dim(values_in, 0, extent - 1, axis=along_dim)
    else:
        remain = lax.slice_in_dim(values_in, 1, extent, axis=along_dim)
    return pad_face(remain, along_dim, before)


def face_terms(permeab, inside):
    face_x = (
        harmonic(permeab[:, :, :-1, :], permeab[:, :, 1:, :]) * (inside[:-1] * inside[1:])[:, None]
    )
    face_y = harmonic(permeab[:, :, :, :-1], permeab[:, :, :, 1:])
    face_z = VERTICAL * harmonic(permeab[:, :-1], permeab[:, 1:])
    return (face_x, face_y, face_z)


def neighbours(face_sets, values_in):
    flow_sum = 0.0
    weight_sum = 0.0
    for faces_dim, along_dim in zip(face_sets, (2, 3, 1)):
        lower = pad_face(faces_dim, along_dim, True)
        upper = pad_face(faces_dim, along_dim, False)
        flow_sum = (
            flow_sum
            + lower * slide_by(values_in, along_dim, True)
            + upper * slide_by(values_in, along_dim, False)
        )
        weight_sum = weight_sum + lower + upper
    return (flow_sum, weight_sum)


def jacobi(pressure, baseline, storage_term, face_sets):
    flow_sum, weight_sum = neighbours(face_sets, pressure)
    return (baseline + flow_sum) / (storage_term + weight_sum)


def water_frac(values_in):
    squared = values_in * values_in
    return squared / (squared + VISCOSITY_RATIO * (1.0 - values_in) * (1.0 - values_in))


def transport(pressure, saturation, face_sets):
    fraction = water_frac(saturation)
    change = 0.0
    for faces_dim, along_dim in zip(face_sets, (2, 3, 1)):
        extent = pressure.shape[along_dim]
        lower_press = lax.slice_in_dim(pressure, 0, extent - 1, axis=along_dim)
        upper_press = lax.slice_in_dim(pressure, 1, extent, axis=along_dim)
        lower_frac = lax.slice_in_dim(fraction, 0, extent - 1, axis=along_dim)
        upper_frac = lax.slice_in_dim(fraction, 1, extent, axis=along_dim)
        velocity = faces_dim * (lower_press - upper_press)
        carried = velocity * jnp.where(velocity > 0, lower_frac, upper_frac)
        change = change + pad_face(carried, along_dim, True) - pad_face(carried, along_dim, False)
    return saturation + STEP_COEF * change


def solve_spd(gram_matrix, cross_matrix):
    factor = jnp.linalg.cholesky(gram_matrix + jnp.eye(gram_matrix.shape[0], dtype=jnp.float32))
    halfway = lax.linalg.triangular_solve(factor, cross_matrix, left_side=True, lower=True)
    return lax.linalg.triangular_solve(
        factor, halfway, left_side=True, lower=True, transpose_a=True
    )


def trim_rim(values_in, rim_cut):
    return values_in[:, :, rim_cut : values_in.shape[2] - rim_cut, :]


def exchange_kernel(member_count, part_ref, full_ref,
                    recv_a, send_a, recv_a_sem, send_m, recv_m_sem, send_t, recv_t_sem):
    tile_count = part_ref.shape[0]
    me_t = lax.axis_index("tile")
    me_m = lax.axis_index("member")
    mesh_ids = pl.DeviceIdType.MESH

    barrier = pltpu.get_barrier_semaphore()

    def greet_tile(k, carry):
        pl.semaphore_signal(
            barrier, 1, device_id=(lax.rem(me_t + k, tile_count), me_m), device_id_type=mesh_ids
        )
        return carry

    def greet_member(k, carry):
        pl.semaphore_signal(
            barrier, 1, device_id=(me_t, lax.rem(me_m + k, member_count)), device_id_type=mesh_ids
        )
        return carry

    lax.fori_loop(1, tile_count, greet_tile, 0)
    lax.fori_loop(1, member_count, greet_member, 0)
    pl.semaphore_wait(barrier, tile_count + member_count - 2)

    def copy_a(dst_t, src_t):
        return pltpu.make_async_remote_copy(
            src_ref=part_ref.at[dst_t], dst_ref=recv_a.at[src_t],
            send_sem=send_a.at[dst_t], recv_sem=recv_a_sem.at[src_t],
            device_id=(dst_t, me_m), device_id_type=mesh_ids,
        )

    def start_a(k, carry):
        copy_a(lax.rem(me_t + k, tile_count), me_t).start()
        return carry

    lax.fori_loop(1, tile_count, start_a, 0)

    def wait_a(k, acc):
        src_t = lax.rem(me_t + k, tile_count)
        copy_a(me_t, src_t).wait_recv()
        return acc + recv_a[src_t]

    acc = lax.fori_loop(1, tile_count, wait_a, part_ref[me_t])

    def wait_a_send(k, carry):
        copy_a(lax.rem(me_t + k, tile_count), me_t).wait_send()
        return carry

    lax.fori_loop(1, tile_count, wait_a_send, 0)

    full_ref[me_t, me_m] = acc

    def copy_m(dst_m, src_m):
        return pltpu.make_async_remote_copy(
            src_ref=full_ref.at[me_t, src_m], dst_ref=full_ref.at[me_t, src_m],
            send_sem=send_m.at[dst_m], recv_sem=recv_m_sem.at[src_m],
            device_id=(me_t, dst_m), device_id_type=mesh_ids,
        )

    def start_m(k, carry):
        copy_m(lax.rem(me_m + k, member_count), me_m).start()
        return carry

    lax.fori_loop(1, member_count, start_m, 0)

    def wait_m(k, carry):
        copy_m(me_m, lax.rem(me_m + k, member_count)).wait_recv()
        return carry

    lax.fori_loop(1, member_count, wait_m, 0)

    def wait_m_send(k, carry):
        copy_m(lax.rem(me_m + k, member_count), me_m).wait_send()
        return carry

    lax.fori_loop(1, member_count, wait_m_send, 0)

    def copy_t(dst_t, src_t):
        return pltpu.make_async_remote_copy(
            src_ref=full_ref.at[src_t], dst_ref=full_ref.at[src_t],
            send_sem=send_t.at[dst_t], recv_sem=recv_t_sem.at[src_t],
            device_id=(dst_t, me_m), device_id_type=mesh_ids,
        )

    def start_t(k, carry):
        copy_t(lax.rem(me_t + k, tile_count), me_t).start()
        return carry

    lax.fori_loop(1, tile_count, start_t, 0)

    def wait_t(k, carry):
        copy_t(me_t, lax.rem(me_t + k, tile_count)).wait_recv()
        return carry

    lax.fori_loop(1, tile_count, wait_t, 0)

    def wait_t_send(k, carry):
        copy_t(lax.rem(me_t + k, tile_count), me_t).wait_send()
        return carry

    lax.fori_loop(1, tile_count, wait_t_send, 0)


def halo_kernel(out_ref, in_ref, send_sem, recv_sem):
    tile_count = lax.axis_size("tile")
    me_t = lax.axis_index("tile")
    me_m = lax.axis_index("member")
    mesh_ids = pl.DeviceIdType.MESH
    left = lax.rem(me_t + tile_count - 1, tile_count)
    right = lax.rem(me_t + 1, tile_count)
    barrier = pltpu.get_barrier_semaphore()
    for peer in (left, right):
        pl.semaphore_signal(barrier, 1, device_id=(peer, me_m), device_id_type=mesh_ids)
    pl.semaphore_wait(barrier, 2)
    to_right = pltpu.make_async_remote_copy(
        src_ref=out_ref.at[1], dst_ref=in_ref.at[0], send_sem=send_sem.at[1],
        recv_sem=recv_sem.at[0], device_id=(right, me_m), device_id_type=mesh_ids,
    )
    to_left = pltpu.make_async_remote_copy(
        src_ref=out_ref.at[0], dst_ref=in_ref.at[1], send_sem=send_sem.at[0],
        recv_sem=recv_sem.at[1], device_id=(left, me_m), device_id_type=mesh_ids,
    )
    to_right.start()
    to_left.start()
    to_right.wait()
    to_left.wait()


def halo_exchange(outgoing):
    vmem = pl.BlockSpec(memory_space=pltpu.VMEM)
    return pl.pallas_call(
        halo_kernel,
        out_shape=jax.ShapeDtypeStruct(outgoing.shape, outgoing.dtype),
        in_specs=[vmem],
        out_specs=vmem,
        scratch_shapes=[pltpu.SemaphoreType.DMA((2,)), pltpu.SemaphoreType.DMA((2,))],
        compiler_params=pltpu.CompilerParams(collective_id=1, has_side_effects=True),
    )(outgoing)


def rates_exchange(pieces, member_count):
    tile_count, rows, lanes = pieces.shape
    vmem = pl.BlockSpec(memory_space=pltpu.VMEM)
    return pl.pallas_call(
        functools.partial(exchange_kernel, member_count),
        out_shape=jax.ShapeDtypeStruct((tile_count, member_count, rows, lanes), jnp.float32),
        in_specs=[vmem],
        out_specs=vmem,
        scratch_shapes=[
            pltpu.VMEM((tile_count, rows, lanes), jnp.float32),
            pltpu.SemaphoreType.DMA((tile_count,)),
            pltpu.SemaphoreType.DMA((tile_count,)),
            pltpu.SemaphoreType.DMA((member_count,)),
            pltpu.SemaphoreType.DMA((member_count,)),
            pltpu.SemaphoreType.DMA((tile_count,)),
            pltpu.SemaphoreType.DMA((tile_count,)),
        ],
        compiler_params=pltpu.CompilerParams(collective_id=0, has_side_effects=True),
    )(pieces)


def per_device(
    log_perm,
    start_pressure,
    start_sat,
    source,
    storage,
    well_press,
    perf_cell,
    perf_well,
    perf_count,
    observed,
    obs_var,
    obs_noise,
):
    local_count, layers, strip_width, strip_depth = log_perm.shape
    tile_count = lax.axis_size("tile")
    members = local_count * lax.axis_size("member")
    well_count = well_press.shape[0]
    well_share = well_count // tile_count
    tile_rank = lax.axis_index("tile")
    member_rank = lax.axis_index("member")
    rim = SWEEPS + 1
    fields = jnp.stack([start_pressure, start_sat, source, storage])
    halo_rows = local_count * layers * rim + fields.shape[0] * layers * rim

    def rim_rows(first):
        return jnp.concatenate(
            [
                lax.slice_in_dim(log_perm, first, first + rim, axis=2).reshape(-1, strip_depth),
                lax.slice_in_dim(fields, first, first + rim, axis=2).reshape(-1, strip_depth),
            ]
        )

    outgoing = jnp.stack([rim_rows(0), rim_rows(strip_width - rim)])
    incoming = halo_exchange(outgoing)
    lp_count = local_count * layers * rim

    def unpack(side):
        lp_part = incoming[side, :lp_count].reshape(local_count, layers, rim, strip_depth)
        field_part = incoming[side, lp_count:].reshape(fields.shape[0], layers, rim, strip_depth)
        return lp_part, field_part

    low_lp, low_fields = unpack(0)
    high_lp, high_fields = unpack(1)
    lp_ext = jnp.concatenate([low_lp, log_perm, high_lp], axis=2)
    fields_ext = jnp.concatenate([low_fields, fields, high_fields], axis=2)
    permeab = jnp.exp(lp_ext)
    column = tile_rank * strip_width - rim + jnp.arange(strip_width + 2 * rim, dtype=jnp.int32)
    inside = (column >= 0) & (column < strip_width * tile_count)
    face_sets = face_terms(permeab, inside.astype(jnp.float32))
    press_ext, sat_ext, source_ext, storage_ext = (fields_ext[i] for i in range(4))
    baseline = (source_ext + storage_ext * press_ext)[None]
    storage_term = jnp.where(inside[None, :, None], storage_ext, 1.0)[None]
    pressure = jnp.broadcast_to(press_ext[None], (local_count,) + press_ext.shape)
    for sweep_idx in range(SWEEPS):
        pressure = jacobi(pressure, baseline, storage_term, face_sets)
    saturation = trim_rim(transport(pressure, sat_ext[None], face_sets), rim)
    pressure = trim_rim(pressure, rim)
    permeab = trim_rim(permeab, rim)
    cell_count = layers * strip_width * strip_depth
    mobility = (permeab * water_frac(saturation)).reshape(local_count, cell_count)
    cell_press = pressure.reshape(local_count, cell_count)
    perf_mob = jnp.take(mobility, perf_cell, axis=1)
    perf_press = jnp.take(cell_press, perf_cell, axis=1)
    selector = (perf_well[:, None] == jnp.arange(well_count, dtype=jnp.int32)[None, :]).astype(
        jnp.float32
    )
    perf_bhp = jnp.dot(selector, well_press, precision=lax.Precision.HIGHEST)
    live_mask = (jnp.arange(perf_cell.shape[0], dtype=jnp.int32) < perf_count[0]).astype(
        jnp.float32
    )
    perf_terms = perf_mob * (perf_press - perf_bhp[None]) * live_mask[None]
    partial_rates = jnp.dot(
        perf_terms, selector, precision=lax.Precision.HIGHEST, preferred_element_type=jnp.float32
    )
    member_root = (members - 1) ** 0.5
    spread = jnp.sqrt(INFLATION * obs_var)
    member_count = lax.axis_size("member")
    block_rows = local_count * well_share // 128
    pieces = partial_rates.reshape(local_count, tile_count, well_share).transpose(1, 0, 2)
    pieces = pieces.reshape(tile_count, block_rows, 128)
    full = rates_exchange(pieces, member_count)
    full = full.reshape(tile_count, member_count, local_count, well_share)
    rates_all = full.transpose(1, 2, 0, 3).reshape(members, well_count)
    well_rates = lax.dynamic_index_in_dim(
        lax.dynamic_index_in_dim(full, tile_rank, 0, keepdims=False), member_rank, 0, keepdims=False
    )
    rates_own = lax.dynamic_index_in_dim(full, member_rank, 1, keepdims=False)
    rates_own = rates_own.transpose(1, 0, 2).reshape(local_count, well_count)
    innov_own = (observed - rates_own) / spread + obs_noise
    mean_rate = jnp.sum(rates_all, 0) / members
    scaled_all = (rates_all - mean_rate) / (spread * member_root)
    gram_matrix = jnp.dot(
        scaled_all, scaled_all.T, precision=lax.Precision.HIGHEST, preferred_element_type=jnp.float32
    )
    cross_matrix = jnp.dot(
        scaled_all, innov_own.T, precision=lax.Precision.HIGHEST, preferred_element_type=jnp.float32
    )
    weights_low = solve_spd(gram_matrix, cross_matrix).astype(jnp.bfloat16)
    anomaly = (log_perm / member_root).astype(jnp.bfloat16).reshape(local_count, cell_count)
    anomaly_parts = [anomaly]
    for shift in range(1, member_count):
        pairs = [(i, (i + shift) % member_count) for i in range(member_count)]
        anomaly_parts.append(lax.ppermute(anomaly, "member", pairs))
    anomaly_all = jnp.concatenate(anomaly_parts, axis=0)
    own_cols = jnp.concatenate(
        [
            lax.dynamic_slice_in_dim(
                weights_low, lax.rem(member_rank - shift + member_count, member_count) * local_count,
                local_count, 0,
            )
            for shift in range(member_count)
        ],
        axis=0,
    )
    contract = (((0,), (0,)), ((), ()))
    update_sum = lax.dot_general(own_cols, anomaly_all, contract, preferred_element_type=jnp.float32)
    new_log_perm = log_perm + update_sum.reshape(log_perm.shape)
    return (new_log_perm, pressure, saturation, well_rates)


def solution(mesh):
    return jax.shard_map(
        per_device,
        mesh=mesh,
        in_specs=(
            P("member", None, "tile", None),
            P(None, "tile", None),
            P(None, "tile", None),
            P(None, "tile", None),
            P(None, "tile", None),
            P(),
            P("tile"),
            P("tile"),
            P("tile"),
            P(),
            P(),
            P("member", None),
        ),
        out_specs=(
            P("member", None, "tile", None),
            P("member", None, "tile", None),
            P("member", None, "tile", None),
            P("member", "tile"),
        ),
        check_vma=False,
    )
```

```python
import functools

import jax
import jax.numpy as jnp
from jax import lax
from jax.experimental import pallas as pl
from jax.experimental.pallas import tpu as pltpu
from jax.sharding import PartitionSpec as P

SWEEPS = 2


VERTICAL = 0.5
VISCOSITY_RATIO = 2.0
STEP_COEF = 0.1
INFLATION = 4.0


def extended_2(block, sides, width):
    for axis, dim in sides:
        count = lax.axis_size(axis)
        forward = [(i, i + 1) for i in range(count - 1)]
        backward = [(target, source) for source, target in forward]
        low = lax.ppermute(
            lax.slice_in_dim(block, block.shape[dim] - width, None, axis=dim), axis, forward
        )
        high = lax.ppermute(lax.slice_in_dim(block, 0, width, axis=dim), axis, backward)
        block = jnp.concatenate([low, block, high], axis=dim)
    return block


def harmonic(lower_val, upper_val):
    return 2.0 * lower_val * upper_val / (lower_val + upper_val)


def pad_face(values_in, along_dim, before):
    widths = [(0, 0)] * values_in.ndim
    widths[along_dim] = (1, 0) if before else (0, 1)
    return jnp.pad(values_in, widths)


def slide_by(values_in, along_dim, before):
    extent = values_in.shape[along_dim]
    if before:
        remain = lax.slice_in_dim(values_in, 0, extent - 1, axis=along_dim)
    else:
        remain = lax.slice_in_dim(values_in, 1, extent, axis=along_dim)
    return pad_face(remain, along_dim, before)


def face_terms(permeab, inside):
    face_x = (
        harmonic(permeab[:, :, :-1, :], permeab[:, :, 1:, :]) * (inside[:-1] * inside[1:])[:, None]
    )
    face_y = harmonic(permeab[:, :, :, :-1], permeab[:, :, :, 1:])
    face_z = VERTICAL * harmonic(permeab[:, :-1], permeab[:, 1:])
    return (face_x, face_y, face_z)


def neighbours(face_sets, values_in):
    flow_sum = 0.0
    weight_sum = 0.0
    for faces_dim, along_dim in zip(face_sets, (2, 3, 1)):
        lower = pad_face(faces_dim, along_dim, True)
        upper = pad_face(faces_dim, along_dim, False)
        flow_sum = (
            flow_sum
            + lower * slide_by(values_in, along_dim, True)
            + upper * slide_by(values_in, along_dim, False)
        )
        weight_sum = weight_sum + lower + upper
    return (flow_sum, weight_sum)


def jacobi(pressure, baseline, storage_term, face_sets):
    flow_sum, weight_sum = neighbours(face_sets, pressure)
    return (baseline + flow_sum) / (storage_term + weight_sum)


def water_frac(values_in):
    squared = values_in * values_in
    return squared / (squared + VISCOSITY_RATIO * (1.0 - values_in) * (1.0 - values_in))


def transport(pressure, saturation, face_sets):
    fraction = water_frac(saturation)
    change = 0.0
    for faces_dim, along_dim in zip(face_sets, (2, 3, 1)):
        extent = pressure.shape[along_dim]
        lower_press = lax.slice_in_dim(pressure, 0, extent - 1, axis=along_dim)
        upper_press = lax.slice_in_dim(pressure, 1, extent, axis=along_dim)
        lower_frac = lax.slice_in_dim(fraction, 0, extent - 1, axis=along_dim)
        upper_frac = lax.slice_in_dim(fraction, 1, extent, axis=along_dim)
        velocity = faces_dim * (lower_press - upper_press)
        carried = velocity * jnp.where(velocity > 0, lower_frac, upper_frac)
        change = change + pad_face(carried, along_dim, True) - pad_face(carried, along_dim, False)
    return saturation + STEP_COEF * change


def solve_spd(gram_matrix, cross_matrix):
    factor = jnp.linalg.cholesky(gram_matrix + jnp.eye(gram_matrix.shape[0], dtype=jnp.float32))
    halfway = lax.linalg.triangular_solve(factor, cross_matrix, left_side=True, lower=True)
    return lax.linalg.triangular_solve(
        factor, halfway, left_side=True, lower=True, transpose_a=True
    )


def trim_rim(values_in, rim_cut):
    return values_in[:, :, rim_cut : values_in.shape[2] - rim_cut, :]


def exchange_kernel(member_count, part_ref, full_ref,
                    recv_a, send_a, recv_a_sem, send_m, recv_m_sem, send_t, recv_t_sem):
    tile_count = part_ref.shape[0]
    me_t = lax.axis_index("tile")
    me_m = lax.axis_index("member")
    mesh_ids = pl.DeviceIdType.MESH

    barrier = pltpu.get_barrier_semaphore()

    def greet_tile(k, carry):
        pl.semaphore_signal(
            barrier, 1, device_id=(lax.rem(me_t + k, tile_count), me_m), device_id_type=mesh_ids
        )
        return carry

    def greet_member(k, carry):
        pl.semaphore_signal(
            barrier, 1, device_id=(me_t, lax.rem(me_m + k, member_count)), device_id_type=mesh_ids
        )
        return carry

    lax.fori_loop(1, tile_count, greet_tile, 0)
    lax.fori_loop(1, member_count, greet_member, 0)
    pl.semaphore_wait(barrier, tile_count + member_count - 2)

    def copy_a(dst_t, src_t):
        return pltpu.make_async_remote_copy(
            src_ref=part_ref.at[dst_t], dst_ref=recv_a.at[src_t],
            send_sem=send_a.at[dst_t], recv_sem=recv_a_sem.at[src_t],
            device_id=(dst_t, me_m), device_id_type=mesh_ids,
        )

    def start_a(k, carry):
        copy_a(lax.rem(me_t + k, tile_count), me_t).start()
        return carry

    lax.fori_loop(1, tile_count, start_a, 0)

    def wait_a(k, acc):
        src_t = lax.rem(me_t + k, tile_count)
        copy_a(me_t, src_t).wait_recv()
        return acc + recv_a[src_t]

    acc = lax.fori_loop(1, tile_count, wait_a, part_ref[me_t])

    def wait_a_send(k, carry):
        copy_a(lax.rem(me_t + k, tile_count), me_t).wait_send()
        return carry

    lax.fori_loop(1, tile_count, wait_a_send, 0)

    full_ref[me_t, me_m] = acc

    def copy_m(dst_m, src_m):
        return pltpu.make_async_remote_copy(
            src_ref=full_ref.at[me_t, src_m], dst_ref=full_ref.at[me_t, src_m],
            send_sem=send_m.at[dst_m], recv_sem=recv_m_sem.at[src_m],
            device_id=(me_t, dst_m), device_id_type=mesh_ids,
        )

    def start_m(k, carry):
        copy_m(lax.rem(me_m + k, member_count), me_m).start()
        return carry

    lax.fori_loop(1, member_count, start_m, 0)

    def wait_m(k, carry):
        copy_m(me_m, lax.rem(me_m + k, member_count)).wait_recv()
        return carry

    lax.fori_loop(1, member_count, wait_m, 0)

    def wait_m_send(k, carry):
        copy_m(lax.rem(me_m + k, member_count), me_m).wait_send()
        return carry

    lax.fori_loop(1, member_count, wait_m_send, 0)

    def copy_t(dst_t, src_t):
        return pltpu.make_async_remote_copy(
            src_ref=full_ref.at[src_t], dst_ref=full_ref.at[src_t],
            send_sem=send_t.at[dst_t], recv_sem=recv_t_sem.at[src_t],
            device_id=(dst_t, me_m), device_id_type=mesh_ids,
        )

    def start_t(k, carry):
        copy_t(lax.rem(me_t + k, tile_count), me_t).start()
        return carry

    lax.fori_loop(1, tile_count, start_t, 0)

    def wait_t(k, carry):
        copy_t(me_t, lax.rem(me_t + k, tile_count)).wait_recv()
        return carry

    lax.fori_loop(1, tile_count, wait_t, 0)

    def wait_t_send(k, carry):
        copy_t(lax.rem(me_t + k, tile_count), me_t).wait_send()
        return carry

    lax.fori_loop(1, tile_count, wait_t_send, 0)


def halo_kernel(out_ref, in_ref, send_sem, recv_sem):
    tile_count = lax.axis_size("tile")
    me_t = lax.axis_index("tile")
    me_m = lax.axis_index("member")
    mesh_ids = pl.DeviceIdType.MESH
    left = lax.rem(me_t + tile_count - 1, tile_count)
    right = lax.rem(me_t + 1, tile_count)
    barrier = pltpu.get_barrier_semaphore()
    for peer in (left, right):
        pl.semaphore_signal(barrier, 1, device_id=(peer, me_m), device_id_type=mesh_ids)
    pl.semaphore_wait(barrier, 2)
    to_right = pltpu.make_async_remote_copy(
        src_ref=out_ref.at[1], dst_ref=in_ref.at[0], send_sem=send_sem.at[1],
        recv_sem=recv_sem.at[0], device_id=(right, me_m), device_id_type=mesh_ids,
    )
    to_left = pltpu.make_async_remote_copy(
        src_ref=out_ref.at[0], dst_ref=in_ref.at[1], send_sem=send_sem.at[0],
        recv_sem=recv_sem.at[1], device_id=(left, me_m), device_id_type=mesh_ids,
    )
    to_right.start()
    to_left.start()
    to_right.wait()
    to_left.wait()


def halo_exchange(outgoing):
    vmem = pl.BlockSpec(memory_space=pltpu.VMEM)
    return pl.pallas_call(
        halo_kernel,
        out_shape=jax.ShapeDtypeStruct(outgoing.shape, outgoing.dtype),
        in_specs=[vmem],
        out_specs=vmem,
        scratch_shapes=[pltpu.SemaphoreType.DMA((2,)), pltpu.SemaphoreType.DMA((2,))],
        compiler_params=pltpu.CompilerParams(collective_id=1, has_side_effects=True),
    )(outgoing)


def rates_exchange(pieces, member_count):
    tile_count, rows, lanes = pieces.shape
    vmem = pl.BlockSpec(memory_space=pltpu.VMEM)
    return pl.pallas_call(
        functools.partial(exchange_kernel, member_count),
        out_shape=jax.ShapeDtypeStruct((tile_count, member_count, rows, lanes), jnp.float32),
        in_specs=[vmem],
        out_specs=vmem,
        scratch_shapes=[
            pltpu.VMEM((tile_count, rows, lanes), jnp.float32),
            pltpu.SemaphoreType.DMA((tile_count,)),
            pltpu.SemaphoreType.DMA((tile_count,)),
            pltpu.SemaphoreType.DMA((member_count,)),
            pltpu.SemaphoreType.DMA((member_count,)),
            pltpu.SemaphoreType.DMA((tile_count,)),
            pltpu.SemaphoreType.DMA((tile_count,)),
        ],
        compiler_params=pltpu.CompilerParams(collective_id=0, has_side_effects=True),
    )(pieces)


def per_device(
    log_perm,
    start_pressure,
    start_sat,
    source,
    storage,
    well_press,
    perf_cell,
    perf_well,
    perf_count,
    observed,
    obs_var,
    obs_noise,
):
    local_count, layers, strip_width, strip_depth = log_perm.shape
    tile_count = lax.axis_size("tile")
    members = local_count * lax.axis_size("member")
    well_count = well_press.shape[0]
    well_share = well_count // tile_count
    tile_rank = lax.axis_index("tile")
    member_rank = lax.axis_index("member")
    rim = SWEEPS + 1
    fields = jnp.stack([start_pressure, start_sat, source, storage])
    halo_rows = local_count * layers * rim + fields.shape[0] * layers * rim

    def rim_rows(first):
        return jnp.concatenate(
            [
                lax.slice_in_dim(log_perm, first, first + rim, axis=2).reshape(-1, strip_depth),
                lax.slice_in_dim(fields, first, first + rim, axis=2).reshape(-1, strip_depth),
            ]
        )

    outgoing = jnp.stack([rim_rows(0), rim_rows(strip_width - rim)])
    incoming = halo_exchange(outgoing)
    lp_count = local_count * layers * rim

    def unpack(side):
        lp_part = incoming[side, :lp_count].reshape(local_count, layers, rim, strip_depth)
        field_part = incoming[side, lp_count:].reshape(fields.shape[0], layers, rim, strip_depth)
        return lp_part, field_part

    low_lp, low_fields = unpack(0)
    high_lp, high_fields = unpack(1)
    lp_ext = jnp.concatenate([low_lp, log_perm, high_lp], axis=2)
    fields_ext = jnp.concatenate([low_fields, fields, high_fields], axis=2)
    permeab = jnp.exp(lp_ext)
    column = tile_rank * strip_width - rim + jnp.arange(strip_width + 2 * rim, dtype=jnp.int32)
    inside = (column >= 0) & (column < strip_width * tile_count)
    face_sets = face_terms(permeab, inside.astype(jnp.float32))
    press_ext, sat_ext, source_ext, storage_ext = (fields_ext[i] for i in range(4))
    baseline = (source_ext + storage_ext * press_ext)[None]
    storage_term = jnp.where(inside[None, :, None], storage_ext, 1.0)[None]
    pressure = jnp.broadcast_to(press_ext[None], (local_count,) + press_ext.shape)
    for sweep_idx in range(SWEEPS):
        pressure = jacobi(pressure, baseline, storage_term, face_sets)
    saturation = trim_rim(transport(pressure, sat_ext[None], face_sets), rim)
    pressure = trim_rim(pressure, rim)
    permeab = trim_rim(permeab, rim)
    cell_count = layers * strip_width * strip_depth
    mobility = permeab * water_frac(saturation)
    cell_layer = perf_cell // (strip_width * strip_depth)
    cell_row = lax.rem(perf_cell // strip_depth, strip_width)
    cell_col = lax.rem(perf_cell, strip_depth)
    perf_mob = mobility[:, cell_layer, cell_row, cell_col]
    perf_press = pressure[:, cell_layer, cell_row, cell_col]
    selector = (perf_well[:, None] == jnp.arange(well_count, dtype=jnp.int32)[None, :]).astype(
        jnp.float32
    )
    perf_bhp = jnp.dot(selector, well_press, precision=lax.Precision.HIGHEST)
    live_mask = (jnp.arange(perf_cell.shape[0], dtype=jnp.int32) < perf_count[0]).astype(
        jnp.float32
    )
    perf_terms = perf_mob * (perf_press - perf_bhp[None]) * live_mask[None]
    partial_rates = jnp.dot(
        perf_terms, selector, precision=lax.Precision.HIGHEST, preferred_element_type=jnp.float32
    )
    member_root = (members - 1) ** 0.5
    spread = jnp.sqrt(INFLATION * obs_var)
    member_count = lax.axis_size("member")
    block_rows = local_count * well_share // 128
    pieces = partial_rates.reshape(local_count, tile_count, well_share).transpose(1, 0, 2)
    pieces = pieces.reshape(tile_count, block_rows, 128)
    full = rates_exchange(pieces, member_count)
    full = full.reshape(tile_count, member_count, local_count, well_share)
    rates_all = full.transpose(1, 2, 0, 3).reshape(members, well_count)
    well_rates = lax.dynamic_index_in_dim(
        lax.dynamic_index_in_dim(full, tile_rank, 0, keepdims=False), member_rank, 0, keepdims=False
    )
    rates_own = lax.dynamic_slice_in_dim(rates_all, member_rank * local_count, local_count, 0)
    innov_own = (observed - rates_own) / spread + obs_noise
    mean_rate = jnp.sum(rates_all, 0) / members
    scaled_all = (rates_all - mean_rate) / (spread * member_root)
    gram_matrix = jnp.dot(
        scaled_all, scaled_all.T, precision=lax.Precision.HIGHEST, preferred_element_type=jnp.float32
    )
    cross_matrix = jnp.dot(
        scaled_all, innov_own.T, precision=lax.Precision.HIGHEST, preferred_element_type=jnp.float32
    )
    weights_low = solve_spd(gram_matrix, cross_matrix).astype(jnp.bfloat16)
    anomaly = (log_perm / member_root).astype(jnp.bfloat16).reshape(local_count, cell_count)
    anomaly_parts = [anomaly]
    for shift in range(1, member_count):
        pairs = [(i, (i + shift) % member_count) for i in range(member_count)]
        anomaly_parts.append(lax.ppermute(anomaly, "member", pairs))
    anomaly_all = jnp.concatenate(anomaly_parts, axis=0)
    own_cols = jnp.concatenate(
        [
            lax.dynamic_slice_in_dim(
                weights_low, lax.rem(member_rank - shift + member_count, member_count) * local_count,
                local_count, 0,
            )
            for shift in range(member_count)
        ],
        axis=0,
    )
    contract = (((0,), (0,)), ((), ()))
    update_sum = lax.dot_general(own_cols, anomaly_all, contract, preferred_element_type=jnp.float32)
    new_log_perm = log_perm + update_sum.reshape(log_perm.shape)
    return (new_log_perm, pressure, saturation, well_rates)


def solution(mesh):
    return jax.shard_map(
        per_device,
        mesh=mesh,
        in_specs=(
            P("member", None, "tile", None),
            P(None, "tile", None),
            P(None, "tile", None),
            P(None, "tile", None),
            P(None, "tile", None),
            P(),
            P("tile"),
            P("tile"),
            P("tile"),
            P(),
            P(),
            P("member", None),
        ),
        out_specs=(
            P("member", None, "tile", None),
            P("member", None, "tile", None),
            P("member", None, "tile", None),
            P("member", "tile"),
        ),
        check_vma=False,
    )
```

```python
import functools

import jax
import jax.numpy as jnp
from jax import lax
from jax.experimental import pallas as pl
from jax.experimental.pallas import tpu as pltpu
from jax.sharding import PartitionSpec as P

SWEEPS = 2


VERTICAL = 0.5
VISCOSITY_RATIO = 2.0
STEP_COEF = 0.1
INFLATION = 4.0


def extended_2(block, sides, width):
    for axis, dim in sides:
        count = lax.axis_size(axis)
        forward = [(i, i + 1) for i in range(count - 1)]
        backward = [(target, source) for source, target in forward]
        low = lax.ppermute(
            lax.slice_in_dim(block, block.shape[dim] - width, None, axis=dim), axis, forward
        )
        high = lax.ppermute(lax.slice_in_dim(block, 0, width, axis=dim), axis, backward)
        block = jnp.concatenate([low, block, high], axis=dim)
    return block


def harmonic(lower_val, upper_val):
    return 2.0 * lower_val * upper_val / (lower_val + upper_val)


def pad_face(values_in, along_dim, before):
    widths = [(0, 0)] * values_in.ndim
    widths[along_dim] = (1, 0) if before else (0, 1)
    return jnp.pad(values_in, widths)


def slide_by(values_in, along_dim, before):
    extent = values_in.shape[along_dim]
    if before:
        remain = lax.slice_in_dim(values_in, 0, extent - 1, axis=along_dim)
    else:
        remain = lax.slice_in_dim(values_in, 1, extent, axis=along_dim)
    return pad_face(remain, along_dim, before)


def face_terms(permeab, inside):
    face_x = (
        harmonic(permeab[:, :, :-1, :], permeab[:, :, 1:, :]) * (inside[:-1] * inside[1:])[:, None]
    )
    face_y = harmonic(permeab[:, :, :, :-1], permeab[:, :, :, 1:])
    face_z = VERTICAL * harmonic(permeab[:, :-1], permeab[:, 1:])
    return (face_x, face_y, face_z)


def neighbours(face_sets, values_in):
    flow_sum = 0.0
    weight_sum = 0.0
    for faces_dim, along_dim in zip(face_sets, (2, 3, 1)):
        lower = pad_face(faces_dim, along_dim, True)
        upper = pad_face(faces_dim, along_dim, False)
        flow_sum = (
            flow_sum
            + lower * slide_by(values_in, along_dim, True)
            + upper * slide_by(values_in, along_dim, False)
        )
        weight_sum = weight_sum + lower + upper
    return (flow_sum, weight_sum)


def jacobi(pressure, baseline, storage_term, face_sets):
    flow_sum, weight_sum = neighbours(face_sets, pressure)
    return (baseline + flow_sum) / (storage_term + weight_sum)


def water_frac(values_in):
    squared = values_in * values_in
    return squared / (squared + VISCOSITY_RATIO * (1.0 - values_in) * (1.0 - values_in))


def transport(pressure, saturation, face_sets):
    fraction = water_frac(saturation)
    change = 0.0
    for faces_dim, along_dim in zip(face_sets, (2, 3, 1)):
        extent = pressure.shape[along_dim]
        lower_press = lax.slice_in_dim(pressure, 0, extent - 1, axis=along_dim)
        upper_press = lax.slice_in_dim(pressure, 1, extent, axis=along_dim)
        lower_frac = lax.slice_in_dim(fraction, 0, extent - 1, axis=along_dim)
        upper_frac = lax.slice_in_dim(fraction, 1, extent, axis=along_dim)
        velocity = faces_dim * (lower_press - upper_press)
        carried = velocity * jnp.where(velocity > 0, lower_frac, upper_frac)
        change = change + pad_face(carried, along_dim, True) - pad_face(carried, along_dim, False)
    return saturation + STEP_COEF * change


def solve_spd(gram_matrix, cross_matrix):
    factor = jnp.linalg.cholesky(gram_matrix + jnp.eye(gram_matrix.shape[0], dtype=jnp.float32))
    halfway = lax.linalg.triangular_solve(factor, cross_matrix, left_side=True, lower=True)
    return lax.linalg.triangular_solve(
        factor, halfway, left_side=True, lower=True, transpose_a=True
    )


def trim_rim(values_in, rim_cut):
    return values_in[:, :, rim_cut : values_in.shape[2] - rim_cut, :]


def exchange_kernel(member_count, part_ref, anom_ref, full_ref, anom_all_ref,
                    recv_a, send_a, recv_a_sem, send_m, recv_m_sem, send_t, recv_t_sem,
                    send_n, recv_n_sem):
    tile_count = part_ref.shape[0]
    me_t = lax.axis_index("tile")
    me_m = lax.axis_index("member")
    mesh_ids = pl.DeviceIdType.MESH

    barrier = pltpu.get_barrier_semaphore()

    def greet_tile(k, carry):
        pl.semaphore_signal(
            barrier, 1, device_id=(lax.rem(me_t + k, tile_count), me_m), device_id_type=mesh_ids
        )
        return carry

    def greet_member(k, carry):
        pl.semaphore_signal(
            barrier, 1, device_id=(me_t, lax.rem(me_m + k, member_count)), device_id_type=mesh_ids
        )
        return carry

    lax.fori_loop(1, tile_count, greet_tile, 0)
    lax.fori_loop(1, member_count, greet_member, 0)
    pl.semaphore_wait(barrier, tile_count + member_count - 2)

    def copy_n(dst_m, src_m):
        return pltpu.make_async_remote_copy(
            src_ref=anom_ref, dst_ref=anom_all_ref.at[src_m],
            send_sem=send_n.at[dst_m], recv_sem=recv_n_sem.at[src_m],
            device_id=(me_t, dst_m), device_id_type=mesh_ids,
        )

    def start_n(k, carry):
        copy_n(lax.rem(me_m + k, member_count), me_m).start()
        return carry

    lax.fori_loop(1, member_count, start_n, 0)
    anom_all_ref[me_m] = anom_ref[...]

    def copy_a(dst_t, src_t):
        return pltpu.make_async_remote_copy(
            src_ref=part_ref.at[dst_t], dst_ref=recv_a.at[src_t],
            send_sem=send_a.at[dst_t], recv_sem=recv_a_sem.at[src_t],
            device_id=(dst_t, me_m), device_id_type=mesh_ids,
        )

    def start_a(k, carry):
        copy_a(lax.rem(me_t + k, tile_count), me_t).start()
        return carry

    lax.fori_loop(1, tile_count, start_a, 0)

    def wait_a(k, acc):
        src_t = lax.rem(me_t + k, tile_count)
        copy_a(me_t, src_t).wait_recv()
        return acc + recv_a[src_t]

    acc = lax.fori_loop(1, tile_count, wait_a, part_ref[me_t])

    def wait_a_send(k, carry):
        copy_a(lax.rem(me_t + k, tile_count), me_t).wait_send()
        return carry

    lax.fori_loop(1, tile_count, wait_a_send, 0)

    full_ref[me_t, me_m] = acc

    def copy_m(dst_m, src_m):
        return pltpu.make_async_remote_copy(
            src_ref=full_ref.at[me_t, src_m], dst_ref=full_ref.at[me_t, src_m],
            send_sem=send_m.at[dst_m], recv_sem=recv_m_sem.at[src_m],
            device_id=(me_t, dst_m), device_id_type=mesh_ids,
        )

    def start_m(k, carry):
        copy_m(lax.rem(me_m + k, member_count), me_m).start()
        return carry

    lax.fori_loop(1, member_count, start_m, 0)

    def wait_m(k, carry):
        copy_m(me_m, lax.rem(me_m + k, member_count)).wait_recv()
        return carry

    lax.fori_loop(1, member_count, wait_m, 0)

    def wait_m_send(k, carry):
        copy_m(lax.rem(me_m + k, member_count), me_m).wait_send()
        return carry

    lax.fori_loop(1, member_count, wait_m_send, 0)

    def copy_t(dst_t, src_t):
        return pltpu.make_async_remote_copy(
            src_ref=full_ref.at[src_t], dst_ref=full_ref.at[src_t],
            send_sem=send_t.at[dst_t], recv_sem=recv_t_sem.at[src_t],
            device_id=(dst_t, me_m), device_id_type=mesh_ids,
        )

    def start_t(k, carry):
        copy_t(lax.rem(me_t + k, tile_count), me_t).start()
        return carry

    lax.fori_loop(1, tile_count, start_t, 0)

    def wait_t(k, carry):
        copy_t(me_t, lax.rem(me_t + k, tile_count)).wait_recv()
        return carry

    lax.fori_loop(1, tile_count, wait_t, 0)

    def wait_t_send(k, carry):
        copy_t(lax.rem(me_t + k, tile_count), me_t).wait_send()
        return carry

    lax.fori_loop(1, tile_count, wait_t_send, 0)

    def wait_n(k, carry):
        copy_n(me_m, lax.rem(me_m + k, member_count)).wait_recv()
        return carry

    lax.fori_loop(1, member_count, wait_n, 0)

    def wait_n_send(k, carry):
        copy_n(lax.rem(me_m + k, member_count), me_m).wait_send()
        return carry

    lax.fori_loop(1, member_count, wait_n_send, 0)


def halo_kernel(out_ref, in_ref, send_sem, recv_sem):
    tile_count = lax.axis_size("tile")
    me_t = lax.axis_index("tile")
    me_m = lax.axis_index("member")
    mesh_ids = pl.DeviceIdType.MESH
    left = lax.rem(me_t + tile_count - 1, tile_count)
    right = lax.rem(me_t + 1, tile_count)
    barrier = pltpu.get_barrier_semaphore()
    for peer in (left, right):
        pl.semaphore_signal(barrier, 1, device_id=(peer, me_m), device_id_type=mesh_ids)
    pl.semaphore_wait(barrier, 2)
    to_right = pltpu.make_async_remote_copy(
        src_ref=out_ref.at[1], dst_ref=in_ref.at[0], send_sem=send_sem.at[1],
        recv_sem=recv_sem.at[0], device_id=(right, me_m), device_id_type=mesh_ids,
    )
    to_left = pltpu.make_async_remote_copy(
        src_ref=out_ref.at[0], dst_ref=in_ref.at[1], send_sem=send_sem.at[0],
        recv_sem=recv_sem.at[1], device_id=(left, me_m), device_id_type=mesh_ids,
    )
    to_right.start()
    to_left.start()
    to_right.wait()
    to_left.wait()


def halo_exchange(outgoing):
    vmem = pl.BlockSpec(memory_space=pltpu.VMEM)
    return pl.pallas_call(
        halo_kernel,
        out_shape=jax.ShapeDtypeStruct(outgoing.shape, outgoing.dtype),
        in_specs=[vmem],
        out_specs=vmem,
        scratch_shapes=[pltpu.SemaphoreType.DMA((2,)), pltpu.SemaphoreType.DMA((2,))],
        compiler_params=pltpu.CompilerParams(collective_id=1, has_side_effects=True),
    )(outgoing)


def rates_exchange(pieces, anomaly, member_count):
    tile_count, rows, lanes = pieces.shape
    vmem = pl.BlockSpec(memory_space=pltpu.VMEM)
    return pl.pallas_call(
        functools.partial(exchange_kernel, member_count),
        out_shape=(
            jax.ShapeDtypeStruct((tile_count, member_count, rows, lanes), jnp.float32),
            jax.ShapeDtypeStruct((member_count,) + anomaly.shape, anomaly.dtype),
        ),
        in_specs=[vmem, vmem],
        out_specs=(vmem, vmem),
        scratch_shapes=[
            pltpu.VMEM((tile_count, rows, lanes), jnp.float32),
            pltpu.SemaphoreType.DMA((tile_count,)),
            pltpu.SemaphoreType.DMA((tile_count,)),
            pltpu.SemaphoreType.DMA((member_count,)),
            pltpu.SemaphoreType.DMA((member_count,)),
            pltpu.SemaphoreType.DMA((tile_count,)),
            pltpu.SemaphoreType.DMA((tile_count,)),
            pltpu.SemaphoreType.DMA((member_count,)),
            pltpu.SemaphoreType.DMA((member_count,)),
        ],
        compiler_params=pltpu.CompilerParams(collective_id=0, has_side_effects=True),
    )(pieces, anomaly)


def per_device(
    log_perm,
    start_pressure,
    start_sat,
    source,
    storage,
    well_press,
    perf_cell,
    perf_well,
    perf_count,
    observed,
    obs_var,
    obs_noise,
):
    local_count, layers, strip_width, strip_depth = log_perm.shape
    tile_count = lax.axis_size("tile")
    members = local_count * lax.axis_size("member")
    well_count = well_press.shape[0]
    well_share = well_count // tile_count
    tile_rank = lax.axis_index("tile")
    member_rank = lax.axis_index("member")
    rim = SWEEPS + 1
    fields = jnp.stack([start_pressure, start_sat, source, storage])
    halo_rows = local_count * layers * rim + fields.shape[0] * layers * rim

    def rim_rows(first):
        return jnp.concatenate(
            [
                lax.slice_in_dim(log_perm, first, first + rim, axis=2).reshape(-1, strip_depth),
                lax.slice_in_dim(fields, first, first + rim, axis=2).reshape(-1, strip_depth),
            ]
        )

    outgoing = jnp.stack([rim_rows(0), rim_rows(strip_width - rim)])
    incoming = halo_exchange(outgoing)
    lp_count = local_count * layers * rim

    def unpack(side):
        lp_part = incoming[side, :lp_count].reshape(local_count, layers, rim, strip_depth)
        field_part = incoming[side, lp_count:].reshape(fields.shape[0], layers, rim, strip_depth)
        return lp_part, field_part

    low_lp, low_fields = unpack(0)
    high_lp, high_fields = unpack(1)
    lp_ext = jnp.concatenate([low_lp, log_perm, high_lp], axis=2)
    fields_ext = jnp.concatenate([low_fields, fields, high_fields], axis=2)
    permeab = jnp.exp(lp_ext)
    column = tile_rank * strip_width - rim + jnp.arange(strip_width + 2 * rim, dtype=jnp.int32)
    inside = (column >= 0) & (column < strip_width * tile_count)
    face_sets = face_terms(permeab, inside.astype(jnp.float32))
    press_ext, sat_ext, source_ext, storage_ext = (fields_ext[i] for i in range(4))
    baseline = (source_ext + storage_ext * press_ext)[None]
    storage_term = jnp.where(inside[None, :, None], storage_ext, 1.0)[None]
    pressure = jnp.broadcast_to(press_ext[None], (local_count,) + press_ext.shape)
    for sweep_idx in range(SWEEPS):
        pressure = jacobi(pressure, baseline, storage_term, face_sets)
    saturation = trim_rim(transport(pressure, sat_ext[None], face_sets), rim)
    pressure = trim_rim(pressure, rim)
    permeab = trim_rim(permeab, rim)
    cell_count = layers * strip_width * strip_depth
    mobility = permeab * water_frac(saturation)
    cell_layer = perf_cell // (strip_width * strip_depth)
    cell_row = lax.rem(perf_cell // strip_depth, strip_width)
    cell_col = lax.rem(perf_cell, strip_depth)
    perf_mob = mobility[:, cell_layer, cell_row, cell_col]
    perf_press = pressure[:, cell_layer, cell_row, cell_col]
    selector = (perf_well[:, None] == jnp.arange(well_count, dtype=jnp.int32)[None, :]).astype(
        jnp.float32
    )
    perf_bhp = jnp.dot(selector, well_press, precision=lax.Precision.HIGHEST)
    live_mask = (jnp.arange(perf_cell.shape[0], dtype=jnp.int32) < perf_count[0]).astype(
        jnp.float32
    )
    perf_terms = perf_mob * (perf_press - perf_bhp[None]) * live_mask[None]
    partial_rates = jnp.dot(
        perf_terms, selector, precision=lax.Precision.HIGHEST, preferred_element_type=jnp.float32
    )
    member_root = (members - 1) ** 0.5
    spread = jnp.sqrt(INFLATION * obs_var)
    member_count = lax.axis_size("member")
    block_rows = local_count * well_share // 128
    pieces = partial_rates.reshape(local_count, tile_count, well_share).transpose(1, 0, 2)
    pieces = pieces.reshape(tile_count, block_rows, 128)
    anomaly = (log_perm / member_root).astype(jnp.bfloat16).reshape(local_count, cell_count)
    full, anomaly_all = rates_exchange(pieces, anomaly, member_count)
    full = full.reshape(tile_count, member_count, local_count, well_share)
    rates_all = full.transpose(1, 2, 0, 3).reshape(members, well_count)
    well_rates = lax.dynamic_index_in_dim(
        lax.dynamic_index_in_dim(full, tile_rank, 0, keepdims=False), member_rank, 0, keepdims=False
    )
    rates_own = lax.dynamic_slice_in_dim(rates_all, member_rank * local_count, local_count, 0)
    innov_own = (observed - rates_own) / spread + obs_noise
    mean_rate = jnp.sum(rates_all, 0) / members
    scaled_all = (rates_all - mean_rate) / (spread * member_root)
    gram_matrix = jnp.dot(
        scaled_all, scaled_all.T, precision=lax.Precision.HIGHEST, preferred_element_type=jnp.float32
    )
    cross_matrix = jnp.dot(
        scaled_all, innov_own.T, precision=lax.Precision.HIGHEST, preferred_element_type=jnp.float32
    )
    weights_low = solve_spd(gram_matrix, cross_matrix).astype(jnp.bfloat16)
    anomaly_all = anomaly_all.reshape(members, cell_count)
    own_cols = weights_low
    contract = (((0,), (0,)), ((), ()))
    update_sum = lax.dot_general(own_cols, anomaly_all, contract, preferred_element_type=jnp.float32)
    new_log_perm = log_perm + update_sum.reshape(log_perm.shape)
    return (new_log_perm, pressure, saturation, well_rates)


def solution(mesh):
    return jax.shard_map(
        per_device,
        mesh=mesh,
        in_specs=(
            P("member", None, "tile", None),
            P(None, "tile", None),
            P(None, "tile", None),
            P(None, "tile", None),
            P(None, "tile", None),
            P(),
            P("tile"),
            P("tile"),
            P("tile"),
            P(),
            P(),
            P("member", None),
        ),
        out_specs=(
            P("member", None, "tile", None),
            P("member", None, "tile", None),
            P("member", None, "tile", None),
            P("member", "tile"),
        ),
        check_vma=False,
    )
```

```python
import functools

import jax
import jax.numpy as jnp
from jax import lax
from jax.experimental import pallas as pl
from jax.experimental.pallas import tpu as pltpu
from jax.sharding import PartitionSpec as P

SWEEPS = 2


VERTICAL = 0.5
VISCOSITY_RATIO = 2.0
STEP_COEF = 0.1
INFLATION = 4.0


def extended_2(block, sides, width):
    for axis, dim in sides:
        count = lax.axis_size(axis)
        forward = [(i, i + 1) for i in range(count - 1)]
        backward = [(target, source) for source, target in forward]
        low = lax.ppermute(
            lax.slice_in_dim(block, block.shape[dim] - width, None, axis=dim), axis, forward
        )
        high = lax.ppermute(lax.slice_in_dim(block, 0, width, axis=dim), axis, backward)
        block = jnp.concatenate([low, block, high], axis=dim)
    return block


def harmonic(lower_val, upper_val):
    return 2.0 * lower_val * upper_val / (lower_val + upper_val)


def pad_face(values_in, along_dim, before):
    widths = [(0, 0)] * values_in.ndim
    widths[along_dim] = (1, 0) if before else (0, 1)
    return jnp.pad(values_in, widths)


def slide_by(values_in, along_dim, before):
    extent = values_in.shape[along_dim]
    if before:
        remain = lax.slice_in_dim(values_in, 0, extent - 1, axis=along_dim)
    else:
        remain = lax.slice_in_dim(values_in, 1, extent, axis=along_dim)
    return pad_face(remain, along_dim, before)


def face_terms(permeab, inside):
    face_x = (
        harmonic(permeab[:, :, :-1, :], permeab[:, :, 1:, :]) * (inside[:-1] * inside[1:])[:, None]
    )
    face_y = harmonic(permeab[:, :, :, :-1], permeab[:, :, :, 1:])
    face_z = VERTICAL * harmonic(permeab[:, :-1], permeab[:, 1:])
    return (face_x, face_y, face_z)


def neighbours(face_sets, values_in):
    flow_sum = 0.0
    weight_sum = 0.0
    for faces_dim, along_dim in zip(face_sets, (2, 3, 1)):
        lower = pad_face(faces_dim, along_dim, True)
        upper = pad_face(faces_dim, along_dim, False)
        flow_sum = (
            flow_sum
            + lower * slide_by(values_in, along_dim, True)
            + upper * slide_by(values_in, along_dim, False)
        )
        weight_sum = weight_sum + lower + upper
    return (flow_sum, weight_sum)


def jacobi(pressure, baseline, storage_term, face_sets):
    flow_sum, weight_sum = neighbours(face_sets, pressure)
    return (baseline + flow_sum) / (storage_term + weight_sum)


def water_frac(values_in):
    squared = values_in * values_in
    return squared / (squared + VISCOSITY_RATIO * (1.0 - values_in) * (1.0 - values_in))


def transport(pressure, saturation, face_sets):
    fraction = water_frac(saturation)
    change = 0.0
    for faces_dim, along_dim in zip(face_sets, (2, 3, 1)):
        extent = pressure.shape[along_dim]
        lower_press = lax.slice_in_dim(pressure, 0, extent - 1, axis=along_dim)
        upper_press = lax.slice_in_dim(pressure, 1, extent, axis=along_dim)
        lower_frac = lax.slice_in_dim(fraction, 0, extent - 1, axis=along_dim)
        upper_frac = lax.slice_in_dim(fraction, 1, extent, axis=along_dim)
        velocity = faces_dim * (lower_press - upper_press)
        carried = velocity * jnp.where(velocity > 0, lower_frac, upper_frac)
        change = change + pad_face(carried, along_dim, True) - pad_face(carried, along_dim, False)
    return saturation + STEP_COEF * change


def solve_spd(gram_matrix, cross_matrix):
    factor = jnp.linalg.cholesky(gram_matrix + jnp.eye(gram_matrix.shape[0], dtype=jnp.float32))
    halfway = lax.linalg.triangular_solve(factor, cross_matrix, left_side=True, lower=True)
    return lax.linalg.triangular_solve(
        factor, halfway, left_side=True, lower=True, transpose_a=True
    )


def trim_rim(values_in, rim_cut):
    return values_in[:, :, rim_cut : values_in.shape[2] - rim_cut, :]


def exchange_kernel(member_count, part_ref, full_ref,
                    recv_a, send_a, recv_a_sem, send_m, recv_m_sem, send_t, recv_t_sem):
    tile_count = part_ref.shape[0]
    me_t = lax.axis_index("tile")
    me_m = lax.axis_index("member")
    mesh_ids = pl.DeviceIdType.MESH

    barrier = pltpu.get_barrier_semaphore()

    def greet_tile(k, carry):
        pl.semaphore_signal(
            barrier, 1, device_id=(lax.rem(me_t + k, tile_count), me_m), device_id_type=mesh_ids
        )
        return carry

    def greet_member(k, carry):
        pl.semaphore_signal(
            barrier, 1, device_id=(me_t, lax.rem(me_m + k, member_count)), device_id_type=mesh_ids
        )
        return carry

    lax.fori_loop(1, tile_count, greet_tile, 0)
    lax.fori_loop(1, member_count, greet_member, 0)
    pl.semaphore_wait(barrier, tile_count + member_count - 2)

    def copy_a(dst_t, src_t):
        return pltpu.make_async_remote_copy(
            src_ref=part_ref.at[dst_t], dst_ref=recv_a.at[src_t],
            send_sem=send_a.at[dst_t], recv_sem=recv_a_sem.at[src_t],
            device_id=(dst_t, me_m), device_id_type=mesh_ids,
        )

    def start_a(k, carry):
        copy_a(lax.rem(me_t + k, tile_count), me_t).start()
        return carry

    lax.fori_loop(1, tile_count, start_a, 0)

    def wait_a(k, acc):
        src_t = lax.rem(me_t + k, tile_count)
        copy_a(me_t, src_t).wait_recv()
        return acc + recv_a[src_t]

    acc = lax.fori_loop(1, tile_count, wait_a, part_ref[me_t])

    def wait_a_send(k, carry):
        copy_a(lax.rem(me_t + k, tile_count), me_t).wait_send()
        return carry

    lax.fori_loop(1, tile_count, wait_a_send, 0)

    full_ref[me_t, me_m] = acc

    def copy_m(dst_m, src_m):
        return pltpu.make_async_remote_copy(
            src_ref=full_ref.at[me_t, src_m], dst_ref=full_ref.at[me_t, src_m],
            send_sem=send_m.at[dst_m], recv_sem=recv_m_sem.at[src_m],
            device_id=(me_t, dst_m), device_id_type=mesh_ids,
        )

    def start_m(k, carry):
        copy_m(lax.rem(me_m + k, member_count), me_m).start()
        return carry

    lax.fori_loop(1, member_count, start_m, 0)

    def wait_m(k, carry):
        copy_m(me_m, lax.rem(me_m + k, member_count)).wait_recv()
        return carry

    lax.fori_loop(1, member_count, wait_m, 0)

    def wait_m_send(k, carry):
        copy_m(lax.rem(me_m + k, member_count), me_m).wait_send()
        return carry

    lax.fori_loop(1, member_count, wait_m_send, 0)

    def copy_t(dst_t, src_t):
        return pltpu.make_async_remote_copy(
            src_ref=full_ref.at[src_t], dst_ref=full_ref.at[src_t],
            send_sem=send_t.at[dst_t], recv_sem=recv_t_sem.at[src_t],
            device_id=(dst_t, me_m), device_id_type=mesh_ids,
        )

    def start_t(k, carry):
        copy_t(lax.rem(me_t + k, tile_count), me_t).start()
        return carry

    lax.fori_loop(1, tile_count, start_t, 0)

    def wait_t(k, carry):
        copy_t(me_t, lax.rem(me_t + k, tile_count)).wait_recv()
        return carry

    lax.fori_loop(1, tile_count, wait_t, 0)

    def wait_t_send(k, carry):
        copy_t(lax.rem(me_t + k, tile_count), me_t).wait_send()
        return carry

    lax.fori_loop(1, tile_count, wait_t_send, 0)


def halo_kernel(out_ref, in_ref, send_sem, recv_sem):
    tile_count = lax.axis_size("tile")
    me_t = lax.axis_index("tile")
    me_m = lax.axis_index("member")
    mesh_ids = pl.DeviceIdType.MESH
    left = lax.rem(me_t + tile_count - 1, tile_count)
    right = lax.rem(me_t + 1, tile_count)
    barrier = pltpu.get_barrier_semaphore()
    for peer in (left, right):
        pl.semaphore_signal(barrier, 1, device_id=(peer, me_m), device_id_type=mesh_ids)
    pl.semaphore_wait(barrier, 2)
    to_right = pltpu.make_async_remote_copy(
        src_ref=out_ref.at[1], dst_ref=in_ref.at[0], send_sem=send_sem.at[1],
        recv_sem=recv_sem.at[0], device_id=(right, me_m), device_id_type=mesh_ids,
    )
    to_left = pltpu.make_async_remote_copy(
        src_ref=out_ref.at[0], dst_ref=in_ref.at[1], send_sem=send_sem.at[0],
        recv_sem=recv_sem.at[1], device_id=(left, me_m), device_id_type=mesh_ids,
    )
    to_right.start()
    to_left.start()
    to_right.wait()
    to_left.wait()


def halo_exchange(outgoing):
    vmem = pl.BlockSpec(memory_space=pltpu.VMEM)
    return pl.pallas_call(
        halo_kernel,
        out_shape=jax.ShapeDtypeStruct(outgoing.shape, outgoing.dtype),
        in_specs=[vmem],
        out_specs=vmem,
        scratch_shapes=[pltpu.SemaphoreType.DMA((2,)), pltpu.SemaphoreType.DMA((2,))],
        compiler_params=pltpu.CompilerParams(collective_id=1, has_side_effects=True),
    )(outgoing)


def rates_exchange(pieces, member_count):
    tile_count, rows, lanes = pieces.shape
    vmem = pl.BlockSpec(memory_space=pltpu.VMEM)
    return pl.pallas_call(
        functools.partial(exchange_kernel, member_count),
        out_shape=jax.ShapeDtypeStruct((tile_count, member_count, rows, lanes), jnp.float32),
        in_specs=[vmem],
        out_specs=vmem,
        scratch_shapes=[
            pltpu.VMEM((tile_count, rows, lanes), jnp.float32),
            pltpu.SemaphoreType.DMA((tile_count,)),
            pltpu.SemaphoreType.DMA((tile_count,)),
            pltpu.SemaphoreType.DMA((member_count,)),
            pltpu.SemaphoreType.DMA((member_count,)),
            pltpu.SemaphoreType.DMA((tile_count,)),
            pltpu.SemaphoreType.DMA((tile_count,)),
        ],
        compiler_params=pltpu.CompilerParams(collective_id=0, has_side_effects=True),
    )(pieces)


def per_device(
    log_perm,
    start_pressure,
    start_sat,
    source,
    storage,
    well_press,
    perf_cell,
    perf_well,
    perf_count,
    observed,
    obs_var,
    obs_noise,
):
    local_count, layers, strip_width, strip_depth = log_perm.shape
    tile_count = lax.axis_size("tile")
    members = local_count * lax.axis_size("member")
    well_count = well_press.shape[0]
    well_share = well_count // tile_count
    tile_rank = lax.axis_index("tile")
    member_rank = lax.axis_index("member")
    rim = SWEEPS + 1
    fields = jnp.stack([start_pressure, start_sat, source, storage])
    halo_rows = local_count * layers * rim + fields.shape[0] * layers * rim

    def rim_rows(first):
        return jnp.concatenate(
            [
                lax.slice_in_dim(log_perm, first, first + rim, axis=2).reshape(-1, strip_depth),
                lax.slice_in_dim(fields, first, first + rim, axis=2).reshape(-1, strip_depth),
            ]
        )

    outgoing = jnp.stack([rim_rows(0), rim_rows(strip_width - rim)])
    incoming = halo_exchange(outgoing)
    lp_count = local_count * layers * rim

    def unpack(side):
        lp_part = incoming[side, :lp_count].reshape(local_count, layers, rim, strip_depth)
        field_part = incoming[side, lp_count:].reshape(fields.shape[0], layers, rim, strip_depth)
        return lp_part, field_part

    low_lp, low_fields = unpack(0)
    high_lp, high_fields = unpack(1)
    lp_ext = jnp.concatenate([low_lp, log_perm, high_lp], axis=2)
    fields_ext = jnp.concatenate([low_fields, fields, high_fields], axis=2)
    permeab = jnp.exp(lp_ext)
    column = tile_rank * strip_width - rim + jnp.arange(strip_width + 2 * rim, dtype=jnp.int32)
    inside = (column >= 0) & (column < strip_width * tile_count)
    face_sets = face_terms(permeab, inside.astype(jnp.float32))
    press_ext, sat_ext, source_ext, storage_ext = (fields_ext[i] for i in range(4))
    baseline = (source_ext + storage_ext * press_ext)[None]
    storage_term = jnp.where(inside[None, :, None], storage_ext, 1.0)[None]
    pressure = jnp.broadcast_to(press_ext[None], (local_count,) + press_ext.shape)
    for sweep_idx in range(SWEEPS):
        pressure = jacobi(pressure, baseline, storage_term, face_sets)
    saturation = trim_rim(transport(pressure, sat_ext[None], face_sets), rim)
    pressure = trim_rim(pressure, rim)
    permeab = trim_rim(permeab, rim)
    cell_count = layers * strip_width * strip_depth
    mobility = permeab * water_frac(saturation)
    plane_rows = layers * strip_width
    cell_row = perf_cell // strip_depth
    cell_col = lax.rem(perf_cell, strip_depth)
    col_pick = (jnp.arange(strip_depth, dtype=jnp.int32)[:, None] == cell_col[None, :]).astype(
        jnp.float32
    )
    row_pick = jnp.arange(plane_rows, dtype=jnp.int32)[:, None] == cell_row[None, :]

    def pick_cells(values_in):
        by_col = jnp.dot(
            values_in.reshape(local_count * plane_rows, strip_depth), col_pick,
            precision=lax.Precision.HIGHEST, preferred_element_type=jnp.float32,
        ).reshape(local_count, plane_rows, -1)
        return jnp.sum(jnp.where(row_pick[None], by_col, 0.0), axis=1)

    perf_mob = pick_cells(mobility)
    perf_press = pick_cells(pressure)
    selector = (perf_well[:, None] == jnp.arange(well_count, dtype=jnp.int32)[None, :]).astype(
        jnp.float32
    )
    perf_bhp = jnp.dot(selector, well_press, precision=lax.Precision.HIGHEST)
    live_mask = (jnp.arange(perf_cell.shape[0], dtype=jnp.int32) < perf_count[0]).astype(
        jnp.float32
    )
    perf_terms = perf_mob * (perf_press - perf_bhp[None]) * live_mask[None]
    partial_rates = jnp.dot(
        perf_terms, selector, precision=lax.Precision.HIGHEST, preferred_element_type=jnp.float32
    )
    member_root = (members - 1) ** 0.5
    spread = jnp.sqrt(INFLATION * obs_var)
    member_count = lax.axis_size("member")
    block_rows = local_count * well_share // 128
    pieces = partial_rates.reshape(local_count, tile_count, well_share).transpose(1, 0, 2)
    pieces = pieces.reshape(tile_count, block_rows, 128)
    full = rates_exchange(pieces, member_count)
    full = full.reshape(tile_count, member_count, local_count, well_share)
    rates_all = full.transpose(1, 2, 0, 3).reshape(members, well_count)
    well_rates = lax.dynamic_index_in_dim(
        lax.dynamic_index_in_dim(full, tile_rank, 0, keepdims=False), member_rank, 0, keepdims=False
    )
    rates_own = lax.dynamic_slice_in_dim(rates_all, member_rank * local_count, local_count, 0)
    innov_own = (observed - rates_own) / spread + obs_noise
    mean_rate = jnp.sum(rates_all, 0) / members
    scaled_all = (rates_all - mean_rate) / (spread * member_root)
    gram_matrix = jnp.dot(
        scaled_all, scaled_all.T, precision=lax.Precision.HIGHEST, preferred_element_type=jnp.float32
    )
    cross_matrix = jnp.dot(
        scaled_all, innov_own.T, precision=lax.Precision.HIGHEST, preferred_element_type=jnp.float32
    )
    weights_low = solve_spd(gram_matrix, cross_matrix).astype(jnp.bfloat16)
    anomaly = (log_perm / member_root).astype(jnp.bfloat16).reshape(local_count, cell_count)
    anomaly_parts = [anomaly]
    for shift in range(1, member_count):
        pairs = [(i, (i + shift) % member_count) for i in range(member_count)]
        anomaly_parts.append(lax.ppermute(anomaly, "member", pairs))
    anomaly_all = jnp.concatenate(anomaly_parts, axis=0)
    own_cols = jnp.concatenate(
        [
            lax.dynamic_slice_in_dim(
                weights_low, lax.rem(member_rank - shift + member_count, member_count) * local_count,
                local_count, 0,
            )
            for shift in range(member_count)
        ],
        axis=0,
    )
    contract = (((0,), (0,)), ((), ()))
    update_sum = lax.dot_general(own_cols, anomaly_all, contract, preferred_element_type=jnp.float32)
    new_log_perm = log_perm + update_sum.reshape(log_perm.shape)
    return (new_log_perm, pressure, saturation, well_rates)


def solution(mesh):
    return jax.shard_map(
        per_device,
        mesh=mesh,
        in_specs=(
            P("member", None, "tile", None),
            P(None, "tile", None),
            P(None, "tile", None),
            P(None, "tile", None),
            P(None, "tile", None),
            P(),
            P("tile"),
            P("tile"),
            P("tile"),
            P(),
            P(),
            P("member", None),
        ),
        out_specs=(
            P("member", None, "tile", None),
            P("member", None, "tile", None),
            P("member", None, "tile", None),
            P("member", "tile"),
        ),
        check_vma=False,
    )
```

```python
import functools

import jax
import jax.numpy as jnp
from jax import lax
from jax.experimental import pallas as pl
from jax.experimental.pallas import tpu as pltpu
from jax.sharding import PartitionSpec as P

SWEEPS = 2


VERTICAL = 0.5
VISCOSITY_RATIO = 2.0
STEP_COEF = 0.1
INFLATION = 4.0


def extended_2(block, sides, width):
    for axis, dim in sides:
        count = lax.axis_size(axis)
        forward = [(i, i + 1) for i in range(count - 1)]
        backward = [(target, source) for source, target in forward]
        low = lax.ppermute(
            lax.slice_in_dim(block, block.shape[dim] - width, None, axis=dim), axis, forward
        )
        high = lax.ppermute(lax.slice_in_dim(block, 0, width, axis=dim), axis, backward)
        block = jnp.concatenate([low, block, high], axis=dim)
    return block


def harmonic(lower_val, upper_val):
    return 2.0 * lower_val * upper_val / (lower_val + upper_val)


def pad_face(values_in, along_dim, before):
    widths = [(0, 0)] * values_in.ndim
    widths[along_dim] = (1, 0) if before else (0, 1)
    return jnp.pad(values_in, widths)


def slide_by(values_in, along_dim, before):
    extent = values_in.shape[along_dim]
    if before:
        remain = lax.slice_in_dim(values_in, 0, extent - 1, axis=along_dim)
    else:
        remain = lax.slice_in_dim(values_in, 1, extent, axis=along_dim)
    return pad_face(remain, along_dim, before)


def face_terms(permeab, inside):
    face_x = (
        harmonic(permeab[:, :, :-1, :], permeab[:, :, 1:, :]) * (inside[:-1] * inside[1:])[:, None]
    )
    face_y = harmonic(permeab[:, :, :, :-1], permeab[:, :, :, 1:])
    face_z = VERTICAL * harmonic(permeab[:, :-1], permeab[:, 1:])
    return (face_x, face_y, face_z)


def neighbours(face_sets, values_in):
    flow_sum = 0.0
    weight_sum = 0.0
    for faces_dim, along_dim in zip(face_sets, (2, 3, 1)):
        lower = pad_face(faces_dim, along_dim, True)
        upper = pad_face(faces_dim, along_dim, False)
        flow_sum = (
            flow_sum
            + lower * slide_by(values_in, along_dim, True)
            + upper * slide_by(values_in, along_dim, False)
        )
        weight_sum = weight_sum + lower + upper
    return (flow_sum, weight_sum)


def jacobi(pressure, baseline, storage_term, face_sets):
    flow_sum, weight_sum = neighbours(face_sets, pressure)
    return (baseline + flow_sum) / (storage_term + weight_sum)


def water_frac(values_in):
    squared = values_in * values_in
    return squared / (squared + VISCOSITY_RATIO * (1.0 - values_in) * (1.0 - values_in))


def transport(pressure, saturation, face_sets):
    fraction = water_frac(saturation)
    change = 0.0
    for faces_dim, along_dim in zip(face_sets, (2, 3, 1)):
        extent = pressure.shape[along_dim]
        lower_press = lax.slice_in_dim(pressure, 0, extent - 1, axis=along_dim)
        upper_press = lax.slice_in_dim(pressure, 1, extent, axis=along_dim)
        lower_frac = lax.slice_in_dim(fraction, 0, extent - 1, axis=along_dim)
        upper_frac = lax.slice_in_dim(fraction, 1, extent, axis=along_dim)
        velocity = faces_dim * (lower_press - upper_press)
        carried = velocity * jnp.where(velocity > 0, lower_frac, upper_frac)
        change = change + pad_face(carried, along_dim, True) - pad_face(carried, along_dim, False)
    return saturation + STEP_COEF * change


def solve_spd(gram_matrix, cross_matrix):
    factor = lax.linalg.cholesky(
        gram_matrix + jnp.eye(gram_matrix.shape[0], dtype=jnp.float32), symmetrize_input=False
    )
    halfway = lax.linalg.triangular_solve(factor, cross_matrix, left_side=True, lower=True)
    return lax.linalg.triangular_solve(
        factor, halfway, left_side=True, lower=True, transpose_a=True
    )


def trim_rim(values_in, rim_cut):
    return values_in[:, :, rim_cut : values_in.shape[2] - rim_cut, :]


def exchange_kernel(member_count, part_ref, full_ref,
                    recv_a, send_a, recv_a_sem, send_m, recv_m_sem, send_t, recv_t_sem):
    tile_count = part_ref.shape[0]
    me_t = lax.axis_index("tile")
    me_m = lax.axis_index("member")
    mesh_ids = pl.DeviceIdType.MESH

    barrier = pltpu.get_barrier_semaphore()

    def greet_tile(k, carry):
        pl.semaphore_signal(
            barrier, 1, device_id=(lax.rem(me_t + k, tile_count), me_m), device_id_type=mesh_ids
        )
        return carry

    def greet_member(k, carry):
        pl.semaphore_signal(
            barrier, 1, device_id=(me_t, lax.rem(me_m + k, member_count)), device_id_type=mesh_ids
        )
        return carry

    lax.fori_loop(1, tile_count, greet_tile, 0)
    lax.fori_loop(1, member_count, greet_member, 0)
    pl.semaphore_wait(barrier, tile_count + member_count - 2)

    def copy_a(dst_t, src_t):
        return pltpu.make_async_remote_copy(
            src_ref=part_ref.at[dst_t], dst_ref=recv_a.at[src_t],
            send_sem=send_a.at[dst_t], recv_sem=recv_a_sem.at[src_t],
            device_id=(dst_t, me_m), device_id_type=mesh_ids,
        )

    def start_a(k, carry):
        copy_a(lax.rem(me_t + k, tile_count), me_t).start()
        return carry

    lax.fori_loop(1, tile_count, start_a, 0)

    def wait_a(k, acc):
        src_t = lax.rem(me_t + k, tile_count)
        copy_a(me_t, src_t).wait_recv()
        return acc + recv_a[src_t]

    acc = lax.fori_loop(1, tile_count, wait_a, part_ref[me_t])

    def wait_a_send(k, carry):
        copy_a(lax.rem(me_t + k, tile_count), me_t).wait_send()
        return carry

    lax.fori_loop(1, tile_count, wait_a_send, 0)

    full_ref[me_t, me_m] = acc

    def copy_m(dst_m, src_m):
        return pltpu.make_async_remote_copy(
            src_ref=full_ref.at[me_t, src_m], dst_ref=full_ref.at[me_t, src_m],
            send_sem=send_m.at[dst_m], recv_sem=recv_m_sem.at[src_m],
            device_id=(me_t, dst_m), device_id_type=mesh_ids,
        )

    def start_m(k, carry):
        copy_m(lax.rem(me_m + k, member_count), me_m).start()
        return carry

    lax.fori_loop(1, member_count, start_m, 0)

    def wait_m(k, carry):
        copy_m(me_m, lax.rem(me_m + k, member_count)).wait_recv()
        return carry

    lax.fori_loop(1, member_count, wait_m, 0)

    def wait_m_send(k, carry):
        copy_m(lax.rem(me_m + k, member_count), me_m).wait_send()
        return carry

    lax.fori_loop(1, member_count, wait_m_send, 0)

    def copy_t(dst_t, src_t):
        return pltpu.make_async_remote_copy(
            src_ref=full_ref.at[src_t], dst_ref=full_ref.at[src_t],
            send_sem=send_t.at[dst_t], recv_sem=recv_t_sem.at[src_t],
            device_id=(dst_t, me_m), device_id_type=mesh_ids,
        )

    def start_t(k, carry):
        copy_t(lax.rem(me_t + k, tile_count), me_t).start()
        return carry

    lax.fori_loop(1, tile_count, start_t, 0)

    def wait_t(k, carry):
        copy_t(me_t, lax.rem(me_t + k, tile_count)).wait_recv()
        return carry

    lax.fori_loop(1, tile_count, wait_t, 0)

    def wait_t_send(k, carry):
        copy_t(lax.rem(me_t + k, tile_count), me_t).wait_send()
        return carry

    lax.fori_loop(1, tile_count, wait_t_send, 0)


def halo_kernel(out_ref, in_ref, send_sem, recv_sem):
    tile_count = lax.axis_size("tile")
    me_t = lax.axis_index("tile")
    me_m = lax.axis_index("member")
    mesh_ids = pl.DeviceIdType.MESH
    left = lax.rem(me_t + tile_count - 1, tile_count)
    right = lax.rem(me_t + 1, tile_count)
    barrier = pltpu.get_barrier_semaphore()
    for peer in (left, right):
        pl.semaphore_signal(barrier, 1, device_id=(peer, me_m), device_id_type=mesh_ids)
    pl.semaphore_wait(barrier, 2)
    to_right = pltpu.make_async_remote_copy(
        src_ref=out_ref.at[1], dst_ref=in_ref.at[0], send_sem=send_sem.at[1],
        recv_sem=recv_sem.at[0], device_id=(right, me_m), device_id_type=mesh_ids,
    )
    to_left = pltpu.make_async_remote_copy(
        src_ref=out_ref.at[0], dst_ref=in_ref.at[1], send_sem=send_sem.at[0],
        recv_sem=recv_sem.at[1], device_id=(left, me_m), device_id_type=mesh_ids,
    )
    to_right.start()
    to_left.start()
    to_right.wait()
    to_left.wait()


def halo_exchange(outgoing):
    vmem = pl.BlockSpec(memory_space=pltpu.VMEM)
    return pl.pallas_call(
        halo_kernel,
        out_shape=jax.ShapeDtypeStruct(outgoing.shape, outgoing.dtype),
        in_specs=[vmem],
        out_specs=vmem,
        scratch_shapes=[pltpu.SemaphoreType.DMA((2,)), pltpu.SemaphoreType.DMA((2,))],
        compiler_params=pltpu.CompilerParams(collective_id=1, has_side_effects=True),
    )(outgoing)


def rates_exchange(pieces, member_count):
    tile_count, rows, lanes = pieces.shape
    vmem = pl.BlockSpec(memory_space=pltpu.VMEM)
    return pl.pallas_call(
        functools.partial(exchange_kernel, member_count),
        out_shape=jax.ShapeDtypeStruct((tile_count, member_count, rows, lanes), jnp.float32),
        in_specs=[vmem],
        out_specs=vmem,
        scratch_shapes=[
            pltpu.VMEM((tile_count, rows, lanes), jnp.float32),
            pltpu.SemaphoreType.DMA((tile_count,)),
            pltpu.SemaphoreType.DMA((tile_count,)),
            pltpu.SemaphoreType.DMA((member_count,)),
            pltpu.SemaphoreType.DMA((member_count,)),
            pltpu.SemaphoreType.DMA((tile_count,)),
            pltpu.SemaphoreType.DMA((tile_count,)),
        ],
        compiler_params=pltpu.CompilerParams(collective_id=0, has_side_effects=True),
    )(pieces)


def per_device(
    log_perm,
    start_pressure,
    start_sat,
    source,
    storage,
    well_press,
    perf_cell,
    perf_well,
    perf_count,
    observed,
    obs_var,
    obs_noise,
):
    local_count, layers, strip_width, strip_depth = log_perm.shape
    tile_count = lax.axis_size("tile")
    members = local_count * lax.axis_size("member")
    well_count = well_press.shape[0]
    well_share = well_count // tile_count
    tile_rank = lax.axis_index("tile")
    member_rank = lax.axis_index("member")
    rim = SWEEPS + 1
    fields = jnp.stack([start_pressure, start_sat, source, storage])
    halo_rows = local_count * layers * rim + fields.shape[0] * layers * rim

    def rim_rows(first):
        return jnp.concatenate(
            [
                lax.slice_in_dim(log_perm, first, first + rim, axis=2).reshape(-1, strip_depth),
                lax.slice_in_dim(fields, first, first + rim, axis=2).reshape(-1, strip_depth),
            ]
        )

    outgoing = jnp.stack([rim_rows(0), rim_rows(strip_width - rim)])
    incoming = halo_exchange(outgoing)
    incoming, log_perm_after = lax.optimization_barrier((incoming, log_perm))
    lp_count = local_count * layers * rim

    def unpack(side):
        lp_part = incoming[side, :lp_count].reshape(local_count, layers, rim, strip_depth)
        field_part = incoming[side, lp_count:].reshape(fields.shape[0], layers, rim, strip_depth)
        return lp_part, field_part

    low_lp, low_fields = unpack(0)
    high_lp, high_fields = unpack(1)
    lp_ext = jnp.concatenate([low_lp, log_perm, high_lp], axis=2)
    fields_ext = jnp.concatenate([low_fields, fields, high_fields], axis=2)
    permeab = jnp.exp(lp_ext)
    column = tile_rank * strip_width - rim + jnp.arange(strip_width + 2 * rim, dtype=jnp.int32)
    inside = (column >= 0) & (column < strip_width * tile_count)
    face_sets = face_terms(permeab, inside.astype(jnp.float32))
    press_ext, sat_ext, source_ext, storage_ext = (fields_ext[i] for i in range(4))
    baseline = (source_ext + storage_ext * press_ext)[None]
    storage_term = jnp.where(inside[None, :, None], storage_ext, 1.0)[None]
    pressure = jnp.broadcast_to(press_ext[None], (local_count,) + press_ext.shape)
    for sweep_idx in range(SWEEPS):
        pressure = jacobi(pressure, baseline, storage_term, face_sets)
    saturation = trim_rim(transport(pressure, sat_ext[None], face_sets), rim)
    pressure = trim_rim(pressure, rim)
    permeab = trim_rim(permeab, rim)
    cell_count = layers * strip_width * strip_depth
    mobility = permeab * water_frac(saturation)
    plane_rows = layers * strip_width
    cell_row = perf_cell // strip_depth
    cell_col = lax.rem(perf_cell, strip_depth)
    col_pick = (jnp.arange(strip_depth, dtype=jnp.int32)[:, None] == cell_col[None, :]).astype(
        jnp.float32
    )
    row_pick = jnp.arange(plane_rows, dtype=jnp.int32)[:, None] == cell_row[None, :]

    def pick_cells(values_in):
        by_col = jnp.dot(
            values_in.reshape(local_count * plane_rows, strip_depth), col_pick,
            precision=lax.Precision.HIGHEST, preferred_element_type=jnp.float32,
        ).reshape(local_count, plane_rows, -1)
        return jnp.sum(jnp.where(row_pick[None], by_col, 0.0), axis=1)

    perf_mob = pick_cells(mobility)
    perf_press = pick_cells(pressure)
    selector = (perf_well[:, None] == jnp.arange(well_count, dtype=jnp.int32)[None, :]).astype(
        jnp.float32
    )
    perf_bhp = jnp.dot(selector, well_press, precision=lax.Precision.HIGHEST)
    live_mask = (jnp.arange(perf_cell.shape[0], dtype=jnp.int32) < perf_count[0]).astype(
        jnp.float32
    )
    perf_terms = perf_mob * (perf_press - perf_bhp[None]) * live_mask[None]
    partial_rates = jnp.dot(
        perf_terms, selector, precision=lax.Precision.HIGHEST, preferred_element_type=jnp.float32
    )
    member_root = (members - 1) ** 0.5
    spread = jnp.sqrt(INFLATION * obs_var)
    member_count = lax.axis_size("member")
    block_rows = local_count * well_share // 128
    pieces = partial_rates.reshape(local_count, tile_count, well_share).transpose(1, 0, 2)
    pieces = pieces.reshape(tile_count, block_rows, 128)
    full = rates_exchange(pieces, member_count)
    full = full.reshape(tile_count, member_count, local_count, well_share)
    rates_all = full.transpose(1, 2, 0, 3).reshape(members, well_count)
    well_rates = lax.dynamic_index_in_dim(
        lax.dynamic_index_in_dim(full, tile_rank, 0, keepdims=False), member_rank, 0, keepdims=False
    )
    rates_own = lax.dynamic_slice_in_dim(rates_all, member_rank * local_count, local_count, 0)
    innov_own = (observed - rates_own) / spread + obs_noise
    mean_rate = jnp.sum(rates_all, 0) / members
    scaled_all = (rates_all - mean_rate) / (spread * member_root)
    gram_matrix = jnp.dot(
        scaled_all, scaled_all.T, precision=lax.Precision.HIGHEST, preferred_element_type=jnp.float32
    )
    cross_matrix = jnp.dot(
        scaled_all, innov_own.T, precision=lax.Precision.HIGHEST, preferred_element_type=jnp.float32
    )
    weights_low = solve_spd(gram_matrix, cross_matrix).astype(jnp.bfloat16)
    anomaly = (log_perm_after / member_root).astype(jnp.bfloat16).reshape(local_count, cell_count)
    anomaly_parts = [anomaly]
    for shift in range(1, member_count):
        pairs = [(i, (i + shift) % member_count) for i in range(member_count)]
        anomaly_parts.append(lax.ppermute(anomaly, "member", pairs))
    anomaly_all = jnp.concatenate(anomaly_parts, axis=0)
    own_cols = jnp.concatenate(
        [
            lax.dynamic_slice_in_dim(
                weights_low, lax.rem(member_rank - shift + member_count, member_count) * local_count,
                local_count, 0,
            )
            for shift in range(member_count)
        ],
        axis=0,
    )
    contract = (((0,), (0,)), ((), ()))
    update_sum = lax.dot_general(own_cols, anomaly_all, contract, preferred_element_type=jnp.float32)
    new_log_perm = log_perm + update_sum.reshape(log_perm.shape)
    return (new_log_perm, pressure, saturation, well_rates)


def solution(mesh):
    return jax.shard_map(
        per_device,
        mesh=mesh,
        in_specs=(
            P("member", None, "tile", None),
            P(None, "tile", None),
            P(None, "tile", None),
            P(None, "tile", None),
            P(None, "tile", None),
            P(),
            P("tile"),
            P("tile"),
            P("tile"),
            P(),
            P(),
            P("member", None),
        ),
        out_specs=(
            P("member", None, "tile", None),
            P("member", None, "tile", None),
            P("member", None, "tile", None),
            P("member", "tile"),
        ),
        check_vma=False,
    )
```

```python
import functools

import jax
import jax.numpy as jnp
from jax import lax
from jax.experimental import pallas as pl
from jax.experimental.pallas import tpu as pltpu
from jax.sharding import PartitionSpec as P

SWEEPS = 2


VERTICAL = 0.5
VISCOSITY_RATIO = 2.0
STEP_COEF = 0.1
INFLATION = 4.0


def extended_2(block, sides, width):
    for axis, dim in sides:
        count = lax.axis_size(axis)
        forward = [(i, i + 1) for i in range(count - 1)]
        backward = [(target, source) for source, target in forward]
        low = lax.ppermute(
            lax.slice_in_dim(block, block.shape[dim] - width, None, axis=dim), axis, forward
        )
        high = lax.ppermute(lax.slice_in_dim(block, 0, width, axis=dim), axis, backward)
        block = jnp.concatenate([low, block, high], axis=dim)
    return block


def harmonic(lower_val, upper_val):
    return 2.0 * lower_val * upper_val / (lower_val + upper_val)


def pad_face(values_in, along_dim, before):
    widths = [(0, 0)] * values_in.ndim
    widths[along_dim] = (1, 0) if before else (0, 1)
    return jnp.pad(values_in, widths)


def slide_by(values_in, along_dim, before):
    extent = values_in.shape[along_dim]
    if before:
        remain = lax.slice_in_dim(values_in, 0, extent - 1, axis=along_dim)
    else:
        remain = lax.slice_in_dim(values_in, 1, extent, axis=along_dim)
    return pad_face(remain, along_dim, before)


def face_terms(permeab, inside):
    face_x = (
        harmonic(permeab[:, :, :-1, :], permeab[:, :, 1:, :]) * (inside[:-1] * inside[1:])[:, None]
    )
    face_y = harmonic(permeab[:, :, :, :-1], permeab[:, :, :, 1:])
    face_z = VERTICAL * harmonic(permeab[:, :-1], permeab[:, 1:])
    return (face_x, face_y, face_z)


def neighbours(face_sets, values_in):
    flow_sum = 0.0
    weight_sum = 0.0
    for faces_dim, along_dim in zip(face_sets, (2, 3, 1)):
        lower = pad_face(faces_dim, along_dim, True)
        upper = pad_face(faces_dim, along_dim, False)
        flow_sum = (
            flow_sum
            + lower * slide_by(values_in, along_dim, True)
            + upper * slide_by(values_in, along_dim, False)
        )
        weight_sum = weight_sum + lower + upper
    return (flow_sum, weight_sum)


def jacobi(pressure, baseline, storage_term, face_sets):
    flow_sum, weight_sum = neighbours(face_sets, pressure)
    return (baseline + flow_sum) / (storage_term + weight_sum)


def water_frac(values_in):
    squared = values_in * values_in
    return squared / (squared + VISCOSITY_RATIO * (1.0 - values_in) * (1.0 - values_in))


def transport(pressure, saturation, face_sets):
    fraction = water_frac(saturation)
    change = 0.0
    for faces_dim, along_dim in zip(face_sets, (2, 3, 1)):
        extent = pressure.shape[along_dim]
        lower_press = lax.slice_in_dim(pressure, 0, extent - 1, axis=along_dim)
        upper_press = lax.slice_in_dim(pressure, 1, extent, axis=along_dim)
        lower_frac = lax.slice_in_dim(fraction, 0, extent - 1, axis=along_dim)
        upper_frac = lax.slice_in_dim(fraction, 1, extent, axis=along_dim)
        velocity = faces_dim * (lower_press - upper_press)
        carried = velocity * jnp.where(velocity > 0, lower_frac, upper_frac)
        change = change + pad_face(carried, along_dim, True) - pad_face(carried, along_dim, False)
    return saturation + STEP_COEF * change


def solve_spd(gram_matrix, cross_matrix):
    factor = lax.linalg.cholesky(
        gram_matrix + jnp.eye(gram_matrix.shape[0], dtype=jnp.float32), symmetrize_input=False
    )
    halfway = lax.linalg.triangular_solve(factor, cross_matrix, left_side=True, lower=True)
    return lax.linalg.triangular_solve(
        factor, halfway, left_side=True, lower=True, transpose_a=True
    )


def trim_rim(values_in, rim_cut):
    return values_in[:, :, rim_cut : values_in.shape[2] - rim_cut, :]


def exchange_kernel(member_count, part_ref, full_ref,
                    recv_a, send_a, recv_a_sem, send_m, recv_m_sem, send_t, recv_t_sem):
    tile_count = part_ref.shape[0]
    me_t = lax.axis_index("tile")
    me_m = lax.axis_index("member")
    mesh_ids = pl.DeviceIdType.MESH

    barrier = pltpu.get_barrier_semaphore()

    def greet_tile(k, carry):
        pl.semaphore_signal(
            barrier, 1, device_id=(lax.rem(me_t + k, tile_count), me_m), device_id_type=mesh_ids
        )
        return carry

    def greet_member(k, carry):
        pl.semaphore_signal(
            barrier, 1, device_id=(me_t, lax.rem(me_m + k, member_count)), device_id_type=mesh_ids
        )
        return carry

    lax.fori_loop(1, tile_count, greet_tile, 0)
    lax.fori_loop(1, member_count, greet_member, 0)
    pl.semaphore_wait(barrier, tile_count + member_count - 2)

    def copy_a(dst_t, src_t):
        return pltpu.make_async_remote_copy(
            src_ref=part_ref.at[dst_t], dst_ref=recv_a.at[src_t],
            send_sem=send_a.at[dst_t], recv_sem=recv_a_sem.at[src_t],
            device_id=(dst_t, me_m), device_id_type=mesh_ids,
        )

    def start_a(k, carry):
        copy_a(lax.rem(me_t + k, tile_count), me_t).start()
        return carry

    lax.fori_loop(1, tile_count, start_a, 0)

    def wait_a(k, acc):
        src_t = lax.rem(me_t + k, tile_count)
        copy_a(me_t, src_t).wait_recv()
        return acc + recv_a[src_t]

    acc = lax.fori_loop(1, tile_count, wait_a, part_ref[me_t])

    def wait_a_send(k, carry):
        copy_a(lax.rem(me_t + k, tile_count), me_t).wait_send()
        return carry

    lax.fori_loop(1, tile_count, wait_a_send, 0)

    full_ref[me_t, me_m] = acc

    def copy_m(dst_m, src_m):
        return pltpu.make_async_remote_copy(
            src_ref=full_ref.at[me_t, src_m], dst_ref=full_ref.at[me_t, src_m],
            send_sem=send_m.at[dst_m], recv_sem=recv_m_sem.at[src_m],
            device_id=(me_t, dst_m), device_id_type=mesh_ids,
        )

    def start_m(k, carry):
        copy_m(lax.rem(me_m + k, member_count), me_m).start()
        return carry

    lax.fori_loop(1, member_count, start_m, 0)

    def wait_m(k, carry):
        copy_m(me_m, lax.rem(me_m + k, member_count)).wait_recv()
        return carry

    lax.fori_loop(1, member_count, wait_m, 0)

    def wait_m_send(k, carry):
        copy_m(lax.rem(me_m + k, member_count), me_m).wait_send()
        return carry

    lax.fori_loop(1, member_count, wait_m_send, 0)

    def copy_t(dst_t, src_t):
        return pltpu.make_async_remote_copy(
            src_ref=full_ref.at[src_t], dst_ref=full_ref.at[src_t],
            send_sem=send_t.at[dst_t], recv_sem=recv_t_sem.at[src_t],
            device_id=(dst_t, me_m), device_id_type=mesh_ids,
        )

    def start_t(k, carry):
        copy_t(lax.rem(me_t + k, tile_count), me_t).start()
        return carry

    lax.fori_loop(1, tile_count, start_t, 0)

    def wait_t(k, carry):
        copy_t(me_t, lax.rem(me_t + k, tile_count)).wait_recv()
        return carry

    lax.fori_loop(1, tile_count, wait_t, 0)

    def wait_t_send(k, carry):
        copy_t(lax.rem(me_t + k, tile_count), me_t).wait_send()
        return carry

    lax.fori_loop(1, tile_count, wait_t_send, 0)


def halo_kernel(out_ref, in_ref, send_sem, recv_sem):
    tile_count = lax.axis_size("tile")
    me_t = lax.axis_index("tile")
    me_m = lax.axis_index("member")
    mesh_ids = pl.DeviceIdType.MESH
    left = lax.rem(me_t + tile_count - 1, tile_count)
    right = lax.rem(me_t + 1, tile_count)
    barrier = pltpu.get_barrier_semaphore()
    for peer in (left, right):
        pl.semaphore_signal(barrier, 1, device_id=(peer, me_m), device_id_type=mesh_ids)
    pl.semaphore_wait(barrier, 2)
    to_right = pltpu.make_async_remote_copy(
        src_ref=out_ref.at[1], dst_ref=in_ref.at[0], send_sem=send_sem.at[1],
        recv_sem=recv_sem.at[0], device_id=(right, me_m), device_id_type=mesh_ids,
    )
    to_left = pltpu.make_async_remote_copy(
        src_ref=out_ref.at[0], dst_ref=in_ref.at[1], send_sem=send_sem.at[0],
        recv_sem=recv_sem.at[1], device_id=(left, me_m), device_id_type=mesh_ids,
    )
    to_right.start()
    to_left.start()
    to_right.wait()
    to_left.wait()


def halo_exchange(outgoing):
    vmem = pl.BlockSpec(memory_space=pltpu.VMEM)
    return pl.pallas_call(
        halo_kernel,
        out_shape=jax.ShapeDtypeStruct(outgoing.shape, outgoing.dtype),
        in_specs=[vmem],
        out_specs=vmem,
        scratch_shapes=[pltpu.SemaphoreType.DMA((2,)), pltpu.SemaphoreType.DMA((2,))],
        compiler_params=pltpu.CompilerParams(collective_id=1, has_side_effects=True),
    )(outgoing)


def rates_exchange(pieces, member_count):
    tile_count, rows, lanes = pieces.shape
    vmem = pl.BlockSpec(memory_space=pltpu.VMEM)
    return pl.pallas_call(
        functools.partial(exchange_kernel, member_count),
        out_shape=jax.ShapeDtypeStruct((tile_count, member_count, rows, lanes), jnp.float32),
        in_specs=[vmem],
        out_specs=vmem,
        scratch_shapes=[
            pltpu.VMEM((tile_count, rows, lanes), jnp.float32),
            pltpu.SemaphoreType.DMA((tile_count,)),
            pltpu.SemaphoreType.DMA((tile_count,)),
            pltpu.SemaphoreType.DMA((member_count,)),
            pltpu.SemaphoreType.DMA((member_count,)),
            pltpu.SemaphoreType.DMA((tile_count,)),
            pltpu.SemaphoreType.DMA((tile_count,)),
        ],
        compiler_params=pltpu.CompilerParams(collective_id=0, has_side_effects=True),
    )(pieces)


def per_device(
    log_perm,
    start_pressure,
    start_sat,
    source,
    storage,
    well_press,
    perf_cell,
    perf_well,
    perf_count,
    observed,
    obs_var,
    obs_noise,
):
    local_count, layers, strip_width, strip_depth = log_perm.shape
    tile_count = lax.axis_size("tile")
    members = local_count * lax.axis_size("member")
    well_count = well_press.shape[0]
    well_share = well_count // tile_count
    tile_rank = lax.axis_index("tile")
    member_rank = lax.axis_index("member")
    rim = SWEEPS + 1
    fields = jnp.stack([start_pressure, start_sat, source, storage])
    halo_rows = local_count * layers * rim + fields.shape[0] * layers * rim

    def rim_rows(first):
        return jnp.concatenate(
            [
                lax.slice_in_dim(log_perm, first, first + rim, axis=2).reshape(-1, strip_depth),
                lax.slice_in_dim(fields, first, first + rim, axis=2).reshape(-1, strip_depth),
            ]
        )

    outgoing = jnp.stack([rim_rows(0), rim_rows(strip_width - rim)])
    incoming = halo_exchange(outgoing)
    incoming, log_perm_after = lax.optimization_barrier((incoming, log_perm))
    lp_count = local_count * layers * rim

    def unpack(side):
        lp_part = incoming[side, :lp_count].reshape(local_count, layers, rim, strip_depth)
        field_part = incoming[side, lp_count:].reshape(fields.shape[0], layers, rim, strip_depth)
        return lp_part, field_part

    low_lp, low_fields = unpack(0)
    high_lp, high_fields = unpack(1)
    lp_ext = jnp.concatenate([low_lp, log_perm, high_lp], axis=2)
    fields_ext = jnp.concatenate([low_fields, fields, high_fields], axis=2)
    permeab = jnp.exp(lp_ext)
    column = tile_rank * strip_width - rim + jnp.arange(strip_width + 2 * rim, dtype=jnp.int32)
    inside = (column >= 0) & (column < strip_width * tile_count)
    face_sets = face_terms(permeab, inside.astype(jnp.float32))
    press_ext, sat_ext, source_ext, storage_ext = (fields_ext[i] for i in range(4))
    baseline = (source_ext + storage_ext * press_ext)[None]
    storage_term = jnp.where(inside[None, :, None], storage_ext, 1.0)[None]
    pressure = jnp.broadcast_to(press_ext[None], (local_count,) + press_ext.shape)
    for sweep_idx in range(SWEEPS):
        pressure = jacobi(pressure, baseline, storage_term, face_sets)
    saturation = trim_rim(transport(pressure, sat_ext[None], face_sets), rim)
    pressure = trim_rim(pressure, rim)
    permeab = trim_rim(permeab, rim)
    cell_count = layers * strip_width * strip_depth
    mobility = permeab * water_frac(saturation)
    plane_rows = layers * strip_width
    cell_row = perf_cell // strip_depth
    cell_col = lax.rem(perf_cell, strip_depth)
    col_pick = (jnp.arange(strip_depth, dtype=jnp.int32)[:, None] == cell_col[None, :]).astype(
        jnp.float32
    )
    row_pick = jnp.arange(plane_rows, dtype=jnp.int32)[:, None] == cell_row[None, :]

    def pick_cells(values_in):
        by_col = jnp.dot(
            values_in.reshape(local_count * plane_rows, strip_depth), col_pick,
            precision=lax.Precision.HIGHEST, preferred_element_type=jnp.float32,
        ).reshape(local_count, plane_rows, -1)
        return jnp.sum(jnp.where(row_pick[None], by_col, 0.0), axis=1)

    perf_mob = pick_cells(mobility)
    perf_press = pick_cells(pressure)
    selector = (perf_well[:, None] == jnp.arange(well_count, dtype=jnp.int32)[None, :]).astype(
        jnp.float32
    )
    perf_bhp = jnp.dot(selector, well_press, precision=lax.Precision.HIGHEST)
    live_mask = (jnp.arange(perf_cell.shape[0], dtype=jnp.int32) < perf_count[0]).astype(
        jnp.float32
    )
    perf_terms = perf_mob * (perf_press - perf_bhp[None]) * live_mask[None]
    partial_rates = jnp.dot(
        perf_terms, selector, precision=lax.Precision.HIGHEST, preferred_element_type=jnp.float32
    )
    member_root = (members - 1) ** 0.5
    spread = jnp.sqrt(INFLATION * obs_var)
    member_count = lax.axis_size("member")
    block_rows = local_count * well_share // 128
    pieces = partial_rates.reshape(local_count, tile_count, well_share).transpose(1, 0, 2)
    pieces = pieces.reshape(tile_count, block_rows, 128)
    full = rates_exchange(pieces, member_count)
    lane_groups = 128 // well_share
    well_rates = lax.dynamic_index_in_dim(
        lax.dynamic_index_in_dim(full, tile_rank, 0, keepdims=False), member_rank, 0, keepdims=False
    ).reshape(local_count, well_share)
    rates_t = full.reshape(tile_count, member_count, block_rows, lane_groups, well_share)
    rates_t = rates_t.transpose(0, 4, 1, 2, 3).reshape(well_count, members)
    mean_rate = jnp.sum(rates_t, 1) / members
    scaled_t = (rates_t - mean_rate[:, None]) / (spread * member_root)[:, None]
    rates_own_t = lax.dynamic_slice_in_dim(rates_t, member_rank * local_count, local_count, 1)
    innov_own_t = (observed[:, None] - rates_own_t) / spread[:, None] + obs_noise.T
    contract_wells = (((0,), (0,)), ((), ()))
    gram_matrix = lax.dot_general(
        scaled_t, scaled_t, contract_wells, precision=lax.Precision.HIGHEST,
        preferred_element_type=jnp.float32,
    )
    cross_matrix = lax.dot_general(
        scaled_t, innov_own_t, contract_wells, precision=lax.Precision.HIGHEST,
        preferred_element_type=jnp.float32,
    )
    weights_low = solve_spd(gram_matrix, cross_matrix).astype(jnp.bfloat16)
    anomaly = (log_perm_after / member_root).astype(jnp.bfloat16).reshape(local_count, cell_count)
    anomaly_parts = [anomaly]
    for shift in range(1, member_count):
        pairs = [(i, (i + shift) % member_count) for i in range(member_count)]
        anomaly_parts.append(lax.ppermute(anomaly, "member", pairs))
    anomaly_all = jnp.concatenate(anomaly_parts, axis=0)
    own_cols = jnp.concatenate(
        [
            lax.dynamic_slice_in_dim(
                weights_low, lax.rem(member_rank - shift + member_count, member_count) * local_count,
                local_count, 0,
            )
            for shift in range(member_count)
        ],
        axis=0,
    )
    contract = (((0,), (0,)), ((), ()))
    update_sum = lax.dot_general(own_cols, anomaly_all, contract, preferred_element_type=jnp.float32)
    new_log_perm = log_perm + update_sum.reshape(log_perm.shape)
    return (new_log_perm, pressure, saturation, well_rates)


def solution(mesh):
    return jax.shard_map(
        per_device,
        mesh=mesh,
        in_specs=(
            P("member", None, "tile", None),
            P(None, "tile", None),
            P(None, "tile", None),
            P(None, "tile", None),
            P(None, "tile", None),
            P(),
            P("tile"),
            P("tile"),
            P("tile"),
            P(),
            P(),
            P("member", None),
        ),
        out_specs=(
            P("member", None, "tile", None),
            P("member", None, "tile", None),
            P("member", None, "tile", None),
            P("member", "tile"),
        ),
        check_vma=False,
    )
```

```python
import functools

import jax
import jax.numpy as jnp
from jax import lax
from jax.experimental import pallas as pl
from jax.experimental.pallas import tpu as pltpu
from jax.sharding import PartitionSpec as P

SWEEPS = 2


VERTICAL = 0.5
VISCOSITY_RATIO = 2.0
STEP_COEF = 0.1
INFLATION = 4.0


def extended_2(block, sides, width):
    for axis, dim in sides:
        count = lax.axis_size(axis)
        forward = [(i, i + 1) for i in range(count - 1)]
        backward = [(target, source) for source, target in forward]
        low = lax.ppermute(
            lax.slice_in_dim(block, block.shape[dim] - width, None, axis=dim), axis, forward
        )
        high = lax.ppermute(lax.slice_in_dim(block, 0, width, axis=dim), axis, backward)
        block = jnp.concatenate([low, block, high], axis=dim)
    return block


def harmonic(lower_val, upper_val):
    return 2.0 * lower_val * upper_val / (lower_val + upper_val)


def pad_face(values_in, along_dim, before):
    widths = [(0, 0)] * values_in.ndim
    widths[along_dim] = (1, 0) if before else (0, 1)
    return jnp.pad(values_in, widths)


def slide_by(values_in, along_dim, before):
    extent = values_in.shape[along_dim]
    if before:
        remain = lax.slice_in_dim(values_in, 0, extent - 1, axis=along_dim)
    else:
        remain = lax.slice_in_dim(values_in, 1, extent, axis=along_dim)
    return pad_face(remain, along_dim, before)


def face_terms(permeab, inside):
    face_x = (
        harmonic(permeab[:, :, :-1, :], permeab[:, :, 1:, :]) * (inside[:-1] * inside[1:])[:, None]
    )
    face_y = harmonic(permeab[:, :, :, :-1], permeab[:, :, :, 1:])
    face_z = VERTICAL * harmonic(permeab[:, :-1], permeab[:, 1:])
    return (face_x, face_y, face_z)


def neighbours(face_sets, values_in):
    flow_sum = 0.0
    weight_sum = 0.0
    for faces_dim, along_dim in zip(face_sets, (2, 3, 1)):
        lower = pad_face(faces_dim, along_dim, True)
        upper = pad_face(faces_dim, along_dim, False)
        flow_sum = (
            flow_sum
            + lower * slide_by(values_in, along_dim, True)
            + upper * slide_by(values_in, along_dim, False)
        )
        weight_sum = weight_sum + lower + upper
    return (flow_sum, weight_sum)


def jacobi(pressure, baseline, storage_term, face_sets):
    flow_sum, weight_sum = neighbours(face_sets, pressure)
    return (baseline + flow_sum) / (storage_term + weight_sum)


def water_frac(values_in):
    squared = values_in * values_in
    return squared / (squared + VISCOSITY_RATIO * (1.0 - values_in) * (1.0 - values_in))


def transport(pressure, saturation, face_sets):
    fraction = water_frac(saturation)
    change = 0.0
    for faces_dim, along_dim in zip(face_sets, (2, 3, 1)):
        extent = pressure.shape[along_dim]
        lower_press = lax.slice_in_dim(pressure, 0, extent - 1, axis=along_dim)
        upper_press = lax.slice_in_dim(pressure, 1, extent, axis=along_dim)
        lower_frac = lax.slice_in_dim(fraction, 0, extent - 1, axis=along_dim)
        upper_frac = lax.slice_in_dim(fraction, 1, extent, axis=along_dim)
        velocity = faces_dim * (lower_press - upper_press)
        carried = velocity * jnp.where(velocity > 0, lower_frac, upper_frac)
        change = change + pad_face(carried, along_dim, True) - pad_face(carried, along_dim, False)
    return saturation + STEP_COEF * change


def solve_spd(gram_matrix, cross_matrix):
    factor = lax.linalg.cholesky(
        gram_matrix + jnp.eye(gram_matrix.shape[0], dtype=jnp.float32), symmetrize_input=False
    )
    halfway = lax.linalg.triangular_solve(factor, cross_matrix, left_side=True, lower=True)
    return lax.linalg.triangular_solve(
        factor, halfway, left_side=True, lower=True, transpose_a=True
    )


def trim_rim(values_in, rim_cut):
    return values_in[:, :, rim_cut : values_in.shape[2] - rim_cut, :]


def exchange_kernel(member_count, part_ref, full_ref,
                    recv_a, send_a, recv_a_sem, send_m, recv_m_sem, send_t, recv_t_sem):
    tile_count = part_ref.shape[0]
    me_t = lax.axis_index("tile")
    me_m = lax.axis_index("member")
    mesh_ids = pl.DeviceIdType.MESH

    barrier = pltpu.get_barrier_semaphore()

    def greet_tile(k, carry):
        pl.semaphore_signal(
            barrier, 1, device_id=(lax.rem(me_t + k, tile_count), me_m), device_id_type=mesh_ids
        )
        return carry

    def greet_member(k, carry):
        pl.semaphore_signal(
            barrier, 1, device_id=(me_t, lax.rem(me_m + k, member_count)), device_id_type=mesh_ids
        )
        return carry

    lax.fori_loop(1, tile_count, greet_tile, 0)
    lax.fori_loop(1, member_count, greet_member, 0)
    pl.semaphore_wait(barrier, tile_count + member_count - 2)

    def copy_a(dst_t, src_t):
        return pltpu.make_async_remote_copy(
            src_ref=part_ref.at[dst_t], dst_ref=recv_a.at[src_t],
            send_sem=send_a.at[dst_t], recv_sem=recv_a_sem.at[src_t],
            device_id=(dst_t, me_m), device_id_type=mesh_ids,
        )

    def start_a(k, carry):
        copy_a(lax.rem(me_t + k, tile_count), me_t).start()
        return carry

    lax.fori_loop(1, tile_count, start_a, 0)

    def wait_a(k, acc):
        src_t = lax.rem(me_t + k, tile_count)
        copy_a(me_t, src_t).wait_recv()
        return acc + recv_a[src_t]

    acc = lax.fori_loop(1, tile_count, wait_a, part_ref[me_t])

    def wait_a_send(k, carry):
        copy_a(lax.rem(me_t + k, tile_count), me_t).wait_send()
        return carry

    lax.fori_loop(1, tile_count, wait_a_send, 0)

    full_ref[me_t, me_m] = acc

    def copy_m(dst_m, src_m):
        return pltpu.make_async_remote_copy(
            src_ref=full_ref.at[me_t, src_m], dst_ref=full_ref.at[me_t, src_m],
            send_sem=send_m.at[dst_m], recv_sem=recv_m_sem.at[src_m],
            device_id=(me_t, dst_m), device_id_type=mesh_ids,
        )

    def start_m(k, carry):
        copy_m(lax.rem(me_m + k, member_count), me_m).start()
        return carry

    lax.fori_loop(1, member_count, start_m, 0)

    def wait_m(k, carry):
        copy_m(me_m, lax.rem(me_m + k, member_count)).wait_recv()
        return carry

    lax.fori_loop(1, member_count, wait_m, 0)

    def wait_m_send(k, carry):
        copy_m(lax.rem(me_m + k, member_count), me_m).wait_send()
        return carry

    lax.fori_loop(1, member_count, wait_m_send, 0)

    def copy_t(dst_t, src_t):
        return pltpu.make_async_remote_copy(
            src_ref=full_ref.at[src_t], dst_ref=full_ref.at[src_t],
            send_sem=send_t.at[dst_t], recv_sem=recv_t_sem.at[src_t],
            device_id=(dst_t, me_m), device_id_type=mesh_ids,
        )

    def start_t(k, carry):
        copy_t(lax.rem(me_t + k, tile_count), me_t).start()
        return carry

    lax.fori_loop(1, tile_count, start_t, 0)

    def wait_t(k, carry):
        copy_t(me_t, lax.rem(me_t + k, tile_count)).wait_recv()
        return carry

    lax.fori_loop(1, tile_count, wait_t, 0)

    def wait_t_send(k, carry):
        copy_t(lax.rem(me_t + k, tile_count), me_t).wait_send()
        return carry

    lax.fori_loop(1, tile_count, wait_t_send, 0)


def stencil_kernel(rim, lp_ref, fields_ref, inside_ref, press_ref, sat_ref, mob_ref):
    inside = inside_ref[...]
    permeab = jnp.exp(lp_ref[...])
    face_sets = face_terms(permeab, inside)
    press_ext = fields_ref[0]
    sat_ext = fields_ref[1]
    source_ext = fields_ref[2]
    storage_ext = fields_ref[3]
    baseline = (source_ext + storage_ext * press_ext)[None]
    storage_term = jnp.where(inside[None, :, None] > 0.0, storage_ext, 1.0)[None]
    pressure = jnp.broadcast_to(press_ext[None], permeab.shape)
    for sweep_idx in range(SWEEPS):
        pressure = jacobi(pressure, baseline, storage_term, face_sets)
    saturation = trim_rim(transport(pressure, sat_ext[None], face_sets), rim)
    press_ref[...] = trim_rim(pressure, rim)
    sat_ref[...] = saturation
    mob_ref[...] = trim_rim(permeab, rim) * water_frac(saturation)


def stencil(lp_ext, fields_ext, inside, rim):
    members, layers, rows, depth = lp_ext.shape
    block = 4
    out_rows = rows - 2 * rim
    out_spec = pl.BlockSpec((block, layers, out_rows, depth), lambda i: (i, 0, 0, 0))
    out_shape = jax.ShapeDtypeStruct((members, layers, out_rows, depth), jnp.float32)
    return pl.pallas_call(
        functools.partial(stencil_kernel, rim),
        grid=(members // block,),
        in_specs=[
            pl.BlockSpec((block, layers, rows, depth), lambda i: (i, 0, 0, 0)),
            pl.BlockSpec(fields_ext.shape, lambda i: (0, 0, 0, 0)),
            pl.BlockSpec(inside.shape, lambda i: (0,)),
        ],
        out_specs=[out_spec, out_spec, out_spec],
        out_shape=[out_shape, out_shape, out_shape],
    )(lp_ext, fields_ext, inside)


def halo_kernel(out_ref, in_ref, send_sem, recv_sem):
    tile_count = lax.axis_size("tile")
    me_t = lax.axis_index("tile")
    me_m = lax.axis_index("member")
    mesh_ids = pl.DeviceIdType.MESH
    left = lax.rem(me_t + tile_count - 1, tile_count)
    right = lax.rem(me_t + 1, tile_count)
    barrier = pltpu.get_barrier_semaphore()
    for peer in (left, right):
        pl.semaphore_signal(barrier, 1, device_id=(peer, me_m), device_id_type=mesh_ids)
    pl.semaphore_wait(barrier, 2)
    to_right = pltpu.make_async_remote_copy(
        src_ref=out_ref.at[1], dst_ref=in_ref.at[0], send_sem=send_sem.at[1],
        recv_sem=recv_sem.at[0], device_id=(right, me_m), device_id_type=mesh_ids,
    )
    to_left = pltpu.make_async_remote_copy(
        src_ref=out_ref.at[0], dst_ref=in_ref.at[1], send_sem=send_sem.at[0],
        recv_sem=recv_sem.at[1], device_id=(left, me_m), device_id_type=mesh_ids,
    )
    to_right.start()
    to_left.start()
    to_right.wait()
    to_left.wait()


def halo_exchange(outgoing):
    vmem = pl.BlockSpec(memory_space=pltpu.VMEM)
    return pl.pallas_call(
        halo_kernel,
        out_shape=jax.ShapeDtypeStruct(outgoing.shape, outgoing.dtype),
        in_specs=[vmem],
        out_specs=vmem,
        scratch_shapes=[pltpu.SemaphoreType.DMA((2,)), pltpu.SemaphoreType.DMA((2,))],
        compiler_params=pltpu.CompilerParams(collective_id=1, has_side_effects=True),
    )(outgoing)


def rates_exchange(pieces, member_count):
    tile_count, rows, lanes = pieces.shape
    vmem = pl.BlockSpec(memory_space=pltpu.VMEM)
    return pl.pallas_call(
        functools.partial(exchange_kernel, member_count),
        out_shape=jax.ShapeDtypeStruct((tile_count, member_count, rows, lanes), jnp.float32),
        in_specs=[vmem],
        out_specs=vmem,
        scratch_shapes=[
            pltpu.VMEM((tile_count, rows, lanes), jnp.float32),
            pltpu.SemaphoreType.DMA((tile_count,)),
            pltpu.SemaphoreType.DMA((tile_count,)),
            pltpu.SemaphoreType.DMA((member_count,)),
            pltpu.SemaphoreType.DMA((member_count,)),
            pltpu.SemaphoreType.DMA((tile_count,)),
            pltpu.SemaphoreType.DMA((tile_count,)),
        ],
        compiler_params=pltpu.CompilerParams(collective_id=0, has_side_effects=True),
    )(pieces)


def per_device(
    log_perm,
    start_pressure,
    start_sat,
    source,
    storage,
    well_press,
    perf_cell,
    perf_well,
    perf_count,
    observed,
    obs_var,
    obs_noise,
):
    local_count, layers, strip_width, strip_depth = log_perm.shape
    tile_count = lax.axis_size("tile")
    members = local_count * lax.axis_size("member")
    well_count = well_press.shape[0]
    well_share = well_count // tile_count
    tile_rank = lax.axis_index("tile")
    member_rank = lax.axis_index("member")
    rim = SWEEPS + 1
    fields = jnp.stack([start_pressure, start_sat, source, storage])
    halo_rows = local_count * layers * rim + fields.shape[0] * layers * rim

    def rim_rows(first):
        return jnp.concatenate(
            [
                lax.slice_in_dim(log_perm, first, first + rim, axis=2).reshape(-1, strip_depth),
                lax.slice_in_dim(fields, first, first + rim, axis=2).reshape(-1, strip_depth),
            ]
        )

    outgoing = jnp.stack([rim_rows(0), rim_rows(strip_width - rim)])
    incoming = halo_exchange(outgoing)
    incoming, log_perm_after = lax.optimization_barrier((incoming, log_perm))
    lp_count = local_count * layers * rim

    def unpack(side):
        lp_part = incoming[side, :lp_count].reshape(local_count, layers, rim, strip_depth)
        field_part = incoming[side, lp_count:].reshape(fields.shape[0], layers, rim, strip_depth)
        return lp_part, field_part

    low_lp, low_fields = unpack(0)
    high_lp, high_fields = unpack(1)
    lp_ext = jnp.concatenate([low_lp, log_perm, high_lp], axis=2)
    fields_ext = jnp.concatenate([low_fields, fields, high_fields], axis=2)
    column = tile_rank * strip_width - rim + jnp.arange(strip_width + 2 * rim, dtype=jnp.int32)
    inside = ((column >= 0) & (column < strip_width * tile_count)).astype(jnp.float32)
    pressure, saturation, mobility = stencil(lp_ext, fields_ext, inside, rim)
    cell_count = layers * strip_width * strip_depth
    plane_rows = layers * strip_width
    cell_row = perf_cell // strip_depth
    cell_col = lax.rem(perf_cell, strip_depth)
    col_pick = (jnp.arange(strip_depth, dtype=jnp.int32)[:, None] == cell_col[None, :]).astype(
        jnp.float32
    )
    row_pick = jnp.arange(plane_rows, dtype=jnp.int32)[:, None] == cell_row[None, :]

    def pick_cells(values_in):
        by_col = jnp.dot(
            values_in.reshape(local_count * plane_rows, strip_depth), col_pick,
            precision=lax.Precision.HIGHEST, preferred_element_type=jnp.float32,
        ).reshape(local_count, plane_rows, -1)
        return jnp.sum(jnp.where(row_pick[None], by_col, 0.0), axis=1)

    perf_mob = pick_cells(mobility)
    perf_press = pick_cells(pressure)
    selector = (perf_well[:, None] == jnp.arange(well_count, dtype=jnp.int32)[None, :]).astype(
        jnp.float32
    )
    perf_bhp = jnp.dot(selector, well_press, precision=lax.Precision.HIGHEST)
    live_mask = (jnp.arange(perf_cell.shape[0], dtype=jnp.int32) < perf_count[0]).astype(
        jnp.float32
    )
    perf_terms = perf_mob * (perf_press - perf_bhp[None]) * live_mask[None]
    partial_rates = jnp.dot(
        perf_terms, selector, precision=lax.Precision.HIGHEST, preferred_element_type=jnp.float32
    )
    member_root = (members - 1) ** 0.5
    spread = jnp.sqrt(INFLATION * obs_var)
    member_count = lax.axis_size("member")
    block_rows = local_count * well_share // 128
    pieces = partial_rates.reshape(local_count, tile_count, well_share).transpose(1, 0, 2)
    pieces = pieces.reshape(tile_count, block_rows, 128)
    full = rates_exchange(pieces, member_count)
    lane_groups = 128 // well_share
    well_rates = lax.dynamic_index_in_dim(
        lax.dynamic_index_in_dim(full, tile_rank, 0, keepdims=False), member_rank, 0, keepdims=False
    ).reshape(local_count, well_share)
    rates_t = full.reshape(tile_count, member_count, block_rows, lane_groups, well_share)
    rates_t = rates_t.transpose(0, 4, 1, 2, 3).reshape(well_count, members)
    mean_rate = jnp.sum(rates_t, 1) / members
    scaled_t = (rates_t - mean_rate[:, None]) / (spread * member_root)[:, None]
    rates_own_t = lax.dynamic_slice_in_dim(rates_t, member_rank * local_count, local_count, 1)
    innov_own_t = (observed[:, None] - rates_own_t) / spread[:, None] + obs_noise.T
    contract_wells = (((0,), (0,)), ((), ()))
    gram_matrix = lax.dot_general(
        scaled_t, scaled_t, contract_wells, precision=lax.Precision.HIGHEST,
        preferred_element_type=jnp.float32,
    )
    cross_matrix = lax.dot_general(
        scaled_t, innov_own_t, contract_wells, precision=lax.Precision.HIGHEST,
        preferred_element_type=jnp.float32,
    )
    weights_low = solve_spd(gram_matrix, cross_matrix).astype(jnp.bfloat16)
    anomaly = (log_perm_after / member_root).astype(jnp.bfloat16).reshape(local_count, cell_count)
    anomaly_parts = [anomaly]
    for shift in range(1, member_count):
        pairs = [(i, (i + shift) % member_count) for i in range(member_count)]
        anomaly_parts.append(lax.ppermute(anomaly, "member", pairs))
    anomaly_all = jnp.concatenate(anomaly_parts, axis=0)
    own_cols = jnp.concatenate(
        [
            lax.dynamic_slice_in_dim(
                weights_low, lax.rem(member_rank - shift + member_count, member_count) * local_count,
                local_count, 0,
            )
            for shift in range(member_count)
        ],
        axis=0,
    )
    contract = (((0,), (0,)), ((), ()))
    update_sum = lax.dot_general(own_cols, anomaly_all, contract, preferred_element_type=jnp.float32)
    new_log_perm = log_perm + update_sum.reshape(log_perm.shape)
    return (new_log_perm, pressure, saturation, well_rates)


def solution(mesh):
    return jax.shard_map(
        per_device,
        mesh=mesh,
        in_specs=(
            P("member", None, "tile", None),
            P(None, "tile", None),
            P(None, "tile", None),
            P(None, "tile", None),
            P(None, "tile", None),
            P(),
            P("tile"),
            P("tile"),
            P("tile"),
            P(),
            P(),
            P("member", None),
        ),
        out_specs=(
            P("member", None, "tile", None),
            P("member", None, "tile", None),
            P("member", None, "tile", None),
            P("member", "tile"),
        ),
        check_vma=False,
    )
```

```python
import functools

import jax
import jax.numpy as jnp
from jax import lax
from jax.experimental import pallas as pl
from jax.experimental.pallas import tpu as pltpu
from jax.sharding import PartitionSpec as P

SWEEPS = 2


VERTICAL = 0.5
VISCOSITY_RATIO = 2.0
STEP_COEF = 0.1
INFLATION = 4.0


def extended_2(block, sides, width):
    for axis, dim in sides:
        count = lax.axis_size(axis)
        forward = [(i, i + 1) for i in range(count - 1)]
        backward = [(target, source) for source, target in forward]
        low = lax.ppermute(
            lax.slice_in_dim(block, block.shape[dim] - width, None, axis=dim), axis, forward
        )
        high = lax.ppermute(lax.slice_in_dim(block, 0, width, axis=dim), axis, backward)
        block = jnp.concatenate([low, block, high], axis=dim)
    return block


def harmonic(lower_val, upper_val):
    return 2.0 * lower_val * upper_val / (lower_val + upper_val)


def pad_face(values_in, along_dim, before):
    widths = [(0, 0)] * values_in.ndim
    widths[along_dim] = (1, 0) if before else (0, 1)
    return jnp.pad(values_in, widths)


def slide_by(values_in, along_dim, before):
    extent = values_in.shape[along_dim]
    if before:
        remain = lax.slice_in_dim(values_in, 0, extent - 1, axis=along_dim)
    else:
        remain = lax.slice_in_dim(values_in, 1, extent, axis=along_dim)
    return pad_face(remain, along_dim, before)


def face_terms(permeab, inside):
    face_x = (
        harmonic(permeab[:, :, :-1, :], permeab[:, :, 1:, :]) * (inside[:-1] * inside[1:])[:, None]
    )
    face_y = harmonic(permeab[:, :, :, :-1], permeab[:, :, :, 1:])
    face_z = VERTICAL * harmonic(permeab[:, :-1], permeab[:, 1:])
    return (face_x, face_y, face_z)


def neighbours(face_sets, values_in):
    flow_sum = 0.0
    weight_sum = 0.0
    for faces_dim, along_dim in zip(face_sets, (2, 3, 1)):
        lower = pad_face(faces_dim, along_dim, True)
        upper = pad_face(faces_dim, along_dim, False)
        flow_sum = (
            flow_sum
            + lower * slide_by(values_in, along_dim, True)
            + upper * slide_by(values_in, along_dim, False)
        )
        weight_sum = weight_sum + lower + upper
    return (flow_sum, weight_sum)


def jacobi(pressure, baseline, storage_term, face_sets):
    flow_sum, weight_sum = neighbours(face_sets, pressure)
    return (baseline + flow_sum) / (storage_term + weight_sum)


def water_frac(values_in):
    squared = values_in * values_in
    return squared / (squared + VISCOSITY_RATIO * (1.0 - values_in) * (1.0 - values_in))


def transport(pressure, saturation, face_sets):
    fraction = water_frac(saturation)
    change = 0.0
    for faces_dim, along_dim in zip(face_sets, (2, 3, 1)):
        extent = pressure.shape[along_dim]
        lower_press = lax.slice_in_dim(pressure, 0, extent - 1, axis=along_dim)
        upper_press = lax.slice_in_dim(pressure, 1, extent, axis=along_dim)
        lower_frac = lax.slice_in_dim(fraction, 0, extent - 1, axis=along_dim)
        upper_frac = lax.slice_in_dim(fraction, 1, extent, axis=along_dim)
        velocity = faces_dim * (lower_press - upper_press)
        carried = velocity * jnp.where(velocity > 0, lower_frac, upper_frac)
        change = change + pad_face(carried, along_dim, True) - pad_face(carried, along_dim, False)
    return saturation + STEP_COEF * change


def solve_spd(gram_matrix, cross_matrix):
    factor = lax.linalg.cholesky(
        gram_matrix + jnp.eye(gram_matrix.shape[0], dtype=jnp.float32), symmetrize_input=False
    )
    halfway = lax.linalg.triangular_solve(factor, cross_matrix, left_side=True, lower=True)
    return lax.linalg.triangular_solve(
        factor, halfway, left_side=True, lower=True, transpose_a=True
    )


def trim_rim(values_in, rim_cut):
    return values_in[:, :, rim_cut : values_in.shape[2] - rim_cut, :]


def exchange_kernel(member_count, part_ref, full_ref,
                    recv_a, own_blk, recv_m, send_a, recv_a_sem, send_m, recv_m_sem, send_t, recv_t_sem):
    tile_count = part_ref.shape[0]
    me_t = lax.axis_index("tile")
    me_m = lax.axis_index("member")
    mesh_ids = pl.DeviceIdType.MESH

    barrier = pltpu.get_barrier_semaphore()

    def greet_tile(k, carry):
        pl.semaphore_signal(
            barrier, 1, device_id=(lax.rem(me_t + k, tile_count), me_m), device_id_type=mesh_ids
        )
        return carry

    def greet_member(k, carry):
        pl.semaphore_signal(
            barrier, 1, device_id=(me_t, lax.rem(me_m + k, member_count)), device_id_type=mesh_ids
        )
        return carry

    lax.fori_loop(1, tile_count, greet_tile, 0)
    lax.fori_loop(1, member_count, greet_member, 0)
    pl.semaphore_wait(barrier, tile_count + member_count - 2)

    def copy_a(dst_t, src_t):
        return pltpu.make_async_remote_copy(
            src_ref=part_ref.at[dst_t], dst_ref=recv_a.at[src_t],
            send_sem=send_a.at[dst_t], recv_sem=recv_a_sem.at[src_t],
            device_id=(dst_t, me_m), device_id_type=mesh_ids,
        )

    def start_a(k, carry):
        copy_a(lax.rem(me_t + k, tile_count), me_t).start()
        return carry

    lax.fori_loop(1, tile_count, start_a, 0)

    def wait_a(k, acc):
        src_t = lax.rem(me_t + k, tile_count)
        copy_a(me_t, src_t).wait_recv()
        return acc + recv_a[src_t]

    acc = lax.fori_loop(1, tile_count, wait_a, part_ref[me_t])

    def wait_a_send(k, carry):
        copy_a(lax.rem(me_t + k, tile_count), me_t).wait_send()
        return carry

    lax.fori_loop(1, tile_count, wait_a_send, 0)

    own_blk[...] = acc

    def copy_m(dst_m, src_m):
        return pltpu.make_async_remote_copy(
            src_ref=own_blk, dst_ref=recv_m.at[src_m],
            send_sem=send_m.at[dst_m], recv_sem=recv_m_sem.at[src_m],
            device_id=(me_t, dst_m), device_id_type=mesh_ids,
        )

    def start_m(k, carry):
        copy_m(lax.rem(me_m + k, member_count), me_m).start()
        return carry

    lax.fori_loop(1, member_count, start_m, 0)

    def wait_m(k, total):
        src_m = lax.rem(me_m + k, member_count)
        copy_m(me_m, src_m).wait_recv()
        return total + recv_m[src_m]

    full_ref[me_t] = lax.fori_loop(1, member_count, wait_m, acc)

    def wait_m_send(k, carry):
        copy_m(lax.rem(me_m + k, member_count), me_m).wait_send()
        return carry

    lax.fori_loop(1, member_count, wait_m_send, 0)

    def copy_t(dst_t, src_t):
        return pltpu.make_async_remote_copy(
            src_ref=full_ref.at[src_t], dst_ref=full_ref.at[src_t],
            send_sem=send_t.at[dst_t], recv_sem=recv_t_sem.at[src_t],
            device_id=(dst_t, me_m), device_id_type=mesh_ids,
        )

    def start_t(k, carry):
        copy_t(lax.rem(me_t + k, tile_count), me_t).start()
        return carry

    lax.fori_loop(1, tile_count, start_t, 0)

    def wait_t(k, carry):
        copy_t(me_t, lax.rem(me_t + k, tile_count)).wait_recv()
        return carry

    lax.fori_loop(1, tile_count, wait_t, 0)

    def wait_t_send(k, carry):
        copy_t(lax.rem(me_t + k, tile_count), me_t).wait_send()
        return carry

    lax.fori_loop(1, tile_count, wait_t_send, 0)


def stencil_kernel(rim, lp_ref, fields_ref, inside_ref, press_ref, sat_ref, mob_ref):
    inside = inside_ref[...]
    permeab = jnp.exp(lp_ref[...])
    face_sets = face_terms(permeab, inside)
    press_ext = fields_ref[0]
    sat_ext = fields_ref[1]
    source_ext = fields_ref[2]
    storage_ext = fields_ref[3]
    baseline = (source_ext + storage_ext * press_ext)[None]
    storage_term = jnp.where(inside[None, :, None] > 0.0, storage_ext, 1.0)[None]
    pressure = jnp.broadcast_to(press_ext[None], permeab.shape)
    for sweep_idx in range(SWEEPS):
        pressure = jacobi(pressure, baseline, storage_term, face_sets)
    saturation = trim_rim(transport(pressure, sat_ext[None], face_sets), rim)
    press_ref[...] = trim_rim(pressure, rim)
    sat_ref[...] = saturation
    mob_ref[...] = trim_rim(permeab, rim) * water_frac(saturation)


def stencil(lp_ext, fields_ext, inside, rim):
    members, layers, rows, depth = lp_ext.shape
    block = 4
    out_rows = rows - 2 * rim
    out_spec = pl.BlockSpec((block, layers, out_rows, depth), lambda i: (i, 0, 0, 0))
    out_shape = jax.ShapeDtypeStruct((members, layers, out_rows, depth), jnp.float32)
    return pl.pallas_call(
        functools.partial(stencil_kernel, rim),
        grid=(members // block,),
        in_specs=[
            pl.BlockSpec((block, layers, rows, depth), lambda i: (i, 0, 0, 0)),
            pl.BlockSpec(fields_ext.shape, lambda i: (0, 0, 0, 0)),
            pl.BlockSpec(inside.shape, lambda i: (0,)),
        ],
        out_specs=[out_spec, out_spec, out_spec],
        out_shape=[out_shape, out_shape, out_shape],
    )(lp_ext, fields_ext, inside)


def halo_kernel(out_ref, in_ref, send_sem, recv_sem):
    tile_count = lax.axis_size("tile")
    me_t = lax.axis_index("tile")
    me_m = lax.axis_index("member")
    mesh_ids = pl.DeviceIdType.MESH
    left = lax.rem(me_t + tile_count - 1, tile_count)
    right = lax.rem(me_t + 1, tile_count)
    barrier = pltpu.get_barrier_semaphore()
    for peer in (left, right):
        pl.semaphore_signal(barrier, 1, device_id=(peer, me_m), device_id_type=mesh_ids)
    pl.semaphore_wait(barrier, 2)
    to_right = pltpu.make_async_remote_copy(
        src_ref=out_ref.at[1], dst_ref=in_ref.at[0], send_sem=send_sem.at[1],
        recv_sem=recv_sem.at[0], device_id=(right, me_m), device_id_type=mesh_ids,
    )
    to_left = pltpu.make_async_remote_copy(
        src_ref=out_ref.at[0], dst_ref=in_ref.at[1], send_sem=send_sem.at[0],
        recv_sem=recv_sem.at[1], device_id=(left, me_m), device_id_type=mesh_ids,
    )
    to_right.start()
    to_left.start()
    to_right.wait()
    to_left.wait()


def halo_exchange(outgoing):
    vmem = pl.BlockSpec(memory_space=pltpu.VMEM)
    return pl.pallas_call(
        halo_kernel,
        out_shape=jax.ShapeDtypeStruct(outgoing.shape, outgoing.dtype),
        in_specs=[vmem],
        out_specs=vmem,
        scratch_shapes=[pltpu.SemaphoreType.DMA((2,)), pltpu.SemaphoreType.DMA((2,))],
        compiler_params=pltpu.CompilerParams(collective_id=1, has_side_effects=True),
    )(outgoing)


def rates_exchange(pieces, member_count):
    tile_count, rows, lanes = pieces.shape
    vmem = pl.BlockSpec(memory_space=pltpu.VMEM)
    return pl.pallas_call(
        functools.partial(exchange_kernel, member_count),
        out_shape=jax.ShapeDtypeStruct((tile_count, rows, lanes), jnp.float32),
        in_specs=[vmem],
        out_specs=vmem,
        scratch_shapes=[
            pltpu.VMEM((tile_count, rows, lanes), jnp.float32),
            pltpu.VMEM((rows, lanes), jnp.float32),
            pltpu.VMEM((member_count, rows, lanes), jnp.float32),
            pltpu.SemaphoreType.DMA((tile_count,)),
            pltpu.SemaphoreType.DMA((tile_count,)),
            pltpu.SemaphoreType.DMA((member_count,)),
            pltpu.SemaphoreType.DMA((member_count,)),
            pltpu.SemaphoreType.DMA((tile_count,)),
            pltpu.SemaphoreType.DMA((tile_count,)),
        ],
        compiler_params=pltpu.CompilerParams(collective_id=0, has_side_effects=True),
    )(pieces)


def per_device(
    log_perm,
    start_pressure,
    start_sat,
    source,
    storage,
    well_press,
    perf_cell,
    perf_well,
    perf_count,
    observed,
    obs_var,
    obs_noise,
):
    local_count, layers, strip_width, strip_depth = log_perm.shape
    tile_count = lax.axis_size("tile")
    members = local_count * lax.axis_size("member")
    well_count = well_press.shape[0]
    well_share = well_count // tile_count
    tile_rank = lax.axis_index("tile")
    member_rank = lax.axis_index("member")
    rim = SWEEPS + 1
    fields = jnp.stack([start_pressure, start_sat, source, storage])
    halo_rows = local_count * layers * rim + fields.shape[0] * layers * rim

    def rim_rows(first):
        return jnp.concatenate(
            [
                lax.slice_in_dim(log_perm, first, first + rim, axis=2).reshape(-1, strip_depth),
                lax.slice_in_dim(fields, first, first + rim, axis=2).reshape(-1, strip_depth),
            ]
        )

    outgoing = jnp.stack([rim_rows(0), rim_rows(strip_width - rim)])
    incoming = halo_exchange(outgoing)
    incoming, log_perm_after = lax.optimization_barrier((incoming, log_perm))
    lp_count = local_count * layers * rim

    def unpack(side):
        lp_part = incoming[side, :lp_count].reshape(local_count, layers, rim, strip_depth)
        field_part = incoming[side, lp_count:].reshape(fields.shape[0], layers, rim, strip_depth)
        return lp_part, field_part

    low_lp, low_fields = unpack(0)
    high_lp, high_fields = unpack(1)
    lp_ext = jnp.concatenate([low_lp, log_perm, high_lp], axis=2)
    fields_ext = jnp.concatenate([low_fields, fields, high_fields], axis=2)
    column = tile_rank * strip_width - rim + jnp.arange(strip_width + 2 * rim, dtype=jnp.int32)
    inside = ((column >= 0) & (column < strip_width * tile_count)).astype(jnp.float32)
    pressure, saturation, mobility = stencil(lp_ext, fields_ext, inside, rim)
    cell_count = layers * strip_width * strip_depth
    plane_rows = layers * strip_width
    cell_row = perf_cell // strip_depth
    cell_col = lax.rem(perf_cell, strip_depth)
    col_pick = (jnp.arange(strip_depth, dtype=jnp.int32)[:, None] == cell_col[None, :]).astype(
        jnp.float32
    )
    row_pick = jnp.arange(plane_rows, dtype=jnp.int32)[:, None] == cell_row[None, :]

    def pick_cells(values_in):
        by_col = jnp.dot(
            values_in.reshape(local_count * plane_rows, strip_depth), col_pick,
            precision=lax.Precision.HIGHEST, preferred_element_type=jnp.float32,
        ).reshape(local_count, plane_rows, -1)
        return jnp.sum(jnp.where(row_pick[None], by_col, 0.0), axis=1)

    perf_mob = pick_cells(mobility)
    perf_press = pick_cells(pressure)
    selector = (perf_well[:, None] == jnp.arange(well_count, dtype=jnp.int32)[None, :]).astype(
        jnp.float32
    )
    perf_bhp = jnp.dot(selector, well_press, precision=lax.Precision.HIGHEST)
    live_mask = (jnp.arange(perf_cell.shape[0], dtype=jnp.int32) < perf_count[0]).astype(
        jnp.float32
    )
    perf_terms = perf_mob * (perf_press - perf_bhp[None]) * live_mask[None]
    member_root = (members - 1) ** 0.5
    spread = jnp.sqrt(INFLATION * obs_var)
    member_count = lax.axis_size("member")
    lane_group = jnp.arange(members, dtype=jnp.int32) // local_count
    terms_wide = jnp.where(
        (lane_group == member_rank)[:, None], jnp.tile(perf_terms, (member_count, 1)), 0.0
    )
    contract_slots = (((0,), (1,)), ((), ()))
    pieces = lax.dot_general(
        selector, terms_wide, contract_slots, precision=lax.Precision.HIGHEST,
        preferred_element_type=jnp.float32,
    ).reshape(tile_count, well_share, members)
    full = rates_exchange(pieces, member_count)
    own_block = lax.dynamic_index_in_dim(full, tile_rank, 0, keepdims=False)
    well_rates = lax.dynamic_slice_in_dim(own_block, member_rank * local_count, local_count, 1).T
    rates_t = full.reshape(well_count, members)
    mean_rate = jnp.sum(rates_t, 1) / members
    scaled_t = (rates_t - mean_rate[:, None]) / (spread * member_root)[:, None]
    rates_own_t = lax.dynamic_slice_in_dim(rates_t, member_rank * local_count, local_count, 1)
    innov_own_t = (observed[:, None] - rates_own_t) / spread[:, None] + obs_noise.T
    contract_wells = (((0,), (0,)), ((), ()))
    gram_matrix = lax.dot_general(
        scaled_t, scaled_t, contract_wells, precision=lax.Precision.HIGHEST,
        preferred_element_type=jnp.float32,
    )
    cross_matrix = lax.dot_general(
        scaled_t, innov_own_t, contract_wells, precision=lax.Precision.HIGHEST,
        preferred_element_type=jnp.float32,
    )
    weights_low = solve_spd(gram_matrix, cross_matrix).astype(jnp.bfloat16)
    anomaly = (log_perm_after / member_root).astype(jnp.bfloat16).reshape(local_count, cell_count)
    anomaly_parts = [anomaly]
    for shift in range(1, member_count):
        pairs = [(i, (i + shift) % member_count) for i in range(member_count)]
        anomaly_parts.append(lax.ppermute(anomaly, "member", pairs))
    anomaly_all = jnp.concatenate(anomaly_parts, axis=0)
    own_cols = jnp.concatenate(
        [
            lax.dynamic_slice_in_dim(
                weights_low, lax.rem(member_rank - shift + member_count, member_count) * local_count,
                local_count, 0,
            )
            for shift in range(member_count)
        ],
        axis=0,
    )
    contract = (((0,), (0,)), ((), ()))
    update_sum = lax.dot_general(own_cols, anomaly_all, contract, preferred_element_type=jnp.float32)
    new_log_perm = log_perm + update_sum.reshape(log_perm.shape)
    return (new_log_perm, pressure, saturation, well_rates)


def solution(mesh):
    return jax.shard_map(
        per_device,
        mesh=mesh,
        in_specs=(
            P("member", None, "tile", None),
            P(None, "tile", None),
            P(None, "tile", None),
            P(None, "tile", None),
            P(None, "tile", None),
            P(),
            P("tile"),
            P("tile"),
            P("tile"),
            P(),
            P(),
            P("member", None),
        ),
        out_specs=(
            P("member", None, "tile", None),
            P("member", None, "tile", None),
            P("member", None, "tile", None),
            P("member", "tile"),
        ),
        check_vma=False,
    )
```

```python
import functools

import jax
import jax.numpy as jnp
from jax import lax
from jax.experimental import pallas as pl
from jax.experimental.pallas import tpu as pltpu
from jax.sharding import PartitionSpec as P

SWEEPS = 2


VERTICAL = 0.5
VISCOSITY_RATIO = 2.0
STEP_COEF = 0.1
INFLATION = 4.0


def extended_2(block, sides, width):
    for axis, dim in sides:
        count = lax.axis_size(axis)
        forward = [(i, i + 1) for i in range(count - 1)]
        backward = [(target, source) for source, target in forward]
        low = lax.ppermute(
            lax.slice_in_dim(block, block.shape[dim] - width, None, axis=dim), axis, forward
        )
        high = lax.ppermute(lax.slice_in_dim(block, 0, width, axis=dim), axis, backward)
        block = jnp.concatenate([low, block, high], axis=dim)
    return block


def harmonic(lower_val, upper_val):
    return 2.0 * lower_val * upper_val / (lower_val + upper_val)


def pad_face(values_in, along_dim, before):
    widths = [(0, 0)] * values_in.ndim
    widths[along_dim] = (1, 0) if before else (0, 1)
    return jnp.pad(values_in, widths)


def slide_by(values_in, along_dim, before):
    extent = values_in.shape[along_dim]
    if before:
        remain = lax.slice_in_dim(values_in, 0, extent - 1, axis=along_dim)
    else:
        remain = lax.slice_in_dim(values_in, 1, extent, axis=along_dim)
    return pad_face(remain, along_dim, before)


def face_terms(permeab, inside):
    face_x = (
        harmonic(permeab[:, :, :-1, :], permeab[:, :, 1:, :]) * (inside[:-1] * inside[1:])[:, None]
    )
    face_y = harmonic(permeab[:, :, :, :-1], permeab[:, :, :, 1:])
    face_z = VERTICAL * harmonic(permeab[:, :-1], permeab[:, 1:])
    return (face_x, face_y, face_z)


def neighbours(face_sets, values_in):
    flow_sum = 0.0
    weight_sum = 0.0
    for faces_dim, along_dim in zip(face_sets, (2, 3, 1)):
        lower = pad_face(faces_dim, along_dim, True)
        upper = pad_face(faces_dim, along_dim, False)
        flow_sum = (
            flow_sum
            + lower * slide_by(values_in, along_dim, True)
            + upper * slide_by(values_in, along_dim, False)
        )
        weight_sum = weight_sum + lower + upper
    return (flow_sum, weight_sum)


def jacobi(pressure, baseline, storage_term, face_sets):
    flow_sum, weight_sum = neighbours(face_sets, pressure)
    return (baseline + flow_sum) / (storage_term + weight_sum)


def water_frac(values_in):
    squared = values_in * values_in
    return squared / (squared + VISCOSITY_RATIO * (1.0 - values_in) * (1.0 - values_in))


def transport(pressure, saturation, face_sets):
    fraction = water_frac(saturation)
    change = 0.0
    for faces_dim, along_dim in zip(face_sets, (2, 3, 1)):
        extent = pressure.shape[along_dim]
        lower_press = lax.slice_in_dim(pressure, 0, extent - 1, axis=along_dim)
        upper_press = lax.slice_in_dim(pressure, 1, extent, axis=along_dim)
        lower_frac = lax.slice_in_dim(fraction, 0, extent - 1, axis=along_dim)
        upper_frac = lax.slice_in_dim(fraction, 1, extent, axis=along_dim)
        velocity = faces_dim * (lower_press - upper_press)
        carried = velocity * jnp.where(velocity > 0, lower_frac, upper_frac)
        change = change + pad_face(carried, along_dim, True) - pad_face(carried, along_dim, False)
    return saturation + STEP_COEF * change


def solve_spd(gram_matrix, cross_matrix):
    factor = lax.linalg.cholesky(
        gram_matrix + jnp.eye(gram_matrix.shape[0], dtype=jnp.float32), symmetrize_input=False
    )
    halfway = lax.linalg.triangular_solve(factor, cross_matrix, left_side=True, lower=True)
    return lax.linalg.triangular_solve(
        factor, halfway, left_side=True, lower=True, transpose_a=True
    )


def trim_rim(values_in, rim_cut):
    return values_in[:, :, rim_cut : values_in.shape[2] - rim_cut, :]


def exchange_kernel(member_count, part_ref, full_ref,
                    recv_a, own_blk, recv_m, send_a, recv_a_sem, send_m, recv_m_sem, send_t, recv_t_sem):
    tile_count = part_ref.shape[0]
    me_t = lax.axis_index("tile")
    me_m = lax.axis_index("member")
    mesh_ids = pl.DeviceIdType.MESH

    barrier = pltpu.get_barrier_semaphore()

    def greet_tile(k, carry):
        pl.semaphore_signal(
            barrier, 1, device_id=(lax.rem(me_t + k, tile_count), me_m), device_id_type=mesh_ids
        )
        return carry

    def greet_member(k, carry):
        pl.semaphore_signal(
            barrier, 1, device_id=(me_t, lax.rem(me_m + k, member_count)), device_id_type=mesh_ids
        )
        return carry

    lax.fori_loop(1, tile_count, greet_tile, 0)
    lax.fori_loop(1, member_count, greet_member, 0)
    pl.semaphore_wait(barrier, tile_count + member_count - 2)

    def copy_a(dst_t, src_t):
        return pltpu.make_async_remote_copy(
            src_ref=part_ref.at[dst_t], dst_ref=recv_a.at[src_t],
            send_sem=send_a.at[dst_t], recv_sem=recv_a_sem.at[src_t],
            device_id=(dst_t, me_m), device_id_type=mesh_ids,
        )

    def start_a(k, carry):
        copy_a(lax.rem(me_t + k, tile_count), me_t).start()
        return carry

    lax.fori_loop(1, tile_count, start_a, 0)

    def wait_a(k, acc):
        src_t = lax.rem(me_t + k, tile_count)
        copy_a(me_t, src_t).wait_recv()
        return acc + recv_a[src_t]

    acc = lax.fori_loop(1, tile_count, wait_a, part_ref[me_t])

    def wait_a_send(k, carry):
        copy_a(lax.rem(me_t + k, tile_count), me_t).wait_send()
        return carry

    lax.fori_loop(1, tile_count, wait_a_send, 0)

    groups = part_ref.shape[2] // member_count
    lane_ids = lax.broadcasted_iota(jnp.int32, acc.shape, 1)
    for q in range(member_count):
        moved = pltpu.roll(acc, lax.rem((me_m - q + member_count) * groups, part_ref.shape[2]), 1)
        own_blk[pl.ds(q, acc.shape[0], stride=member_count), :] = jnp.where(
            lane_ids // groups == me_m, moved, 0.0
        )
    acc = own_blk[...]

    def copy_m(dst_m, src_m):
        return pltpu.make_async_remote_copy(
            src_ref=own_blk, dst_ref=recv_m.at[src_m],
            send_sem=send_m.at[dst_m], recv_sem=recv_m_sem.at[src_m],
            device_id=(me_t, dst_m), device_id_type=mesh_ids,
        )

    def start_m(k, carry):
        copy_m(lax.rem(me_m + k, member_count), me_m).start()
        return carry

    lax.fori_loop(1, member_count, start_m, 0)

    def wait_m(k, total):
        src_m = lax.rem(me_m + k, member_count)
        copy_m(me_m, src_m).wait_recv()
        return total + recv_m[src_m]

    full_ref[me_t] = lax.fori_loop(1, member_count, wait_m, acc)

    def wait_m_send(k, carry):
        copy_m(lax.rem(me_m + k, member_count), me_m).wait_send()
        return carry

    lax.fori_loop(1, member_count, wait_m_send, 0)

    def copy_t(dst_t, src_t):
        return pltpu.make_async_remote_copy(
            src_ref=full_ref.at[src_t], dst_ref=full_ref.at[src_t],
            send_sem=send_t.at[dst_t], recv_sem=recv_t_sem.at[src_t],
            device_id=(dst_t, me_m), device_id_type=mesh_ids,
        )

    def start_t(k, carry):
        copy_t(lax.rem(me_t + k, tile_count), me_t).start()
        return carry

    lax.fori_loop(1, tile_count, start_t, 0)

    def wait_t(k, carry):
        copy_t(me_t, lax.rem(me_t + k, tile_count)).wait_recv()
        return carry

    lax.fori_loop(1, tile_count, wait_t, 0)

    def wait_t_send(k, carry):
        copy_t(lax.rem(me_t + k, tile_count), me_t).wait_send()
        return carry

    lax.fori_loop(1, tile_count, wait_t_send, 0)


def stencil_kernel(rim, lp_ref, fields_ref, inside_ref, press_ref, sat_ref, mob_ref):
    inside = inside_ref[...]
    permeab = jnp.exp(lp_ref[...])
    face_sets = face_terms(permeab, inside)
    press_ext = fields_ref[0]
    sat_ext = fields_ref[1]
    source_ext = fields_ref[2]
    storage_ext = fields_ref[3]
    baseline = (source_ext + storage_ext * press_ext)[None]
    storage_term = jnp.where(inside[None, :, None] > 0.0, storage_ext, 1.0)[None]
    pressure = jnp.broadcast_to(press_ext[None], permeab.shape)
    for sweep_idx in range(SWEEPS):
        pressure = jacobi(pressure, baseline, storage_term, face_sets)
    saturation = trim_rim(transport(pressure, sat_ext[None], face_sets), rim)
    press_ref[...] = trim_rim(pressure, rim)
    sat_ref[...] = saturation
    mob_ref[...] = trim_rim(permeab, rim) * water_frac(saturation)


def stencil(lp_ext, fields_ext, inside, rim):
    members, layers, rows, depth = lp_ext.shape
    block = 4
    out_rows = rows - 2 * rim
    out_spec = pl.BlockSpec((block, layers, out_rows, depth), lambda i: (i, 0, 0, 0))
    out_shape = jax.ShapeDtypeStruct((members, layers, out_rows, depth), jnp.float32)
    return pl.pallas_call(
        functools.partial(stencil_kernel, rim),
        grid=(members // block,),
        in_specs=[
            pl.BlockSpec((block, layers, rows, depth), lambda i: (i, 0, 0, 0)),
            pl.BlockSpec(fields_ext.shape, lambda i: (0, 0, 0, 0)),
            pl.BlockSpec(inside.shape, lambda i: (0,)),
        ],
        out_specs=[out_spec, out_spec, out_spec],
        out_shape=[out_shape, out_shape, out_shape],
    )(lp_ext, fields_ext, inside)


def halo_kernel(out_ref, in_ref, send_sem, recv_sem):
    tile_count = lax.axis_size("tile")
    me_t = lax.axis_index("tile")
    me_m = lax.axis_index("member")
    mesh_ids = pl.DeviceIdType.MESH
    left = lax.rem(me_t + tile_count - 1, tile_count)
    right = lax.rem(me_t + 1, tile_count)
    barrier = pltpu.get_barrier_semaphore()
    for peer in (left, right):
        pl.semaphore_signal(barrier, 1, device_id=(peer, me_m), device_id_type=mesh_ids)
    pl.semaphore_wait(barrier, 2)
    to_right = pltpu.make_async_remote_copy(
        src_ref=out_ref.at[1], dst_ref=in_ref.at[0], send_sem=send_sem.at[1],
        recv_sem=recv_sem.at[0], device_id=(right, me_m), device_id_type=mesh_ids,
    )
    to_left = pltpu.make_async_remote_copy(
        src_ref=out_ref.at[0], dst_ref=in_ref.at[1], send_sem=send_sem.at[0],
        recv_sem=recv_sem.at[1], device_id=(left, me_m), device_id_type=mesh_ids,
    )
    to_right.start()
    to_left.start()
    to_right.wait()
    to_left.wait()


def halo_exchange(outgoing):
    vmem = pl.BlockSpec(memory_space=pltpu.VMEM)
    return pl.pallas_call(
        halo_kernel,
        out_shape=jax.ShapeDtypeStruct(outgoing.shape, outgoing.dtype),
        in_specs=[vmem],
        out_specs=vmem,
        scratch_shapes=[pltpu.SemaphoreType.DMA((2,)), pltpu.SemaphoreType.DMA((2,))],
        compiler_params=pltpu.CompilerParams(collective_id=1, has_side_effects=True),
    )(outgoing)


def rates_exchange(pieces, member_count):
    tile_count, rows, lanes = pieces.shape
    vmem = pl.BlockSpec(memory_space=pltpu.VMEM)
    return pl.pallas_call(
        functools.partial(exchange_kernel, member_count),
        out_shape=jax.ShapeDtypeStruct((tile_count, rows * member_count, lanes), jnp.float32),
        in_specs=[vmem],
        out_specs=vmem,
        scratch_shapes=[
            pltpu.VMEM((tile_count, rows, lanes), jnp.float32),
            pltpu.VMEM((rows * member_count, lanes), jnp.float32),
            pltpu.VMEM((member_count, rows * member_count, lanes), jnp.float32),
            pltpu.SemaphoreType.DMA((tile_count,)),
            pltpu.SemaphoreType.DMA((tile_count,)),
            pltpu.SemaphoreType.DMA((member_count,)),
            pltpu.SemaphoreType.DMA((member_count,)),
            pltpu.SemaphoreType.DMA((tile_count,)),
            pltpu.SemaphoreType.DMA((tile_count,)),
        ],
        compiler_params=pltpu.CompilerParams(collective_id=0, has_side_effects=True),
    )(pieces)


def per_device(
    log_perm,
    start_pressure,
    start_sat,
    source,
    storage,
    well_press,
    perf_cell,
    perf_well,
    perf_count,
    observed,
    obs_var,
    obs_noise,
):
    local_count, layers, strip_width, strip_depth = log_perm.shape
    tile_count = lax.axis_size("tile")
    members = local_count * lax.axis_size("member")
    well_count = well_press.shape[0]
    well_share = well_count // tile_count
    tile_rank = lax.axis_index("tile")
    member_rank = lax.axis_index("member")
    rim = SWEEPS + 1
    fields = jnp.stack([start_pressure, start_sat, source, storage])
    halo_rows = local_count * layers * rim + fields.shape[0] * layers * rim

    def rim_rows(first):
        return jnp.concatenate(
            [
                lax.slice_in_dim(log_perm, first, first + rim, axis=2).reshape(-1, strip_depth),
                lax.slice_in_dim(fields, first, first + rim, axis=2).reshape(-1, strip_depth),
            ]
        )

    outgoing = jnp.stack([rim_rows(0), rim_rows(strip_width - rim)])
    incoming = halo_exchange(outgoing)
    incoming, log_perm_after = lax.optimization_barrier((incoming, log_perm))
    lp_count = local_count * layers * rim

    def unpack(side):
        lp_part = incoming[side, :lp_count].reshape(local_count, layers, rim, strip_depth)
        field_part = incoming[side, lp_count:].reshape(fields.shape[0], layers, rim, strip_depth)
        return lp_part, field_part

    low_lp, low_fields = unpack(0)
    high_lp, high_fields = unpack(1)
    lp_ext = jnp.concatenate([low_lp, log_perm, high_lp], axis=2)
    fields_ext = jnp.concatenate([low_fields, fields, high_fields], axis=2)
    column = tile_rank * strip_width - rim + jnp.arange(strip_width + 2 * rim, dtype=jnp.int32)
    inside = ((column >= 0) & (column < strip_width * tile_count)).astype(jnp.float32)
    pressure, saturation, mobility = stencil(lp_ext, fields_ext, inside, rim)
    cell_count = layers * strip_width * strip_depth
    plane_rows = layers * strip_width
    cell_row = perf_cell // strip_depth
    cell_col = lax.rem(perf_cell, strip_depth)
    col_pick = (jnp.arange(strip_depth, dtype=jnp.int32)[:, None] == cell_col[None, :]).astype(
        jnp.float32
    )
    row_pick = jnp.arange(plane_rows, dtype=jnp.int32)[:, None] == cell_row[None, :]

    def pick_cells(values_in):
        by_col = jnp.dot(
            values_in.reshape(local_count * plane_rows, strip_depth), col_pick,
            precision=lax.Precision.HIGHEST, preferred_element_type=jnp.float32,
        ).reshape(local_count, plane_rows, -1)
        return jnp.sum(jnp.where(row_pick[None], by_col, 0.0), axis=1)

    perf_mob = pick_cells(mobility)
    perf_press = pick_cells(pressure)
    selector = (perf_well[:, None] == jnp.arange(well_count, dtype=jnp.int32)[None, :]).astype(
        jnp.float32
    )
    perf_bhp = jnp.dot(selector, well_press, precision=lax.Precision.HIGHEST)
    live_mask = (jnp.arange(perf_cell.shape[0], dtype=jnp.int32) < perf_count[0]).astype(
        jnp.float32
    )
    perf_terms = perf_mob * (perf_press - perf_bhp[None]) * live_mask[None]
    member_root = (members - 1) ** 0.5
    spread = jnp.sqrt(INFLATION * obs_var)
    member_count = lax.axis_size("member")
    contract_slots = (((0,), (1,)), ((), ()))
    pieces = lax.dot_general(
        selector, perf_terms, contract_slots, precision=lax.Precision.HIGHEST,
        preferred_element_type=jnp.float32,
    ).reshape(tile_count, well_share * local_count // 128, 128)
    full = rates_exchange(pieces, member_count)
    own_block = lax.dynamic_index_in_dim(full, tile_rank, 0, keepdims=False)
    well_rates = lax.dynamic_slice_in_dim(own_block, member_rank * local_count, local_count, 1).T
    rates_t = full.reshape(well_count, members)
    mean_rate = jnp.sum(rates_t, 1) / members
    scaled_t = (rates_t - mean_rate[:, None]) / (spread * member_root)[:, None]
    rates_own_t = lax.dynamic_slice_in_dim(rates_t, member_rank * local_count, local_count, 1)
    innov_own_t = (observed[:, None] - rates_own_t) / spread[:, None] + obs_noise.T
    contract_wells = (((0,), (0,)), ((), ()))
    gram_matrix = lax.dot_general(
        scaled_t, scaled_t, contract_wells, precision=lax.Precision.HIGHEST,
        preferred_element_type=jnp.float32,
    )
    cross_matrix = lax.dot_general(
        scaled_t, innov_own_t, contract_wells, precision=lax.Precision.HIGHEST,
        preferred_element_type=jnp.float32,
    )
    weights_low = solve_spd(gram_matrix, cross_matrix).astype(jnp.bfloat16)
    anomaly = (log_perm_after / member_root).astype(jnp.bfloat16).reshape(local_count, cell_count)
    anomaly_parts = [anomaly]
    for shift in range(1, member_count):
        pairs = [(i, (i + shift) % member_count) for i in range(member_count)]
        anomaly_parts.append(lax.ppermute(anomaly, "member", pairs))
    anomaly_all = jnp.concatenate(anomaly_parts, axis=0)
    own_cols = jnp.concatenate(
        [
            lax.dynamic_slice_in_dim(
                weights_low, lax.rem(member_rank - shift + member_count, member_count) * local_count,
                local_count, 0,
            )
            for shift in range(member_count)
        ],
        axis=0,
    )
    contract = (((0,), (0,)), ((), ()))
    update_sum = lax.dot_general(own_cols, anomaly_all, contract, preferred_element_type=jnp.float32)
    new_log_perm = log_perm + update_sum.reshape(log_perm.shape)
    return (new_log_perm, pressure, saturation, well_rates)


def solution(mesh):
    return jax.shard_map(
        per_device,
        mesh=mesh,
        in_specs=(
            P("member", None, "tile", None),
            P(None, "tile", None),
            P(None, "tile", None),
            P(None, "tile", None),
            P(None, "tile", None),
            P(),
            P("tile"),
            P("tile"),
            P("tile"),
            P(),
            P(),
            P("member", None),
        ),
        out_specs=(
            P("member", None, "tile", None),
            P("member", None, "tile", None),
            P("member", None, "tile", None),
            P("member", "tile"),
        ),
        check_vma=False,
    )
```

```python
import functools

import jax
import jax.numpy as jnp
from jax import lax
from jax.experimental import pallas as pl
from jax.experimental.pallas import tpu as pltpu
from jax.sharding import PartitionSpec as P

SWEEPS = 2


VERTICAL = 0.5
VISCOSITY_RATIO = 2.0
STEP_COEF = 0.1
INFLATION = 4.0


def extended_2(block, sides, width):
    for axis, dim in sides:
        count = lax.axis_size(axis)
        forward = [(i, i + 1) for i in range(count - 1)]
        backward = [(target, source) for source, target in forward]
        low = lax.ppermute(
            lax.slice_in_dim(block, block.shape[dim] - width, None, axis=dim), axis, forward
        )
        high = lax.ppermute(lax.slice_in_dim(block, 0, width, axis=dim), axis, backward)
        block = jnp.concatenate([low, block, high], axis=dim)
    return block


def harmonic(lower_val, upper_val):
    return 2.0 * lower_val * upper_val / (lower_val + upper_val)


def pad_face(values_in, along_dim, before):
    widths = [(0, 0)] * values_in.ndim
    widths[along_dim] = (1, 0) if before else (0, 1)
    return jnp.pad(values_in, widths)


def slide_by(values_in, along_dim, before):
    extent = values_in.shape[along_dim]
    if before:
        remain = lax.slice_in_dim(values_in, 0, extent - 1, axis=along_dim)
    else:
        remain = lax.slice_in_dim(values_in, 1, extent, axis=along_dim)
    return pad_face(remain, along_dim, before)


def face_terms(permeab, inside):
    face_x = (
        harmonic(permeab[:, :, :-1, :], permeab[:, :, 1:, :]) * (inside[:-1] * inside[1:])[:, None]
    )
    face_y = harmonic(permeab[:, :, :, :-1], permeab[:, :, :, 1:])
    face_z = VERTICAL * harmonic(permeab[:, :-1], permeab[:, 1:])
    return (face_x, face_y, face_z)


def neighbours(face_sets, values_in):
    flow_sum = 0.0
    weight_sum = 0.0
    for faces_dim, along_dim in zip(face_sets, (2, 3, 1)):
        lower = pad_face(faces_dim, along_dim, True)
        upper = pad_face(faces_dim, along_dim, False)
        flow_sum = (
            flow_sum
            + lower * slide_by(values_in, along_dim, True)
            + upper * slide_by(values_in, along_dim, False)
        )
        weight_sum = weight_sum + lower + upper
    return (flow_sum, weight_sum)


def jacobi(pressure, baseline, storage_term, face_sets):
    flow_sum, weight_sum = neighbours(face_sets, pressure)
    return (baseline + flow_sum) / (storage_term + weight_sum)


def water_frac(values_in):
    squared = values_in * values_in
    return squared / (squared + VISCOSITY_RATIO * (1.0 - values_in) * (1.0 - values_in))


def transport(pressure, saturation, face_sets):
    fraction = water_frac(saturation)
    change = 0.0
    for faces_dim, along_dim in zip(face_sets, (2, 3, 1)):
        extent = pressure.shape[along_dim]
        lower_press = lax.slice_in_dim(pressure, 0, extent - 1, axis=along_dim)
        upper_press = lax.slice_in_dim(pressure, 1, extent, axis=along_dim)
        lower_frac = lax.slice_in_dim(fraction, 0, extent - 1, axis=along_dim)
        upper_frac = lax.slice_in_dim(fraction, 1, extent, axis=along_dim)
        velocity = faces_dim * (lower_press - upper_press)
        carried = velocity * jnp.where(velocity > 0, lower_frac, upper_frac)
        change = change + pad_face(carried, along_dim, True) - pad_face(carried, along_dim, False)
    return saturation + STEP_COEF * change


def solve_spd(gram_matrix, cross_matrix):
    factor = lax.linalg.cholesky(
        gram_matrix + jnp.eye(gram_matrix.shape[0], dtype=jnp.float32), symmetrize_input=False
    )
    halfway = lax.linalg.triangular_solve(factor, cross_matrix, left_side=True, lower=True)
    return lax.linalg.triangular_solve(
        factor, halfway, left_side=True, lower=True, transpose_a=True
    )


def trim_rim(values_in, rim_cut):
    return values_in[:, :, rim_cut : values_in.shape[2] - rim_cut, :]


def exchange_kernel(member_count, part_ref, full_ref,
                    recv_a, own_blk, recv_m, send_a, recv_a_sem, send_m, recv_m_sem, send_t, recv_t_sem):
    tile_count = part_ref.shape[0]
    me_t = lax.axis_index("tile")
    me_m = lax.axis_index("member")
    mesh_ids = pl.DeviceIdType.MESH

    barrier = pltpu.get_barrier_semaphore()

    def greet_tile(k, carry):
        pl.semaphore_signal(
            barrier, 1, device_id=(lax.rem(me_t + k, tile_count), me_m), device_id_type=mesh_ids
        )
        return carry

    def greet_member(k, carry):
        pl.semaphore_signal(
            barrier, 1, device_id=(me_t, lax.rem(me_m + k, member_count)), device_id_type=mesh_ids
        )
        return carry

    lax.fori_loop(1, tile_count, greet_tile, 0)
    lax.fori_loop(1, member_count, greet_member, 0)
    pl.semaphore_wait(barrier, tile_count + member_count - 2)

    def copy_a(dst_t, src_t):
        return pltpu.make_async_remote_copy(
            src_ref=part_ref.at[dst_t], dst_ref=recv_a.at[src_t],
            send_sem=send_a.at[dst_t], recv_sem=recv_a_sem.at[src_t],
            device_id=(dst_t, me_m), device_id_type=mesh_ids,
        )

    def start_a(k, carry):
        copy_a(lax.rem(me_t + k, tile_count), me_t).start()
        return carry

    lax.fori_loop(1, tile_count, start_a, 0)

    def wait_a(k, acc):
        src_t = lax.rem(me_t + k, tile_count)
        copy_a(me_t, src_t).wait_recv()
        return acc + recv_a[src_t]

    acc = lax.fori_loop(1, tile_count, wait_a, part_ref[me_t])

    def wait_a_send(k, carry):
        copy_a(lax.rem(me_t + k, tile_count), me_t).wait_send()
        return carry

    lax.fori_loop(1, tile_count, wait_a_send, 0)

    groups = part_ref.shape[2] // member_count
    lane_ids = lax.broadcasted_iota(jnp.int32, acc.shape, 1)
    for q in range(member_count):
        moved = pltpu.roll(acc, lax.rem((me_m - q + member_count) * groups, part_ref.shape[2]), 1)
        own_blk[pl.ds(q, acc.shape[0], stride=member_count), :] = jnp.where(
            lane_ids // groups == me_m, moved, 0.0
        )
    acc = own_blk[...]

    def copy_m(dst_m, src_m):
        return pltpu.make_async_remote_copy(
            src_ref=own_blk, dst_ref=recv_m.at[src_m],
            send_sem=send_m.at[dst_m], recv_sem=recv_m_sem.at[src_m],
            device_id=(me_t, dst_m), device_id_type=mesh_ids,
        )

    def start_m(k, carry):
        copy_m(lax.rem(me_m + k, member_count), me_m).start()
        return carry

    lax.fori_loop(1, member_count, start_m, 0)

    def wait_m(k, total):
        src_m = lax.rem(me_m + k, member_count)
        copy_m(me_m, src_m).wait_recv()
        return total + recv_m[src_m]

    full_ref[me_t] = lax.fori_loop(1, member_count, wait_m, acc)

    def wait_m_send(k, carry):
        copy_m(lax.rem(me_m + k, member_count), me_m).wait_send()
        return carry

    lax.fori_loop(1, member_count, wait_m_send, 0)

    def copy_t(dst_t, src_t):
        return pltpu.make_async_remote_copy(
            src_ref=full_ref.at[src_t], dst_ref=full_ref.at[src_t],
            send_sem=send_t.at[dst_t], recv_sem=recv_t_sem.at[src_t],
            device_id=(dst_t, me_m), device_id_type=mesh_ids,
        )

    def start_t(k, carry):
        copy_t(lax.rem(me_t + k, tile_count), me_t).start()
        return carry

    lax.fori_loop(1, tile_count, start_t, 0)

    def wait_t(k, carry):
        copy_t(me_t, lax.rem(me_t + k, tile_count)).wait_recv()
        return carry

    lax.fori_loop(1, tile_count, wait_t, 0)

    def wait_t_send(k, carry):
        copy_t(lax.rem(me_t + k, tile_count), me_t).wait_send()
        return carry

    lax.fori_loop(1, tile_count, wait_t_send, 0)


def stencil_kernel(rim, lp_ref, fields_ref, inside_ref, press_ref, sat_ref, mob_ref):
    inside = inside_ref[...]
    permeab = jnp.exp(lp_ref[...])
    face_sets = face_terms(permeab, inside)
    press_ext = fields_ref[0]
    sat_ext = fields_ref[1]
    source_ext = fields_ref[2]
    storage_ext = fields_ref[3]
    baseline = (source_ext + storage_ext * press_ext)[None]
    storage_term = jnp.where(inside[None, :, None] > 0.0, storage_ext, 1.0)[None]
    pressure = jnp.broadcast_to(press_ext[None], permeab.shape)
    for sweep_idx in range(SWEEPS):
        pressure = jacobi(pressure, baseline, storage_term, face_sets)
    saturation = trim_rim(transport(pressure, sat_ext[None], face_sets), rim)
    press_ref[...] = trim_rim(pressure, rim)
    sat_ref[...] = saturation
    mob_ref[...] = trim_rim(permeab, rim) * water_frac(saturation)


def stencil(lp_ext, fields_ext, inside, rim):
    members, layers, rows, depth = lp_ext.shape
    block = 8
    out_rows = rows - 2 * rim
    out_spec = pl.BlockSpec((block, layers, out_rows, depth), lambda i: (i, 0, 0, 0))
    out_shape = jax.ShapeDtypeStruct((members, layers, out_rows, depth), jnp.float32)
    return pl.pallas_call(
        functools.partial(stencil_kernel, rim),
        grid=(members // block,),
        in_specs=[
            pl.BlockSpec((block, layers, rows, depth), lambda i: (i, 0, 0, 0)),
            pl.BlockSpec(fields_ext.shape, lambda i: (0, 0, 0, 0)),
            pl.BlockSpec(inside.shape, lambda i: (0,)),
        ],
        out_specs=[out_spec, out_spec, out_spec],
        out_shape=[out_shape, out_shape, out_shape],
    )(lp_ext, fields_ext, inside)


def halo_kernel(out_ref, in_ref, send_sem, recv_sem):
    tile_count = lax.axis_size("tile")
    me_t = lax.axis_index("tile")
    me_m = lax.axis_index("member")
    mesh_ids = pl.DeviceIdType.MESH
    left = lax.rem(me_t + tile_count - 1, tile_count)
    right = lax.rem(me_t + 1, tile_count)
    barrier = pltpu.get_barrier_semaphore()
    for peer in (left, right):
        pl.semaphore_signal(barrier, 1, device_id=(peer, me_m), device_id_type=mesh_ids)
    pl.semaphore_wait(barrier, 2)
    to_right = pltpu.make_async_remote_copy(
        src_ref=out_ref.at[1], dst_ref=in_ref.at[0], send_sem=send_sem.at[1],
        recv_sem=recv_sem.at[0], device_id=(right, me_m), device_id_type=mesh_ids,
    )
    to_left = pltpu.make_async_remote_copy(
        src_ref=out_ref.at[0], dst_ref=in_ref.at[1], send_sem=send_sem.at[0],
        recv_sem=recv_sem.at[1], device_id=(left, me_m), device_id_type=mesh_ids,
    )
    to_right.start()
    to_left.start()
    to_right.wait()
    to_left.wait()


def halo_exchange(outgoing):
    vmem = pl.BlockSpec(memory_space=pltpu.VMEM)
    return pl.pallas_call(
        halo_kernel,
        out_shape=jax.ShapeDtypeStruct(outgoing.shape, outgoing.dtype),
        in_specs=[vmem],
        out_specs=vmem,
        scratch_shapes=[pltpu.SemaphoreType.DMA((2,)), pltpu.SemaphoreType.DMA((2,))],
        compiler_params=pltpu.CompilerParams(collective_id=1, has_side_effects=True),
    )(outgoing)


def rates_exchange(pieces, member_count):
    tile_count, rows, lanes = pieces.shape
    vmem = pl.BlockSpec(memory_space=pltpu.VMEM)
    return pl.pallas_call(
        functools.partial(exchange_kernel, member_count),
        out_shape=jax.ShapeDtypeStruct((tile_count, rows * member_count, lanes), jnp.float32),
        in_specs=[vmem],
        out_specs=vmem,
        scratch_shapes=[
            pltpu.VMEM((tile_count, rows, lanes), jnp.float32),
            pltpu.VMEM((rows * member_count, lanes), jnp.float32),
            pltpu.VMEM((member_count, rows * member_count, lanes), jnp.float32),
            pltpu.SemaphoreType.DMA((tile_count,)),
            pltpu.SemaphoreType.DMA((tile_count,)),
            pltpu.SemaphoreType.DMA((member_count,)),
            pltpu.SemaphoreType.DMA((member_count,)),
            pltpu.SemaphoreType.DMA((tile_count,)),
            pltpu.SemaphoreType.DMA((tile_count,)),
        ],
        compiler_params=pltpu.CompilerParams(collective_id=0, has_side_effects=True),
    )(pieces)


def per_device(
    log_perm,
    start_pressure,
    start_sat,
    source,
    storage,
    well_press,
    perf_cell,
    perf_well,
    perf_count,
    observed,
    obs_var,
    obs_noise,
):
    local_count, layers, strip_width, strip_depth = log_perm.shape
    tile_count = lax.axis_size("tile")
    members = local_count * lax.axis_size("member")
    well_count = well_press.shape[0]
    well_share = well_count // tile_count
    tile_rank = lax.axis_index("tile")
    member_rank = lax.axis_index("member")
    rim = SWEEPS + 1
    fields = jnp.stack([start_pressure, start_sat, source, storage])
    halo_rows = local_count * layers * rim + fields.shape[0] * layers * rim

    def rim_rows(first):
        return jnp.concatenate(
            [
                lax.slice_in_dim(log_perm, first, first + rim, axis=2).reshape(-1, strip_depth),
                lax.slice_in_dim(fields, first, first + rim, axis=2).reshape(-1, strip_depth),
            ]
        )

    outgoing = jnp.stack([rim_rows(0), rim_rows(strip_width - rim)])
    incoming = halo_exchange(outgoing)
    incoming, log_perm_after = lax.optimization_barrier((incoming, log_perm))
    lp_count = local_count * layers * rim

    def unpack(side):
        lp_part = incoming[side, :lp_count].reshape(local_count, layers, rim, strip_depth)
        field_part = incoming[side, lp_count:].reshape(fields.shape[0], layers, rim, strip_depth)
        return lp_part, field_part

    low_lp, low_fields = unpack(0)
    high_lp, high_fields = unpack(1)
    lp_ext = jnp.concatenate([low_lp, log_perm, high_lp], axis=2)
    fields_ext = jnp.concatenate([low_fields, fields, high_fields], axis=2)
    column = tile_rank * strip_width - rim + jnp.arange(strip_width + 2 * rim, dtype=jnp.int32)
    inside = ((column >= 0) & (column < strip_width * tile_count)).astype(jnp.float32)
    pressure, saturation, mobility = stencil(lp_ext, fields_ext, inside, rim)
    cell_count = layers * strip_width * strip_depth
    plane_rows = layers * strip_width
    cell_row = perf_cell // strip_depth
    cell_col = lax.rem(perf_cell, strip_depth)
    col_pick = (jnp.arange(strip_depth, dtype=jnp.int32)[:, None] == cell_col[None, :]).astype(
        jnp.float32
    )
    row_pick = jnp.arange(plane_rows, dtype=jnp.int32)[:, None] == cell_row[None, :]

    def pick_cells(values_in):
        by_col = jnp.dot(
            values_in.reshape(local_count * plane_rows, strip_depth), col_pick,
            precision=lax.Precision.HIGHEST, preferred_element_type=jnp.float32,
        ).reshape(local_count, plane_rows, -1)
        return jnp.sum(jnp.where(row_pick[None], by_col, 0.0), axis=1)

    perf_mob = pick_cells(mobility)
    perf_press = pick_cells(pressure)
    selector = (perf_well[:, None] == jnp.arange(well_count, dtype=jnp.int32)[None, :]).astype(
        jnp.float32
    )
    perf_bhp = jnp.dot(selector, well_press, precision=lax.Precision.HIGHEST)
    live_mask = (jnp.arange(perf_cell.shape[0], dtype=jnp.int32) < perf_count[0]).astype(
        jnp.float32
    )
    perf_terms = perf_mob * (perf_press - perf_bhp[None]) * live_mask[None]
    member_root = (members - 1) ** 0.5
    spread = jnp.sqrt(INFLATION * obs_var)
    member_count = lax.axis_size("member")
    contract_slots = (((0,), (1,)), ((), ()))
    pieces = lax.dot_general(
        selector, perf_terms, contract_slots, precision=lax.Precision.HIGHEST,
        preferred_element_type=jnp.float32,
    ).reshape(tile_count, well_share * local_count // 128, 128)
    full = rates_exchange(pieces, member_count)
    own_block = lax.dynamic_index_in_dim(full, tile_rank, 0, keepdims=False)
    well_rates = lax.dynamic_slice_in_dim(own_block, member_rank * local_count, local_count, 1).T
    rates_t = full.reshape(well_count, members)
    mean_rate = jnp.sum(rates_t, 1) / members
    scaled_t = (rates_t - mean_rate[:, None]) / (spread * member_root)[:, None]
    rates_own_t = lax.dynamic_slice_in_dim(rates_t, member_rank * local_count, local_count, 1)
    innov_own_t = (observed[:, None] - rates_own_t) / spread[:, None] + obs_noise.T
    contract_wells = (((0,), (0,)), ((), ()))
    gram_matrix = lax.dot_general(
        scaled_t, scaled_t, contract_wells, precision=lax.Precision.HIGHEST,
        preferred_element_type=jnp.float32,
    )
    cross_matrix = lax.dot_general(
        scaled_t, innov_own_t, contract_wells, precision=lax.Precision.HIGHEST,
        preferred_element_type=jnp.float32,
    )
    weights_low = solve_spd(gram_matrix, cross_matrix).astype(jnp.bfloat16)
    anomaly = (log_perm_after / member_root).astype(jnp.bfloat16).reshape(local_count, cell_count)
    anomaly_parts = [anomaly]
    for shift in range(1, member_count):
        pairs = [(i, (i + shift) % member_count) for i in range(member_count)]
        anomaly_parts.append(lax.ppermute(anomaly, "member", pairs))
    anomaly_all = jnp.concatenate(anomaly_parts, axis=0)
    own_cols = jnp.concatenate(
        [
            lax.dynamic_slice_in_dim(
                weights_low, lax.rem(member_rank - shift + member_count, member_count) * local_count,
                local_count, 0,
            )
            for shift in range(member_count)
        ],
        axis=0,
    )
    contract = (((0,), (0,)), ((), ()))
    update_sum = lax.dot_general(own_cols, anomaly_all, contract, preferred_element_type=jnp.float32)
    new_log_perm = log_perm + update_sum.reshape(log_perm.shape)
    return (new_log_perm, pressure, saturation, well_rates)


def solution(mesh):
    return jax.shard_map(
        per_device,
        mesh=mesh,
        in_specs=(
            P("member", None, "tile", None),
            P(None, "tile", None),
            P(None, "tile", None),
            P(None, "tile", None),
            P(None, "tile", None),
            P(),
            P("tile"),
            P("tile"),
            P("tile"),
            P(),
            P(),
            P("member", None),
        ),
        out_specs=(
            P("member", None, "tile", None),
            P("member", None, "tile", None),
            P("member", None, "tile", None),
            P("member", "tile"),
        ),
        check_vma=False,
    )
```

```python
import functools

import jax
import jax.numpy as jnp
from jax import lax
from jax.experimental import pallas as pl
from jax.experimental.pallas import tpu as pltpu
from jax.sharding import PartitionSpec as P

SWEEPS = 2


VERTICAL = 0.5
VISCOSITY_RATIO = 2.0
STEP_COEF = 0.1
INFLATION = 4.0


def extended_2(block, sides, width):
    for axis, dim in sides:
        count = lax.axis_size(axis)
        forward = [(i, i + 1) for i in range(count - 1)]
        backward = [(target, source) for source, target in forward]
        low = lax.ppermute(
            lax.slice_in_dim(block, block.shape[dim] - width, None, axis=dim), axis, forward
        )
        high = lax.ppermute(lax.slice_in_dim(block, 0, width, axis=dim), axis, backward)
        block = jnp.concatenate([low, block, high], axis=dim)
    return block


def harmonic(lower_val, upper_val):
    return 2.0 * lower_val * upper_val / (lower_val + upper_val)


def pad_face(values_in, along_dim, before):
    widths = [(0, 0)] * values_in.ndim
    widths[along_dim] = (1, 0) if before else (0, 1)
    return jnp.pad(values_in, widths)


def slide_by(values_in, along_dim, before):
    extent = values_in.shape[along_dim]
    if before:
        remain = lax.slice_in_dim(values_in, 0, extent - 1, axis=along_dim)
    else:
        remain = lax.slice_in_dim(values_in, 1, extent, axis=along_dim)
    return pad_face(remain, along_dim, before)


def face_terms(permeab, inside):
    face_x = (
        harmonic(permeab[:, :, :-1, :], permeab[:, :, 1:, :]) * (inside[:-1] * inside[1:])[:, None]
    )
    face_y = harmonic(permeab[:, :, :, :-1], permeab[:, :, :, 1:])
    face_z = VERTICAL * harmonic(permeab[:, :-1], permeab[:, 1:])
    return (face_x, face_y, face_z)


def neighbours(face_sets, values_in):
    flow_sum = 0.0
    weight_sum = 0.0
    for faces_dim, along_dim in zip(face_sets, (2, 3, 1)):
        lower = pad_face(faces_dim, along_dim, True)
        upper = pad_face(faces_dim, along_dim, False)
        flow_sum = (
            flow_sum
            + lower * slide_by(values_in, along_dim, True)
            + upper * slide_by(values_in, along_dim, False)
        )
        weight_sum = weight_sum + lower + upper
    return (flow_sum, weight_sum)


def jacobi(pressure, baseline, storage_term, face_sets):
    flow_sum, weight_sum = neighbours(face_sets, pressure)
    return (baseline + flow_sum) / (storage_term + weight_sum)


def water_frac(values_in):
    squared = values_in * values_in
    return squared / (squared + VISCOSITY_RATIO * (1.0 - values_in) * (1.0 - values_in))


def transport(pressure, saturation, face_sets):
    fraction = water_frac(saturation)
    change = 0.0
    for faces_dim, along_dim in zip(face_sets, (2, 3, 1)):
        extent = pressure.shape[along_dim]
        lower_press = lax.slice_in_dim(pressure, 0, extent - 1, axis=along_dim)
        upper_press = lax.slice_in_dim(pressure, 1, extent, axis=along_dim)
        lower_frac = lax.slice_in_dim(fraction, 0, extent - 1, axis=along_dim)
        upper_frac = lax.slice_in_dim(fraction, 1, extent, axis=along_dim)
        velocity = faces_dim * (lower_press - upper_press)
        carried = velocity * jnp.where(velocity > 0, lower_frac, upper_frac)
        change = change + pad_face(carried, along_dim, True) - pad_face(carried, along_dim, False)
    return saturation + STEP_COEF * change


def solve_spd(gram_matrix, cross_matrix):
    factor = lax.linalg.cholesky(
        gram_matrix + jnp.eye(gram_matrix.shape[0], dtype=jnp.float32), symmetrize_input=False
    )
    halfway = lax.linalg.triangular_solve(factor, cross_matrix, left_side=True, lower=True)
    return lax.linalg.triangular_solve(
        factor, halfway, left_side=True, lower=True, transpose_a=True
    )


def trim_rim(values_in, rim_cut):
    return values_in[:, :, rim_cut : values_in.shape[2] - rim_cut, :]


def exchange_kernel(member_count, part_ref, full_ref,
                    recv_a, own_blk, recv_m, send_a, recv_a_sem, send_m, recv_m_sem, send_t, recv_t_sem):
    tile_count = part_ref.shape[0]
    me_t = lax.axis_index("tile")
    me_m = lax.axis_index("member")
    mesh_ids = pl.DeviceIdType.MESH

    barrier = pltpu.get_barrier_semaphore()

    def greet_tile(k, carry):
        pl.semaphore_signal(
            barrier, 1, device_id=(lax.rem(me_t + k, tile_count), me_m), device_id_type=mesh_ids
        )
        return carry

    def greet_member(k, carry):
        pl.semaphore_signal(
            barrier, 1, device_id=(me_t, lax.rem(me_m + k, member_count)), device_id_type=mesh_ids
        )
        return carry

    lax.fori_loop(1, tile_count, greet_tile, 0)
    lax.fori_loop(1, member_count, greet_member, 0)
    pl.semaphore_wait(barrier, tile_count + member_count - 2)

    def copy_a(dst_t, src_t):
        return pltpu.make_async_remote_copy(
            src_ref=part_ref.at[dst_t], dst_ref=recv_a.at[src_t],
            send_sem=send_a.at[dst_t], recv_sem=recv_a_sem.at[src_t],
            device_id=(dst_t, me_m), device_id_type=mesh_ids,
        )

    def start_a(k, carry):
        copy_a(lax.rem(me_t + k, tile_count), me_t).start()
        return carry

    lax.fori_loop(1, tile_count, start_a, 0)

    def wait_a(k, acc):
        src_t = lax.rem(me_t + k, tile_count)
        copy_a(me_t, src_t).wait_recv()
        return acc + recv_a[src_t]

    acc = lax.fori_loop(1, tile_count, wait_a, part_ref[me_t])

    def wait_a_send(k, carry):
        copy_a(lax.rem(me_t + k, tile_count), me_t).wait_send()
        return carry

    lax.fori_loop(1, tile_count, wait_a_send, 0)

    groups = part_ref.shape[2] // member_count
    lane_ids = lax.broadcasted_iota(jnp.int32, acc.shape, 1)
    for q in range(member_count):
        moved = pltpu.roll(acc, lax.rem((me_m - q + member_count) * groups, part_ref.shape[2]), 1)
        own_blk[pl.ds(q, acc.shape[0], stride=member_count), :] = jnp.where(
            lane_ids // groups == me_m, moved, 0.0
        )
    acc = own_blk[...]

    def copy_m(dst_m, src_m):
        return pltpu.make_async_remote_copy(
            src_ref=own_blk, dst_ref=recv_m.at[src_m],
            send_sem=send_m.at[dst_m], recv_sem=recv_m_sem.at[src_m],
            device_id=(me_t, dst_m), device_id_type=mesh_ids,
        )

    def start_m(k, carry):
        copy_m(lax.rem(me_m + k, member_count), me_m).start()
        return carry

    lax.fori_loop(1, member_count, start_m, 0)

    def wait_m(k, total):
        src_m = lax.rem(me_m + k, member_count)
        copy_m(me_m, src_m).wait_recv()
        return total + recv_m[src_m]

    full_ref[me_t] = lax.fori_loop(1, member_count, wait_m, acc)

    def wait_m_send(k, carry):
        copy_m(lax.rem(me_m + k, member_count), me_m).wait_send()
        return carry

    lax.fori_loop(1, member_count, wait_m_send, 0)

    def copy_t(dst_t, src_t):
        return pltpu.make_async_remote_copy(
            src_ref=full_ref.at[src_t], dst_ref=full_ref.at[src_t],
            send_sem=send_t.at[dst_t], recv_sem=recv_t_sem.at[src_t],
            device_id=(dst_t, me_m), device_id_type=mesh_ids,
        )

    def start_t(k, carry):
        copy_t(lax.rem(me_t + k, tile_count), me_t).start()
        return carry

    lax.fori_loop(1, tile_count, start_t, 0)

    def wait_t(k, carry):
        copy_t(me_t, lax.rem(me_t + k, tile_count)).wait_recv()
        return carry

    lax.fori_loop(1, tile_count, wait_t, 0)

    def wait_t_send(k, carry):
        copy_t(lax.rem(me_t + k, tile_count), me_t).wait_send()
        return carry

    lax.fori_loop(1, tile_count, wait_t_send, 0)


def stencil_kernel(rim, lp_ref, fields_ref, inside_ref, press_ref, sat_ref, mob_ref):
    inside = inside_ref[...]
    permeab = jnp.exp(lp_ref[...])
    face_sets = face_terms(permeab, inside)
    press_ext = fields_ref[0]
    sat_ext = fields_ref[1]
    source_ext = fields_ref[2]
    storage_ext = fields_ref[3]
    baseline = (source_ext + storage_ext * press_ext)[None]
    storage_term = jnp.where(inside[None, :, None] > 0.0, storage_ext, 1.0)[None]
    pressure = jnp.broadcast_to(press_ext[None], permeab.shape)
    for sweep_idx in range(SWEEPS):
        pressure = jacobi(pressure, baseline, storage_term, face_sets)
    saturation = trim_rim(transport(pressure, sat_ext[None], face_sets), rim)
    press_ref[...] = trim_rim(pressure, rim)
    sat_ref[...] = saturation
    mob_ref[...] = trim_rim(permeab, rim) * water_frac(saturation)


def stencil(lp_ext, fields_ext, inside, rim):
    members, layers, rows, depth = lp_ext.shape
    block = 4
    out_rows = rows - 2 * rim
    out_spec = pl.BlockSpec((block, layers, out_rows, depth), lambda i: (i, 0, 0, 0))
    out_shape = jax.ShapeDtypeStruct((members, layers, out_rows, depth), jnp.float32)
    return pl.pallas_call(
        functools.partial(stencil_kernel, rim),
        grid=(members // block,),
        in_specs=[
            pl.BlockSpec((block, layers, rows, depth), lambda i: (i, 0, 0, 0)),
            pl.BlockSpec(fields_ext.shape, lambda i: (0, 0, 0, 0)),
            pl.BlockSpec(inside.shape, lambda i: (0,)),
        ],
        out_specs=[out_spec, out_spec, out_spec],
        out_shape=[out_shape, out_shape, out_shape],
    )(lp_ext, fields_ext, inside)


def halo_kernel(out_ref, in_ref, send_sem, recv_sem):
    tile_count = lax.axis_size("tile")
    me_t = lax.axis_index("tile")
    me_m = lax.axis_index("member")
    mesh_ids = pl.DeviceIdType.MESH
    left = lax.rem(me_t + tile_count - 1, tile_count)
    right = lax.rem(me_t + 1, tile_count)
    barrier = pltpu.get_barrier_semaphore()
    for peer in (left, right):
        pl.semaphore_signal(barrier, 1, device_id=(peer, me_m), device_id_type=mesh_ids)
    pl.semaphore_wait(barrier, 2)
    to_right = pltpu.make_async_remote_copy(
        src_ref=out_ref.at[1], dst_ref=in_ref.at[0], send_sem=send_sem.at[1],
        recv_sem=recv_sem.at[0], device_id=(right, me_m), device_id_type=mesh_ids,
    )
    to_left = pltpu.make_async_remote_copy(
        src_ref=out_ref.at[0], dst_ref=in_ref.at[1], send_sem=send_sem.at[0],
        recv_sem=recv_sem.at[1], device_id=(left, me_m), device_id_type=mesh_ids,
    )
    to_right.start()
    to_left.start()
    to_right.wait()
    to_left.wait()


def halo_exchange(outgoing):
    vmem = pl.BlockSpec(memory_space=pltpu.VMEM)
    return pl.pallas_call(
        halo_kernel,
        out_shape=jax.ShapeDtypeStruct(outgoing.shape, outgoing.dtype),
        in_specs=[vmem],
        out_specs=vmem,
        scratch_shapes=[pltpu.SemaphoreType.DMA((2,)), pltpu.SemaphoreType.DMA((2,))],
        compiler_params=pltpu.CompilerParams(collective_id=1, has_side_effects=True),
    )(outgoing)


def rates_exchange(pieces, member_count):
    tile_count, rows, lanes = pieces.shape
    vmem = pl.BlockSpec(memory_space=pltpu.VMEM)
    return pl.pallas_call(
        functools.partial(exchange_kernel, member_count),
        out_shape=jax.ShapeDtypeStruct((tile_count, rows * member_count, lanes), jnp.float32),
        in_specs=[vmem],
        out_specs=vmem,
        scratch_shapes=[
            pltpu.VMEM((tile_count, rows, lanes), jnp.float32),
            pltpu.VMEM((rows * member_count, lanes), jnp.float32),
            pltpu.VMEM((member_count, rows * member_count, lanes), jnp.float32),
            pltpu.SemaphoreType.DMA((tile_count,)),
            pltpu.SemaphoreType.DMA((tile_count,)),
            pltpu.SemaphoreType.DMA((member_count,)),
            pltpu.SemaphoreType.DMA((member_count,)),
            pltpu.SemaphoreType.DMA((tile_count,)),
            pltpu.SemaphoreType.DMA((tile_count,)),
        ],
        compiler_params=pltpu.CompilerParams(collective_id=0, has_side_effects=True),
    )(pieces)


def per_device(
    log_perm,
    start_pressure,
    start_sat,
    source,
    storage,
    well_press,
    perf_cell,
    perf_well,
    perf_count,
    observed,
    obs_var,
    obs_noise,
):
    local_count, layers, strip_width, strip_depth = log_perm.shape
    tile_count = lax.axis_size("tile")
    members = local_count * lax.axis_size("member")
    well_count = well_press.shape[0]
    well_share = well_count // tile_count
    tile_rank = lax.axis_index("tile")
    member_rank = lax.axis_index("member")
    rim = SWEEPS + 1
    fields = jnp.stack([start_pressure, start_sat, source, storage])
    halo_rows = local_count * layers * rim + fields.shape[0] * layers * rim

    def rim_rows(first):
        return jnp.concatenate(
            [
                lax.slice_in_dim(log_perm, first, first + rim, axis=2).reshape(-1, strip_depth),
                lax.slice_in_dim(fields, first, first + rim, axis=2).reshape(-1, strip_depth),
            ]
        )

    outgoing = jnp.stack([rim_rows(0), rim_rows(strip_width - rim)])
    incoming = halo_exchange(outgoing)
    incoming, log_perm_after = lax.optimization_barrier((incoming, log_perm))
    lp_count = local_count * layers * rim

    def unpack(side):
        lp_part = incoming[side, :lp_count].reshape(local_count, layers, rim, strip_depth)
        field_part = incoming[side, lp_count:].reshape(fields.shape[0], layers, rim, strip_depth)
        return lp_part, field_part

    low_lp, low_fields = unpack(0)
    high_lp, high_fields = unpack(1)
    lp_ext = jnp.concatenate([low_lp, log_perm, high_lp], axis=2)
    fields_ext = jnp.concatenate([low_fields, fields, high_fields], axis=2)
    column = tile_rank * strip_width - rim + jnp.arange(strip_width + 2 * rim, dtype=jnp.int32)
    inside = ((column >= 0) & (column < strip_width * tile_count)).astype(jnp.float32)
    pressure, saturation, mobility = stencil(lp_ext, fields_ext, inside, rim)
    cell_count = layers * strip_width * strip_depth
    plane_rows = layers * strip_width
    cell_row = perf_cell // strip_depth
    cell_col = lax.rem(perf_cell, strip_depth)
    col_pick = (jnp.arange(strip_depth, dtype=jnp.int32)[:, None] == cell_col[None, :]).astype(
        jnp.float32
    )
    row_pick = jnp.arange(plane_rows, dtype=jnp.int32)[:, None] == cell_row[None, :]

    col_pick_low = col_pick.astype(jnp.bfloat16)

    def pick_cells(values_in):
        flat = values_in.reshape(local_count * plane_rows, strip_depth)
        high = lax.reduce_precision(flat, exponent_bits=8, mantissa_bits=7)
        rest = flat - high
        middle = lax.reduce_precision(rest, exponent_bits=8, mantissa_bits=7)
        low = rest - middle
        split = jnp.concatenate([high, middle, low]).astype(jnp.bfloat16)
        parts = jnp.dot(split, col_pick_low, preferred_element_type=jnp.float32)
        parts = parts.reshape(3, local_count, plane_rows, -1)
        by_col = parts[0] + parts[1] + parts[2]
        return jnp.sum(jnp.where(row_pick[None], by_col, 0.0), axis=1)

    perf_mob = pick_cells(mobility)
    perf_press = pick_cells(pressure)
    selector = (perf_well[:, None] == jnp.arange(well_count, dtype=jnp.int32)[None, :]).astype(
        jnp.float32
    )
    perf_bhp = jnp.dot(selector, well_press, precision=lax.Precision.HIGHEST)
    live_mask = (jnp.arange(perf_cell.shape[0], dtype=jnp.int32) < perf_count[0]).astype(
        jnp.float32
    )
    perf_terms = perf_mob * (perf_press - perf_bhp[None]) * live_mask[None]
    member_root = (members - 1) ** 0.5
    spread = jnp.sqrt(INFLATION * obs_var)
    member_count = lax.axis_size("member")
    contract_slots = (((0,), (1,)), ((), ()))
    pieces = lax.dot_general(
        selector, perf_terms, contract_slots, precision=lax.Precision.HIGHEST,
        preferred_element_type=jnp.float32,
    ).reshape(tile_count, well_share * local_count // 128, 128)
    full = rates_exchange(pieces, member_count)
    own_block = lax.dynamic_index_in_dim(full, tile_rank, 0, keepdims=False)
    well_rates = lax.dynamic_slice_in_dim(own_block, member_rank * local_count, local_count, 1).T
    rates_t = full.reshape(well_count, members)
    mean_rate = jnp.sum(rates_t, 1) / members
    scaled_t = (rates_t - mean_rate[:, None]) / (spread * member_root)[:, None]
    rates_own_t = lax.dynamic_slice_in_dim(rates_t, member_rank * local_count, local_count, 1)
    innov_own_t = (observed[:, None] - rates_own_t) / spread[:, None] + obs_noise.T
    contract_wells = (((0,), (0,)), ((), ()))
    gram_matrix = lax.dot_general(
        scaled_t, scaled_t, contract_wells, precision=lax.Precision.HIGHEST,
        preferred_element_type=jnp.float32,
    )
    cross_matrix = lax.dot_general(
        scaled_t, innov_own_t, contract_wells, precision=lax.Precision.HIGHEST,
        preferred_element_type=jnp.float32,
    )
    weights_low = solve_spd(gram_matrix, cross_matrix).astype(jnp.bfloat16)
    anomaly = (log_perm_after / member_root).astype(jnp.bfloat16).reshape(local_count, cell_count)
    anomaly_parts = [anomaly]
    for shift in range(1, member_count):
        pairs = [(i, (i + shift) % member_count) for i in range(member_count)]
        anomaly_parts.append(lax.ppermute(anomaly, "member", pairs))
    anomaly_all = jnp.concatenate(anomaly_parts, axis=0)
    own_cols = jnp.concatenate(
        [
            lax.dynamic_slice_in_dim(
                weights_low, lax.rem(member_rank - shift + member_count, member_count) * local_count,
                local_count, 0,
            )
            for shift in range(member_count)
        ],
        axis=0,
    )
    contract = (((0,), (0,)), ((), ()))
    update_sum = lax.dot_general(own_cols, anomaly_all, contract, preferred_element_type=jnp.float32)
    new_log_perm = log_perm + update_sum.reshape(log_perm.shape)
    return (new_log_perm, pressure, saturation, well_rates)


def solution(mesh):
    return jax.shard_map(
        per_device,
        mesh=mesh,
        in_specs=(
            P("member", None, "tile", None),
            P(None, "tile", None),
            P(None, "tile", None),
            P(None, "tile", None),
            P(None, "tile", None),
            P(),
            P("tile"),
            P("tile"),
            P("tile"),
            P(),
            P(),
            P("member", None),
        ),
        out_specs=(
            P("member", None, "tile", None),
            P("member", None, "tile", None),
            P("member", None, "tile", None),
            P("member", "tile"),
        ),
        check_vma=False,
    )
```

```python
import functools

import jax
import jax.numpy as jnp
from jax import lax
from jax.experimental import pallas as pl
from jax.experimental.pallas import tpu as pltpu
from jax.sharding import PartitionSpec as P

SWEEPS = 2


VERTICAL = 0.5
VISCOSITY_RATIO = 2.0
STEP_COEF = 0.1
INFLATION = 4.0


def extended_2(block, sides, width):
    for axis, dim in sides:
        count = lax.axis_size(axis)
        forward = [(i, i + 1) for i in range(count - 1)]
        backward = [(target, source) for source, target in forward]
        low = lax.ppermute(
            lax.slice_in_dim(block, block.shape[dim] - width, None, axis=dim), axis, forward
        )
        high = lax.ppermute(lax.slice_in_dim(block, 0, width, axis=dim), axis, backward)
        block = jnp.concatenate([low, block, high], axis=dim)
    return block


def harmonic(lower_val, upper_val):
    return 2.0 * lower_val * upper_val / (lower_val + upper_val)


def pad_face(values_in, along_dim, before):
    widths = [(0, 0)] * values_in.ndim
    widths[along_dim] = (1, 0) if before else (0, 1)
    return jnp.pad(values_in, widths)


def slide_by(values_in, along_dim, before):
    extent = values_in.shape[along_dim]
    if before:
        remain = lax.slice_in_dim(values_in, 0, extent - 1, axis=along_dim)
    else:
        remain = lax.slice_in_dim(values_in, 1, extent, axis=along_dim)
    return pad_face(remain, along_dim, before)


def face_terms(permeab, inside):
    face_x = (
        harmonic(permeab[:, :, :-1, :], permeab[:, :, 1:, :]) * (inside[:-1] * inside[1:])[:, None]
    )
    face_y = harmonic(permeab[:, :, :, :-1], permeab[:, :, :, 1:])
    face_z = VERTICAL * harmonic(permeab[:, :-1], permeab[:, 1:])
    return (face_x, face_y, face_z)


def neighbours(face_sets, values_in):
    flow_sum = 0.0
    weight_sum = 0.0
    for faces_dim, along_dim in zip(face_sets, (2, 3, 1)):
        lower = pad_face(faces_dim, along_dim, True)
        upper = pad_face(faces_dim, along_dim, False)
        flow_sum = (
            flow_sum
            + lower * slide_by(values_in, along_dim, True)
            + upper * slide_by(values_in, along_dim, False)
        )
        weight_sum = weight_sum + lower + upper
    return (flow_sum, weight_sum)


def jacobi(pressure, baseline, storage_term, face_sets):
    flow_sum, weight_sum = neighbours(face_sets, pressure)
    return (baseline + flow_sum) / (storage_term + weight_sum)


def water_frac(values_in):
    squared = values_in * values_in
    return squared / (squared + VISCOSITY_RATIO * (1.0 - values_in) * (1.0 - values_in))


def transport(pressure, saturation, face_sets):
    fraction = water_frac(saturation)
    change = 0.0
    for faces_dim, along_dim in zip(face_sets, (2, 3, 1)):
        extent = pressure.shape[along_dim]
        lower_press = lax.slice_in_dim(pressure, 0, extent - 1, axis=along_dim)
        upper_press = lax.slice_in_dim(pressure, 1, extent, axis=along_dim)
        lower_frac = lax.slice_in_dim(fraction, 0, extent - 1, axis=along_dim)
        upper_frac = lax.slice_in_dim(fraction, 1, extent, axis=along_dim)
        velocity = faces_dim * (lower_press - upper_press)
        carried = velocity * jnp.where(velocity > 0, lower_frac, upper_frac)
        change = change + pad_face(carried, along_dim, True) - pad_face(carried, along_dim, False)
    return saturation + STEP_COEF * change


def solve_spd(gram_matrix, cross_matrix):
    factor = lax.linalg.cholesky(
        gram_matrix + jnp.eye(gram_matrix.shape[0], dtype=jnp.float32), symmetrize_input=False
    )
    halfway = lax.linalg.triangular_solve(factor, cross_matrix, left_side=True, lower=True)
    return lax.linalg.triangular_solve(
        factor, halfway, left_side=True, lower=True, transpose_a=True
    )


def trim_rim(values_in, rim_cut):
    return values_in[:, :, rim_cut : values_in.shape[2] - rim_cut, :]


def exchange_kernel(member_count, part_ref, full_ref,
                    recv_a, own_blk, recv_m, send_a, recv_a_sem, send_m, recv_m_sem, send_t, recv_t_sem):
    tile_count = part_ref.shape[0]
    me_t = lax.axis_index("tile")
    me_m = lax.axis_index("member")
    mesh_ids = pl.DeviceIdType.MESH

    barrier = pltpu.get_barrier_semaphore()

    def greet_tile(k, carry):
        pl.semaphore_signal(
            barrier, 1, device_id=(lax.rem(me_t + k, tile_count), me_m), device_id_type=mesh_ids
        )
        return carry

    def greet_member(k, carry):
        pl.semaphore_signal(
            barrier, 1, device_id=(me_t, lax.rem(me_m + k, member_count)), device_id_type=mesh_ids
        )
        return carry

    lax.fori_loop(1, tile_count, greet_tile, 0)
    lax.fori_loop(1, member_count, greet_member, 0)
    pl.semaphore_wait(barrier, tile_count + member_count - 2)

    def copy_a(dst_t, src_t):
        return pltpu.make_async_remote_copy(
            src_ref=part_ref.at[dst_t], dst_ref=recv_a.at[src_t],
            send_sem=send_a.at[dst_t], recv_sem=recv_a_sem.at[src_t],
            device_id=(dst_t, me_m), device_id_type=mesh_ids,
        )

    def start_a(k, carry):
        copy_a(lax.rem(me_t + k, tile_count), me_t).start()
        return carry

    lax.fori_loop(1, tile_count, start_a, 0)

    def wait_a(k, acc):
        src_t = lax.rem(me_t + k, tile_count)
        copy_a(me_t, src_t).wait_recv()
        return acc + recv_a[src_t]

    acc = lax.fori_loop(1, tile_count, wait_a, part_ref[me_t])

    def wait_a_send(k, carry):
        copy_a(lax.rem(me_t + k, tile_count), me_t).wait_send()
        return carry

    lax.fori_loop(1, tile_count, wait_a_send, 0)

    groups = part_ref.shape[2] // member_count
    lane_ids = lax.broadcasted_iota(jnp.int32, acc.shape, 1)
    for q in range(member_count):
        moved = pltpu.roll(acc, lax.rem((me_m - q + member_count) * groups, part_ref.shape[2]), 1)
        own_blk[pl.ds(q, acc.shape[0], stride=member_count), :] = jnp.where(
            lane_ids // groups == me_m, moved, 0.0
        )
    acc = own_blk[...]

    def copy_m(dst_m, src_m):
        return pltpu.make_async_remote_copy(
            src_ref=own_blk, dst_ref=recv_m.at[src_m],
            send_sem=send_m.at[dst_m], recv_sem=recv_m_sem.at[src_m],
            device_id=(me_t, dst_m), device_id_type=mesh_ids,
        )

    def start_m(k, carry):
        copy_m(lax.rem(me_m + k, member_count), me_m).start()
        return carry

    lax.fori_loop(1, member_count, start_m, 0)

    def wait_m(k, total):
        src_m = lax.rem(me_m + k, member_count)
        copy_m(me_m, src_m).wait_recv()
        return total + recv_m[src_m]

    full_ref[me_t] = lax.fori_loop(1, member_count, wait_m, acc)

    def wait_m_send(k, carry):
        copy_m(lax.rem(me_m + k, member_count), me_m).wait_send()
        return carry

    lax.fori_loop(1, member_count, wait_m_send, 0)

    def copy_t(dst_t, src_t):
        return pltpu.make_async_remote_copy(
            src_ref=full_ref.at[src_t], dst_ref=full_ref.at[src_t],
            send_sem=send_t.at[dst_t], recv_sem=recv_t_sem.at[src_t],
            device_id=(dst_t, me_m), device_id_type=mesh_ids,
        )

    def start_t(k, carry):
        copy_t(lax.rem(me_t + k, tile_count), me_t).start()
        return carry

    lax.fori_loop(1, tile_count, start_t, 0)

    def wait_t(k, carry):
        copy_t(me_t, lax.rem(me_t + k, tile_count)).wait_recv()
        return carry

    lax.fori_loop(1, tile_count, wait_t, 0)

    def wait_t_send(k, carry):
        copy_t(lax.rem(me_t + k, tile_count), me_t).wait_send()
        return carry

    lax.fori_loop(1, tile_count, wait_t_send, 0)


def stencil_kernel(rim, lp_low, lp_mid, lp_high, f_low, f_mid, f_high, inside_ref,
                   press_ref, sat_ref, mob_ref):
    inside = inside_ref[...]
    permeab = jnp.exp(jnp.concatenate([lp_low[...], lp_mid[...], lp_high[...]], axis=2))
    face_sets = face_terms(permeab, inside)
    fields = jnp.concatenate([f_low[...], f_mid[...], f_high[...]], axis=2)
    press_ext = fields[0]
    sat_ext = fields[1]
    source_ext = fields[2]
    storage_ext = fields[3]
    baseline = (source_ext + storage_ext * press_ext)[None]
    storage_term = jnp.where(inside[None, :, None] > 0.0, storage_ext, 1.0)[None]
    pressure = jnp.broadcast_to(press_ext[None], permeab.shape)
    for sweep_idx in range(SWEEPS):
        pressure = jacobi(pressure, baseline, storage_term, face_sets)
    saturation = trim_rim(transport(pressure, sat_ext[None], face_sets), rim)
    press_ref[...] = trim_rim(pressure, rim)
    sat_ref[...] = saturation
    mob_ref[...] = trim_rim(permeab, rim) * water_frac(saturation)


def stencil(lp_parts, field_parts, inside, rim):
    members, layers, out_rows, depth = lp_parts[1].shape
    block = 4

    def member_block(part):
        return pl.BlockSpec((block,) + part.shape[1:], lambda i: (i, 0, 0, 0))

    def whole(part):
        return pl.BlockSpec(part.shape, lambda i: (0, 0, 0, 0))

    out_spec = pl.BlockSpec((block, layers, out_rows, depth), lambda i: (i, 0, 0, 0))
    out_shape = jax.ShapeDtypeStruct((members, layers, out_rows, depth), jnp.float32)
    return pl.pallas_call(
        functools.partial(stencil_kernel, rim),
        grid=(members // block,),
        in_specs=[member_block(p) for p in lp_parts]
        + [whole(p) for p in field_parts]
        + [pl.BlockSpec(inside.shape, lambda i: (0,))],
        out_specs=[out_spec, out_spec, out_spec],
        out_shape=[out_shape, out_shape, out_shape],
    )(*lp_parts, *field_parts, inside)


def halo_kernel(out_ref, in_ref, send_sem, recv_sem):
    tile_count = lax.axis_size("tile")
    me_t = lax.axis_index("tile")
    me_m = lax.axis_index("member")
    mesh_ids = pl.DeviceIdType.MESH
    left = lax.rem(me_t + tile_count - 1, tile_count)
    right = lax.rem(me_t + 1, tile_count)
    barrier = pltpu.get_barrier_semaphore()
    for peer in (left, right):
        pl.semaphore_signal(barrier, 1, device_id=(peer, me_m), device_id_type=mesh_ids)
    pl.semaphore_wait(barrier, 2)
    to_right = pltpu.make_async_remote_copy(
        src_ref=out_ref.at[1], dst_ref=in_ref.at[0], send_sem=send_sem.at[1],
        recv_sem=recv_sem.at[0], device_id=(right, me_m), device_id_type=mesh_ids,
    )
    to_left = pltpu.make_async_remote_copy(
        src_ref=out_ref.at[0], dst_ref=in_ref.at[1], send_sem=send_sem.at[0],
        recv_sem=recv_sem.at[1], device_id=(left, me_m), device_id_type=mesh_ids,
    )
    to_right.start()
    to_left.start()
    to_right.wait()
    to_left.wait()


def halo_exchange(outgoing):
    vmem = pl.BlockSpec(memory_space=pltpu.VMEM)
    return pl.pallas_call(
        halo_kernel,
        out_shape=jax.ShapeDtypeStruct(outgoing.shape, outgoing.dtype),
        in_specs=[vmem],
        out_specs=vmem,
        scratch_shapes=[pltpu.SemaphoreType.DMA((2,)), pltpu.SemaphoreType.DMA((2,))],
        compiler_params=pltpu.CompilerParams(collective_id=1, has_side_effects=True),
    )(outgoing)


def rates_exchange(pieces, member_count):
    tile_count, rows, lanes = pieces.shape
    vmem = pl.BlockSpec(memory_space=pltpu.VMEM)
    return pl.pallas_call(
        functools.partial(exchange_kernel, member_count),
        out_shape=jax.ShapeDtypeStruct((tile_count, rows * member_count, lanes), jnp.float32),
        in_specs=[vmem],
        out_specs=vmem,
        scratch_shapes=[
            pltpu.VMEM((tile_count, rows, lanes), jnp.float32),
            pltpu.VMEM((rows * member_count, lanes), jnp.float32),
            pltpu.VMEM((member_count, rows * member_count, lanes), jnp.float32),
            pltpu.SemaphoreType.DMA((tile_count,)),
            pltpu.SemaphoreType.DMA((tile_count,)),
            pltpu.SemaphoreType.DMA((member_count,)),
            pltpu.SemaphoreType.DMA((member_count,)),
            pltpu.SemaphoreType.DMA((tile_count,)),
            pltpu.SemaphoreType.DMA((tile_count,)),
        ],
        compiler_params=pltpu.CompilerParams(collective_id=0, has_side_effects=True),
    )(pieces)


def per_device(
    log_perm,
    start_pressure,
    start_sat,
    source,
    storage,
    well_press,
    perf_cell,
    perf_well,
    perf_count,
    observed,
    obs_var,
    obs_noise,
):
    local_count, layers, strip_width, strip_depth = log_perm.shape
    tile_count = lax.axis_size("tile")
    members = local_count * lax.axis_size("member")
    well_count = well_press.shape[0]
    well_share = well_count // tile_count
    tile_rank = lax.axis_index("tile")
    member_rank = lax.axis_index("member")
    rim = SWEEPS + 1
    fields = jnp.stack([start_pressure, start_sat, source, storage])
    halo_rows = local_count * layers * rim + fields.shape[0] * layers * rim

    def rim_rows(first):
        return jnp.concatenate(
            [
                lax.slice_in_dim(log_perm, first, first + rim, axis=2).reshape(-1, strip_depth),
                lax.slice_in_dim(fields, first, first + rim, axis=2).reshape(-1, strip_depth),
            ]
        )

    outgoing = jnp.stack([rim_rows(0), rim_rows(strip_width - rim)])
    incoming = halo_exchange(outgoing)
    incoming, log_perm_after = lax.optimization_barrier((incoming, log_perm))
    lp_count = local_count * layers * rim

    def unpack(side):
        lp_part = incoming[side, :lp_count].reshape(local_count, layers, rim, strip_depth)
        field_part = incoming[side, lp_count:].reshape(fields.shape[0], layers, rim, strip_depth)
        return lp_part, field_part

    low_lp, low_fields = unpack(0)
    high_lp, high_fields = unpack(1)
    column = tile_rank * strip_width - rim + jnp.arange(strip_width + 2 * rim, dtype=jnp.int32)
    inside = ((column >= 0) & (column < strip_width * tile_count)).astype(jnp.float32)
    pressure, saturation, mobility = stencil(
        (low_lp, log_perm, high_lp), (low_fields, fields, high_fields), inside, rim
    )
    cell_count = layers * strip_width * strip_depth
    plane_rows = layers * strip_width
    cell_row = perf_cell // strip_depth
    cell_col = lax.rem(perf_cell, strip_depth)
    col_pick = (jnp.arange(strip_depth, dtype=jnp.int32)[:, None] == cell_col[None, :]).astype(
        jnp.float32
    )
    row_pick = jnp.arange(plane_rows, dtype=jnp.int32)[:, None] == cell_row[None, :]

    def pick_cells(values_in):
        by_col = jnp.dot(
            values_in.reshape(local_count * plane_rows, strip_depth), col_pick,
            precision=lax.Precision.HIGHEST, preferred_element_type=jnp.float32,
        ).reshape(local_count, plane_rows, -1)
        return jnp.sum(jnp.where(row_pick[None], by_col, 0.0), axis=1)

    perf_mob = pick_cells(mobility)
    perf_press = pick_cells(pressure)
    selector = (perf_well[:, None] == jnp.arange(well_count, dtype=jnp.int32)[None, :]).astype(
        jnp.float32
    )
    perf_bhp = jnp.dot(selector, well_press, precision=lax.Precision.HIGHEST)
    live_mask = (jnp.arange(perf_cell.shape[0], dtype=jnp.int32) < perf_count[0]).astype(
        jnp.float32
    )
    perf_terms = perf_mob * (perf_press - perf_bhp[None]) * live_mask[None]
    member_root = (members - 1) ** 0.5
    spread = jnp.sqrt(INFLATION * obs_var)
    member_count = lax.axis_size("member")
    contract_slots = (((0,), (1,)), ((), ()))
    pieces = lax.dot_general(
        selector, perf_terms, contract_slots, precision=lax.Precision.HIGHEST,
        preferred_element_type=jnp.float32,
    ).reshape(tile_count, well_share * local_count // 128, 128)
    full = rates_exchange(pieces, member_count)
    own_block = lax.dynamic_index_in_dim(full, tile_rank, 0, keepdims=False)
    well_rates = lax.dynamic_slice_in_dim(own_block, member_rank * local_count, local_count, 1).T
    rates_t = full.reshape(well_count, members)
    mean_rate = jnp.sum(rates_t, 1) / members
    scaled_t = (rates_t - mean_rate[:, None]) / (spread * member_root)[:, None]
    rates_own_t = lax.dynamic_slice_in_dim(rates_t, member_rank * local_count, local_count, 1)
    innov_own_t = (observed[:, None] - rates_own_t) / spread[:, None] + obs_noise.T
    contract_wells = (((0,), (0,)), ((), ()))
    gram_matrix = lax.dot_general(
        scaled_t, scaled_t, contract_wells, precision=lax.Precision.HIGHEST,
        preferred_element_type=jnp.float32,
    )
    cross_matrix = lax.dot_general(
        scaled_t, innov_own_t, contract_wells, precision=lax.Precision.HIGHEST,
        preferred_element_type=jnp.float32,
    )
    weights_low = solve_spd(gram_matrix, cross_matrix).astype(jnp.bfloat16)
    anomaly = (log_perm_after / member_root).astype(jnp.bfloat16).reshape(local_count, cell_count)
    anomaly_parts = [anomaly]
    for shift in range(1, member_count):
        pairs = [(i, (i + shift) % member_count) for i in range(member_count)]
        anomaly_parts.append(lax.ppermute(anomaly, "member", pairs))
    anomaly_all = jnp.concatenate(anomaly_parts, axis=0)
    own_cols = jnp.concatenate(
        [
            lax.dynamic_slice_in_dim(
                weights_low, lax.rem(member_rank - shift + member_count, member_count) * local_count,
                local_count, 0,
            )
            for shift in range(member_count)
        ],
        axis=0,
    )
    contract = (((0,), (0,)), ((), ()))
    update_sum = lax.dot_general(own_cols, anomaly_all, contract, preferred_element_type=jnp.float32)
    new_log_perm = log_perm + update_sum.reshape(log_perm.shape)
    return (new_log_perm, pressure, saturation, well_rates)


def solution(mesh):
    return jax.shard_map(
        per_device,
        mesh=mesh,
        in_specs=(
            P("member", None, "tile", None),
            P(None, "tile", None),
            P(None, "tile", None),
            P(None, "tile", None),
            P(None, "tile", None),
            P(),
            P("tile"),
            P("tile"),
            P("tile"),
            P(),
            P(),
            P("member", None),
        ),
        out_specs=(
            P("member", None, "tile", None),
            P("member", None, "tile", None),
            P("member", None, "tile", None),
            P("member", "tile"),
        ),
        check_vma=False,
    )
```

```python
import functools

import jax
import jax.numpy as jnp
from jax import lax
from jax.experimental import pallas as pl
from jax.experimental.pallas import tpu as pltpu
from jax.sharding import PartitionSpec as P

SWEEPS = 2


VERTICAL = 0.5
VISCOSITY_RATIO = 2.0
STEP_COEF = 0.1
INFLATION = 4.0


def extended_2(block, sides, width):
    for axis, dim in sides:
        count = lax.axis_size(axis)
        forward = [(i, i + 1) for i in range(count - 1)]
        backward = [(target, source) for source, target in forward]
        low = lax.ppermute(
            lax.slice_in_dim(block, block.shape[dim] - width, None, axis=dim), axis, forward
        )
        high = lax.ppermute(lax.slice_in_dim(block, 0, width, axis=dim), axis, backward)
        block = jnp.concatenate([low, block, high], axis=dim)
    return block


def harmonic(lower_val, upper_val):
    return 2.0 * lower_val * upper_val / (lower_val + upper_val)


def pad_face(values_in, along_dim, before):
    widths = [(0, 0)] * values_in.ndim
    widths[along_dim] = (1, 0) if before else (0, 1)
    return jnp.pad(values_in, widths)


def slide_by(values_in, along_dim, before):
    extent = values_in.shape[along_dim]
    if before:
        remain = lax.slice_in_dim(values_in, 0, extent - 1, axis=along_dim)
    else:
        remain = lax.slice_in_dim(values_in, 1, extent, axis=along_dim)
    return pad_face(remain, along_dim, before)


def face_terms(permeab, inside):
    face_x = (
        harmonic(permeab[:, :, :-1, :], permeab[:, :, 1:, :]) * (inside[:-1] * inside[1:])[:, None]
    )
    face_y = harmonic(permeab[:, :, :, :-1], permeab[:, :, :, 1:])
    face_z = VERTICAL * harmonic(permeab[:, :-1], permeab[:, 1:])
    return (face_x, face_y, face_z)


def neighbours(face_sets, values_in):
    flow_sum = 0.0
    weight_sum = 0.0
    for faces_dim, along_dim in zip(face_sets, (2, 3, 1)):
        lower = pad_face(faces_dim, along_dim, True)
        upper = pad_face(faces_dim, along_dim, False)
        flow_sum = (
            flow_sum
            + lower * slide_by(values_in, along_dim, True)
            + upper * slide_by(values_in, along_dim, False)
        )
        weight_sum = weight_sum + lower + upper
    return (flow_sum, weight_sum)


def jacobi(pressure, baseline, storage_term, face_sets):
    flow_sum, weight_sum = neighbours(face_sets, pressure)
    return (baseline + flow_sum) / (storage_term + weight_sum)


def water_frac(values_in):
    squared = values_in * values_in
    return squared / (squared + VISCOSITY_RATIO * (1.0 - values_in) * (1.0 - values_in))


def transport(pressure, saturation, face_sets):
    fraction = water_frac(saturation)
    change = 0.0
    for faces_dim, along_dim in zip(face_sets, (2, 3, 1)):
        extent = pressure.shape[along_dim]
        lower_press = lax.slice_in_dim(pressure, 0, extent - 1, axis=along_dim)
        upper_press = lax.slice_in_dim(pressure, 1, extent, axis=along_dim)
        lower_frac = lax.slice_in_dim(fraction, 0, extent - 1, axis=along_dim)
        upper_frac = lax.slice_in_dim(fraction, 1, extent, axis=along_dim)
        velocity = faces_dim * (lower_press - upper_press)
        carried = velocity * jnp.where(velocity > 0, lower_frac, upper_frac)
        change = change + pad_face(carried, along_dim, True) - pad_face(carried, along_dim, False)
    return saturation + STEP_COEF * change


def solve_spd(gram_matrix, cross_matrix):
    factor = lax.linalg.cholesky(
        gram_matrix + jnp.eye(gram_matrix.shape[0], dtype=jnp.float32), symmetrize_input=False
    )
    halfway = lax.linalg.triangular_solve(factor, cross_matrix, left_side=True, lower=True)
    return lax.linalg.triangular_solve(
        factor, halfway, left_side=True, lower=True, transpose_a=True
    )


def trim_rim(values_in, rim_cut):
    return values_in[:, :, rim_cut : values_in.shape[2] - rim_cut, :]


def exchange_kernel(member_count, part_ref, full_ref,
                    recv_a, own_blk, recv_m, send_a, recv_a_sem, send_m, recv_m_sem, send_t, recv_t_sem):
    tile_count = part_ref.shape[0]
    me_t = lax.axis_index("tile")
    me_m = lax.axis_index("member")
    mesh_ids = pl.DeviceIdType.MESH

    barrier = pltpu.get_barrier_semaphore()

    def greet_tile(k, carry):
        pl.semaphore_signal(
            barrier, 1, device_id=(lax.rem(me_t + k, tile_count), me_m), device_id_type=mesh_ids
        )
        return carry

    def greet_member(k, carry):
        pl.semaphore_signal(
            barrier, 1, device_id=(me_t, lax.rem(me_m + k, member_count)), device_id_type=mesh_ids
        )
        return carry

    lax.fori_loop(1, tile_count, greet_tile, 0)
    lax.fori_loop(1, member_count, greet_member, 0)
    pl.semaphore_wait(barrier, tile_count + member_count - 2)

    def copy_a(dst_t, src_t):
        return pltpu.make_async_remote_copy(
            src_ref=part_ref.at[dst_t], dst_ref=recv_a.at[src_t],
            send_sem=send_a.at[dst_t], recv_sem=recv_a_sem.at[src_t],
            device_id=(dst_t, me_m), device_id_type=mesh_ids,
        )

    def start_a(k, carry):
        copy_a(lax.rem(me_t + k, tile_count), me_t).start()
        return carry

    lax.fori_loop(1, tile_count, start_a, 0)

    def wait_a(k, acc):
        src_t = lax.rem(me_t + k, tile_count)
        copy_a(me_t, src_t).wait_recv()
        return acc + recv_a[src_t]

    acc = lax.fori_loop(1, tile_count, wait_a, part_ref[me_t])

    def wait_a_send(k, carry):
        copy_a(lax.rem(me_t + k, tile_count), me_t).wait_send()
        return carry

    lax.fori_loop(1, tile_count, wait_a_send, 0)

    groups = part_ref.shape[2] // member_count
    lane_ids = lax.broadcasted_iota(jnp.int32, acc.shape, 1)
    for q in range(member_count):
        moved = pltpu.roll(acc, lax.rem((me_m - q + member_count) * groups, part_ref.shape[2]), 1)
        own_blk[pl.ds(q, acc.shape[0], stride=member_count), :] = jnp.where(
            lane_ids // groups == me_m, moved, 0.0
        )
    acc = own_blk[...]

    def copy_m(dst_m, src_m):
        return pltpu.make_async_remote_copy(
            src_ref=own_blk, dst_ref=recv_m.at[src_m],
            send_sem=send_m.at[dst_m], recv_sem=recv_m_sem.at[src_m],
            device_id=(me_t, dst_m), device_id_type=mesh_ids,
        )

    def start_m(k, carry):
        copy_m(lax.rem(me_m + k, member_count), me_m).start()
        return carry

    lax.fori_loop(1, member_count, start_m, 0)

    def wait_m(k, total):
        src_m = lax.rem(me_m + k, member_count)
        copy_m(me_m, src_m).wait_recv()
        return total + recv_m[src_m]

    full_ref[me_t] = lax.fori_loop(1, member_count, wait_m, acc)

    def wait_m_send(k, carry):
        copy_m(lax.rem(me_m + k, member_count), me_m).wait_send()
        return carry

    lax.fori_loop(1, member_count, wait_m_send, 0)

    def copy_t(dst_t, src_t):
        return pltpu.make_async_remote_copy(
            src_ref=full_ref.at[src_t], dst_ref=full_ref.at[src_t],
            send_sem=send_t.at[dst_t], recv_sem=recv_t_sem.at[src_t],
            device_id=(dst_t, me_m), device_id_type=mesh_ids,
        )

    def start_t(k, carry):
        copy_t(lax.rem(me_t + k, tile_count), me_t).start()
        return carry

    lax.fori_loop(1, tile_count, start_t, 0)

    def wait_t(k, carry):
        copy_t(me_t, lax.rem(me_t + k, tile_count)).wait_recv()
        return carry

    lax.fori_loop(1, tile_count, wait_t, 0)

    def wait_t_send(k, carry):
        copy_t(lax.rem(me_t + k, tile_count), me_t).wait_send()
        return carry

    lax.fori_loop(1, tile_count, wait_t_send, 0)


def stencil_kernel(rim, lp_low, lp_mid, lp_high, f_low, f_mid, f_high, inside_ref,
                   press_ref, sat_ref, mob_ref):
    inside = inside_ref[...]
    permeab = jnp.exp(jnp.concatenate([lp_low[...], lp_mid[...], lp_high[...]], axis=2))
    face_sets = face_terms(permeab, inside)
    fields = jnp.concatenate([f_low[...], f_mid[...], f_high[...]], axis=2)
    press_ext = fields[0]
    sat_ext = fields[1]
    source_ext = fields[2]
    storage_ext = fields[3]
    baseline = (source_ext + storage_ext * press_ext)[None]
    storage_term = jnp.where(inside[None, :, None] > 0.0, storage_ext, 1.0)[None]
    pressure = jnp.broadcast_to(press_ext[None], permeab.shape)
    for sweep_idx in range(SWEEPS):
        pressure = jacobi(pressure, baseline, storage_term, face_sets)
    saturation = trim_rim(transport(pressure, sat_ext[None], face_sets), rim)
    press_ref[...] = trim_rim(pressure, rim)
    sat_ref[...] = saturation
    mob_ref[...] = trim_rim(permeab, rim) * water_frac(saturation)


def stencil(lp_parts, field_parts, inside, rim):
    members, layers, out_rows, depth = lp_parts[1].shape
    block = 4

    def member_block(part):
        return pl.BlockSpec((block,) + part.shape[1:], lambda i: (i, 0, 0, 0))

    def whole(part):
        return pl.BlockSpec(part.shape, lambda i: (0, 0, 0, 0))

    out_spec = pl.BlockSpec((block, layers, out_rows, depth), lambda i: (i, 0, 0, 0))
    out_shape = jax.ShapeDtypeStruct((members, layers, out_rows, depth), jnp.float32)
    return pl.pallas_call(
        functools.partial(stencil_kernel, rim),
        grid=(members // block,),
        in_specs=[member_block(p) for p in lp_parts]
        + [whole(p) for p in field_parts]
        + [pl.BlockSpec(inside.shape, lambda i: (0,))],
        out_specs=[out_spec, out_spec, out_spec],
        out_shape=[out_shape, out_shape, out_shape],
    )(*lp_parts, *field_parts, inside)


def halo_kernel(out_ref, in_ref, send_sem, recv_sem):
    tile_count = lax.axis_size("tile")
    me_t = lax.axis_index("tile")
    me_m = lax.axis_index("member")
    mesh_ids = pl.DeviceIdType.MESH
    left = lax.rem(me_t + tile_count - 1, tile_count)
    right = lax.rem(me_t + 1, tile_count)
    barrier = pltpu.get_barrier_semaphore()
    for peer in (left, right):
        pl.semaphore_signal(barrier, 1, device_id=(peer, me_m), device_id_type=mesh_ids)
    pl.semaphore_wait(barrier, 2)
    to_right = pltpu.make_async_remote_copy(
        src_ref=out_ref.at[1], dst_ref=in_ref.at[0], send_sem=send_sem.at[1],
        recv_sem=recv_sem.at[0], device_id=(right, me_m), device_id_type=mesh_ids,
    )
    to_left = pltpu.make_async_remote_copy(
        src_ref=out_ref.at[0], dst_ref=in_ref.at[1], send_sem=send_sem.at[0],
        recv_sem=recv_sem.at[1], device_id=(left, me_m), device_id_type=mesh_ids,
    )
    to_right.start()
    to_left.start()
    to_right.wait()
    to_left.wait()


def halo_exchange(outgoing):
    vmem = pl.BlockSpec(memory_space=pltpu.VMEM)
    return pl.pallas_call(
        halo_kernel,
        out_shape=jax.ShapeDtypeStruct(outgoing.shape, outgoing.dtype),
        in_specs=[vmem],
        out_specs=vmem,
        scratch_shapes=[pltpu.SemaphoreType.DMA((2,)), pltpu.SemaphoreType.DMA((2,))],
        compiler_params=pltpu.CompilerParams(collective_id=1, has_side_effects=True),
    )(outgoing)


def rates_exchange(pieces, member_count):
    tile_count, rows, lanes = pieces.shape
    vmem = pl.BlockSpec(memory_space=pltpu.VMEM)
    return pl.pallas_call(
        functools.partial(exchange_kernel, member_count),
        out_shape=jax.ShapeDtypeStruct((tile_count, rows * member_count, lanes), jnp.float32),
        in_specs=[vmem],
        out_specs=vmem,
        scratch_shapes=[
            pltpu.VMEM((tile_count, rows, lanes), jnp.float32),
            pltpu.VMEM((rows * member_count, lanes), jnp.float32),
            pltpu.VMEM((member_count, rows * member_count, lanes), jnp.float32),
            pltpu.SemaphoreType.DMA((tile_count,)),
            pltpu.SemaphoreType.DMA((tile_count,)),
            pltpu.SemaphoreType.DMA((member_count,)),
            pltpu.SemaphoreType.DMA((member_count,)),
            pltpu.SemaphoreType.DMA((tile_count,)),
            pltpu.SemaphoreType.DMA((tile_count,)),
        ],
        compiler_params=pltpu.CompilerParams(collective_id=0, has_side_effects=True),
    )(pieces)


def per_device(
    log_perm,
    start_pressure,
    start_sat,
    source,
    storage,
    well_press,
    perf_cell,
    perf_well,
    perf_count,
    observed,
    obs_var,
    obs_noise,
):
    local_count, layers, strip_width, strip_depth = log_perm.shape
    tile_count = lax.axis_size("tile")
    members = local_count * lax.axis_size("member")
    well_count = well_press.shape[0]
    well_share = well_count // tile_count
    tile_rank = lax.axis_index("tile")
    member_rank = lax.axis_index("member")
    rim = SWEEPS + 1
    fields = jnp.stack([start_pressure, start_sat, source, storage])
    halo_rows = local_count * layers * rim + fields.shape[0] * layers * rim

    def rim_rows(first):
        return jnp.concatenate(
            [
                lax.slice_in_dim(log_perm, first, first + rim, axis=2).reshape(-1, strip_depth),
                lax.slice_in_dim(fields, first, first + rim, axis=2).reshape(-1, strip_depth),
            ]
        )

    outgoing = jnp.stack([rim_rows(0), rim_rows(strip_width - rim)])
    incoming = halo_exchange(outgoing)
    lp_count = local_count * layers * rim

    def unpack(side):
        lp_part = incoming[side, :lp_count].reshape(local_count, layers, rim, strip_depth)
        field_part = incoming[side, lp_count:].reshape(fields.shape[0], layers, rim, strip_depth)
        return lp_part, field_part

    low_lp, low_fields = unpack(0)
    high_lp, high_fields = unpack(1)
    column = tile_rank * strip_width - rim + jnp.arange(strip_width + 2 * rim, dtype=jnp.int32)
    inside = ((column >= 0) & (column < strip_width * tile_count)).astype(jnp.float32)
    pressure, saturation, mobility = stencil(
        (low_lp, log_perm, high_lp), (low_fields, fields, high_fields), inside, rim
    )
    cell_count = layers * strip_width * strip_depth
    mobility, log_perm_after = lax.optimization_barrier((mobility, log_perm))
    plane_rows = layers * strip_width
    cell_row = perf_cell // strip_depth
    cell_col = lax.rem(perf_cell, strip_depth)
    col_pick = (jnp.arange(strip_depth, dtype=jnp.int32)[:, None] == cell_col[None, :]).astype(
        jnp.float32
    )
    row_pick = jnp.arange(plane_rows, dtype=jnp.int32)[:, None] == cell_row[None, :]

    def pick_cells(values_in):
        by_col = jnp.dot(
            values_in.reshape(local_count * plane_rows, strip_depth), col_pick,
            precision=lax.Precision.HIGHEST, preferred_element_type=jnp.float32,
        ).reshape(local_count, plane_rows, -1)
        return jnp.sum(jnp.where(row_pick[None], by_col, 0.0), axis=1)

    perf_mob = pick_cells(mobility)
    perf_press = pick_cells(pressure)
    selector = (perf_well[:, None] == jnp.arange(well_count, dtype=jnp.int32)[None, :]).astype(
        jnp.float32
    )
    perf_bhp = jnp.dot(selector, well_press, precision=lax.Precision.HIGHEST)
    live_mask = (jnp.arange(perf_cell.shape[0], dtype=jnp.int32) < perf_count[0]).astype(
        jnp.float32
    )
    perf_terms = perf_mob * (perf_press - perf_bhp[None]) * live_mask[None]
    member_root = (members - 1) ** 0.5
    spread = jnp.sqrt(INFLATION * obs_var)
    member_count = lax.axis_size("member")
    contract_slots = (((0,), (1,)), ((), ()))
    pieces = lax.dot_general(
        selector, perf_terms, contract_slots, precision=lax.Precision.HIGHEST,
        preferred_element_type=jnp.float32,
    ).reshape(tile_count, well_share * local_count // 128, 128)
    full = rates_exchange(pieces, member_count)
    own_block = lax.dynamic_index_in_dim(full, tile_rank, 0, keepdims=False)
    well_rates = lax.dynamic_slice_in_dim(own_block, member_rank * local_count, local_count, 1).T
    rates_t = full.reshape(well_count, members)
    mean_rate = jnp.sum(rates_t, 1) / members
    scaled_t = (rates_t - mean_rate[:, None]) / (spread * member_root)[:, None]
    rates_own_t = lax.dynamic_slice_in_dim(rates_t, member_rank * local_count, local_count, 1)
    innov_own_t = (observed[:, None] - rates_own_t) / spread[:, None] + obs_noise.T
    contract_wells = (((0,), (0,)), ((), ()))
    gram_matrix = lax.dot_general(
        scaled_t, scaled_t, contract_wells, precision=lax.Precision.HIGHEST,
        preferred_element_type=jnp.float32,
    )
    cross_matrix = lax.dot_general(
        scaled_t, innov_own_t, contract_wells, precision=lax.Precision.HIGHEST,
        preferred_element_type=jnp.float32,
    )
    weights_low = solve_spd(gram_matrix, cross_matrix).astype(jnp.bfloat16)
    anomaly = (log_perm_after / member_root).astype(jnp.bfloat16).reshape(local_count, cell_count)
    anomaly_parts = [anomaly]
    for shift in range(1, member_count):
        pairs = [(i, (i + shift) % member_count) for i in range(member_count)]
        anomaly_parts.append(lax.ppermute(anomaly, "member", pairs))
    anomaly_all = jnp.concatenate(anomaly_parts, axis=0)
    own_cols = jnp.concatenate(
        [
            lax.dynamic_slice_in_dim(
                weights_low, lax.rem(member_rank - shift + member_count, member_count) * local_count,
                local_count, 0,
            )
            for shift in range(member_count)
        ],
        axis=0,
    )
    contract = (((0,), (0,)), ((), ()))
    update_sum = lax.dot_general(own_cols, anomaly_all, contract, preferred_element_type=jnp.float32)
    new_log_perm = log_perm + update_sum.reshape(log_perm.shape)
    return (new_log_perm, pressure, saturation, well_rates)


def solution(mesh):
    return jax.shard_map(
        per_device,
        mesh=mesh,
        in_specs=(
            P("member", None, "tile", None),
            P(None, "tile", None),
            P(None, "tile", None),
            P(None, "tile", None),
            P(None, "tile", None),
            P(),
            P("tile"),
            P("tile"),
            P("tile"),
            P(),
            P(),
            P("member", None),
        ),
        out_specs=(
            P("member", None, "tile", None),
            P("member", None, "tile", None),
            P("member", None, "tile", None),
            P("member", "tile"),
        ),
        check_vma=False,
    )
```

```python
import functools

import jax
import jax.numpy as jnp
from jax import lax
from jax.experimental import pallas as pl
from jax.experimental.pallas import tpu as pltpu
from jax.sharding import PartitionSpec as P

SWEEPS = 2


VERTICAL = 0.5
VISCOSITY_RATIO = 2.0
STEP_COEF = 0.1
INFLATION = 4.0


def extended_2(block, sides, width):
    for axis, dim in sides:
        count = lax.axis_size(axis)
        forward = [(i, i + 1) for i in range(count - 1)]
        backward = [(target, source) for source, target in forward]
        low = lax.ppermute(
            lax.slice_in_dim(block, block.shape[dim] - width, None, axis=dim), axis, forward
        )
        high = lax.ppermute(lax.slice_in_dim(block, 0, width, axis=dim), axis, backward)
        block = jnp.concatenate([low, block, high], axis=dim)
    return block


def harmonic(lower_val, upper_val):
    return 2.0 * lower_val * upper_val / (lower_val + upper_val)


def pad_face(values_in, along_dim, before):
    widths = [(0, 0)] * values_in.ndim
    widths[along_dim] = (1, 0) if before else (0, 1)
    return jnp.pad(values_in, widths)


def slide_by(values_in, along_dim, before):
    extent = values_in.shape[along_dim]
    if before:
        remain = lax.slice_in_dim(values_in, 0, extent - 1, axis=along_dim)
    else:
        remain = lax.slice_in_dim(values_in, 1, extent, axis=along_dim)
    return pad_face(remain, along_dim, before)


def face_terms(permeab, inside):
    face_x = (
        harmonic(permeab[:, :, :-1, :], permeab[:, :, 1:, :]) * (inside[:-1] * inside[1:])[:, None]
    )
    face_y = harmonic(permeab[:, :, :, :-1], permeab[:, :, :, 1:])
    face_z = VERTICAL * harmonic(permeab[:, :-1], permeab[:, 1:])
    return (face_x, face_y, face_z)


def neighbours(face_sets, values_in):
    flow_sum = 0.0
    weight_sum = 0.0
    for faces_dim, along_dim in zip(face_sets, (2, 3, 1)):
        lower = pad_face(faces_dim, along_dim, True)
        upper = pad_face(faces_dim, along_dim, False)
        flow_sum = (
            flow_sum
            + lower * slide_by(values_in, along_dim, True)
            + upper * slide_by(values_in, along_dim, False)
        )
        weight_sum = weight_sum + lower + upper
    return (flow_sum, weight_sum)


def jacobi(pressure, baseline, storage_term, face_sets):
    flow_sum, weight_sum = neighbours(face_sets, pressure)
    return (baseline + flow_sum) / (storage_term + weight_sum)


def water_frac(values_in):
    squared = values_in * values_in
    return squared / (squared + VISCOSITY_RATIO * (1.0 - values_in) * (1.0 - values_in))


def transport(pressure, saturation, face_sets):
    fraction = water_frac(saturation)
    change = 0.0
    for faces_dim, along_dim in zip(face_sets, (2, 3, 1)):
        extent = pressure.shape[along_dim]
        lower_press = lax.slice_in_dim(pressure, 0, extent - 1, axis=along_dim)
        upper_press = lax.slice_in_dim(pressure, 1, extent, axis=along_dim)
        lower_frac = lax.slice_in_dim(fraction, 0, extent - 1, axis=along_dim)
        upper_frac = lax.slice_in_dim(fraction, 1, extent, axis=along_dim)
        velocity = faces_dim * (lower_press - upper_press)
        carried = velocity * jnp.where(velocity > 0, lower_frac, upper_frac)
        change = change + pad_face(carried, along_dim, True) - pad_face(carried, along_dim, False)
    return saturation + STEP_COEF * change


def solve_spd(gram_matrix, cross_matrix):
    factor = lax.linalg.cholesky(
        gram_matrix + jnp.eye(gram_matrix.shape[0], dtype=jnp.float32), symmetrize_input=False
    )
    halfway = lax.linalg.triangular_solve(factor, cross_matrix, left_side=True, lower=True)
    return lax.linalg.triangular_solve(
        factor, halfway, left_side=True, lower=True, transpose_a=True
    )


def trim_rim(values_in, rim_cut):
    return values_in[:, :, rim_cut : values_in.shape[2] - rim_cut, :]


def exchange_kernel(member_count, part_ref, full_ref,
                    recv_a, own_blk, recv_m, send_a, recv_a_sem, send_m, recv_m_sem, send_t, recv_t_sem):
    tile_count = part_ref.shape[0]
    me_t = lax.axis_index("tile")
    me_m = lax.axis_index("member")
    mesh_ids = pl.DeviceIdType.MESH

    barrier = pltpu.get_barrier_semaphore()

    def greet_tile(k, carry):
        pl.semaphore_signal(
            barrier, 1, device_id=(lax.rem(me_t + k, tile_count), me_m), device_id_type=mesh_ids
        )
        return carry

    def greet_member(k, carry):
        pl.semaphore_signal(
            barrier, 1, device_id=(me_t, lax.rem(me_m + k, member_count)), device_id_type=mesh_ids
        )
        return carry

    lax.fori_loop(1, tile_count, greet_tile, 0)
    lax.fori_loop(1, member_count, greet_member, 0)
    pl.semaphore_wait(barrier, tile_count + member_count - 2)

    def copy_a(dst_t, src_t):
        return pltpu.make_async_remote_copy(
            src_ref=part_ref.at[dst_t], dst_ref=recv_a.at[src_t],
            send_sem=send_a.at[dst_t], recv_sem=recv_a_sem.at[src_t],
            device_id=(dst_t, me_m), device_id_type=mesh_ids,
        )

    def start_a(k, carry):
        copy_a(lax.rem(me_t + k, tile_count), me_t).start()
        return carry

    lax.fori_loop(1, tile_count, start_a, 0)

    def wait_a(k, acc):
        src_t = lax.rem(me_t + k, tile_count)
        copy_a(me_t, src_t).wait_recv()
        return acc + recv_a[src_t]

    acc = lax.fori_loop(1, tile_count, wait_a, part_ref[me_t])

    def wait_a_send(k, carry):
        copy_a(lax.rem(me_t + k, tile_count), me_t).wait_send()
        return carry

    lax.fori_loop(1, tile_count, wait_a_send, 0)

    groups = part_ref.shape[2] // member_count
    lane_ids = lax.broadcasted_iota(jnp.int32, acc.shape, 1)
    for q in range(member_count):
        moved = pltpu.roll(acc, lax.rem((me_m - q + member_count) * groups, part_ref.shape[2]), 1)
        own_blk[pl.ds(q, acc.shape[0], stride=member_count), :] = jnp.where(
            lane_ids // groups == me_m, moved, 0.0
        )
    acc = own_blk[...]

    def copy_m(dst_m, src_m):
        return pltpu.make_async_remote_copy(
            src_ref=own_blk, dst_ref=recv_m.at[src_m],
            send_sem=send_m.at[dst_m], recv_sem=recv_m_sem.at[src_m],
            device_id=(me_t, dst_m), device_id_type=mesh_ids,
        )

    def start_m(k, carry):
        copy_m(lax.rem(me_m + k, member_count), me_m).start()
        return carry

    lax.fori_loop(1, member_count, start_m, 0)

    def wait_m(k, total):
        src_m = lax.rem(me_m + k, member_count)
        copy_m(me_m, src_m).wait_recv()
        return total + recv_m[src_m]

    full_ref[me_t] = lax.fori_loop(1, member_count, wait_m, acc)

    def wait_m_send(k, carry):
        copy_m(lax.rem(me_m + k, member_count), me_m).wait_send()
        return carry

    lax.fori_loop(1, member_count, wait_m_send, 0)

    def copy_t(dst_t, src_t):
        return pltpu.make_async_remote_copy(
            src_ref=full_ref.at[src_t], dst_ref=full_ref.at[src_t],
            send_sem=send_t.at[dst_t], recv_sem=recv_t_sem.at[src_t],
            device_id=(dst_t, me_m), device_id_type=mesh_ids,
        )

    def start_t(k, carry):
        copy_t(lax.rem(me_t + k, tile_count), me_t).start()
        return carry

    lax.fori_loop(1, tile_count, start_t, 0)

    def wait_t(k, carry):
        copy_t(me_t, lax.rem(me_t + k, tile_count)).wait_recv()
        return carry

    lax.fori_loop(1, tile_count, wait_t, 0)

    def wait_t_send(k, carry):
        copy_t(lax.rem(me_t + k, tile_count), me_t).wait_send()
        return carry

    lax.fori_loop(1, tile_count, wait_t_send, 0)


def stencil_kernel(rim, lp_low, lp_mid, lp_high, f_low, f_mid, f_high, inside_ref,
                   col_ref, row_ref, press_ref, sat_ref, pmob_ref, ppress_ref):
    inside = inside_ref[...]
    permeab = jnp.exp(jnp.concatenate([lp_low[...], lp_mid[...], lp_high[...]], axis=2))
    face_sets = face_terms(permeab, inside)
    fields = jnp.concatenate([f_low[...], f_mid[...], f_high[...]], axis=2)
    press_ext = fields[0]
    sat_ext = fields[1]
    source_ext = fields[2]
    storage_ext = fields[3]
    baseline = (source_ext + storage_ext * press_ext)[None]
    storage_term = jnp.where(inside[None, :, None] > 0.0, storage_ext, 1.0)[None]
    pressure = jnp.broadcast_to(press_ext[None], permeab.shape)
    for sweep_idx in range(SWEEPS):
        pressure = jacobi(pressure, baseline, storage_term, face_sets)
    saturation = trim_rim(transport(pressure, sat_ext[None], face_sets), rim)
    pressure = trim_rim(pressure, rim)
    press_ref[...] = pressure
    sat_ref[...] = saturation
    mobility = trim_rim(permeab, rim) * water_frac(saturation)
    block, layers, rows, depth = pressure.shape
    row_pick = row_ref[...] > 0.0
    for values_in, out_ref in ((mobility, pmob_ref), (pressure, ppress_ref)):
        by_col = jnp.dot(
            values_in.reshape(block * layers * rows, depth), col_ref[...],
            precision=lax.Precision.HIGHEST, preferred_element_type=jnp.float32,
        ).reshape(block, layers * rows, -1)
        out_ref[0] = jnp.sum(jnp.where(row_pick[None], by_col, 0.0), axis=1)


def stencil(lp_parts, field_parts, inside, col_pick, row_pick, rim):
    members, layers, out_rows, depth = lp_parts[1].shape
    block = 4

    def member_block(part):
        return pl.BlockSpec((block,) + part.shape[1:], lambda i: (i, 0, 0, 0))

    def whole(part):
        return pl.BlockSpec(part.shape, lambda i: (0, 0, 0, 0))

    out_spec = pl.BlockSpec((block, layers, out_rows, depth), lambda i: (i, 0, 0, 0))
    out_shape = jax.ShapeDtypeStruct((members, layers, out_rows, depth), jnp.float32)
    slots = col_pick.shape[1]
    pick_spec = pl.BlockSpec((1, block, slots), lambda i: (i, 0, 0))
    pick_shape = jax.ShapeDtypeStruct((members // block, block, slots), jnp.float32)
    return pl.pallas_call(
        functools.partial(stencil_kernel, rim),
        grid=(members // block,),
        in_specs=[member_block(p) for p in lp_parts]
        + [whole(p) for p in field_parts]
        + [
            pl.BlockSpec(inside.shape, lambda i: (0,)),
            pl.BlockSpec(col_pick.shape, lambda i: (0, 0)),
            pl.BlockSpec(row_pick.shape, lambda i: (0, 0)),
        ],
        out_specs=[out_spec, out_spec, pick_spec, pick_spec],
        out_shape=[out_shape, out_shape, pick_shape, pick_shape],
    )(*lp_parts, *field_parts, inside, col_pick, row_pick)


def halo_kernel(out_ref, in_ref, send_sem, recv_sem):
    tile_count = lax.axis_size("tile")
    me_t = lax.axis_index("tile")
    me_m = lax.axis_index("member")
    mesh_ids = pl.DeviceIdType.MESH
    left = lax.rem(me_t + tile_count - 1, tile_count)
    right = lax.rem(me_t + 1, tile_count)
    barrier = pltpu.get_barrier_semaphore()
    for peer in (left, right):
        pl.semaphore_signal(barrier, 1, device_id=(peer, me_m), device_id_type=mesh_ids)
    pl.semaphore_wait(barrier, 2)
    to_right = pltpu.make_async_remote_copy(
        src_ref=out_ref.at[1], dst_ref=in_ref.at[0], send_sem=send_sem.at[1],
        recv_sem=recv_sem.at[0], device_id=(right, me_m), device_id_type=mesh_ids,
    )
    to_left = pltpu.make_async_remote_copy(
        src_ref=out_ref.at[0], dst_ref=in_ref.at[1], send_sem=send_sem.at[0],
        recv_sem=recv_sem.at[1], device_id=(left, me_m), device_id_type=mesh_ids,
    )
    to_right.start()
    to_left.start()
    to_right.wait()
    to_left.wait()


def halo_exchange(outgoing):
    vmem = pl.BlockSpec(memory_space=pltpu.VMEM)
    return pl.pallas_call(
        halo_kernel,
        out_shape=jax.ShapeDtypeStruct(outgoing.shape, outgoing.dtype),
        in_specs=[vmem],
        out_specs=vmem,
        scratch_shapes=[pltpu.SemaphoreType.DMA((2,)), pltpu.SemaphoreType.DMA((2,))],
        compiler_params=pltpu.CompilerParams(collective_id=1, has_side_effects=True),
    )(outgoing)


def rates_exchange(pieces, member_count):
    tile_count, rows, lanes = pieces.shape
    vmem = pl.BlockSpec(memory_space=pltpu.VMEM)
    return pl.pallas_call(
        functools.partial(exchange_kernel, member_count),
        out_shape=jax.ShapeDtypeStruct((tile_count, rows * member_count, lanes), jnp.float32),
        in_specs=[vmem],
        out_specs=vmem,
        scratch_shapes=[
            pltpu.VMEM((tile_count, rows, lanes), jnp.float32),
            pltpu.VMEM((rows * member_count, lanes), jnp.float32),
            pltpu.VMEM((member_count, rows * member_count, lanes), jnp.float32),
            pltpu.SemaphoreType.DMA((tile_count,)),
            pltpu.SemaphoreType.DMA((tile_count,)),
            pltpu.SemaphoreType.DMA((member_count,)),
            pltpu.SemaphoreType.DMA((member_count,)),
            pltpu.SemaphoreType.DMA((tile_count,)),
            pltpu.SemaphoreType.DMA((tile_count,)),
        ],
        compiler_params=pltpu.CompilerParams(collective_id=0, has_side_effects=True),
    )(pieces)


def per_device(
    log_perm,
    start_pressure,
    start_sat,
    source,
    storage,
    well_press,
    perf_cell,
    perf_well,
    perf_count,
    observed,
    obs_var,
    obs_noise,
):
    local_count, layers, strip_width, strip_depth = log_perm.shape
    tile_count = lax.axis_size("tile")
    members = local_count * lax.axis_size("member")
    well_count = well_press.shape[0]
    well_share = well_count // tile_count
    tile_rank = lax.axis_index("tile")
    member_rank = lax.axis_index("member")
    rim = SWEEPS + 1
    fields = jnp.stack([start_pressure, start_sat, source, storage])
    halo_rows = local_count * layers * rim + fields.shape[0] * layers * rim

    def rim_rows(first):
        return jnp.concatenate(
            [
                lax.slice_in_dim(log_perm, first, first + rim, axis=2).reshape(-1, strip_depth),
                lax.slice_in_dim(fields, first, first + rim, axis=2).reshape(-1, strip_depth),
            ]
        )

    outgoing = jnp.stack([rim_rows(0), rim_rows(strip_width - rim)])
    incoming = halo_exchange(outgoing)
    incoming, log_perm_after = lax.optimization_barrier((incoming, log_perm))
    lp_count = local_count * layers * rim

    def unpack(side):
        lp_part = incoming[side, :lp_count].reshape(local_count, layers, rim, strip_depth)
        field_part = incoming[side, lp_count:].reshape(fields.shape[0], layers, rim, strip_depth)
        return lp_part, field_part

    low_lp, low_fields = unpack(0)
    high_lp, high_fields = unpack(1)
    column = tile_rank * strip_width - rim + jnp.arange(strip_width + 2 * rim, dtype=jnp.int32)
    inside = ((column >= 0) & (column < strip_width * tile_count)).astype(jnp.float32)
    plane_rows = layers * strip_width
    cell_row = perf_cell // strip_depth
    cell_col = lax.rem(perf_cell, strip_depth)
    col_pick = (jnp.arange(strip_depth, dtype=jnp.int32)[:, None] == cell_col[None, :]).astype(
        jnp.float32
    )
    row_pick = (jnp.arange(plane_rows, dtype=jnp.int32)[:, None] == cell_row[None, :]).astype(
        jnp.float32
    )
    pressure, saturation, perf_mob, perf_press = stencil(
        (low_lp, log_perm, high_lp), (low_fields, fields, high_fields), inside, col_pick, row_pick, rim
    )
    cell_count = layers * strip_width * strip_depth
    perf_mob = perf_mob.reshape(local_count, -1)
    perf_press = perf_press.reshape(local_count, -1)
    selector = (perf_well[:, None] == jnp.arange(well_count, dtype=jnp.int32)[None, :]).astype(
        jnp.float32
    )
    perf_bhp = jnp.dot(selector, well_press, precision=lax.Precision.HIGHEST)
    live_mask = (jnp.arange(perf_cell.shape[0], dtype=jnp.int32) < perf_count[0]).astype(
        jnp.float32
    )
    perf_terms = perf_mob * (perf_press - perf_bhp[None]) * live_mask[None]
    member_root = (members - 1) ** 0.5
    spread = jnp.sqrt(INFLATION * obs_var)
    member_count = lax.axis_size("member")
    contract_slots = (((0,), (1,)), ((), ()))
    pieces = lax.dot_general(
        selector, perf_terms, contract_slots, precision=lax.Precision.HIGHEST,
        preferred_element_type=jnp.float32,
    ).reshape(tile_count, well_share * local_count // 128, 128)
    full = rates_exchange(pieces, member_count)
    own_block = lax.dynamic_index_in_dim(full, tile_rank, 0, keepdims=False)
    well_rates = lax.dynamic_slice_in_dim(own_block, member_rank * local_count, local_count, 1).T
    rates_t = full.reshape(well_count, members)
    mean_rate = jnp.sum(rates_t, 1) / members
    scaled_t = (rates_t - mean_rate[:, None]) / (spread * member_root)[:, None]
    rates_own_t = lax.dynamic_slice_in_dim(rates_t, member_rank * local_count, local_count, 1)
    innov_own_t = (observed[:, None] - rates_own_t) / spread[:, None] + obs_noise.T
    contract_wells = (((0,), (0,)), ((), ()))
    gram_matrix = lax.dot_general(
        scaled_t, scaled_t, contract_wells, precision=lax.Precision.HIGHEST,
        preferred_element_type=jnp.float32,
    )
    cross_matrix = lax.dot_general(
        scaled_t, innov_own_t, contract_wells, precision=lax.Precision.HIGHEST,
        preferred_element_type=jnp.float32,
    )
    weights_low = solve_spd(gram_matrix, cross_matrix).astype(jnp.bfloat16)
    anomaly = (log_perm_after / member_root).astype(jnp.bfloat16).reshape(local_count, cell_count)
    anomaly_parts = [anomaly]
    for shift in range(1, member_count):
        pairs = [(i, (i + shift) % member_count) for i in range(member_count)]
        anomaly_parts.append(lax.ppermute(anomaly, "member", pairs))
    anomaly_all = jnp.concatenate(anomaly_parts, axis=0)
    own_cols = jnp.concatenate(
        [
            lax.dynamic_slice_in_dim(
                weights_low, lax.rem(member_rank - shift + member_count, member_count) * local_count,
                local_count, 0,
            )
            for shift in range(member_count)
        ],
        axis=0,
    )
    contract = (((0,), (0,)), ((), ()))
    update_sum = lax.dot_general(own_cols, anomaly_all, contract, preferred_element_type=jnp.float32)
    new_log_perm = log_perm + update_sum.reshape(log_perm.shape)
    return (new_log_perm, pressure, saturation, well_rates)


def solution(mesh):
    return jax.shard_map(
        per_device,
        mesh=mesh,
        in_specs=(
            P("member", None, "tile", None),
            P(None, "tile", None),
            P(None, "tile", None),
            P(None, "tile", None),
            P(None, "tile", None),
            P(),
            P("tile"),
            P("tile"),
            P("tile"),
            P(),
            P(),
            P("member", None),
        ),
        out_specs=(
            P("member", None, "tile", None),
            P("member", None, "tile", None),
            P("member", None, "tile", None),
            P("member", "tile"),
        ),
        check_vma=False,
    )
```

```python
import functools

import jax
import jax.numpy as jnp
from jax import lax
from jax.experimental import pallas as pl
from jax.experimental.pallas import tpu as pltpu
from jax.sharding import PartitionSpec as P

SWEEPS = 2


VERTICAL = 0.5
VISCOSITY_RATIO = 2.0
STEP_COEF = 0.1
INFLATION = 4.0


def extended_2(block, sides, width):
    for axis, dim in sides:
        count = lax.axis_size(axis)
        forward = [(i, i + 1) for i in range(count - 1)]
        backward = [(target, source) for source, target in forward]
        low = lax.ppermute(
            lax.slice_in_dim(block, block.shape[dim] - width, None, axis=dim), axis, forward
        )
        high = lax.ppermute(lax.slice_in_dim(block, 0, width, axis=dim), axis, backward)
        block = jnp.concatenate([low, block, high], axis=dim)
    return block


def harmonic(lower_val, upper_val):
    return 2.0 * lower_val * upper_val / (lower_val + upper_val)


def pad_face(values_in, along_dim, before):
    widths = [(0, 0)] * values_in.ndim
    widths[along_dim] = (1, 0) if before else (0, 1)
    return jnp.pad(values_in, widths)


def slide_by(values_in, along_dim, before):
    extent = values_in.shape[along_dim]
    if before:
        remain = lax.slice_in_dim(values_in, 0, extent - 1, axis=along_dim)
    else:
        remain = lax.slice_in_dim(values_in, 1, extent, axis=along_dim)
    return pad_face(remain, along_dim, before)


def face_terms(permeab, inside):
    face_x = (
        harmonic(permeab[:, :, :-1, :], permeab[:, :, 1:, :]) * (inside[:-1] * inside[1:])[:, None]
    )
    face_y = harmonic(permeab[:, :, :, :-1], permeab[:, :, :, 1:])
    face_z = VERTICAL * harmonic(permeab[:, :-1], permeab[:, 1:])
    return (face_x, face_y, face_z)


def neighbours(face_sets, values_in):
    flow_sum = 0.0
    weight_sum = 0.0
    for faces_dim, along_dim in zip(face_sets, (2, 3, 1)):
        lower = pad_face(faces_dim, along_dim, True)
        upper = pad_face(faces_dim, along_dim, False)
        flow_sum = (
            flow_sum
            + lower * slide_by(values_in, along_dim, True)
            + upper * slide_by(values_in, along_dim, False)
        )
        weight_sum = weight_sum + lower + upper
    return (flow_sum, weight_sum)


def jacobi(pressure, baseline, storage_term, face_sets):
    flow_sum, weight_sum = neighbours(face_sets, pressure)
    return (baseline + flow_sum) / (storage_term + weight_sum)


def water_frac(values_in):
    squared = values_in * values_in
    return squared / (squared + VISCOSITY_RATIO * (1.0 - values_in) * (1.0 - values_in))


def transport(pressure, saturation, face_sets):
    fraction = water_frac(saturation)
    change = 0.0
    for faces_dim, along_dim in zip(face_sets, (2, 3, 1)):
        extent = pressure.shape[along_dim]
        lower_press = lax.slice_in_dim(pressure, 0, extent - 1, axis=along_dim)
        upper_press = lax.slice_in_dim(pressure, 1, extent, axis=along_dim)
        lower_frac = lax.slice_in_dim(fraction, 0, extent - 1, axis=along_dim)
        upper_frac = lax.slice_in_dim(fraction, 1, extent, axis=along_dim)
        velocity = faces_dim * (lower_press - upper_press)
        carried = velocity * jnp.where(velocity > 0, lower_frac, upper_frac)
        change = change + pad_face(carried, along_dim, True) - pad_face(carried, along_dim, False)
    return saturation + STEP_COEF * change


def solve_spd(gram_matrix, cross_matrix):
    factor = lax.linalg.cholesky(
        gram_matrix + jnp.eye(gram_matrix.shape[0], dtype=jnp.float32), symmetrize_input=False
    )
    halfway = lax.linalg.triangular_solve(factor, cross_matrix, left_side=True, lower=True)
    return lax.linalg.triangular_solve(
        factor, halfway, left_side=True, lower=True, transpose_a=True
    )


def trim_rim(values_in, rim_cut):
    return values_in[:, :, rim_cut : values_in.shape[2] - rim_cut, :]


def exchange_kernel(member_count, part_ref, full_ref,
                    recv_a, own_blk, recv_m, send_a, recv_a_sem, send_m, recv_m_sem, send_t, recv_t_sem):
    tile_count = part_ref.shape[0]
    me_t = lax.axis_index("tile")
    me_m = lax.axis_index("member")
    mesh_ids = pl.DeviceIdType.MESH

    barrier = pltpu.get_barrier_semaphore()

    def greet_tile(k, carry):
        pl.semaphore_signal(
            barrier, 1, device_id=(lax.rem(me_t + k, tile_count), me_m), device_id_type=mesh_ids
        )
        return carry

    def greet_member(k, carry):
        pl.semaphore_signal(
            barrier, 1, device_id=(me_t, lax.rem(me_m + k, member_count)), device_id_type=mesh_ids
        )
        return carry

    lax.fori_loop(1, tile_count, greet_tile, 0)
    lax.fori_loop(1, member_count, greet_member, 0)
    pl.semaphore_wait(barrier, tile_count + member_count - 2)

    def copy_a(dst_t, src_t):
        return pltpu.make_async_remote_copy(
            src_ref=part_ref.at[dst_t], dst_ref=recv_a.at[src_t],
            send_sem=send_a.at[dst_t], recv_sem=recv_a_sem.at[src_t],
            device_id=(dst_t, me_m), device_id_type=mesh_ids,
        )

    def start_a(k, carry):
        copy_a(lax.rem(me_t + k, tile_count), me_t).start()
        return carry

    lax.fori_loop(1, tile_count, start_a, 0)

    def wait_a(k, acc):
        src_t = lax.rem(me_t + k, tile_count)
        copy_a(me_t, src_t).wait_recv()
        return acc + recv_a[src_t]

    acc = lax.fori_loop(1, tile_count, wait_a, part_ref[me_t])

    def wait_a_send(k, carry):
        copy_a(lax.rem(me_t + k, tile_count), me_t).wait_send()
        return carry

    lax.fori_loop(1, tile_count, wait_a_send, 0)

    groups = part_ref.shape[2] // member_count
    lane_ids = lax.broadcasted_iota(jnp.int32, acc.shape, 1)
    for q in range(member_count):
        moved = pltpu.roll(acc, lax.rem((me_m - q + member_count) * groups, part_ref.shape[2]), 1)
        own_blk[pl.ds(q, acc.shape[0], stride=member_count), :] = jnp.where(
            lane_ids // groups == me_m, moved, 0.0
        )
    acc = own_blk[...]

    def copy_m(dst_m, src_m):
        return pltpu.make_async_remote_copy(
            src_ref=own_blk, dst_ref=recv_m.at[src_m],
            send_sem=send_m.at[dst_m], recv_sem=recv_m_sem.at[src_m],
            device_id=(me_t, dst_m), device_id_type=mesh_ids,
        )

    def start_m(k, carry):
        copy_m(lax.rem(me_m + k, member_count), me_m).start()
        return carry

    lax.fori_loop(1, member_count, start_m, 0)

    def wait_m(k, total):
        src_m = lax.rem(me_m + k, member_count)
        copy_m(me_m, src_m).wait_recv()
        return total + recv_m[src_m]

    full_ref[me_t] = lax.fori_loop(1, member_count, wait_m, acc)

    def wait_m_send(k, carry):
        copy_m(lax.rem(me_m + k, member_count), me_m).wait_send()
        return carry

    lax.fori_loop(1, member_count, wait_m_send, 0)

    def copy_t(dst_t, src_t):
        return pltpu.make_async_remote_copy(
            src_ref=full_ref.at[src_t], dst_ref=full_ref.at[src_t],
            send_sem=send_t.at[dst_t], recv_sem=recv_t_sem.at[src_t],
            device_id=(dst_t, me_m), device_id_type=mesh_ids,
        )

    def start_t(k, carry):
        copy_t(lax.rem(me_t + k, tile_count), me_t).start()
        return carry

    lax.fori_loop(1, tile_count, start_t, 0)

    def wait_t(k, carry):
        copy_t(me_t, lax.rem(me_t + k, tile_count)).wait_recv()
        return carry

    lax.fori_loop(1, tile_count, wait_t, 0)

    def wait_t_send(k, carry):
        copy_t(lax.rem(me_t + k, tile_count), me_t).wait_send()
        return carry

    lax.fori_loop(1, tile_count, wait_t_send, 0)


def stencil_kernel(rim, lp_low, lp_mid, lp_high, f_low, f_mid, f_high, inside_ref,
                   press_ref, sat_ref, mob_ref):
    inside = inside_ref[...]
    permeab = jnp.exp(jnp.concatenate([lp_low[...], lp_mid[...], lp_high[...]], axis=2))
    face_sets = face_terms(permeab, inside)
    fields = jnp.concatenate([f_low[...], f_mid[...], f_high[...]], axis=2)
    press_ext = fields[0]
    sat_ext = fields[1]
    source_ext = fields[2]
    storage_ext = fields[3]
    baseline = (source_ext + storage_ext * press_ext)[None]
    storage_term = jnp.where(inside[None, :, None] > 0.0, storage_ext, 1.0)[None]
    pressure = jnp.broadcast_to(press_ext[None], permeab.shape)
    for sweep_idx in range(SWEEPS):
        pressure = jacobi(pressure, baseline, storage_term, face_sets)
    saturation = trim_rim(transport(pressure, sat_ext[None], face_sets), rim)
    press_ref[...] = trim_rim(pressure, rim)
    sat_ref[...] = saturation
    mob_ref[...] = trim_rim(permeab, rim) * water_frac(saturation)


def stencil(lp_parts, field_parts, inside, rim):
    members, layers, out_rows, depth = lp_parts[1].shape
    block = 4

    def member_block(part):
        return pl.BlockSpec((block,) + part.shape[1:], lambda i: (i, 0, 0, 0))

    def whole(part):
        return pl.BlockSpec(part.shape, lambda i: (0, 0, 0, 0))

    out_spec = pl.BlockSpec((block, layers, out_rows, depth), lambda i: (i, 0, 0, 0))
    out_shape = jax.ShapeDtypeStruct((members, layers, out_rows, depth), jnp.float32)
    return pl.pallas_call(
        functools.partial(stencil_kernel, rim),
        grid=(members // block,),
        in_specs=[member_block(p) for p in lp_parts]
        + [whole(p) for p in field_parts]
        + [pl.BlockSpec(inside.shape, lambda i: (0,))],
        out_specs=[out_spec, out_spec, out_spec],
        out_shape=[out_shape, out_shape, out_shape],
    )(*lp_parts, *field_parts, inside)


def halo_kernel(out_ref, in_ref, send_sem, recv_sem):
    tile_count = lax.axis_size("tile")
    me_t = lax.axis_index("tile")
    me_m = lax.axis_index("member")
    mesh_ids = pl.DeviceIdType.MESH
    left = lax.rem(me_t + tile_count - 1, tile_count)
    right = lax.rem(me_t + 1, tile_count)
    barrier = pltpu.get_barrier_semaphore()
    for peer in (left, right):
        pl.semaphore_signal(barrier, 1, device_id=(peer, me_m), device_id_type=mesh_ids)
    pl.semaphore_wait(barrier, 2)
    to_right = pltpu.make_async_remote_copy(
        src_ref=out_ref.at[1], dst_ref=in_ref.at[0], send_sem=send_sem.at[1],
        recv_sem=recv_sem.at[0], device_id=(right, me_m), device_id_type=mesh_ids,
    )
    to_left = pltpu.make_async_remote_copy(
        src_ref=out_ref.at[0], dst_ref=in_ref.at[1], send_sem=send_sem.at[0],
        recv_sem=recv_sem.at[1], device_id=(left, me_m), device_id_type=mesh_ids,
    )
    to_right.start()
    to_left.start()
    to_right.wait()
    to_left.wait()


def halo_exchange(outgoing):
    vmem = pl.BlockSpec(memory_space=pltpu.VMEM)
    return pl.pallas_call(
        halo_kernel,
        out_shape=jax.ShapeDtypeStruct(outgoing.shape, outgoing.dtype),
        in_specs=[vmem],
        out_specs=vmem,
        scratch_shapes=[pltpu.SemaphoreType.DMA((2,)), pltpu.SemaphoreType.DMA((2,))],
        compiler_params=pltpu.CompilerParams(collective_id=1, has_side_effects=True),
    )(outgoing)


def rates_exchange(pieces, member_count):
    tile_count, rows, lanes = pieces.shape
    vmem = pl.BlockSpec(memory_space=pltpu.VMEM)
    return pl.pallas_call(
        functools.partial(exchange_kernel, member_count),
        out_shape=jax.ShapeDtypeStruct((tile_count, rows * member_count, lanes), jnp.float32),
        in_specs=[vmem],
        out_specs=vmem,
        scratch_shapes=[
            pltpu.VMEM((tile_count, rows, lanes), jnp.float32),
            pltpu.VMEM((rows * member_count, lanes), jnp.float32),
            pltpu.VMEM((member_count, rows * member_count, lanes), jnp.float32),
            pltpu.SemaphoreType.DMA((tile_count,)),
            pltpu.SemaphoreType.DMA((tile_count,)),
            pltpu.SemaphoreType.DMA((member_count,)),
            pltpu.SemaphoreType.DMA((member_count,)),
            pltpu.SemaphoreType.DMA((tile_count,)),
            pltpu.SemaphoreType.DMA((tile_count,)),
        ],
        compiler_params=pltpu.CompilerParams(collective_id=0, has_side_effects=True),
    )(pieces)


def per_device(
    log_perm,
    start_pressure,
    start_sat,
    source,
    storage,
    well_press,
    perf_cell,
    perf_well,
    perf_count,
    observed,
    obs_var,
    obs_noise,
):
    local_count, layers, strip_width, strip_depth = log_perm.shape
    tile_count = lax.axis_size("tile")
    members = local_count * lax.axis_size("member")
    well_count = well_press.shape[0]
    well_share = well_count // tile_count
    tile_rank = lax.axis_index("tile")
    member_rank = lax.axis_index("member")
    rim = SWEEPS + 1
    fields = jnp.stack([start_pressure, start_sat, source, storage])
    halo_rows = local_count * layers * rim + fields.shape[0] * layers * rim

    def rim_rows(first):
        return jnp.concatenate(
            [
                lax.slice_in_dim(log_perm, first, first + rim, axis=2).reshape(-1, strip_depth),
                lax.slice_in_dim(fields, first, first + rim, axis=2).reshape(-1, strip_depth),
            ]
        )

    outgoing = jnp.stack([rim_rows(0), rim_rows(strip_width - rim)])
    incoming = halo_exchange(outgoing)
    incoming, log_perm_after = lax.optimization_barrier((incoming, log_perm))
    lp_count = local_count * layers * rim

    def unpack(side):
        lp_part = incoming[side, :lp_count].reshape(local_count, layers, rim, strip_depth)
        field_part = incoming[side, lp_count:].reshape(fields.shape[0], layers, rim, strip_depth)
        return lp_part, field_part

    low_lp, low_fields = unpack(0)
    high_lp, high_fields = unpack(1)
    column = tile_rank * strip_width - rim + jnp.arange(strip_width + 2 * rim, dtype=jnp.int32)
    inside = ((column >= 0) & (column < strip_width * tile_count)).astype(jnp.float32)
    pressure, saturation, mobility = stencil(
        (low_lp, log_perm, high_lp), (low_fields, fields, high_fields), inside, rim
    )
    cell_count = layers * strip_width * strip_depth
    plane_rows = layers * strip_width
    cell_row = perf_cell // strip_depth
    cell_col = lax.rem(perf_cell, strip_depth)
    col_pick = (jnp.arange(strip_depth, dtype=jnp.int32)[:, None] == cell_col[None, :]).astype(
        jnp.float32
    )
    row_pick = jnp.arange(plane_rows, dtype=jnp.int32)[:, None] == cell_row[None, :]

    def pick_cells(values_in):
        by_col = jnp.dot(
            values_in.reshape(local_count * plane_rows, strip_depth), col_pick,
            precision=lax.Precision.HIGHEST, preferred_element_type=jnp.float32,
        ).reshape(local_count, plane_rows, -1)
        return jnp.sum(jnp.where(row_pick[None], by_col, 0.0), axis=1)

    perf_mob = pick_cells(mobility)
    perf_press = pick_cells(pressure)
    selector = (perf_well[:, None] == jnp.arange(well_count, dtype=jnp.int32)[None, :]).astype(
        jnp.float32
    )
    perf_bhp = jnp.dot(selector, well_press, precision=lax.Precision.HIGHEST)
    live_mask = (jnp.arange(perf_cell.shape[0], dtype=jnp.int32) < perf_count[0]).astype(
        jnp.float32
    )
    perf_terms = perf_mob * (perf_press - perf_bhp[None]) * live_mask[None]
    member_root = (members - 1) ** 0.5
    spread = jnp.sqrt(INFLATION * obs_var)
    member_count = lax.axis_size("member")
    contract_slots = (((0,), (1,)), ((), ()))
    pieces = lax.dot_general(
        selector, perf_terms, contract_slots, precision=lax.Precision.HIGHEST,
        preferred_element_type=jnp.float32,
    ).reshape(tile_count, well_share * local_count // 128, 128)
    full = rates_exchange(pieces, member_count)
    own_block = lax.dynamic_index_in_dim(full, tile_rank, 0, keepdims=False)
    well_rates = lax.dynamic_slice_in_dim(own_block, member_rank * local_count, local_count, 1).T
    rates_t = full.reshape(well_count, members)
    mean_rate = jnp.sum(rates_t, 1) / members
    scaled_t = (rates_t - mean_rate[:, None]) / (spread * member_root)[:, None]
    rates_own_t = lax.dynamic_slice_in_dim(rates_t, member_rank * local_count, local_count, 1)
    innov_own_t = (observed[:, None] - rates_own_t) / spread[:, None] + obs_noise.T
    contract_wells = (((0,), (0,)), ((), ()))
    gram_matrix = lax.dot_general(
        scaled_t, scaled_t, contract_wells, precision=lax.Precision.HIGHEST,
        preferred_element_type=jnp.float32,
    )
    cross_matrix = lax.dot_general(
        scaled_t, innov_own_t, contract_wells, precision=lax.Precision.HIGHEST,
        preferred_element_type=jnp.float32,
    )
    weights_low = solve_spd(gram_matrix, cross_matrix).astype(jnp.bfloat16)
    anomaly = (log_perm_after / member_root).astype(jnp.bfloat16).transpose(1, 2, 0, 3)
    anomaly_parts = [anomaly]
    for shift in range(1, member_count):
        pairs = [(i, (i + shift) % member_count) for i in range(member_count)]
        anomaly_parts.append(lax.ppermute(anomaly, "member", pairs))
    anomaly_all = jnp.concatenate(anomaly_parts, axis=2)
    own_cols = jnp.concatenate(
        [
            lax.dynamic_slice_in_dim(
                weights_low, lax.rem(member_rank - shift + member_count, member_count) * local_count,
                local_count, 0,
            )
            for shift in range(member_count)
        ],
        axis=0,
    )
    contract = (((0,), (2,)), ((), ()))
    update_sum = lax.dot_general(own_cols, anomaly_all, contract, preferred_element_type=jnp.float32)
    new_log_perm = log_perm + update_sum
    return (new_log_perm, pressure, saturation, well_rates)


def solution(mesh):
    return jax.shard_map(
        per_device,
        mesh=mesh,
        in_specs=(
            P("member", None, "tile", None),
            P(None, "tile", None),
            P(None, "tile", None),
            P(None, "tile", None),
            P(None, "tile", None),
            P(),
            P("tile"),
            P("tile"),
            P("tile"),
            P(),
            P(),
            P("member", None),
        ),
        out_specs=(
            P("member", None, "tile", None),
            P("member", None, "tile", None),
            P("member", None, "tile", None),
            P("member", "tile"),
        ),
        check_vma=False,
    )
```

```python
import functools

import jax
import jax.numpy as jnp
from jax import lax
from jax.experimental import pallas as pl
from jax.experimental.pallas import tpu as pltpu
from jax.sharding import PartitionSpec as P

SWEEPS = 2


VERTICAL = 0.5
VISCOSITY_RATIO = 2.0
STEP_COEF = 0.1
INFLATION = 4.0


def extended_2(block, sides, width):
    for axis, dim in sides:
        count = lax.axis_size(axis)
        forward = [(i, i + 1) for i in range(count - 1)]
        backward = [(target, source) for source, target in forward]
        low = lax.ppermute(
            lax.slice_in_dim(block, block.shape[dim] - width, None, axis=dim), axis, forward
        )
        high = lax.ppermute(lax.slice_in_dim(block, 0, width, axis=dim), axis, backward)
        block = jnp.concatenate([low, block, high], axis=dim)
    return block


def harmonic(lower_val, upper_val):
    return 2.0 * lower_val * upper_val / (lower_val + upper_val)


def pad_face(values_in, along_dim, before):
    widths = [(0, 0)] * values_in.ndim
    widths[along_dim] = (1, 0) if before else (0, 1)
    return jnp.pad(values_in, widths)


def slide_by(values_in, along_dim, before):
    extent = values_in.shape[along_dim]
    if before:
        remain = lax.slice_in_dim(values_in, 0, extent - 1, axis=along_dim)
    else:
        remain = lax.slice_in_dim(values_in, 1, extent, axis=along_dim)
    return pad_face(remain, along_dim, before)


def face_terms(permeab, inside):
    face_x = (
        harmonic(permeab[:, :, :-1, :], permeab[:, :, 1:, :]) * (inside[:-1] * inside[1:])[:, None]
    )
    face_y = harmonic(permeab[:, :, :, :-1], permeab[:, :, :, 1:])
    face_z = VERTICAL * harmonic(permeab[:, :-1], permeab[:, 1:])
    return (face_x, face_y, face_z)


def neighbours(face_sets, values_in):
    flow_sum = 0.0
    weight_sum = 0.0
    for faces_dim, along_dim in zip(face_sets, (2, 3, 1)):
        lower = pad_face(faces_dim, along_dim, True)
        upper = pad_face(faces_dim, along_dim, False)
        flow_sum = (
            flow_sum
            + lower * slide_by(values_in, along_dim, True)
            + upper * slide_by(values_in, along_dim, False)
        )
        weight_sum = weight_sum + lower + upper
    return (flow_sum, weight_sum)


def jacobi(pressure, baseline, storage_term, face_sets):
    flow_sum, weight_sum = neighbours(face_sets, pressure)
    return (baseline + flow_sum) / (storage_term + weight_sum)


def water_frac(values_in):
    squared = values_in * values_in
    return squared / (squared + VISCOSITY_RATIO * (1.0 - values_in) * (1.0 - values_in))


def transport(pressure, saturation, face_sets):
    fraction = water_frac(saturation)
    change = 0.0
    for faces_dim, along_dim in zip(face_sets, (2, 3, 1)):
        extent = pressure.shape[along_dim]
        lower_press = lax.slice_in_dim(pressure, 0, extent - 1, axis=along_dim)
        upper_press = lax.slice_in_dim(pressure, 1, extent, axis=along_dim)
        lower_frac = lax.slice_in_dim(fraction, 0, extent - 1, axis=along_dim)
        upper_frac = lax.slice_in_dim(fraction, 1, extent, axis=along_dim)
        velocity = faces_dim * (lower_press - upper_press)
        carried = velocity * jnp.where(velocity > 0, lower_frac, upper_frac)
        change = change + pad_face(carried, along_dim, True) - pad_face(carried, along_dim, False)
    return saturation + STEP_COEF * change


def solve_spd(gram_matrix, cross_matrix):
    factor = lax.linalg.cholesky(
        gram_matrix + jnp.eye(gram_matrix.shape[0], dtype=jnp.float32), symmetrize_input=False
    )
    halfway = lax.linalg.triangular_solve(factor, cross_matrix, left_side=True, lower=True)
    return lax.linalg.triangular_solve(
        factor, halfway, left_side=True, lower=True, transpose_a=True
    )


def trim_rim(values_in, rim_cut):
    return values_in[:, :, rim_cut : values_in.shape[2] - rim_cut, :]


def exchange_kernel(member_count, part_ref, full_ref,
                    recv_a, own_blk, recv_m, send_a, recv_a_sem, send_m, recv_m_sem, send_t, recv_t_sem):
    tile_count = part_ref.shape[0]
    me_t = lax.axis_index("tile")
    me_m = lax.axis_index("member")
    mesh_ids = pl.DeviceIdType.MESH

    barrier = pltpu.get_barrier_semaphore()

    def greet_tile(k, carry):
        pl.semaphore_signal(
            barrier, 1, device_id=(lax.rem(me_t + k, tile_count), me_m), device_id_type=mesh_ids
        )
        return carry

    def greet_member(k, carry):
        pl.semaphore_signal(
            barrier, 1, device_id=(me_t, lax.rem(me_m + k, member_count)), device_id_type=mesh_ids
        )
        return carry

    lax.fori_loop(1, tile_count, greet_tile, 0)
    lax.fori_loop(1, member_count, greet_member, 0)
    pl.semaphore_wait(barrier, tile_count + member_count - 2)

    def copy_a(dst_t, src_t):
        return pltpu.make_async_remote_copy(
            src_ref=part_ref.at[dst_t], dst_ref=recv_a.at[src_t],
            send_sem=send_a.at[dst_t], recv_sem=recv_a_sem.at[src_t],
            device_id=(dst_t, me_m), device_id_type=mesh_ids,
        )

    def start_a(k, carry):
        copy_a(lax.rem(me_t + k, tile_count), me_t).start()
        return carry

    lax.fori_loop(1, tile_count, start_a, 0)

    def wait_a(k, acc):
        src_t = lax.rem(me_t + k, tile_count)
        copy_a(me_t, src_t).wait_recv()
        return acc + recv_a[src_t]

    acc = lax.fori_loop(1, tile_count, wait_a, part_ref[me_t])

    def wait_a_send(k, carry):
        copy_a(lax.rem(me_t + k, tile_count), me_t).wait_send()
        return carry

    lax.fori_loop(1, tile_count, wait_a_send, 0)

    groups = part_ref.shape[2] // member_count
    lane_ids = lax.broadcasted_iota(jnp.int32, acc.shape, 1)
    for q in range(member_count):
        moved = pltpu.roll(acc, lax.rem((me_m - q + member_count) * groups, part_ref.shape[2]), 1)
        own_blk[pl.ds(q, acc.shape[0], stride=member_count), :] = jnp.where(
            lane_ids // groups == me_m, moved, 0.0
        )
    acc = own_blk[...]

    def copy_m(dst_m, src_m):
        return pltpu.make_async_remote_copy(
            src_ref=own_blk, dst_ref=recv_m.at[src_m],
            send_sem=send_m.at[dst_m], recv_sem=recv_m_sem.at[src_m],
            device_id=(me_t, dst_m), device_id_type=mesh_ids,
        )

    def start_m(k, carry):
        copy_m(lax.rem(me_m + k, member_count), me_m).start()
        return carry

    lax.fori_loop(1, member_count, start_m, 0)

    def wait_m(k, total):
        src_m = lax.rem(me_m + k, member_count)
        copy_m(me_m, src_m).wait_recv()
        return total + recv_m[src_m]

    full_ref[me_t] = lax.fori_loop(1, member_count, wait_m, acc)

    def wait_m_send(k, carry):
        copy_m(lax.rem(me_m + k, member_count), me_m).wait_send()
        return carry

    lax.fori_loop(1, member_count, wait_m_send, 0)

    def copy_t(dst_t, src_t):
        return pltpu.make_async_remote_copy(
            src_ref=full_ref.at[src_t], dst_ref=full_ref.at[src_t],
            send_sem=send_t.at[dst_t], recv_sem=recv_t_sem.at[src_t],
            device_id=(dst_t, me_m), device_id_type=mesh_ids,
        )

    def start_t(k, carry):
        copy_t(lax.rem(me_t + k, tile_count), me_t).start()
        return carry

    lax.fori_loop(1, tile_count, start_t, 0)

    def wait_t(k, carry):
        copy_t(me_t, lax.rem(me_t + k, tile_count)).wait_recv()
        return carry

    lax.fori_loop(1, tile_count, wait_t, 0)

    def wait_t_send(k, carry):
        copy_t(lax.rem(me_t + k, tile_count), me_t).wait_send()
        return carry

    lax.fori_loop(1, tile_count, wait_t_send, 0)


def stencil_kernel(rim, halo_ref, lp_mid, f_mid, inside_ref, press_ref, sat_ref, mob_ref):
    inside = inside_ref[...]
    block, layers = lp_mid.shape[0], lp_mid.shape[1]
    field_count = f_mid.shape[0]
    lp_rows = pl.ds(pl.multiple_of(pl.program_id(0) * block * layers, block * layers), block * layers)
    field_first = halo_ref.shape[2] - field_count * layers

    def halo_piece(side, rows, shape):
        return [halo_ref[side, r, rows, :].reshape(shape) for r in range(rim)]

    lp_shape = (block, layers, 1, lp_mid.shape[3])
    f_shape = (field_count, layers, 1, f_mid.shape[3])
    f_rows = pl.ds(field_first, field_count * layers)
    permeab = jnp.exp(jnp.concatenate(
        halo_piece(0, lp_rows, lp_shape) + [lp_mid[...]] + halo_piece(1, lp_rows, lp_shape), axis=2
    ))
    face_sets = face_terms(permeab, inside)
    fields = jnp.concatenate(
        halo_piece(0, f_rows, f_shape) + [f_mid[...]] + halo_piece(1, f_rows, f_shape), axis=2
    )
    press_ext = fields[0]
    sat_ext = fields[1]
    source_ext = fields[2]
    storage_ext = fields[3]
    baseline = (source_ext + storage_ext * press_ext)[None]
    storage_term = jnp.where(inside[None, :, None] > 0.0, storage_ext, 1.0)[None]
    pressure = jnp.broadcast_to(press_ext[None], permeab.shape)
    for sweep_idx in range(SWEEPS):
        pressure = jacobi(pressure, baseline, storage_term, face_sets)
    saturation = trim_rim(transport(pressure, sat_ext[None], face_sets), rim)
    press_ref[...] = trim_rim(pressure, rim)
    sat_ref[...] = saturation
    mob_ref[...] = trim_rim(permeab, rim) * water_frac(saturation)


def stencil(halo, log_perm, fields, inside, rim):
    members, layers, out_rows, depth = log_perm.shape
    block = 4

    def whole(part):
        return pl.BlockSpec(part.shape, lambda i: (0,) * part.ndim)

    out_spec = pl.BlockSpec((block, layers, out_rows, depth), lambda i: (i, 0, 0, 0))
    out_shape = jax.ShapeDtypeStruct((members, layers, out_rows, depth), jnp.float32)
    return pl.pallas_call(
        functools.partial(stencil_kernel, rim),
        grid=(members // block,),
        in_specs=[
            whole(halo),
            pl.BlockSpec((block, layers, out_rows, depth), lambda i: (i, 0, 0, 0)),
            whole(fields),
            whole(inside),
        ],
        out_specs=[out_spec, out_spec, out_spec],
        out_shape=[out_shape, out_shape, out_shape],
    )(halo, log_perm, fields, inside)


def halo_kernel(out_ref, in_ref, send_sem, recv_sem):
    tile_count = lax.axis_size("tile")
    me_t = lax.axis_index("tile")
    me_m = lax.axis_index("member")
    mesh_ids = pl.DeviceIdType.MESH
    left = lax.rem(me_t + tile_count - 1, tile_count)
    right = lax.rem(me_t + 1, tile_count)
    barrier = pltpu.get_barrier_semaphore()
    for peer in (left, right):
        pl.semaphore_signal(barrier, 1, device_id=(peer, me_m), device_id_type=mesh_ids)
    pl.semaphore_wait(barrier, 2)
    to_right = pltpu.make_async_remote_copy(
        src_ref=out_ref.at[1], dst_ref=in_ref.at[0], send_sem=send_sem.at[1],
        recv_sem=recv_sem.at[0], device_id=(right, me_m), device_id_type=mesh_ids,
    )
    to_left = pltpu.make_async_remote_copy(
        src_ref=out_ref.at[0], dst_ref=in_ref.at[1], send_sem=send_sem.at[0],
        recv_sem=recv_sem.at[1], device_id=(left, me_m), device_id_type=mesh_ids,
    )
    to_right.start()
    to_left.start()
    to_right.wait()
    to_left.wait()


def halo_exchange(outgoing):
    vmem = pl.BlockSpec(memory_space=pltpu.VMEM)
    return pl.pallas_call(
        halo_kernel,
        out_shape=jax.ShapeDtypeStruct(outgoing.shape, outgoing.dtype),
        in_specs=[vmem],
        out_specs=vmem,
        scratch_shapes=[pltpu.SemaphoreType.DMA((2,)), pltpu.SemaphoreType.DMA((2,))],
        compiler_params=pltpu.CompilerParams(collective_id=1, has_side_effects=True),
    )(outgoing)


def rates_exchange(pieces, member_count):
    tile_count, rows, lanes = pieces.shape
    vmem = pl.BlockSpec(memory_space=pltpu.VMEM)
    return pl.pallas_call(
        functools.partial(exchange_kernel, member_count),
        out_shape=jax.ShapeDtypeStruct((tile_count, rows * member_count, lanes), jnp.float32),
        in_specs=[vmem],
        out_specs=vmem,
        scratch_shapes=[
            pltpu.VMEM((tile_count, rows, lanes), jnp.float32),
            pltpu.VMEM((rows * member_count, lanes), jnp.float32),
            pltpu.VMEM((member_count, rows * member_count, lanes), jnp.float32),
            pltpu.SemaphoreType.DMA((tile_count,)),
            pltpu.SemaphoreType.DMA((tile_count,)),
            pltpu.SemaphoreType.DMA((member_count,)),
            pltpu.SemaphoreType.DMA((member_count,)),
            pltpu.SemaphoreType.DMA((tile_count,)),
            pltpu.SemaphoreType.DMA((tile_count,)),
        ],
        compiler_params=pltpu.CompilerParams(collective_id=0, has_side_effects=True),
    )(pieces)


def per_device(
    log_perm,
    start_pressure,
    start_sat,
    source,
    storage,
    well_press,
    perf_cell,
    perf_well,
    perf_count,
    observed,
    obs_var,
    obs_noise,
):
    local_count, layers, strip_width, strip_depth = log_perm.shape
    tile_count = lax.axis_size("tile")
    members = local_count * lax.axis_size("member")
    well_count = well_press.shape[0]
    well_share = well_count // tile_count
    tile_rank = lax.axis_index("tile")
    member_rank = lax.axis_index("member")
    rim = SWEEPS + 1
    fields = jnp.stack([start_pressure, start_sat, source, storage])
    halo_rows = local_count * layers * rim + fields.shape[0] * layers * rim

    def rim_rows(first):
        return jnp.concatenate(
            [
                lax.slice_in_dim(log_perm, first, first + rim, axis=2).transpose(2, 0, 1, 3),
                lax.slice_in_dim(fields, first, first + rim, axis=2).transpose(2, 0, 1, 3),
            ],
            axis=1,
        ).reshape(-1, strip_depth)

    outgoing = jnp.stack([rim_rows(0), rim_rows(strip_width - rim)])
    incoming = halo_exchange(outgoing)
    incoming, log_perm_after = lax.optimization_barrier((incoming, log_perm))
    halo = incoming.reshape(2, rim, -1, strip_depth)
    column = tile_rank * strip_width - rim + jnp.arange(strip_width + 2 * rim, dtype=jnp.int32)
    inside = ((column >= 0) & (column < strip_width * tile_count)).astype(jnp.float32)
    pressure, saturation, mobility = stencil(halo, log_perm, fields, inside, rim)
    cell_count = layers * strip_width * strip_depth
    plane_rows = layers * strip_width
    cell_row = perf_cell // strip_depth
    cell_col = lax.rem(perf_cell, strip_depth)
    col_pick = (jnp.arange(strip_depth, dtype=jnp.int32)[:, None] == cell_col[None, :]).astype(
        jnp.float32
    )
    row_pick = jnp.arange(plane_rows, dtype=jnp.int32)[:, None] == cell_row[None, :]

    def pick_cells(values_in):
        by_col = jnp.dot(
            values_in.reshape(local_count * plane_rows, strip_depth), col_pick,
            precision=lax.Precision.HIGHEST, preferred_element_type=jnp.float32,
        ).reshape(local_count, plane_rows, -1)
        return jnp.sum(jnp.where(row_pick[None], by_col, 0.0), axis=1)

    perf_mob = pick_cells(mobility)
    perf_press = pick_cells(pressure)
    selector = (perf_well[:, None] == jnp.arange(well_count, dtype=jnp.int32)[None, :]).astype(
        jnp.float32
    )
    perf_bhp = jnp.dot(selector, well_press, precision=lax.Precision.HIGHEST)
    live_mask = (jnp.arange(perf_cell.shape[0], dtype=jnp.int32) < perf_count[0]).astype(
        jnp.float32
    )
    perf_terms = perf_mob * (perf_press - perf_bhp[None]) * live_mask[None]
    member_root = (members - 1) ** 0.5
    spread = jnp.sqrt(INFLATION * obs_var)
    member_count = lax.axis_size("member")
    contract_slots = (((0,), (1,)), ((), ()))
    pieces = lax.dot_general(
        selector, perf_terms, contract_slots, precision=lax.Precision.HIGHEST,
        preferred_element_type=jnp.float32,
    ).reshape(tile_count, well_share * local_count // 128, 128)
    full = rates_exchange(pieces, member_count)
    own_block = lax.dynamic_index_in_dim(full, tile_rank, 0, keepdims=False)
    well_rates = lax.dynamic_slice_in_dim(own_block, member_rank * local_count, local_count, 1).T
    rates_t = full.reshape(well_count, members)
    mean_rate = jnp.sum(rates_t, 1) / members
    scaled_t = (rates_t - mean_rate[:, None]) / (spread * member_root)[:, None]
    rates_own_t = lax.dynamic_slice_in_dim(rates_t, member_rank * local_count, local_count, 1)
    innov_own_t = (observed[:, None] - rates_own_t) / spread[:, None] + obs_noise.T
    contract_wells = (((0,), (0,)), ((), ()))
    gram_matrix = lax.dot_general(
        scaled_t, scaled_t, contract_wells, precision=lax.Precision.HIGHEST,
        preferred_element_type=jnp.float32,
    )
    cross_matrix = lax.dot_general(
        scaled_t, innov_own_t, contract_wells, precision=lax.Precision.HIGHEST,
        preferred_element_type=jnp.float32,
    )
    weights_low = solve_spd(gram_matrix, cross_matrix).astype(jnp.bfloat16)
    anomaly = (log_perm_after / member_root).astype(jnp.bfloat16).transpose(1, 2, 0, 3)
    anomaly_parts = [anomaly]
    for shift in range(1, member_count):
        pairs = [(i, (i + shift) % member_count) for i in range(member_count)]
        anomaly_parts.append(lax.ppermute(anomaly, "member", pairs))
    anomaly_all = jnp.concatenate(anomaly_parts, axis=2)
    own_cols = jnp.concatenate(
        [
            lax.dynamic_slice_in_dim(
                weights_low, lax.rem(member_rank - shift + member_count, member_count) * local_count,
                local_count, 0,
            )
            for shift in range(member_count)
        ],
        axis=0,
    )
    contract = (((0,), (2,)), ((), ()))
    update_sum = lax.dot_general(own_cols, anomaly_all, contract, preferred_element_type=jnp.float32)
    new_log_perm = log_perm + update_sum
    return (new_log_perm, pressure, saturation, well_rates)


def solution(mesh):
    return jax.shard_map(
        per_device,
        mesh=mesh,
        in_specs=(
            P("member", None, "tile", None),
            P(None, "tile", None),
            P(None, "tile", None),
            P(None, "tile", None),
            P(None, "tile", None),
            P(),
            P("tile"),
            P("tile"),
            P("tile"),
            P(),
            P(),
            P("member", None),
        ),
        out_specs=(
            P("member", None, "tile", None),
            P("member", None, "tile", None),
            P("member", None, "tile", None),
            P("member", "tile"),
        ),
        check_vma=False,
    )
```

```python
import functools

import jax
import jax.numpy as jnp
from jax import lax
from jax.experimental import pallas as pl
from jax.experimental.pallas import tpu as pltpu
from jax.sharding import PartitionSpec as P

SWEEPS = 2


VERTICAL = 0.5
VISCOSITY_RATIO = 2.0
STEP_COEF = 0.1
INFLATION = 4.0


def extended_2(block, sides, width):
    for axis, dim in sides:
        count = lax.axis_size(axis)
        forward = [(i, i + 1) for i in range(count - 1)]
        backward = [(target, source) for source, target in forward]
        low = lax.ppermute(
            lax.slice_in_dim(block, block.shape[dim] - width, None, axis=dim), axis, forward
        )
        high = lax.ppermute(lax.slice_in_dim(block, 0, width, axis=dim), axis, backward)
        block = jnp.concatenate([low, block, high], axis=dim)
    return block


def harmonic(lower_val, upper_val):
    return 2.0 * lower_val * upper_val / (lower_val + upper_val)


def pad_face(values_in, along_dim, before):
    widths = [(0, 0)] * values_in.ndim
    widths[along_dim] = (1, 0) if before else (0, 1)
    return jnp.pad(values_in, widths)


def slide_by(values_in, along_dim, before):
    extent = values_in.shape[along_dim]
    if before:
        remain = lax.slice_in_dim(values_in, 0, extent - 1, axis=along_dim)
    else:
        remain = lax.slice_in_dim(values_in, 1, extent, axis=along_dim)
    return pad_face(remain, along_dim, before)


def face_terms(permeab, inside):
    face_x = (
        harmonic(permeab[:, :, :-1, :], permeab[:, :, 1:, :]) * (inside[:-1] * inside[1:])[:, None]
    )
    face_y = harmonic(permeab[:, :, :, :-1], permeab[:, :, :, 1:])
    face_z = VERTICAL * harmonic(permeab[:, :-1], permeab[:, 1:])
    return (face_x, face_y, face_z)


def neighbours(face_sets, values_in):
    flow_sum = 0.0
    weight_sum = 0.0
    for faces_dim, along_dim in zip(face_sets, (2, 3, 1)):
        lower = pad_face(faces_dim, along_dim, True)
        upper = pad_face(faces_dim, along_dim, False)
        flow_sum = (
            flow_sum
            + lower * slide_by(values_in, along_dim, True)
            + upper * slide_by(values_in, along_dim, False)
        )
        weight_sum = weight_sum + lower + upper
    return (flow_sum, weight_sum)


def jacobi(pressure, baseline, storage_term, face_sets):
    flow_sum, weight_sum = neighbours(face_sets, pressure)
    return (baseline + flow_sum) / (storage_term + weight_sum)


def water_frac(values_in):
    squared = values_in * values_in
    return squared / (squared + VISCOSITY_RATIO * (1.0 - values_in) * (1.0 - values_in))


def transport(pressure, saturation, face_sets):
    fraction = water_frac(saturation)
    change = 0.0
    for faces_dim, along_dim in zip(face_sets, (2, 3, 1)):
        extent = pressure.shape[along_dim]
        lower_press = lax.slice_in_dim(pressure, 0, extent - 1, axis=along_dim)
        upper_press = lax.slice_in_dim(pressure, 1, extent, axis=along_dim)
        lower_frac = lax.slice_in_dim(fraction, 0, extent - 1, axis=along_dim)
        upper_frac = lax.slice_in_dim(fraction, 1, extent, axis=along_dim)
        velocity = faces_dim * (lower_press - upper_press)
        carried = velocity * jnp.where(velocity > 0, lower_frac, upper_frac)
        change = change + pad_face(carried, along_dim, True) - pad_face(carried, along_dim, False)
    return saturation + STEP_COEF * change


def solve_spd(gram_matrix, cross_matrix):
    factor = lax.linalg.cholesky(
        gram_matrix + jnp.eye(gram_matrix.shape[0], dtype=jnp.float32), symmetrize_input=False
    )
    halfway = lax.linalg.triangular_solve(factor, cross_matrix, left_side=True, lower=True)
    return lax.linalg.triangular_solve(
        factor, halfway, left_side=True, lower=True, transpose_a=True
    )


def trim_rim(values_in, rim_cut):
    return values_in[:, :, rim_cut : values_in.shape[2] - rim_cut, :]


def exchange_kernel(member_count, part_ref, full_ref,
                    recv_a, own_blk, recv_m, send_a, recv_a_sem, send_m, recv_m_sem, send_t, recv_t_sem):
    tile_count = part_ref.shape[0]
    me_t = lax.axis_index("tile")
    me_m = lax.axis_index("member")
    mesh_ids = pl.DeviceIdType.MESH

    barrier = pltpu.get_barrier_semaphore()

    def greet_tile(k, carry):
        pl.semaphore_signal(
            barrier, 1, device_id=(lax.rem(me_t + k, tile_count), me_m), device_id_type=mesh_ids
        )
        return carry

    def greet_member(k, carry):
        pl.semaphore_signal(
            barrier, 1, device_id=(me_t, lax.rem(me_m + k, member_count)), device_id_type=mesh_ids
        )
        return carry

    lax.fori_loop(1, tile_count, greet_tile, 0)
    lax.fori_loop(1, member_count, greet_member, 0)
    pl.semaphore_wait(barrier, tile_count + member_count - 2)

    def copy_a(dst_t, src_t):
        return pltpu.make_async_remote_copy(
            src_ref=part_ref.at[dst_t], dst_ref=recv_a.at[src_t],
            send_sem=send_a.at[dst_t], recv_sem=recv_a_sem.at[src_t],
            device_id=(dst_t, me_m), device_id_type=mesh_ids,
        )

    def start_a(k, carry):
        copy_a(lax.rem(me_t + k, tile_count), me_t).start()
        return carry

    lax.fori_loop(1, tile_count, start_a, 0)

    def wait_a(k, acc):
        src_t = lax.rem(me_t + k, tile_count)
        copy_a(me_t, src_t).wait_recv()
        return acc + recv_a[src_t]

    acc = lax.fori_loop(1, tile_count, wait_a, part_ref[me_t])

    def wait_a_send(k, carry):
        copy_a(lax.rem(me_t + k, tile_count), me_t).wait_send()
        return carry

    lax.fori_loop(1, tile_count, wait_a_send, 0)

    groups = part_ref.shape[2] // member_count
    lane_ids = lax.broadcasted_iota(jnp.int32, acc.shape, 1)
    for q in range(member_count):
        moved = pltpu.roll(acc, lax.rem((me_m - q + member_count) * groups, part_ref.shape[2]), 1)
        own_blk[pl.ds(q, acc.shape[0], stride=member_count), :] = jnp.where(
            lane_ids // groups == me_m, moved, 0.0
        )
    acc = own_blk[...]

    def copy_m(dst_m, src_m):
        return pltpu.make_async_remote_copy(
            src_ref=own_blk, dst_ref=recv_m.at[src_m],
            send_sem=send_m.at[dst_m], recv_sem=recv_m_sem.at[src_m],
            device_id=(me_t, dst_m), device_id_type=mesh_ids,
        )

    def start_m(k, carry):
        copy_m(lax.rem(me_m + k, member_count), me_m).start()
        return carry

    lax.fori_loop(1, member_count, start_m, 0)

    def wait_m(k, total):
        src_m = lax.rem(me_m + k, member_count)
        copy_m(me_m, src_m).wait_recv()
        return total + recv_m[src_m]

    full_ref[me_t] = lax.fori_loop(1, member_count, wait_m, acc)

    def wait_m_send(k, carry):
        copy_m(lax.rem(me_m + k, member_count), me_m).wait_send()
        return carry

    lax.fori_loop(1, member_count, wait_m_send, 0)

    def copy_t(dst_t, src_t):
        return pltpu.make_async_remote_copy(
            src_ref=full_ref.at[src_t], dst_ref=full_ref.at[src_t],
            send_sem=send_t.at[dst_t], recv_sem=recv_t_sem.at[src_t],
            device_id=(dst_t, me_m), device_id_type=mesh_ids,
        )

    def start_t(k, carry):
        copy_t(lax.rem(me_t + k, tile_count), me_t).start()
        return carry

    lax.fori_loop(1, tile_count, start_t, 0)

    def wait_t(k, carry):
        copy_t(me_t, lax.rem(me_t + k, tile_count)).wait_recv()
        return carry

    lax.fori_loop(1, tile_count, wait_t, 0)

    def wait_t_send(k, carry):
        copy_t(lax.rem(me_t + k, tile_count), me_t).wait_send()
        return carry

    lax.fori_loop(1, tile_count, wait_t_send, 0)


def stencil_kernel(rim, halo_ref, lp_mid, f_mid, inside_ref, press_ref, sat_ref, mob_ref):
    inside = inside_ref[...]
    block, layers = lp_mid.shape[0], lp_mid.shape[1]
    field_count = f_mid.shape[0]
    lp_rows = pl.ds(pl.multiple_of(pl.program_id(0) * block * layers, block * layers), block * layers)
    field_first = halo_ref.shape[2] - field_count * layers

    def halo_piece(side, rows, shape):
        return [halo_ref[side, r, rows, :].reshape(shape) for r in range(rim)]

    lp_shape = (block, layers, 1, lp_mid.shape[3])
    f_shape = (field_count, layers, 1, f_mid.shape[3])
    f_rows = pl.ds(field_first, field_count * layers)
    permeab = jnp.exp(jnp.concatenate(
        halo_piece(0, lp_rows, lp_shape) + [lp_mid[...]] + halo_piece(1, lp_rows, lp_shape), axis=2
    ))
    face_sets = face_terms(permeab, inside)
    fields = jnp.concatenate(
        halo_piece(0, f_rows, f_shape) + [f_mid[...]] + halo_piece(1, f_rows, f_shape), axis=2
    )
    press_ext = fields[0]
    sat_ext = fields[1]
    source_ext = fields[2]
    storage_ext = fields[3]
    baseline = (source_ext + storage_ext * press_ext)[None]
    storage_term = jnp.where(inside[None, :, None] > 0.0, storage_ext, 1.0)[None]
    pressure = jnp.broadcast_to(press_ext[None], permeab.shape)
    for sweep_idx in range(SWEEPS):
        pressure = jacobi(pressure, baseline, storage_term, face_sets)
    saturation = trim_rim(transport(pressure, sat_ext[None], face_sets), rim)
    press_ref[...] = trim_rim(pressure, rim)
    sat_ref[...] = saturation
    mob_ref[...] = trim_rim(permeab, rim) * water_frac(saturation)


def stencil(halo, log_perm, fields, inside, rim):
    members, layers, out_rows, depth = log_perm.shape
    block = 4

    def whole(part):
        return pl.BlockSpec(part.shape, lambda i: (0,) * part.ndim)

    out_spec = pl.BlockSpec((block, layers, out_rows, depth), lambda i: (i, 0, 0, 0))
    out_shape = jax.ShapeDtypeStruct((members, layers, out_rows, depth), jnp.float32)
    return pl.pallas_call(
        functools.partial(stencil_kernel, rim),
        grid=(members // block,),
        in_specs=[
            whole(halo),
            pl.BlockSpec((block, layers, out_rows, depth), lambda i: (i, 0, 0, 0)),
            whole(fields),
            whole(inside),
        ],
        out_specs=[out_spec, out_spec, out_spec],
        out_shape=[out_shape, out_shape, out_shape],
    )(halo, log_perm, fields, inside)


def halo_kernel(rim, lp_ref, fields_ref, in_ref, out_ref, send_sem, recv_sem):
    members, layers, rows, depth = lp_ref.shape
    lp_count = members * layers
    for side, first in ((0, 0), (1, rows - rim)):
        for r in range(rim):
            out_ref[side, r, 0:lp_count, :] = lp_ref[:, :, first + r, :].reshape(lp_count, depth)
            out_ref[side, r, lp_count:, :] = fields_ref[:, :, first + r, :].reshape(-1, depth)
    tile_count = lax.axis_size("tile")
    me_t = lax.axis_index("tile")
    me_m = lax.axis_index("member")
    mesh_ids = pl.DeviceIdType.MESH
    left = lax.rem(me_t + tile_count - 1, tile_count)
    right = lax.rem(me_t + 1, tile_count)
    barrier = pltpu.get_barrier_semaphore()
    for peer in (left, right):
        pl.semaphore_signal(barrier, 1, device_id=(peer, me_m), device_id_type=mesh_ids)
    pl.semaphore_wait(barrier, 2)
    to_right = pltpu.make_async_remote_copy(
        src_ref=out_ref.at[1], dst_ref=in_ref.at[0], send_sem=send_sem.at[1],
        recv_sem=recv_sem.at[0], device_id=(right, me_m), device_id_type=mesh_ids,
    )
    to_left = pltpu.make_async_remote_copy(
        src_ref=out_ref.at[0], dst_ref=in_ref.at[1], send_sem=send_sem.at[0],
        recv_sem=recv_sem.at[1], device_id=(left, me_m), device_id_type=mesh_ids,
    )
    to_right.start()
    to_left.start()
    to_right.wait()
    to_left.wait()


def halo_exchange(log_perm, fields, rim):
    members, layers, rows, depth = log_perm.shape
    halo_shape = (2, rim, (members + fields.shape[0]) * layers, depth)
    vmem = pl.BlockSpec(memory_space=pltpu.VMEM)
    return pl.pallas_call(
        functools.partial(halo_kernel, rim),
        out_shape=jax.ShapeDtypeStruct(halo_shape, log_perm.dtype),
        in_specs=[vmem, vmem],
        out_specs=vmem,
        scratch_shapes=[
            pltpu.VMEM(halo_shape, log_perm.dtype),
            pltpu.SemaphoreType.DMA((2,)),
            pltpu.SemaphoreType.DMA((2,)),
        ],
        compiler_params=pltpu.CompilerParams(collective_id=1, has_side_effects=True),
    )(log_perm, fields)


def rates_exchange(pieces, member_count):
    tile_count, rows, lanes = pieces.shape
    vmem = pl.BlockSpec(memory_space=pltpu.VMEM)
    return pl.pallas_call(
        functools.partial(exchange_kernel, member_count),
        out_shape=jax.ShapeDtypeStruct((tile_count, rows * member_count, lanes), jnp.float32),
        in_specs=[vmem],
        out_specs=vmem,
        scratch_shapes=[
            pltpu.VMEM((tile_count, rows, lanes), jnp.float32),
            pltpu.VMEM((rows * member_count, lanes), jnp.float32),
            pltpu.VMEM((member_count, rows * member_count, lanes), jnp.float32),
            pltpu.SemaphoreType.DMA((tile_count,)),
            pltpu.SemaphoreType.DMA((tile_count,)),
            pltpu.SemaphoreType.DMA((member_count,)),
            pltpu.SemaphoreType.DMA((member_count,)),
            pltpu.SemaphoreType.DMA((tile_count,)),
            pltpu.SemaphoreType.DMA((tile_count,)),
        ],
        compiler_params=pltpu.CompilerParams(collective_id=0, has_side_effects=True),
    )(pieces)


def per_device(
    log_perm,
    start_pressure,
    start_sat,
    source,
    storage,
    well_press,
    perf_cell,
    perf_well,
    perf_count,
    observed,
    obs_var,
    obs_noise,
):
    local_count, layers, strip_width, strip_depth = log_perm.shape
    tile_count = lax.axis_size("tile")
    members = local_count * lax.axis_size("member")
    well_count = well_press.shape[0]
    well_share = well_count // tile_count
    tile_rank = lax.axis_index("tile")
    member_rank = lax.axis_index("member")
    rim = SWEEPS + 1
    fields = jnp.stack([start_pressure, start_sat, source, storage])
    halo_rows = local_count * layers * rim + fields.shape[0] * layers * rim

    incoming = halo_exchange(log_perm, fields, rim)
    incoming, log_perm_after = lax.optimization_barrier((incoming, log_perm))
    halo = incoming
    column = tile_rank * strip_width - rim + jnp.arange(strip_width + 2 * rim, dtype=jnp.int32)
    inside = ((column >= 0) & (column < strip_width * tile_count)).astype(jnp.float32)
    pressure, saturation, mobility = stencil(halo, log_perm, fields, inside, rim)
    cell_count = layers * strip_width * strip_depth
    plane_rows = layers * strip_width
    cell_row = perf_cell // strip_depth
    cell_col = lax.rem(perf_cell, strip_depth)
    col_pick = (jnp.arange(strip_depth, dtype=jnp.int32)[:, None] == cell_col[None, :]).astype(
        jnp.float32
    )
    row_pick = jnp.arange(plane_rows, dtype=jnp.int32)[:, None] == cell_row[None, :]

    def pick_cells(values_in):
        by_col = jnp.dot(
            values_in.reshape(local_count * plane_rows, strip_depth), col_pick,
            precision=lax.Precision.HIGHEST, preferred_element_type=jnp.float32,
        ).reshape(local_count, plane_rows, -1)
        return jnp.sum(jnp.where(row_pick[None], by_col, 0.0), axis=1)

    perf_mob = pick_cells(mobility)
    perf_press = pick_cells(pressure)
    selector = (perf_well[:, None] == jnp.arange(well_count, dtype=jnp.int32)[None, :]).astype(
        jnp.float32
    )
    perf_bhp = jnp.dot(selector, well_press, precision=lax.Precision.HIGHEST)
    live_mask = (jnp.arange(perf_cell.shape[0], dtype=jnp.int32) < perf_count[0]).astype(
        jnp.float32
    )
    perf_terms = perf_mob * (perf_press - perf_bhp[None]) * live_mask[None]
    member_root = (members - 1) ** 0.5
    spread = jnp.sqrt(INFLATION * obs_var)
    member_count = lax.axis_size("member")
    contract_slots = (((0,), (1,)), ((), ()))
    pieces = lax.dot_general(
        selector, perf_terms, contract_slots, precision=lax.Precision.HIGHEST,
        preferred_element_type=jnp.float32,
    ).reshape(tile_count, well_share * local_count // 128, 128)
    full = rates_exchange(pieces, member_count)
    own_block = lax.dynamic_index_in_dim(full, tile_rank, 0, keepdims=False)
    well_rates = lax.dynamic_slice_in_dim(own_block, member_rank * local_count, local_count, 1).T
    rates_t = full.reshape(well_count, members)
    mean_rate = jnp.sum(rates_t, 1) / members
    scaled_t = (rates_t - mean_rate[:, None]) / (spread * member_root)[:, None]
    rates_own_t = lax.dynamic_slice_in_dim(rates_t, member_rank * local_count, local_count, 1)
    innov_own_t = (observed[:, None] - rates_own_t) / spread[:, None] + obs_noise.T
    contract_wells = (((0,), (0,)), ((), ()))
    gram_matrix = lax.dot_general(
        scaled_t, scaled_t, contract_wells, precision=lax.Precision.HIGHEST,
        preferred_element_type=jnp.float32,
    )
    cross_matrix = lax.dot_general(
        scaled_t, innov_own_t, contract_wells, precision=lax.Precision.HIGHEST,
        preferred_element_type=jnp.float32,
    )
    weights_low = solve_spd(gram_matrix, cross_matrix).astype(jnp.bfloat16)
    anomaly = (log_perm_after / member_root).astype(jnp.bfloat16).transpose(1, 2, 0, 3)
    anomaly_parts = [anomaly]
    for shift in range(1, member_count):
        pairs = [(i, (i + shift) % member_count) for i in range(member_count)]
        anomaly_parts.append(lax.ppermute(anomaly, "member", pairs))
    anomaly_all = jnp.concatenate(anomaly_parts, axis=2)
    own_cols = jnp.concatenate(
        [
            lax.dynamic_slice_in_dim(
                weights_low, lax.rem(member_rank - shift + member_count, member_count) * local_count,
                local_count, 0,
            )
            for shift in range(member_count)
        ],
        axis=0,
    )
    contract = (((0,), (2,)), ((), ()))
    update_sum = lax.dot_general(own_cols, anomaly_all, contract, preferred_element_type=jnp.float32)
    new_log_perm = log_perm + update_sum
    return (new_log_perm, pressure, saturation, well_rates)


def solution(mesh):
    return jax.shard_map(
        per_device,
        mesh=mesh,
        in_specs=(
            P("member", None, "tile", None),
            P(None, "tile", None),
            P(None, "tile", None),
            P(None, "tile", None),
            P(None, "tile", None),
            P(),
            P("tile"),
            P("tile"),
            P("tile"),
            P(),
            P(),
            P("member", None),
        ),
        out_specs=(
            P("member", None, "tile", None),
            P("member", None, "tile", None),
            P("member", None, "tile", None),
            P("member", "tile"),
        ),
        check_vma=False,
    )
```

```python
import functools

import jax
import jax.numpy as jnp
from jax import lax
from jax.experimental import pallas as pl
from jax.experimental.pallas import tpu as pltpu
from jax.sharding import PartitionSpec as P

SWEEPS = 2


VERTICAL = 0.5
VISCOSITY_RATIO = 2.0
STEP_COEF = 0.1
INFLATION = 4.0


def extended_2(block, sides, width):
    for axis, dim in sides:
        count = lax.axis_size(axis)
        forward = [(i, i + 1) for i in range(count - 1)]
        backward = [(target, source) for source, target in forward]
        low = lax.ppermute(
            lax.slice_in_dim(block, block.shape[dim] - width, None, axis=dim), axis, forward
        )
        high = lax.ppermute(lax.slice_in_dim(block, 0, width, axis=dim), axis, backward)
        block = jnp.concatenate([low, block, high], axis=dim)
    return block


def harmonic(lower_val, upper_val):
    return 2.0 * lower_val * upper_val / (lower_val + upper_val)


def pad_face(values_in, along_dim, before):
    widths = [(0, 0)] * values_in.ndim
    widths[along_dim] = (1, 0) if before else (0, 1)
    return jnp.pad(values_in, widths)


def slide_by(values_in, along_dim, before):
    extent = values_in.shape[along_dim]
    if before:
        remain = lax.slice_in_dim(values_in, 0, extent - 1, axis=along_dim)
    else:
        remain = lax.slice_in_dim(values_in, 1, extent, axis=along_dim)
    return pad_face(remain, along_dim, before)


def face_terms(permeab, inside):
    face_x = (
        harmonic(permeab[:, :, :-1, :], permeab[:, :, 1:, :]) * (inside[:-1] * inside[1:])[:, None]
    )
    face_y = harmonic(permeab[:, :, :, :-1], permeab[:, :, :, 1:])
    face_z = VERTICAL * harmonic(permeab[:, :-1], permeab[:, 1:])
    return (face_x, face_y, face_z)


def neighbours(face_sets, values_in):
    flow_sum = 0.0
    weight_sum = 0.0
    for faces_dim, along_dim in zip(face_sets, (2, 3, 1)):
        lower = pad_face(faces_dim, along_dim, True)
        upper = pad_face(faces_dim, along_dim, False)
        flow_sum = (
            flow_sum
            + lower * slide_by(values_in, along_dim, True)
            + upper * slide_by(values_in, along_dim, False)
        )
        weight_sum = weight_sum + lower + upper
    return (flow_sum, weight_sum)


def jacobi(pressure, baseline, storage_term, face_sets):
    flow_sum, weight_sum = neighbours(face_sets, pressure)
    return (baseline + flow_sum) / (storage_term + weight_sum)


def water_frac(values_in):
    squared = values_in * values_in
    return squared / (squared + VISCOSITY_RATIO * (1.0 - values_in) * (1.0 - values_in))


def transport(pressure, saturation, face_sets):
    fraction = water_frac(saturation)
    change = 0.0
    for faces_dim, along_dim in zip(face_sets, (2, 3, 1)):
        extent = pressure.shape[along_dim]
        lower_press = lax.slice_in_dim(pressure, 0, extent - 1, axis=along_dim)
        upper_press = lax.slice_in_dim(pressure, 1, extent, axis=along_dim)
        lower_frac = lax.slice_in_dim(fraction, 0, extent - 1, axis=along_dim)
        upper_frac = lax.slice_in_dim(fraction, 1, extent, axis=along_dim)
        velocity = faces_dim * (lower_press - upper_press)
        carried = velocity * jnp.where(velocity > 0, lower_frac, upper_frac)
        change = change + pad_face(carried, along_dim, True) - pad_face(carried, along_dim, False)
    return saturation + STEP_COEF * change


def solve_spd(gram_matrix, cross_matrix):
    factor = lax.linalg.cholesky(
        gram_matrix + jnp.eye(gram_matrix.shape[0], dtype=jnp.float32), symmetrize_input=False
    )
    halfway = lax.linalg.triangular_solve(factor, cross_matrix, left_side=True, lower=True)
    return lax.linalg.triangular_solve(
        factor, halfway, left_side=True, lower=True, transpose_a=True
    )


def trim_rim(values_in, rim_cut):
    return values_in[:, :, rim_cut : values_in.shape[2] - rim_cut, :]


def exchange_kernel(member_count, part_ref, full_ref,
                    recv_a, own_blk, recv_m, send_a, recv_a_sem, send_m, recv_m_sem, send_t, recv_t_sem):
    tile_count = part_ref.shape[0]
    me_t = lax.axis_index("tile")
    me_m = lax.axis_index("member")
    mesh_ids = pl.DeviceIdType.MESH

    barrier = pltpu.get_barrier_semaphore()

    def greet_tile(k, carry):
        pl.semaphore_signal(
            barrier, 1, device_id=(lax.rem(me_t + k, tile_count), me_m), device_id_type=mesh_ids
        )
        return carry

    def greet_member(k, carry):
        pl.semaphore_signal(
            barrier, 1, device_id=(me_t, lax.rem(me_m + k, member_count)), device_id_type=mesh_ids
        )
        return carry

    lax.fori_loop(1, tile_count, greet_tile, 0)
    lax.fori_loop(1, member_count, greet_member, 0)
    pl.semaphore_wait(barrier, tile_count + member_count - 2)

    def copy_a(dst_t, src_t):
        return pltpu.make_async_remote_copy(
            src_ref=part_ref.at[dst_t], dst_ref=recv_a.at[src_t],
            send_sem=send_a.at[dst_t], recv_sem=recv_a_sem.at[src_t],
            device_id=(dst_t, me_m), device_id_type=mesh_ids,
        )

    def start_a(k, carry):
        copy_a(lax.rem(me_t + k, tile_count), me_t).start()
        return carry

    lax.fori_loop(1, tile_count, start_a, 0)

    def wait_a(k, acc):
        src_t = lax.rem(me_t + k, tile_count)
        copy_a(me_t, src_t).wait_recv()
        return acc + recv_a[src_t]

    acc = lax.fori_loop(1, tile_count, wait_a, part_ref[me_t])

    def wait_a_send(k, carry):
        copy_a(lax.rem(me_t + k, tile_count), me_t).wait_send()
        return carry

    lax.fori_loop(1, tile_count, wait_a_send, 0)

    groups = part_ref.shape[2] // member_count
    lane_ids = lax.broadcasted_iota(jnp.int32, acc.shape, 1)
    for q in range(member_count):
        moved = pltpu.roll(acc, lax.rem((me_m - q + member_count) * groups, part_ref.shape[2]), 1)
        own_blk[pl.ds(q, acc.shape[0], stride=member_count), :] = jnp.where(
            lane_ids // groups == me_m, moved, 0.0
        )
    acc = own_blk[...]

    def copy_m(dst_m, src_m):
        return pltpu.make_async_remote_copy(
            src_ref=own_blk, dst_ref=recv_m.at[src_m],
            send_sem=send_m.at[dst_m], recv_sem=recv_m_sem.at[src_m],
            device_id=(me_t, dst_m), device_id_type=mesh_ids,
        )

    def start_m(k, carry):
        copy_m(lax.rem(me_m + k, member_count), me_m).start()
        return carry

    lax.fori_loop(1, member_count, start_m, 0)

    def wait_m(k, total):
        src_m = lax.rem(me_m + k, member_count)
        copy_m(me_m, src_m).wait_recv()
        return total + recv_m[src_m]

    full_ref[me_t] = lax.fori_loop(1, member_count, wait_m, acc)

    def wait_m_send(k, carry):
        copy_m(lax.rem(me_m + k, member_count), me_m).wait_send()
        return carry

    lax.fori_loop(1, member_count, wait_m_send, 0)

    def copy_t(dst_t, src_t):
        return pltpu.make_async_remote_copy(
            src_ref=full_ref.at[src_t], dst_ref=full_ref.at[src_t],
            send_sem=send_t.at[dst_t], recv_sem=recv_t_sem.at[src_t],
            device_id=(dst_t, me_m), device_id_type=mesh_ids,
        )

    def start_t(k, carry):
        copy_t(lax.rem(me_t + k, tile_count), me_t).start()
        return carry

    lax.fori_loop(1, tile_count, start_t, 0)

    def wait_t(k, carry):
        copy_t(me_t, lax.rem(me_t + k, tile_count)).wait_recv()
        return carry

    lax.fori_loop(1, tile_count, wait_t, 0)

    def wait_t_send(k, carry):
        copy_t(lax.rem(me_t + k, tile_count), me_t).wait_send()
        return carry

    lax.fori_loop(1, tile_count, wait_t_send, 0)


def stencil_kernel(rim, halo_ref, lp_mid, f0, f1, f2, f3, inside_ref, press_ref, sat_ref, mob_ref):
    f_mid = jnp.stack([f0[...], f1[...], f2[...], f3[...]])
    inside = inside_ref[...]
    block, layers = lp_mid.shape[0], lp_mid.shape[1]
    field_count = 4
    lp_rows = pl.ds(pl.multiple_of(pl.program_id(0) * block * layers, block * layers), block * layers)
    field_first = halo_ref.shape[2] - field_count * layers

    def halo_piece(side, rows, shape):
        return [halo_ref[side, r, rows, :].reshape(shape) for r in range(rim)]

    lp_shape = (block, layers, 1, lp_mid.shape[3])
    f_shape = (field_count, layers, 1, f_mid.shape[3])
    f_rows = pl.ds(field_first, field_count * layers)
    permeab = jnp.exp(jnp.concatenate(
        halo_piece(0, lp_rows, lp_shape) + [lp_mid[...]] + halo_piece(1, lp_rows, lp_shape), axis=2
    ))
    face_sets = face_terms(permeab, inside)
    fields = jnp.concatenate(
        halo_piece(0, f_rows, f_shape) + [f_mid] + halo_piece(1, f_rows, f_shape), axis=2
    )
    press_ext = fields[0]
    sat_ext = fields[1]
    source_ext = fields[2]
    storage_ext = fields[3]
    baseline = (source_ext + storage_ext * press_ext)[None]
    storage_term = jnp.where(inside[None, :, None] > 0.0, storage_ext, 1.0)[None]
    pressure = jnp.broadcast_to(press_ext[None], permeab.shape)
    for sweep_idx in range(SWEEPS):
        pressure = jacobi(pressure, baseline, storage_term, face_sets)
    saturation = trim_rim(transport(pressure, sat_ext[None], face_sets), rim)
    press_ref[...] = trim_rim(pressure, rim)
    sat_ref[...] = saturation
    mob_ref[...] = trim_rim(permeab, rim) * water_frac(saturation)


def stencil(halo, log_perm, fields, inside, rim):
    members, layers, out_rows, depth = log_perm.shape
    block = 4

    def whole(part):
        return pl.BlockSpec(part.shape, lambda i: (0,) * part.ndim)

    out_spec = pl.BlockSpec((block, layers, out_rows, depth), lambda i: (i, 0, 0, 0))
    out_shape = jax.ShapeDtypeStruct((members, layers, out_rows, depth), jnp.float32)
    return pl.pallas_call(
        functools.partial(stencil_kernel, rim),
        grid=(members // block,),
        in_specs=[
            whole(halo),
            pl.BlockSpec((block, layers, out_rows, depth), lambda i: (i, 0, 0, 0)),
            *[whole(f) for f in fields],
            whole(inside),
        ],
        out_specs=[out_spec, out_spec, out_spec],
        out_shape=[out_shape, out_shape, out_shape],
    )(halo, log_perm, *fields, inside)


def halo_kernel(rim, lp_ref, f0, f1, f2, f3, in_ref, out_ref, send_sem, recv_sem):
    members, layers, rows, depth = lp_ref.shape
    lp_count = members * layers
    for side, first in ((0, 0), (1, rows - rim)):
        for r in range(rim):
            out_ref[side, r, 0:lp_count, :] = lp_ref[:, :, first + r, :].reshape(lp_count, depth)
            for fi, f_ref in enumerate((f0, f1, f2, f3)):
                at = lp_count + fi * layers
                out_ref[side, r, at:at + layers, :] = f_ref[:, first + r, :]
    tile_count = lax.axis_size("tile")
    me_t = lax.axis_index("tile")
    me_m = lax.axis_index("member")
    mesh_ids = pl.DeviceIdType.MESH
    left = lax.rem(me_t + tile_count - 1, tile_count)
    right = lax.rem(me_t + 1, tile_count)
    barrier = pltpu.get_barrier_semaphore()
    for peer in (left, right):
        pl.semaphore_signal(barrier, 1, device_id=(peer, me_m), device_id_type=mesh_ids)
    pl.semaphore_wait(barrier, 2)
    to_right = pltpu.make_async_remote_copy(
        src_ref=out_ref.at[1], dst_ref=in_ref.at[0], send_sem=send_sem.at[1],
        recv_sem=recv_sem.at[0], device_id=(right, me_m), device_id_type=mesh_ids,
    )
    to_left = pltpu.make_async_remote_copy(
        src_ref=out_ref.at[0], dst_ref=in_ref.at[1], send_sem=send_sem.at[0],
        recv_sem=recv_sem.at[1], device_id=(left, me_m), device_id_type=mesh_ids,
    )
    to_right.start()
    to_left.start()
    to_right.wait()
    to_left.wait()


def halo_exchange(log_perm, fields, rim):
    members, layers, rows, depth = log_perm.shape
    halo_shape = (2, rim, (members + len(fields)) * layers, depth)
    vmem = pl.BlockSpec(memory_space=pltpu.VMEM)
    return pl.pallas_call(
        functools.partial(halo_kernel, rim),
        out_shape=jax.ShapeDtypeStruct(halo_shape, log_perm.dtype),
        in_specs=[vmem] * (1 + len(fields)),
        out_specs=vmem,
        scratch_shapes=[
            pltpu.VMEM(halo_shape, log_perm.dtype),
            pltpu.SemaphoreType.DMA((2,)),
            pltpu.SemaphoreType.DMA((2,)),
        ],
        compiler_params=pltpu.CompilerParams(collective_id=1, has_side_effects=True),
    )(log_perm, *fields)


def rates_exchange(pieces, member_count):
    tile_count, rows, lanes = pieces.shape
    vmem = pl.BlockSpec(memory_space=pltpu.VMEM)
    return pl.pallas_call(
        functools.partial(exchange_kernel, member_count),
        out_shape=jax.ShapeDtypeStruct((tile_count, rows * member_count, lanes), jnp.float32),
        in_specs=[vmem],
        out_specs=vmem,
        scratch_shapes=[
            pltpu.VMEM((tile_count, rows, lanes), jnp.float32),
            pltpu.VMEM((rows * member_count, lanes), jnp.float32),
            pltpu.VMEM((member_count, rows * member_count, lanes), jnp.float32),
            pltpu.SemaphoreType.DMA((tile_count,)),
            pltpu.SemaphoreType.DMA((tile_count,)),
            pltpu.SemaphoreType.DMA((member_count,)),
            pltpu.SemaphoreType.DMA((member_count,)),
            pltpu.SemaphoreType.DMA((tile_count,)),
            pltpu.SemaphoreType.DMA((tile_count,)),
        ],
        compiler_params=pltpu.CompilerParams(collective_id=0, has_side_effects=True),
    )(pieces)


def per_device(
    log_perm,
    start_pressure,
    start_sat,
    source,
    storage,
    well_press,
    perf_cell,
    perf_well,
    perf_count,
    observed,
    obs_var,
    obs_noise,
):
    local_count, layers, strip_width, strip_depth = log_perm.shape
    tile_count = lax.axis_size("tile")
    members = local_count * lax.axis_size("member")
    well_count = well_press.shape[0]
    well_share = well_count // tile_count
    tile_rank = lax.axis_index("tile")
    member_rank = lax.axis_index("member")
    rim = SWEEPS + 1
    fields = (start_pressure, start_sat, source, storage)

    incoming = halo_exchange(log_perm, fields, rim)
    incoming, log_perm_after = lax.optimization_barrier((incoming, log_perm))
    halo = incoming
    column = tile_rank * strip_width - rim + jnp.arange(strip_width + 2 * rim, dtype=jnp.int32)
    inside = ((column >= 0) & (column < strip_width * tile_count)).astype(jnp.float32)
    pressure, saturation, mobility = stencil(halo, log_perm, fields, inside, rim)
    cell_count = layers * strip_width * strip_depth
    plane_rows = layers * strip_width
    cell_row = perf_cell // strip_depth
    cell_col = lax.rem(perf_cell, strip_depth)
    col_pick = (jnp.arange(strip_depth, dtype=jnp.int32)[:, None] == cell_col[None, :]).astype(
        jnp.float32
    )
    row_pick = jnp.arange(plane_rows, dtype=jnp.int32)[:, None] == cell_row[None, :]

    def pick_cells(values_in):
        by_col = jnp.dot(
            values_in.reshape(local_count * plane_rows, strip_depth), col_pick,
            precision=lax.Precision.HIGHEST, preferred_element_type=jnp.float32,
        ).reshape(local_count, plane_rows, -1)
        return jnp.sum(jnp.where(row_pick[None], by_col, 0.0), axis=1)

    perf_mob = pick_cells(mobility)
    perf_press = pick_cells(pressure)
    selector = (perf_well[:, None] == jnp.arange(well_count, dtype=jnp.int32)[None, :]).astype(
        jnp.float32
    )
    perf_bhp = jnp.dot(selector, well_press, precision=lax.Precision.HIGHEST)
    live_mask = (jnp.arange(perf_cell.shape[0], dtype=jnp.int32) < perf_count[0]).astype(
        jnp.float32
    )
    perf_terms = perf_mob * (perf_press - perf_bhp[None]) * live_mask[None]
    member_root = (members - 1) ** 0.5
    spread = jnp.sqrt(INFLATION * obs_var)
    member_count = lax.axis_size("member")
    contract_slots = (((0,), (1,)), ((), ()))
    pieces = lax.dot_general(
        selector, perf_terms, contract_slots, precision=lax.Precision.HIGHEST,
        preferred_element_type=jnp.float32,
    ).reshape(tile_count, well_share * local_count // 128, 128)
    full = rates_exchange(pieces, member_count)
    own_block = lax.dynamic_index_in_dim(full, tile_rank, 0, keepdims=False)
    well_rates = lax.dynamic_slice_in_dim(own_block, member_rank * local_count, local_count, 1).T
    rates_t = full.reshape(well_count, members)
    mean_rate = jnp.sum(rates_t, 1) / members
    scaled_t = (rates_t - mean_rate[:, None]) / (spread * member_root)[:, None]
    rates_own_t = lax.dynamic_slice_in_dim(rates_t, member_rank * local_count, local_count, 1)
    innov_own_t = (observed[:, None] - rates_own_t) / spread[:, None] + obs_noise.T
    contract_wells = (((0,), (0,)), ((), ()))
    gram_matrix = lax.dot_general(
        scaled_t, scaled_t, contract_wells, precision=lax.Precision.HIGHEST,
        preferred_element_type=jnp.float32,
    )
    cross_matrix = lax.dot_general(
        scaled_t, innov_own_t, contract_wells, precision=lax.Precision.HIGHEST,
        preferred_element_type=jnp.float32,
    )
    weights_low = solve_spd(gram_matrix, cross_matrix).astype(jnp.bfloat16)
    anomaly = (log_perm_after / member_root).astype(jnp.bfloat16).transpose(1, 2, 0, 3)
    anomaly_parts = [anomaly]
    for shift in range(1, member_count):
        pairs = [(i, (i + shift) % member_count) for i in range(member_count)]
        anomaly_parts.append(lax.ppermute(anomaly, "member", pairs))
    anomaly_all = jnp.concatenate(anomaly_parts, axis=2)
    own_cols = jnp.concatenate(
        [
            lax.dynamic_slice_in_dim(
                weights_low, lax.rem(member_rank - shift + member_count, member_count) * local_count,
                local_count, 0,
            )
            for shift in range(member_count)
        ],
        axis=0,
    )
    contract = (((0,), (2,)), ((), ()))
    update_sum = lax.dot_general(own_cols, anomaly_all, contract, preferred_element_type=jnp.float32)
    new_log_perm = log_perm + update_sum
    return (new_log_perm, pressure, saturation, well_rates)


def solution(mesh):
    return jax.shard_map(
        per_device,
        mesh=mesh,
        in_specs=(
            P("member", None, "tile", None),
            P(None, "tile", None),
            P(None, "tile", None),
            P(None, "tile", None),
            P(None, "tile", None),
            P(),
            P("tile"),
            P("tile"),
            P("tile"),
            P(),
            P(),
            P("member", None),
        ),
        out_specs=(
            P("member", None, "tile", None),
            P("member", None, "tile", None),
            P("member", None, "tile", None),
            P("member", "tile"),
        ),
        check_vma=False,
    )
```

```python
import functools

import jax
import jax.numpy as jnp
from jax import lax
from jax.experimental import pallas as pl
from jax.experimental.pallas import tpu as pltpu
from jax.sharding import PartitionSpec as P

SWEEPS = 2


VERTICAL = 0.5
VISCOSITY_RATIO = 2.0
STEP_COEF = 0.1
INFLATION = 4.0


def extended_2(block, sides, width):
    for axis, dim in sides:
        count = lax.axis_size(axis)
        forward = [(i, i + 1) for i in range(count - 1)]
        backward = [(target, source) for source, target in forward]
        low = lax.ppermute(
            lax.slice_in_dim(block, block.shape[dim] - width, None, axis=dim), axis, forward
        )
        high = lax.ppermute(lax.slice_in_dim(block, 0, width, axis=dim), axis, backward)
        block = jnp.concatenate([low, block, high], axis=dim)
    return block


def harmonic(lower_val, upper_val):
    return 2.0 * lower_val * upper_val / (lower_val + upper_val)


def pad_face(values_in, along_dim, before):
    widths = [(0, 0)] * values_in.ndim
    widths[along_dim] = (1, 0) if before else (0, 1)
    return jnp.pad(values_in, widths)


def slide_by(values_in, along_dim, before):
    extent = values_in.shape[along_dim]
    if before:
        remain = lax.slice_in_dim(values_in, 0, extent - 1, axis=along_dim)
    else:
        remain = lax.slice_in_dim(values_in, 1, extent, axis=along_dim)
    return pad_face(remain, along_dim, before)


def face_terms(permeab, inside):
    face_x = (
        harmonic(permeab[:, :, :-1, :], permeab[:, :, 1:, :]) * (inside[:-1] * inside[1:])[:, None]
    )
    face_y = harmonic(permeab[:, :, :, :-1], permeab[:, :, :, 1:])
    face_z = VERTICAL * harmonic(permeab[:, :-1], permeab[:, 1:])
    return (face_x, face_y, face_z)


def neighbours(face_sets, values_in):
    flow_sum = 0.0
    weight_sum = 0.0
    for faces_dim, along_dim in zip(face_sets, (2, 3, 1)):
        lower = pad_face(faces_dim, along_dim, True)
        upper = pad_face(faces_dim, along_dim, False)
        flow_sum = (
            flow_sum
            + lower * slide_by(values_in, along_dim, True)
            + upper * slide_by(values_in, along_dim, False)
        )
        weight_sum = weight_sum + lower + upper
    return (flow_sum, weight_sum)


def jacobi(pressure, baseline, storage_term, face_sets):
    flow_sum, weight_sum = neighbours(face_sets, pressure)
    return (baseline + flow_sum) / (storage_term + weight_sum)


def water_frac(values_in):
    squared = values_in * values_in
    return squared / (squared + VISCOSITY_RATIO * (1.0 - values_in) * (1.0 - values_in))


def transport(pressure, saturation, face_sets):
    fraction = water_frac(saturation)
    change = 0.0
    for faces_dim, along_dim in zip(face_sets, (2, 3, 1)):
        extent = pressure.shape[along_dim]
        lower_press = lax.slice_in_dim(pressure, 0, extent - 1, axis=along_dim)
        upper_press = lax.slice_in_dim(pressure, 1, extent, axis=along_dim)
        lower_frac = lax.slice_in_dim(fraction, 0, extent - 1, axis=along_dim)
        upper_frac = lax.slice_in_dim(fraction, 1, extent, axis=along_dim)
        velocity = faces_dim * (lower_press - upper_press)
        carried = velocity * jnp.where(velocity > 0, lower_frac, upper_frac)
        change = change + pad_face(carried, along_dim, True) - pad_face(carried, along_dim, False)
    return saturation + STEP_COEF * change


def solve_spd(gram_matrix, cross_matrix):
    factor = lax.linalg.cholesky(
        gram_matrix + jnp.eye(gram_matrix.shape[0], dtype=jnp.float32), symmetrize_input=False
    )
    halfway = lax.linalg.triangular_solve(factor, cross_matrix, left_side=True, lower=True)
    return lax.linalg.triangular_solve(
        factor, halfway, left_side=True, lower=True, transpose_a=True
    )


def trim_rim(values_in, rim_cut):
    return values_in[:, :, rim_cut : values_in.shape[2] - rim_cut, :]


def exchange_kernel(member_count, part_ref, full_ref,
                    recv_a, own_blk, recv_m, send_a, recv_a_sem, send_m, recv_m_sem, send_t, recv_t_sem):
    tile_count = part_ref.shape[0]
    me_t = lax.axis_index("tile")
    me_m = lax.axis_index("member")
    mesh_ids = pl.DeviceIdType.MESH

    barrier = pltpu.get_barrier_semaphore()

    def greet_tile(k, carry):
        pl.semaphore_signal(
            barrier, 1, device_id=(lax.rem(me_t + k, tile_count), me_m), device_id_type=mesh_ids
        )
        return carry

    def greet_member(k, carry):
        pl.semaphore_signal(
            barrier, 1, device_id=(me_t, lax.rem(me_m + k, member_count)), device_id_type=mesh_ids
        )
        return carry

    lax.fori_loop(1, tile_count, greet_tile, 0)
    lax.fori_loop(1, member_count, greet_member, 0)
    pl.semaphore_wait(barrier, tile_count + member_count - 2)

    def copy_a(dst_t, src_t):
        return pltpu.make_async_remote_copy(
            src_ref=part_ref.at[dst_t], dst_ref=recv_a.at[src_t],
            send_sem=send_a.at[dst_t], recv_sem=recv_a_sem.at[src_t],
            device_id=(dst_t, me_m), device_id_type=mesh_ids,
        )

    def start_a(k, carry):
        copy_a(lax.rem(me_t + k, tile_count), me_t).start()
        return carry

    lax.fori_loop(1, tile_count, start_a, 0)

    def wait_a(k, acc):
        src_t = lax.rem(me_t + k, tile_count)
        copy_a(me_t, src_t).wait_recv()
        return acc + recv_a[src_t]

    acc = lax.fori_loop(1, tile_count, wait_a, part_ref[me_t])

    def wait_a_send(k, carry):
        copy_a(lax.rem(me_t + k, tile_count), me_t).wait_send()
        return carry

    lax.fori_loop(1, tile_count, wait_a_send, 0)

    groups = part_ref.shape[2] // member_count
    lane_ids = lax.broadcasted_iota(jnp.int32, acc.shape, 1)
    for q in range(member_count):
        moved = pltpu.roll(acc, lax.rem((me_m - q + member_count) * groups, part_ref.shape[2]), 1)
        own_blk[pl.ds(q, acc.shape[0], stride=member_count), :] = jnp.where(
            lane_ids // groups == me_m, moved, 0.0
        )
    acc = own_blk[...]

    def copy_m(dst_m, src_m):
        return pltpu.make_async_remote_copy(
            src_ref=own_blk, dst_ref=recv_m.at[src_m],
            send_sem=send_m.at[dst_m], recv_sem=recv_m_sem.at[src_m],
            device_id=(me_t, dst_m), device_id_type=mesh_ids,
        )

    def start_m(k, carry):
        copy_m(lax.rem(me_m + k, member_count), me_m).start()
        return carry

    lax.fori_loop(1, member_count, start_m, 0)

    def wait_m(k, total):
        src_m = lax.rem(me_m + k, member_count)
        copy_m(me_m, src_m).wait_recv()
        return total + recv_m[src_m]

    full_ref[me_t] = lax.fori_loop(1, member_count, wait_m, acc)

    def wait_m_send(k, carry):
        copy_m(lax.rem(me_m + k, member_count), me_m).wait_send()
        return carry

    lax.fori_loop(1, member_count, wait_m_send, 0)

    def copy_t(dst_t, src_t):
        return pltpu.make_async_remote_copy(
            src_ref=full_ref.at[src_t], dst_ref=full_ref.at[src_t],
            send_sem=send_t.at[dst_t], recv_sem=recv_t_sem.at[src_t],
            device_id=(dst_t, me_m), device_id_type=mesh_ids,
        )

    def start_t(k, carry):
        copy_t(lax.rem(me_t + k, tile_count), me_t).start()
        return carry

    lax.fori_loop(1, tile_count, start_t, 0)

    def wait_t(k, carry):
        copy_t(me_t, lax.rem(me_t + k, tile_count)).wait_recv()
        return carry

    lax.fori_loop(1, tile_count, wait_t, 0)

    def wait_t_send(k, carry):
        copy_t(lax.rem(me_t + k, tile_count), me_t).wait_send()
        return carry

    lax.fori_loop(1, tile_count, wait_t_send, 0)


def stencil_kernel(rim, halo_ref, lp_mid, f0, f1, f2, f3, press_ref, sat_ref, mob_ref):
    f_mid = jnp.stack([f0[...], f1[...], f2[...], f3[...]])
    strip_width = lp_mid.shape[2]
    column = lax.axis_index("tile") * strip_width - rim + jnp.arange(
        strip_width + 2 * rim, dtype=jnp.int32
    )
    inside = ((column >= 0) & (column < strip_width * lax.axis_size("tile"))).astype(jnp.float32)
    block, layers = lp_mid.shape[0], lp_mid.shape[1]
    field_count = 4
    lp_rows = pl.ds(pl.multiple_of(pl.program_id(0) * block * layers, block * layers), block * layers)
    field_first = halo_ref.shape[2] - field_count * layers

    def halo_piece(side, rows, shape):
        return [halo_ref[side, r, rows, :].reshape(shape) for r in range(rim)]

    lp_shape = (block, layers, 1, lp_mid.shape[3])
    f_shape = (field_count, layers, 1, f_mid.shape[3])
    f_rows = pl.ds(field_first, field_count * layers)
    permeab = jnp.exp(jnp.concatenate(
        halo_piece(0, lp_rows, lp_shape) + [lp_mid[...]] + halo_piece(1, lp_rows, lp_shape), axis=2
    ))
    face_sets = face_terms(permeab, inside)
    fields = jnp.concatenate(
        halo_piece(0, f_rows, f_shape) + [f_mid] + halo_piece(1, f_rows, f_shape), axis=2
    )
    press_ext = fields[0]
    sat_ext = fields[1]
    source_ext = fields[2]
    storage_ext = fields[3]
    baseline = (source_ext + storage_ext * press_ext)[None]
    storage_term = jnp.where(inside[None, :, None] > 0.0, storage_ext, 1.0)[None]
    pressure = jnp.broadcast_to(press_ext[None], permeab.shape)
    for sweep_idx in range(SWEEPS):
        pressure = jacobi(pressure, baseline, storage_term, face_sets)
    saturation = trim_rim(transport(pressure, sat_ext[None], face_sets), rim)
    press_ref[...] = trim_rim(pressure, rim)
    sat_ref[...] = saturation
    mob_ref[...] = trim_rim(permeab, rim) * water_frac(saturation)


def stencil(halo, log_perm, fields, rim):
    members, layers, out_rows, depth = log_perm.shape
    block = 4

    def whole(part):
        return pl.BlockSpec(part.shape, lambda i: (0,) * part.ndim)

    out_spec = pl.BlockSpec((block, layers, out_rows, depth), lambda i: (i, 0, 0, 0))
    out_shape = jax.ShapeDtypeStruct((members, layers, out_rows, depth), jnp.float32)
    return pl.pallas_call(
        functools.partial(stencil_kernel, rim),
        grid=(members // block,),
        in_specs=[
            whole(halo),
            pl.BlockSpec((block, layers, out_rows, depth), lambda i: (i, 0, 0, 0)),
            *[whole(f) for f in fields],
        ],
        out_specs=[out_spec, out_spec, out_spec],
        out_shape=[out_shape, out_shape, out_shape],
    )(halo, log_perm, *fields)


def halo_kernel(rim, lp_ref, f0, f1, f2, f3, in_ref, out_ref, send_sem, recv_sem):
    members, layers, rows, depth = lp_ref.shape
    lp_count = members * layers
    for side, first in ((0, 0), (1, rows - rim)):
        for r in range(rim):
            out_ref[side, r, 0:lp_count, :] = lp_ref[:, :, first + r, :].reshape(lp_count, depth)
            for fi, f_ref in enumerate((f0, f1, f2, f3)):
                at = lp_count + fi * layers
                out_ref[side, r, at:at + layers, :] = f_ref[:, first + r, :]
    tile_count = lax.axis_size("tile")
    me_t = lax.axis_index("tile")
    me_m = lax.axis_index("member")
    mesh_ids = pl.DeviceIdType.MESH
    left = lax.rem(me_t + tile_count - 1, tile_count)
    right = lax.rem(me_t + 1, tile_count)
    barrier = pltpu.get_barrier_semaphore()
    for peer in (left, right):
        pl.semaphore_signal(barrier, 1, device_id=(peer, me_m), device_id_type=mesh_ids)
    pl.semaphore_wait(barrier, 2)
    to_right = pltpu.make_async_remote_copy(
        src_ref=out_ref.at[1], dst_ref=in_ref.at[0], send_sem=send_sem.at[1],
        recv_sem=recv_sem.at[0], device_id=(right, me_m), device_id_type=mesh_ids,
    )
    to_left = pltpu.make_async_remote_copy(
        src_ref=out_ref.at[0], dst_ref=in_ref.at[1], send_sem=send_sem.at[0],
        recv_sem=recv_sem.at[1], device_id=(left, me_m), device_id_type=mesh_ids,
    )
    to_right.start()
    to_left.start()
    to_right.wait()
    to_left.wait()


def halo_exchange(log_perm, fields, rim):
    members, layers, rows, depth = log_perm.shape
    halo_shape = (2, rim, (members + len(fields)) * layers, depth)
    vmem = pl.BlockSpec(memory_space=pltpu.VMEM)
    return pl.pallas_call(
        functools.partial(halo_kernel, rim),
        out_shape=jax.ShapeDtypeStruct(halo_shape, log_perm.dtype),
        in_specs=[vmem] * (1 + len(fields)),
        out_specs=vmem,
        scratch_shapes=[
            pltpu.VMEM(halo_shape, log_perm.dtype),
            pltpu.SemaphoreType.DMA((2,)),
            pltpu.SemaphoreType.DMA((2,)),
        ],
        compiler_params=pltpu.CompilerParams(collective_id=1, has_side_effects=True),
    )(log_perm, *fields)


def rates_exchange(pieces, member_count):
    tile_count, rows, lanes = pieces.shape
    vmem = pl.BlockSpec(memory_space=pltpu.VMEM)
    return pl.pallas_call(
        functools.partial(exchange_kernel, member_count),
        out_shape=jax.ShapeDtypeStruct((tile_count, rows * member_count, lanes), jnp.float32),
        in_specs=[vmem],
        out_specs=vmem,
        scratch_shapes=[
            pltpu.VMEM((tile_count, rows, lanes), jnp.float32),
            pltpu.VMEM((rows * member_count, lanes), jnp.float32),
            pltpu.VMEM((member_count, rows * member_count, lanes), jnp.float32),
            pltpu.SemaphoreType.DMA((tile_count,)),
            pltpu.SemaphoreType.DMA((tile_count,)),
            pltpu.SemaphoreType.DMA((member_count,)),
            pltpu.SemaphoreType.DMA((member_count,)),
            pltpu.SemaphoreType.DMA((tile_count,)),
            pltpu.SemaphoreType.DMA((tile_count,)),
        ],
        compiler_params=pltpu.CompilerParams(collective_id=0, has_side_effects=True),
    )(pieces)


def per_device(
    log_perm,
    start_pressure,
    start_sat,
    source,
    storage,
    well_press,
    perf_cell,
    perf_well,
    perf_count,
    observed,
    obs_var,
    obs_noise,
):
    local_count, layers, strip_width, strip_depth = log_perm.shape
    tile_count = lax.axis_size("tile")
    members = local_count * lax.axis_size("member")
    well_count = well_press.shape[0]
    well_share = well_count // tile_count
    tile_rank = lax.axis_index("tile")
    member_rank = lax.axis_index("member")
    rim = SWEEPS + 1
    fields = (start_pressure, start_sat, source, storage)

    incoming = halo_exchange(log_perm, fields, rim)
    incoming, log_perm_after = lax.optimization_barrier((incoming, log_perm))
    halo = incoming
    column = tile_rank * strip_width - rim + jnp.arange(strip_width + 2 * rim, dtype=jnp.int32)
    inside = ((column >= 0) & (column < strip_width * tile_count)).astype(jnp.float32)
    pressure, saturation, mobility = stencil(halo, log_perm, fields, rim)
    cell_count = layers * strip_width * strip_depth
    plane_rows = layers * strip_width
    cell_row = perf_cell // strip_depth
    cell_col = lax.rem(perf_cell, strip_depth)
    col_pick = (jnp.arange(strip_depth, dtype=jnp.int32)[:, None] == cell_col[None, :]).astype(
        jnp.float32
    )
    row_pick = jnp.arange(plane_rows, dtype=jnp.int32)[:, None] == cell_row[None, :]

    def pick_cells(values_in):
        by_col = jnp.dot(
            values_in.reshape(local_count * plane_rows, strip_depth), col_pick,
            precision=lax.Precision.HIGHEST, preferred_element_type=jnp.float32,
        ).reshape(local_count, plane_rows, -1)
        return jnp.sum(jnp.where(row_pick[None], by_col, 0.0), axis=1)

    perf_mob = pick_cells(mobility)
    perf_press = pick_cells(pressure)
    selector = (perf_well[:, None] == jnp.arange(well_count, dtype=jnp.int32)[None, :]).astype(
        jnp.float32
    )
    perf_bhp = jnp.dot(selector, well_press, precision=lax.Precision.HIGHEST)
    live_mask = (jnp.arange(perf_cell.shape[0], dtype=jnp.int32) < perf_count[0]).astype(
        jnp.float32
    )
    perf_terms = perf_mob * (perf_press - perf_bhp[None]) * live_mask[None]
    member_root = (members - 1) ** 0.5
    spread = jnp.sqrt(INFLATION * obs_var)
    member_count = lax.axis_size("member")
    contract_slots = (((0,), (1,)), ((), ()))
    pieces = lax.dot_general(
        selector, perf_terms, contract_slots, precision=lax.Precision.HIGHEST,
        preferred_element_type=jnp.float32,
    ).reshape(tile_count, well_share * local_count // 128, 128)
    full = rates_exchange(pieces, member_count)
    own_block = lax.dynamic_index_in_dim(full, tile_rank, 0, keepdims=False)
    well_rates = lax.dynamic_slice_in_dim(own_block, member_rank * local_count, local_count, 1).T
    rates_t = full.reshape(well_count, members)
    mean_rate = jnp.sum(rates_t, 1) / members
    scaled_t = (rates_t - mean_rate[:, None]) / (spread * member_root)[:, None]
    rates_own_t = lax.dynamic_slice_in_dim(rates_t, member_rank * local_count, local_count, 1)
    innov_own_t = (observed[:, None] - rates_own_t) / spread[:, None] + obs_noise.T
    contract_wells = (((0,), (0,)), ((), ()))
    gram_matrix = lax.dot_general(
        scaled_t, scaled_t, contract_wells, precision=lax.Precision.HIGHEST,
        preferred_element_type=jnp.float32,
    )
    cross_matrix = lax.dot_general(
        scaled_t, innov_own_t, contract_wells, precision=lax.Precision.HIGHEST,
        preferred_element_type=jnp.float32,
    )
    weights_low = solve_spd(gram_matrix, cross_matrix).astype(jnp.bfloat16)
    anomaly = (log_perm_after / member_root).astype(jnp.bfloat16).transpose(1, 2, 0, 3)
    anomaly_parts = [anomaly]
    for shift in range(1, member_count):
        pairs = [(i, (i + shift) % member_count) for i in range(member_count)]
        anomaly_parts.append(lax.ppermute(anomaly, "member", pairs))
    anomaly_all = jnp.concatenate(anomaly_parts, axis=2)
    own_cols = jnp.concatenate(
        [
            lax.dynamic_slice_in_dim(
                weights_low, lax.rem(member_rank - shift + member_count, member_count) * local_count,
                local_count, 0,
            )
            for shift in range(member_count)
        ],
        axis=0,
    )
    contract = (((0,), (2,)), ((), ()))
    update_sum = lax.dot_general(own_cols, anomaly_all, contract, preferred_element_type=jnp.float32)
    new_log_perm = log_perm + update_sum
    return (new_log_perm, pressure, saturation, well_rates)


def solution(mesh):
    return jax.shard_map(
        per_device,
        mesh=mesh,
        in_specs=(
            P("member", None, "tile", None),
            P(None, "tile", None),
            P(None, "tile", None),
            P(None, "tile", None),
            P(None, "tile", None),
            P(),
            P("tile"),
            P("tile"),
            P("tile"),
            P(),
            P(),
            P("member", None),
        ),
        out_specs=(
            P("member", None, "tile", None),
            P("member", None, "tile", None),
            P("member", None, "tile", None),
            P("member", "tile"),
        ),
        check_vma=False,
    )
```

```python
import functools

import jax
import jax.numpy as jnp
from jax import lax
from jax.experimental import pallas as pl
from jax.experimental.pallas import tpu as pltpu
from jax.sharding import PartitionSpec as P

SWEEPS = 2


VERTICAL = 0.5
VISCOSITY_RATIO = 2.0
STEP_COEF = 0.1
INFLATION = 4.0


def extended_2(block, sides, width):
    for axis, dim in sides:
        count = lax.axis_size(axis)
        forward = [(i, i + 1) for i in range(count - 1)]
        backward = [(target, source) for source, target in forward]
        low = lax.ppermute(
            lax.slice_in_dim(block, block.shape[dim] - width, None, axis=dim), axis, forward
        )
        high = lax.ppermute(lax.slice_in_dim(block, 0, width, axis=dim), axis, backward)
        block = jnp.concatenate([low, block, high], axis=dim)
    return block


def harmonic(lower_val, upper_val):
    return 2.0 * lower_val * upper_val / (lower_val + upper_val)


def pad_face(values_in, along_dim, before):
    widths = [(0, 0)] * values_in.ndim
    widths[along_dim] = (1, 0) if before else (0, 1)
    return jnp.pad(values_in, widths)


def slide_by(values_in, along_dim, before):
    extent = values_in.shape[along_dim]
    if before:
        remain = lax.slice_in_dim(values_in, 0, extent - 1, axis=along_dim)
    else:
        remain = lax.slice_in_dim(values_in, 1, extent, axis=along_dim)
    return pad_face(remain, along_dim, before)


def face_terms(permeab, inside):
    face_x = (
        harmonic(permeab[:, :, :-1, :], permeab[:, :, 1:, :]) * (inside[:-1] * inside[1:])[:, None]
    )
    face_y = harmonic(permeab[:, :, :, :-1], permeab[:, :, :, 1:])
    face_z = VERTICAL * harmonic(permeab[:, :-1], permeab[:, 1:])
    return (face_x, face_y, face_z)


def neighbours(face_sets, values_in):
    flow_sum = 0.0
    weight_sum = 0.0
    for faces_dim, along_dim in zip(face_sets, (2, 3, 1)):
        lower = pad_face(faces_dim, along_dim, True)
        upper = pad_face(faces_dim, along_dim, False)
        flow_sum = (
            flow_sum
            + lower * slide_by(values_in, along_dim, True)
            + upper * slide_by(values_in, along_dim, False)
        )
        weight_sum = weight_sum + lower + upper
    return (flow_sum, weight_sum)


def jacobi(pressure, baseline, storage_term, face_sets):
    flow_sum, weight_sum = neighbours(face_sets, pressure)
    return (baseline + flow_sum) / (storage_term + weight_sum)


def water_frac(values_in):
    squared = values_in * values_in
    return squared / (squared + VISCOSITY_RATIO * (1.0 - values_in) * (1.0 - values_in))


def transport(pressure, saturation, face_sets):
    fraction = water_frac(saturation)
    change = 0.0
    for faces_dim, along_dim in zip(face_sets, (2, 3, 1)):
        extent = pressure.shape[along_dim]
        lower_press = lax.slice_in_dim(pressure, 0, extent - 1, axis=along_dim)
        upper_press = lax.slice_in_dim(pressure, 1, extent, axis=along_dim)
        lower_frac = lax.slice_in_dim(fraction, 0, extent - 1, axis=along_dim)
        upper_frac = lax.slice_in_dim(fraction, 1, extent, axis=along_dim)
        velocity = faces_dim * (lower_press - upper_press)
        carried = velocity * jnp.where(velocity > 0, lower_frac, upper_frac)
        change = change + pad_face(carried, along_dim, True) - pad_face(carried, along_dim, False)
    return saturation + STEP_COEF * change


def solve_spd(gram_matrix, cross_matrix):
    factor = lax.linalg.cholesky(
        gram_matrix + jnp.eye(gram_matrix.shape[0], dtype=jnp.float32), symmetrize_input=False
    )
    halfway = lax.linalg.triangular_solve(factor, cross_matrix, left_side=True, lower=True)
    return lax.linalg.triangular_solve(
        factor, halfway, left_side=True, lower=True, transpose_a=True
    )


def trim_rim(values_in, rim_cut):
    return values_in[:, :, rim_cut : values_in.shape[2] - rim_cut, :]


def exchange_kernel(member_count, part_ref, full_ref,
                    recv_a, own_blk, recv_m, send_a, recv_a_sem, send_m, recv_m_sem, send_t, recv_t_sem):
    tile_count = part_ref.shape[0]
    me_t = lax.axis_index("tile")
    me_m = lax.axis_index("member")
    mesh_ids = pl.DeviceIdType.MESH

    barrier = pltpu.get_barrier_semaphore()

    def greet_tile(k, carry):
        pl.semaphore_signal(
            barrier, 1, device_id=(lax.rem(me_t + k, tile_count), me_m), device_id_type=mesh_ids
        )
        return carry

    def greet_member(k, carry):
        pl.semaphore_signal(
            barrier, 1, device_id=(me_t, lax.rem(me_m + k, member_count)), device_id_type=mesh_ids
        )
        return carry

    lax.fori_loop(1, tile_count, greet_tile, 0)
    lax.fori_loop(1, member_count, greet_member, 0)
    pl.semaphore_wait(barrier, tile_count + member_count - 2)

    def copy_a(dst_t, src_t):
        return pltpu.make_async_remote_copy(
            src_ref=part_ref.at[dst_t], dst_ref=recv_a.at[src_t],
            send_sem=send_a.at[dst_t], recv_sem=recv_a_sem.at[src_t],
            device_id=(dst_t, me_m), device_id_type=mesh_ids,
        )

    def start_a(k, carry):
        copy_a(lax.rem(me_t + k, tile_count), me_t).start()
        return carry

    lax.fori_loop(1, tile_count, start_a, 0)

    def wait_a(k, acc):
        src_t = lax.rem(me_t + k, tile_count)
        copy_a(me_t, src_t).wait_recv()
        return acc + recv_a[src_t]

    acc = lax.fori_loop(1, tile_count, wait_a, part_ref[me_t])

    def wait_a_send(k, carry):
        copy_a(lax.rem(me_t + k, tile_count), me_t).wait_send()
        return carry

    lax.fori_loop(1, tile_count, wait_a_send, 0)

    groups = part_ref.shape[2] // member_count
    lane_ids = lax.broadcasted_iota(jnp.int32, acc.shape, 1)
    for q in range(member_count):
        moved = pltpu.roll(acc, lax.rem((me_m - q + member_count) * groups, part_ref.shape[2]), 1)
        own_blk[pl.ds(q, acc.shape[0], stride=member_count), :] = jnp.where(
            lane_ids // groups == me_m, moved, 0.0
        )
    acc = own_blk[...]

    def copy_m(dst_m, src_m):
        return pltpu.make_async_remote_copy(
            src_ref=own_blk, dst_ref=recv_m.at[src_m],
            send_sem=send_m.at[dst_m], recv_sem=recv_m_sem.at[src_m],
            device_id=(me_t, dst_m), device_id_type=mesh_ids,
        )

    def start_m(k, carry):
        copy_m(lax.rem(me_m + k, member_count), me_m).start()
        return carry

    lax.fori_loop(1, member_count, start_m, 0)

    def wait_m(k, total):
        src_m = lax.rem(me_m + k, member_count)
        copy_m(me_m, src_m).wait_recv()
        return total + recv_m[src_m]

    full_ref[me_t] = lax.fori_loop(1, member_count, wait_m, acc)

    def wait_m_send(k, carry):
        copy_m(lax.rem(me_m + k, member_count), me_m).wait_send()
        return carry

    lax.fori_loop(1, member_count, wait_m_send, 0)

    def copy_t(dst_t, src_t):
        return pltpu.make_async_remote_copy(
            src_ref=full_ref.at[src_t], dst_ref=full_ref.at[src_t],
            send_sem=send_t.at[dst_t], recv_sem=recv_t_sem.at[src_t],
            device_id=(dst_t, me_m), device_id_type=mesh_ids,
        )

    def start_t(k, carry):
        copy_t(lax.rem(me_t + k, tile_count), me_t).start()
        return carry

    lax.fori_loop(1, tile_count, start_t, 0)

    def wait_t(k, carry):
        copy_t(me_t, lax.rem(me_t + k, tile_count)).wait_recv()
        return carry

    lax.fori_loop(1, tile_count, wait_t, 0)

    def wait_t_send(k, carry):
        copy_t(lax.rem(me_t + k, tile_count), me_t).wait_send()
        return carry

    lax.fori_loop(1, tile_count, wait_t_send, 0)


def stencil_kernel(rim, halo_ref, lp_mid, f0, f1, f2, f3, press_ref, sat_ref, mob_ref):
    f_mid = jnp.stack([f0[...], f1[...], f2[...], f3[...]])
    strip_width = lp_mid.shape[2]
    column = lax.axis_index("tile") * strip_width - rim + jnp.arange(
        strip_width + 2 * rim, dtype=jnp.int32
    )
    inside = ((column >= 0) & (column < strip_width * lax.axis_size("tile"))).astype(jnp.float32)
    block, layers = lp_mid.shape[0], lp_mid.shape[1]
    field_count = 4
    lp_rows = pl.ds(pl.multiple_of(pl.program_id(0) * block * layers, block * layers), block * layers)
    field_first = halo_ref.shape[2] - field_count * layers

    def halo_piece(side, rows, shape):
        return [halo_ref[side, r, rows, :].reshape(shape) for r in range(rim)]

    lp_shape = (block, layers, 1, lp_mid.shape[3])
    f_shape = (field_count, layers, 1, f_mid.shape[3])
    f_rows = pl.ds(field_first, field_count * layers)
    permeab = jnp.exp(jnp.concatenate(
        halo_piece(0, lp_rows, lp_shape) + [lp_mid[...]] + halo_piece(1, lp_rows, lp_shape), axis=2
    ))
    face_sets = face_terms(permeab, inside)
    fields = jnp.concatenate(
        halo_piece(0, f_rows, f_shape) + [f_mid] + halo_piece(1, f_rows, f_shape), axis=2
    )
    press_ext = fields[0]
    sat_ext = fields[1]
    source_ext = fields[2]
    storage_ext = fields[3]
    baseline = (source_ext + storage_ext * press_ext)[None]
    storage_term = jnp.where(inside[None, :, None] > 0.0, storage_ext, 1.0)[None]
    pressure = jnp.broadcast_to(press_ext[None], permeab.shape)
    for sweep_idx in range(SWEEPS):
        pressure = jacobi(pressure, baseline, storage_term, face_sets)
    saturation = trim_rim(transport(pressure, sat_ext[None], face_sets), rim)
    press_ref[...] = trim_rim(pressure, rim)
    sat_ref[...] = saturation
    mob_ref[...] = trim_rim(permeab, rim) * water_frac(saturation)


def stencil(halo, log_perm, fields, rim):
    members, layers, out_rows, depth = log_perm.shape
    block = 4

    def whole(part):
        return pl.BlockSpec(part.shape, lambda i: (0,) * part.ndim)

    out_spec = pl.BlockSpec((block, layers, out_rows, depth), lambda i: (i, 0, 0, 0))
    out_shape = jax.ShapeDtypeStruct((members, layers, out_rows, depth), jnp.float32)
    return pl.pallas_call(
        functools.partial(stencil_kernel, rim),
        grid=(members // block,),
        in_specs=[
            whole(halo),
            pl.BlockSpec((block, layers, out_rows, depth), lambda i: (i, 0, 0, 0)),
            *[whole(f) for f in fields],
        ],
        out_specs=[out_spec, out_spec, out_spec],
        out_shape=[out_shape, out_shape, out_shape],
    )(halo, log_perm, *fields)


def halo_kernel(rim, lp_ref, f0, f1, f2, f3, in_ref, out_ref, send_sem, recv_sem):
    members, layers, rows, depth = lp_ref.shape
    lp_count = members * layers
    for side, first in ((0, 0), (1, rows - rim)):
        for r in range(rim):
            out_ref[side, r, 0:lp_count, :] = lp_ref[:, :, first + r, :].reshape(lp_count, depth)
            for fi, f_ref in enumerate((f0, f1, f2, f3)):
                at = lp_count + fi * layers
                out_ref[side, r, at:at + layers, :] = f_ref[:, first + r, :]
    tile_count = lax.axis_size("tile")
    me_t = lax.axis_index("tile")
    me_m = lax.axis_index("member")
    mesh_ids = pl.DeviceIdType.MESH
    left = lax.rem(me_t + tile_count - 1, tile_count)
    right = lax.rem(me_t + 1, tile_count)
    barrier = pltpu.get_barrier_semaphore()
    for peer in (left, right):
        pl.semaphore_signal(barrier, 1, device_id=(peer, me_m), device_id_type=mesh_ids)
    pl.semaphore_wait(barrier, 2)
    to_right = pltpu.make_async_remote_copy(
        src_ref=out_ref.at[1], dst_ref=in_ref.at[0], send_sem=send_sem.at[1],
        recv_sem=recv_sem.at[0], device_id=(right, me_m), device_id_type=mesh_ids,
    )
    to_left = pltpu.make_async_remote_copy(
        src_ref=out_ref.at[0], dst_ref=in_ref.at[1], send_sem=send_sem.at[0],
        recv_sem=recv_sem.at[1], device_id=(left, me_m), device_id_type=mesh_ids,
    )
    to_right.start()
    to_left.start()
    to_right.wait()
    to_left.wait()


def halo_exchange(log_perm, fields, rim):
    members, layers, rows, depth = log_perm.shape
    halo_shape = (2, rim, (members + len(fields)) * layers, depth)
    vmem = pl.BlockSpec(memory_space=pltpu.VMEM)
    return pl.pallas_call(
        functools.partial(halo_kernel, rim),
        out_shape=jax.ShapeDtypeStruct(halo_shape, log_perm.dtype),
        in_specs=[vmem] * (1 + len(fields)),
        out_specs=vmem,
        scratch_shapes=[
            pltpu.VMEM(halo_shape, log_perm.dtype),
            pltpu.SemaphoreType.DMA((2,)),
            pltpu.SemaphoreType.DMA((2,)),
        ],
        compiler_params=pltpu.CompilerParams(collective_id=1, has_side_effects=True),
    )(log_perm, *fields)


def rates_exchange(pieces, member_count):
    tile_count, rows, lanes = pieces.shape
    vmem = pl.BlockSpec(memory_space=pltpu.VMEM)
    return pl.pallas_call(
        functools.partial(exchange_kernel, member_count),
        out_shape=jax.ShapeDtypeStruct((tile_count, rows * member_count, lanes), jnp.float32),
        in_specs=[vmem],
        out_specs=vmem,
        scratch_shapes=[
            pltpu.VMEM((tile_count, rows, lanes), jnp.float32),
            pltpu.VMEM((rows * member_count, lanes), jnp.float32),
            pltpu.VMEM((member_count, rows * member_count, lanes), jnp.float32),
            pltpu.SemaphoreType.DMA((tile_count,)),
            pltpu.SemaphoreType.DMA((tile_count,)),
            pltpu.SemaphoreType.DMA((member_count,)),
            pltpu.SemaphoreType.DMA((member_count,)),
            pltpu.SemaphoreType.DMA((tile_count,)),
            pltpu.SemaphoreType.DMA((tile_count,)),
        ],
        compiler_params=pltpu.CompilerParams(collective_id=0, has_side_effects=True),
    )(pieces)


def per_device(
    log_perm,
    start_pressure,
    start_sat,
    source,
    storage,
    well_press,
    perf_cell,
    perf_well,
    perf_count,
    observed,
    obs_var,
    obs_noise,
):
    local_count, layers, strip_width, strip_depth = log_perm.shape
    tile_count = lax.axis_size("tile")
    members = local_count * lax.axis_size("member")
    well_count = well_press.shape[0]
    well_share = well_count // tile_count
    tile_rank = lax.axis_index("tile")
    member_rank = lax.axis_index("member")
    rim = SWEEPS + 1
    fields = (start_pressure, start_sat, source, storage)

    incoming = halo_exchange(log_perm, fields, rim)
    halo = incoming
    column = tile_rank * strip_width - rim + jnp.arange(strip_width + 2 * rim, dtype=jnp.int32)
    inside = ((column >= 0) & (column < strip_width * tile_count)).astype(jnp.float32)
    pressure, saturation, mobility = stencil(halo, log_perm, fields, rim)
    cell_count = layers * strip_width * strip_depth
    plane_rows = layers * strip_width
    cell_row = perf_cell // strip_depth
    cell_col = lax.rem(perf_cell, strip_depth)
    col_pick = (jnp.arange(strip_depth, dtype=jnp.int32)[:, None] == cell_col[None, :]).astype(
        jnp.float32
    )
    row_pick = jnp.arange(plane_rows, dtype=jnp.int32)[:, None] == cell_row[None, :]

    def pick_cells(values_in):
        by_col = jnp.dot(
            values_in.reshape(local_count * plane_rows, strip_depth), col_pick,
            precision=lax.Precision.HIGHEST, preferred_element_type=jnp.float32,
        ).reshape(local_count, plane_rows, -1)
        return jnp.sum(jnp.where(row_pick[None], by_col, 0.0), axis=1)

    perf_mob = pick_cells(mobility)
    perf_press = pick_cells(pressure)
    selector = (perf_well[:, None] == jnp.arange(well_count, dtype=jnp.int32)[None, :]).astype(
        jnp.float32
    )
    perf_bhp = jnp.dot(selector, well_press, precision=lax.Precision.HIGHEST)
    live_mask = (jnp.arange(perf_cell.shape[0], dtype=jnp.int32) < perf_count[0]).astype(
        jnp.float32
    )
    perf_terms = perf_mob * (perf_press - perf_bhp[None]) * live_mask[None]
    member_root = (members - 1) ** 0.5
    spread = jnp.sqrt(INFLATION * obs_var)
    member_count = lax.axis_size("member")
    contract_slots = (((0,), (1,)), ((), ()))
    pieces = lax.dot_general(
        selector, perf_terms, contract_slots, precision=lax.Precision.HIGHEST,
        preferred_element_type=jnp.float32,
    ).reshape(tile_count, well_share * local_count // 128, 128)
    full = rates_exchange(pieces, member_count)
    own_block = lax.dynamic_index_in_dim(full, tile_rank, 0, keepdims=False)
    well_rates = lax.dynamic_slice_in_dim(own_block, member_rank * local_count, local_count, 1).T
    rates_t = full.reshape(well_count, members)
    mean_rate = jnp.sum(rates_t, 1) / members
    scaled_t = (rates_t - mean_rate[:, None]) / (spread * member_root)[:, None]
    rates_own_t = lax.dynamic_slice_in_dim(rates_t, member_rank * local_count, local_count, 1)
    innov_own_t = (observed[:, None] - rates_own_t) / spread[:, None] + obs_noise.T
    contract_wells = (((0,), (0,)), ((), ()))
    gram_matrix = lax.dot_general(
        scaled_t, scaled_t, contract_wells, precision=lax.Precision.HIGHEST,
        preferred_element_type=jnp.float32,
    )
    cross_matrix = lax.dot_general(
        scaled_t, innov_own_t, contract_wells, precision=lax.Precision.HIGHEST,
        preferred_element_type=jnp.float32,
    )
    weights_low = solve_spd(gram_matrix, cross_matrix).astype(jnp.bfloat16)
    anomaly = (log_perm / member_root).astype(jnp.bfloat16).transpose(1, 2, 0, 3)
    anomaly_parts = [anomaly]
    for shift in range(1, member_count):
        pairs = [(i, (i + shift) % member_count) for i in range(member_count)]
        anomaly_parts.append(lax.ppermute(anomaly, "member", pairs))
    anomaly_all = jnp.concatenate(anomaly_parts, axis=2)
    own_cols = jnp.concatenate(
        [
            lax.dynamic_slice_in_dim(
                weights_low, lax.rem(member_rank - shift + member_count, member_count) * local_count,
                local_count, 0,
            )
            for shift in range(member_count)
        ],
        axis=0,
    )
    contract = (((0,), (2,)), ((), ()))
    update_sum = lax.dot_general(own_cols, anomaly_all, contract, preferred_element_type=jnp.float32)
    new_log_perm = log_perm + update_sum
    return (new_log_perm, pressure, saturation, well_rates)


def solution(mesh):
    return jax.shard_map(
        per_device,
        mesh=mesh,
        in_specs=(
            P("member", None, "tile", None),
            P(None, "tile", None),
            P(None, "tile", None),
            P(None, "tile", None),
            P(None, "tile", None),
            P(),
            P("tile"),
            P("tile"),
            P("tile"),
            P(),
            P(),
            P("member", None),
        ),
        out_specs=(
            P("member", None, "tile", None),
            P("member", None, "tile", None),
            P("member", None, "tile", None),
            P("member", "tile"),
        ),
        check_vma=False,
    )
```
